32 devices in a mesh: ctx: 8 (over y, x, core), fsdp: 4 (over z).
Axes of the slice: x: 2, y: 2, z: 4, core: 2. Of those that a mesh axis runs over, the one named last changes fastest.
Arguments:
- hidden_in: bfloat16 [4, 1024, 2048], P('fsdp', 'ctx'), may hold values from -18 to 18
- out_grad: bfloat16 [4, 1024, 2048], P('fsdp', 'ctx'), may hold values from -6 to 6
- positions: int32 [4, 1024], P('fsdp', 'ctx'), may hold values from 0 to 1023, as said below
- block_order: int32 [16], replicated, may hold values from 0 to 15, as said below
- attn_gain: float32 [2048], replicated, may hold values from 0.25 to 1.75
- ffn_gain: float32 [2048], replicated, may hold values from 0.25 to 1.75
- qkv_weight: bfloat16 [2048, 3072], P('fsdp'), may hold values from -1 to 1
- out_weight: bfloat16 [2048, 2048], P('fsdp'), may hold values from -0.5 to 0.5
- ffn_weight: bfloat16 [2048, 3, 8192], P(None, None, 'fsdp'), may hold values from -0.125 to 0.125
Outputs:
- hidden_out: bfloat16 [4, 1024, 2048], P('fsdp', 'ctx')
- input_grad: float32 [4, 1024, 2048], P('fsdp', 'ctx')
- qkv_weight_grad: float32 [2048, 3072], P(('ctx', 'fsdp'))
- out_weight_grad: float32 [2048, 2048], P(('ctx', 'fsdp'))
- ffn_weight_grad: float32 [2048, 3, 8192], P('ctx', None, 'fsdp')
- attn_gain_grad: float32 [2048], P(('ctx', 'fsdp'))
- ffn_gain_grad: float32 [2048], P(('ctx', 'fsdp'))
The draws below stay inside these ranges and needn't reach their ends.
Inputs may be any that keep to these rules, and one draw needn't show every extreme that they name: `block_order`: the two slots 2c and 2c + 1 hold two blocks whose numbers add up to 15, and every block number appears once. In initial token order, a sequence's positions rise by one from token to token and restart at 0 at its first token and at the start of each packed document; the first sequence is a single document; they are listed in storage order.
All inputs are finite; a program needn't handle non-finite values.
Results may differ from the reference program's by a relative error of at most 0.03.
Values may be sent and summed in bfloat16 or wider, within the bound.
No kernel may reach another device: no remote copies, remote signals or barrier semaphores. Data moves between devices by JAX's collectives and lax.ppermute only.
A program may use at most 576 MiB of HBM per device.

```python
import math
import jax
import jax.numpy as jnp
from jax import lax

D = 2048
H = 32
KV = 8
HD = 64
FF = 8192
BLOCK = 64
BLOCKS = 16
SEQ = 1024
SEQS = 4


def mirrored_order(key):
    inner = jax.random.fold_in(key, 7)
    half_count = BLOCKS // 2
    paired = jax.random.permutation(jax.random.fold_in(inner, 1), half_count).astype(jnp.int32)
    flipped = jax.random.randint(jax.random.fold_in(inner, 2), (half_count,), 0, 2)
    first_slot = jnp.where(flipped == 1, paired, BLOCKS - 1 - paired)
    second_slot = BLOCKS - 1 - first_slot
    return jnp.stack([first_slot, second_slot], axis=1).reshape(BLOCKS).astype(jnp.int32)


def draw_block_order(key, part):
    return mirrored_order(key)


def draw_positions(key, part):
    order = mirrored_order(key)
    row_ids = jnp.arange(SEQ, dtype=jnp.int32)
    seq_ids = jnp.arange(SEQS, dtype=jnp.int32)
    starts = jax.random.randint(jax.random.fold_in(key, 13), (SEQS, SEQ), 0, 512) == 0
    starts = starts & (seq_ids[:, None] > 0) | (row_ids[None, :] == 0)
    doc_start = lax.cummax(jnp.where(starts, row_ids[None, :], 0), axis=1)
    in_doc = row_ids[None, :] - doc_start
    stored = (order[:, None] * BLOCK + jnp.arange(BLOCK, dtype=jnp.int32)[None, :]).reshape(SEQ)
    return jnp.take(in_doc, stored, axis=1).astype(jnp.int32)


def draw_hidden_in(key, part):
    noise = jax.random.truncated_normal(jax.random.fold_in(key, 41), -6.0, 6.0, (SEQS, SEQ, D), jnp.float32)
    return noise.astype(jnp.bfloat16)


def draw_qkv_weight(key, part):
    columns = (H + 2 * KV) * HD
    return (jax.random.truncated_normal(jax.random.fold_in(key, 59), -4.0, 4.0, (D, columns), jnp.float32) / math.sqrt(D)).astype(jnp.bfloat16)


def levels(key, extent, pieces, least, top_value):
    gain = 1.0
    for axis_at, blocks in pieces:
        draws = jax.random.uniform(jax.random.fold_in(jax.random.fold_in(key, 6), axis_at), (blocks,), jnp.float32, least / len(pieces), top_value / len(pieces))
        gain = gain * jnp.repeat(jnp.exp(draws), extent[axis_at] // blocks).reshape((-1,) + (1,) * (len(extent) - 1 - axis_at))
    return gain


def centred(stream_key, shape, deviation, bound, shards=(), kind=jnp.bfloat16):
    result = jax.random.normal(stream_key, shape, jnp.float32) * deviation
    if len(shards) > 0:
        result = levels(stream_key, shape, shards, -0.22, 0.18) * result
    return jnp.clip(result, min=-bound, max=bound).astype(kind)


def setup_inputs(seed: int = 0) -> dict:
    arg_keys = jax.random.split(jax.random.key(seed), 10)
    return {
        "hidden_in": draw_hidden_in(jax.random.fold_in(arg_keys[9], 71), 0),
        "out_grad": centred(arg_keys[1], (SEQS, SEQ, D), 1.0, 6.0, ((0, 4), (1, 8))),
        "positions": draw_positions(jax.random.fold_in(arg_keys[9], 71), 0),
        "block_order": draw_block_order(jax.random.fold_in(arg_keys[9], 71), 0),
        "attn_gain": jnp.clip(1.0 + 0.15 * jax.random.normal(arg_keys[4], (D,), jnp.float32), 0.25, 1.75),
        "ffn_gain": jnp.clip(1.0 + 0.15 * jax.random.normal(arg_keys[5], (D,), jnp.float32), 0.25, 1.75),
        "qkv_weight": draw_qkv_weight(jax.random.fold_in(arg_keys[9], 71), 0),
        "out_weight": centred(arg_keys[7], (D, H * HD), (H * HD * 64 // SEQ) ** -0.5, 0.5, ((0, 4),)),
        "ffn_weight": centred(arg_keys[8], (D, 3, FF), D ** -0.5, 0.125, ((2, 4),)),
    }


NORM_EPS = 1e-05
ROPE_BASE = 500000.0

def rotate(values, token_places):
    head_dim = values.shape[-1]
    half_dim = head_dim // 2
    frequency = jnp.power(ROPE_BASE, -(jnp.arange(half_dim, dtype=jnp.float32) * 2.0 / head_dim))
    angles = token_places.astype(jnp.float32)[:, None] * frequency[None, :]
    cosine = jnp.concatenate([jnp.cos(angles), jnp.cos(angles)], axis=-1)[:, None, :]
    sine_part = jnp.concatenate([jnp.sin(angles), jnp.sin(angles)], axis=-1)[:, None, :]
    turned = jnp.concatenate([-values[..., half_dim:], values[..., :half_dim]], axis=-1)
    return values * cosine + turned * sine_part

def norm_scale(values):
    return lax.rsqrt(lax.optimization_barrier(jnp.mean(values * values, axis=-1, keepdims=True)) + NORM_EPS)

def one_sequence(hidden_one, grad_one, token_places, anchor, attn_gain, ffn_gain, qkv_weight, out_weight, ffn_weight):
    seq_len = hidden_one.shape[0]
    groups = H // KV
    score_scale = 1.0 / math.sqrt(HD)
    query_block = math.gcd(seq_len, 512)
    blocks = seq_len // query_block
    inputs = hidden_one.astype(jnp.float32)
    scale_one = norm_scale(inputs)
    normed_one = (inputs * scale_one * attn_gain).astype(jnp.bfloat16)
    projected = jnp.dot(normed_one, qkv_weight, preferred_element_type=jnp.float32)
    queries = rotate(projected[:, :H * HD].reshape(seq_len, H, HD), token_places).astype(jnp.bfloat16)
    key_heads = rotate(projected[:, H * HD:(H + KV) * HD].reshape(seq_len, KV, HD), token_places).astype(jnp.bfloat16)
    value_heads = projected[:, (H + KV) * HD:].reshape(seq_len, KV, HD).astype(jnp.bfloat16)
    key_float = lax.optimization_barrier(key_heads).astype(jnp.float32)
    value_float = lax.optimization_barrier(value_heads).astype(jnp.float32)
    query_blocks = queries.reshape(blocks, query_block, KV, groups, HD)
    anchor_blocks = anchor.reshape(blocks, query_block)

    def scores_of(query_part, query_anchor):
        query_float = lax.optimization_barrier(query_part).astype(jnp.float32)
        scores = jnp.einsum('tkgd,skd->kgts', query_float, key_float) * score_scale
        allowed = anchor[None, :] <= query_anchor[:, None]
        return (jnp.where(allowed[None, None], scores, -1e+30), query_float)

    def attend(block_pair):
        query_part, query_anchor = block_pair
        scores, query_float = scores_of(query_part, query_anchor)
        row_top = lax.optimization_barrier(jnp.max(scores, axis=-1))
        row_total = lax.optimization_barrier(jnp.sum(jnp.exp(scores - row_top[..., None]), axis=-1))
        log_total = row_top + jnp.log(row_total)
        weights = lax.optimization_barrier(jnp.exp(scores - log_total[..., None]).astype(jnp.bfloat16))
        attended = jnp.einsum('kgts,skd->tkgd', weights.astype(jnp.float32), value_float)
        return (attended, log_total)
    attended, log_totals = lax.map(attend, (query_blocks, anchor_blocks))
    attended = attended.reshape(seq_len, KV, groups, HD)
    attn_rows = attended.reshape(seq_len, H * HD).astype(jnp.bfloat16)
    residual = inputs + jnp.dot(attn_rows, out_weight.T, preferred_element_type=jnp.float32)
    scale_two = norm_scale(residual)
    normed_two = (residual * scale_two * ffn_gain).astype(jnp.bfloat16)
    gate_w = ffn_weight[:, 0, :]
    up_w = ffn_weight[:, 1, :]
    down_w = ffn_weight[:, 2, :]
    gate_pre = jnp.dot(normed_two, gate_w, preferred_element_type=jnp.float32)
    up_pre = jnp.dot(normed_two, up_w, preferred_element_type=jnp.float32)
    gate_sig = jax.nn.sigmoid(gate_pre)
    activated = (gate_pre * gate_sig * up_pre).astype(jnp.bfloat16)
    output = (residual + jnp.dot(activated, down_w.T, preferred_element_type=jnp.float32)).astype(jnp.bfloat16)
    act_grad = jnp.dot(grad_one, down_w, preferred_element_type=jnp.float32)
    gate_grad = (act_grad * up_pre * gate_sig * (1.0 + gate_pre * (1.0 - gate_sig))).astype(jnp.bfloat16)
    up_grad = (act_grad * gate_pre * gate_sig).astype(jnp.bfloat16)
    normed_two_grad = jnp.dot(gate_grad, gate_w.T, preferred_element_type=jnp.float32) + jnp.dot(up_grad, up_w.T, preferred_element_type=jnp.float32)
    unit_two = residual * scale_two
    ffn_gain_grad = lax.optimization_barrier(jnp.sum(normed_two_grad * unit_two, axis=0))
    scaled_two = ffn_gain * normed_two_grad
    residual_grad = grad_one.astype(jnp.float32) + scale_two * (scaled_two - unit_two * lax.optimization_barrier(jnp.mean(scaled_two * unit_two, axis=-1, keepdims=True)))
    ffn_weight_grad = jnp.stack([jnp.dot(normed_two.T, gate_grad, preferred_element_type=jnp.float32), jnp.dot(normed_two.T, up_grad, preferred_element_type=jnp.float32), jnp.dot(grad_one.T, activated, preferred_element_type=jnp.float32)], axis=1)
    residual_bf = residual_grad.astype(jnp.bfloat16)
    attn_grad = jnp.dot(residual_bf, out_weight, preferred_element_type=jnp.float32).astype(jnp.bfloat16)
    out_weight_grad = jnp.dot(residual_bf.T, attn_rows, preferred_element_type=jnp.float32)
    attn_grad_heads = attn_grad.reshape(seq_len, KV, groups, HD)
    grad_float = lax.optimization_barrier(attn_grad_heads).astype(jnp.float32)
    row_delta = lax.optimization_barrier(jnp.sum(grad_float * attended, axis=-1))
    delta_blocks = row_delta.reshape(blocks, query_block, KV, groups).transpose(0, 2, 3, 1)
    grad_blocks = grad_float.reshape(blocks, query_block, KV, groups, HD)

    def attend_back(carried, block_items):
        key_grad, value_grad = carried
        query_part, query_anchor, grad_part, delta_part, log_total = block_items
        scores, query_float = scores_of(query_part, query_anchor)
        probs = jnp.exp(scores - log_total[..., None])
        probs_bf = lax.optimization_barrier(probs.astype(jnp.bfloat16)).astype(jnp.float32)
        value_grad = value_grad + jnp.einsum('kgts,tkgd->skd', probs_bf, grad_part)
        prob_grad = jnp.einsum('tkgd,skd->kgts', grad_part, value_float)
        score_grad = (probs * (prob_grad - delta_part[..., None]) * score_scale).astype(jnp.bfloat16)
        score_grad = lax.optimization_barrier(score_grad).astype(jnp.float32)
        query_grad = jnp.einsum('kgts,skd->tkgd', score_grad, key_float)
        key_grad = key_grad + jnp.einsum('kgts,tkgd->skd', score_grad, query_float)
        return ((key_grad, value_grad), query_grad)
    zero_kv = jnp.zeros((seq_len, KV, HD), jnp.float32)
    (key_grad, value_grad), query_grads = lax.scan(attend_back, (zero_kv, zero_kv), (query_blocks, anchor_blocks, grad_blocks, delta_blocks, log_totals))
    query_grad = query_grads.reshape(seq_len, H, HD)
    projected_grad = jnp.concatenate([rotate(query_grad, -token_places).reshape(seq_len, H * HD), rotate(key_grad, -token_places).reshape(seq_len, KV * HD), value_grad.reshape(seq_len, KV * HD)], axis=1).astype(jnp.bfloat16)
    normed_one_grad = jnp.dot(projected_grad, qkv_weight.T, preferred_element_type=jnp.float32)
    qkv_weight_grad = jnp.dot(normed_one.T, projected_grad, preferred_element_type=jnp.float32)
    unit_one = inputs * scale_one
    attn_gain_grad = lax.optimization_barrier(jnp.sum(normed_one_grad * unit_one, axis=0))
    scaled_one = attn_gain * normed_one_grad
    input_grad = residual_grad + scale_one * (scaled_one - unit_one * lax.optimization_barrier(jnp.mean(scaled_one * unit_one, axis=-1, keepdims=True)))
    return (output, input_grad, qkv_weight_grad, out_weight_grad, ffn_weight_grad, attn_gain_grad, ffn_gain_grad)

def reference(hidden_in, out_grad, positions, block_order, attn_gain, ffn_gain, qkv_weight, out_weight, ffn_weight):
    seq_len = hidden_in.shape[1]
    row_ids = jnp.arange(seq_len, dtype=jnp.int32)
    anchor = (jnp.take(block_order, row_ids // BLOCK) * BLOCK + row_ids % BLOCK).astype(jnp.int32)

    def sequence_step(grad_sums, block_items):
        hidden_one, grad_one, token_places = block_items
        results = one_sequence(hidden_one, grad_one, token_places, anchor, attn_gain, ffn_gain, qkv_weight, out_weight, ffn_weight)
        grad_sums = tuple((total_grad + new_grad for total_grad, new_grad in zip(grad_sums, results[2:])))
        return (grad_sums, (results[0], results[1]))
    start_sums = (jnp.zeros(qkv_weight.shape, jnp.float32), jnp.zeros(out_weight.shape, jnp.float32), jnp.zeros(ffn_weight.shape, jnp.float32), jnp.zeros(attn_gain.shape, jnp.float32), jnp.zeros(ffn_gain.shape, jnp.float32))
    grad_sums, (outputs, input_grads) = lax.scan(sequence_step, start_sums, (hidden_in, out_grad, positions))
    return (outputs, input_grads, grad_sums[0], grad_sums[1], grad_sums[2], grad_sums[3], grad_sums[4])
```

```python
import math

import jax
import jax.numpy as jnp
from jax import lax
from jax.sharding import PartitionSpec as P

H = 32
KV = 8
HD = 64

NORM_EPS = 1e-05
ROPE_BASE = 500000.0
KEY_STEP = 512


BF = jnp.bfloat16
F32 = jnp.float32


def mm(a, b, dims):
    return lax.dot_general(a, b, (dims, ((), ())), preferred_element_type=F32)


def nn(a, b):
    return mm(a, b, ((1,), (0,)))


def nt(a, b):
    return mm(a, b, ((1,), (1,)))


def tn(a, b):
    return mm(a, b, ((0,), (0,)))


def swap(value, axis, offset):
    count = lax.axis_size(axis)
    return lax.ppermute(value, axis, [(i, i ^ offset) for i in range(count)])


def rotate(values, token_places):
    head_dim = values.shape[-1]
    half_dim = head_dim // 2
    frequency = jnp.power(ROPE_BASE, -(jnp.arange(half_dim, dtype=F32) * 2.0 / head_dim))
    angles = token_places.astype(F32)[:, None] * frequency[None, :]
    cosine = jnp.concatenate([jnp.cos(angles), jnp.cos(angles)], axis=-1)[:, None, :]
    sine_part = jnp.concatenate([jnp.sin(angles), jnp.sin(angles)], axis=-1)[:, None, :]
    turned = jnp.concatenate([-values[..., half_dim:], values[..., :half_dim]], axis=-1)
    return values * cosine + turned * sine_part


def norm_scale(values):
    return lax.rsqrt(jnp.mean(values * values, axis=-1, keepdims=True) + NORM_EPS)


def lookup(entries, row_ids):
    matches = row_ids[:, None] == jnp.arange(entries.shape[0], dtype=jnp.int32)[None, :]
    return jnp.sum(jnp.where(matches, entries[None, :], 0), axis=1)


def anchors_of(block_order, owner, row_count):
    block_len = row_count // 2
    row_ids = owner * row_count + jnp.arange(row_count, dtype=jnp.int32)
    return lookup(block_order, row_ids // block_len) * block_len + row_ids % block_len


def gather_ctx(piece):
    pairs = lax.axis_size("ctx") // 2
    same = {0: piece}
    if pairs == 4:
        half = piece.shape[0] // 2
        same[2] = swap(piece, "ctx", 2)
        same[4] = swap(piece, "ctx", 4)
        top = swap(same[4][:half], "ctx", 2)
        low = swap(same[2][half:], "ctx", 4)
        same[6] = jnp.concatenate([top, low], axis=0)
    else:
        for pair in range(1, pairs):
            same[2 * pair] = swap(piece, "ctx", 2 * pair)
    other = {key + 1: swap(value, "ctx", 1) for key, value in same.items()}
    return {**same, **other}


def gather_weight(weight):
    ctx_count, fsdp_count = lax.axis_size("ctx"), lax.axis_size("fsdp")
    me, plane = lax.axis_index("ctx"), lax.axis_index("fsdp")
    rows, columns = weight.shape
    part = rows // ctx_count
    mine = lax.dynamic_slice(weight, (me * part, 0), (part, columns))
    full = jnp.zeros((rows * fsdp_count, columns), weight.dtype)
    full = lax.dynamic_update_slice(full, weight, (plane * rows, 0))
    for away in range(1, fsdp_count):
        first = swap(mine, "fsdp", away)
        for offset, piece in gather_ctx(first).items():
            start = (plane ^ away) * rows + (me ^ offset) * part
            full = lax.dynamic_update_slice(full, piece, (start, 0))
    return full


def gather_rows(values):
    count = lax.axis_size("fsdp")
    return jnp.concatenate([values] + [swap(values, "fsdp", away) for away in range(1, count)], axis=0)


def columns_to_owner(values):
    count, plane = lax.axis_size("fsdp"), lax.axis_index("fsdp")
    rows, columns = values.shape
    width = columns // count
    out = []
    for away in range(count):
        piece = lax.dynamic_slice(values, (0, (plane ^ away) * width), (rows, width))
        out.append(piece if away == 0 else swap(piece, "fsdp", away))
    return jnp.concatenate(out, axis=0)


def rows_to_owner(values):
    count, plane = lax.axis_size("fsdp"), lax.axis_index("fsdp")
    rows, columns = values.shape
    height = rows // count
    out = jnp.zeros((height, columns * count), values.dtype)
    for away in range(count):
        piece = lax.dynamic_slice(values, ((plane ^ away) * height, 0), (height, columns))
        piece = piece if away == 0 else swap(piece, "fsdp", away)
        out = lax.dynamic_update_slice(out, piece, (0, (plane ^ away) * columns))
    return out


def sum_over_fsdp(values):
    count = lax.axis_size("fsdp")
    rows = values.shape[0] // count
    total = values[:rows]
    for away in range(1, count):
        part = values[away * rows : (away + 1) * rows].astype(BF)
        total = total + swap(part, "fsdp", away).astype(F32)
    return total


def sum_over_ctx(part_for):
    pairs = lax.axis_size("ctx") // 2
    sums = []
    for pair in range(pairs):
        sent = swap(part_for(2 * pair + 1).astype(BF), "ctx", 1)
        sums.append(part_for(2 * pair) + sent.astype(F32))
    if pairs == 4:
        half = sums[3].shape[0] // 2
        last = sums[3].astype(BF)
        top = swap(last[:half], "ctx", 2).astype(F32)
        low = swap(last[half:], "ctx", 4).astype(F32)
        along_y = jnp.concatenate([sums[2][:half] + top, sums[2][half:]], axis=0)
        along_x = jnp.concatenate([sums[1][:half], sums[1][half:] + low], axis=0)
        return (
            sums[0]
            + swap(along_x.astype(BF), "ctx", 2).astype(F32)
            + swap(along_y.astype(BF), "ctx", 4).astype(F32)
        )
    total = sums[0]
    for pair in range(1, pairs):
        total = total + swap(sums[pair].astype(BF), "ctx", 2 * pair).astype(F32)
    return total


def column_block(values, index, width):
    return lax.dynamic_slice(values, (0, index * width), (values.shape[0], width))


def token_product(left, right):
    width = left.shape[1] // lax.axis_size("ctx")
    me = lax.axis_index("ctx")
    return sum_over_ctx(lambda offset: tn(column_block(left, me ^ offset, width), right))


def sum_all(values):
    ctx_count, fsdp_count = lax.axis_size("ctx"), lax.axis_size("fsdp")
    for axis, count in (("fsdp", fsdp_count), ("ctx", ctx_count)):
        away = 1
        while away < count:
            values = values + swap(values, axis, away)
            away *= 2
    width = values.shape[0] // (ctx_count * fsdp_count)
    index = lax.axis_index("ctx") * fsdp_count + lax.axis_index("fsdp")
    return lax.dynamic_slice(values, (index * width,), (width,))


def sweep_keys(step_fn, carried, pieces):
    row_count = pieces[0].shape[0]

    def loop_step(index, state):
        parts = tuple(lax.dynamic_slice_in_dim(p, index * KEY_STEP, KEY_STEP, 0) for p in pieces)
        return step_fn(state, parts, index * KEY_STEP)

    return lax.fori_loop(0, row_count // KEY_STEP, loop_step, carried)


def body(
    hidden_in,
    out_grad,
    positions,
    block_order,
    attn_gain,
    ffn_gain,
    qkv_weight,
    out_weight,
    ffn_weight,
):
    ctx_count, fsdp_count = lax.axis_size("ctx"), lax.axis_size("fsdp")
    me = lax.axis_index("ctx")
    rows, width = hidden_in.shape[1], hidden_in.shape[2]
    seq_rows = rows * ctx_count
    groups = H // KV
    kv_width = KV * HD
    score_scale = 1.0 / math.sqrt(HD)
    gate_weight, up_weight, down_weight = (ffn_weight[:, k, :] for k in range(3))

    own_anchor = anchors_of(block_order, me, rows)
    key_anchor = jnp.concatenate(
        [anchors_of(block_order, me ^ offset, rows) for offset in range(ctx_count)]
    )
    order = list(range(ctx_count))

    inputs = hidden_in[0].astype(F32)
    grad_in = out_grad[0]
    token_places = positions[0]
    scale_one = norm_scale(inputs)
    normed_one = (inputs * scale_one * attn_gain).astype(BF)

    qkv_full = gather_weight(qkv_weight)
    out_full = gather_weight(out_weight)
    rows_out = gather_rows(grad_in)
    act_grad = nn(rows_out, down_weight)

    projected = nn(normed_one, qkv_full)
    queries = rotate(projected[:, : H * HD].reshape(rows, H, HD), token_places).astype(BF)
    queries = queries.reshape(rows, KV, groups, HD)
    key_local = rotate(
        projected[:, H * HD : (H + KV) * HD].reshape(rows, KV, HD), token_places
    ).astype(BF)
    value_local = projected[:, (H + KV) * HD :].astype(BF)
    pieces = gather_ctx(jnp.concatenate([key_local.reshape(rows, kv_width), value_local], axis=1))
    keys_values = jnp.concatenate([pieces[offset] for offset in order], axis=0)
    key_all, value_all = keys_values[:, :kv_width], keys_values[:, kv_width:]

    def masked_scores(key_heads, anchors):
        scores = (
            jnp.einsum("tkgd,skd->kgts", queries, key_heads, preferred_element_type=F32)
            * score_scale
        )
        allowed = (anchors[None, :] <= own_anchor[:, None])[None, None]
        return (jnp.where(allowed, scores, -1e30), allowed)

    def forward_step(carry_state, parts, first_row):
        top_old, total_old, summed = carry_state
        key_part, value_part, anchors = parts
        count = key_part.shape[0]
        key_heads = key_part.reshape(count, KV, HD)
        value_heads = value_part.reshape(count, KV, HD)
        scores, allowed = masked_scores(key_heads, anchors)
        top_new = jnp.maximum(top_old, jnp.max(scores, axis=-1))
        weights = jnp.where(allowed, jnp.exp(scores - top_new[..., None]), 0.0)
        rescale = jnp.exp(top_old - top_new)
        total_new = total_old * rescale + jnp.sum(weights, axis=-1)
        summed = summed * rescale[..., None] + jnp.einsum(
            "kgts,skd->kgtd", weights.astype(BF), value_heads, preferred_element_type=F32
        )
        return (top_new, total_new, summed)

    start_state = (
        jnp.full((KV, groups, rows), -1e30, F32),
        jnp.zeros((KV, groups, rows), F32),
        jnp.zeros((KV, groups, rows, HD), F32),
    )
    row_top, row_total, summed = sweep_keys(
        forward_step, start_state, (key_all, value_all, key_anchor)
    )
    log_total = row_top + jnp.log(row_total)
    attended = (summed / row_total[..., None]).transpose(2, 0, 1, 3)
    attn_rows = attended.reshape(rows, H * HD).astype(BF)

    residual = inputs + nt(attn_rows, out_full)
    scale_two = norm_scale(residual)
    normed_two = (residual * scale_two * ffn_gain).astype(BF)
    rows_in = gather_rows(normed_two)

    gate_pre = nn(rows_in, gate_weight)
    up_pre = nn(rows_in, up_weight)
    sig = jax.nn.sigmoid(gate_pre)
    activated = (gate_pre * sig * up_pre).astype(BF)
    gate_grad = (act_grad * up_pre * sig * (1.0 + gate_pre * (1.0 - sig))).astype(BF)
    up_grad = (act_grad * gate_pre * sig).astype(BF)
    sum_grad = sum_over_fsdp(nt(gate_grad, gate_weight) + nt(up_grad, up_weight))
    out_sum = sum_over_fsdp(nt(activated, down_weight))
    output = (residual + out_sum).astype(BF)
    ffn_weight_grad = jnp.stack(
        [
            token_product(rows_in, gate_grad),
            token_product(rows_in, up_grad),
            token_product(rows_out, activated),
        ],
        axis=1,
    )

    unit_two = residual * scale_two
    ffn_gain_term = jnp.sum(sum_grad * unit_two, axis=0)
    scaled_two = ffn_gain * sum_grad
    residual_grad = grad_in.astype(F32) + scale_two * (
        scaled_two - unit_two * jnp.mean(scaled_two * unit_two, axis=-1, keepdims=True)
    )
    residual_bf = residual_grad.astype(BF)
    attn_grad = nn(residual_bf, out_full).astype(BF)
    out_weight_grad = rows_to_owner(
        token_product(gather_rows(residual_bf), columns_to_owner(attn_rows)).astype(BF)
    ).astype(F32)

    attn_grad_heads = attn_grad.reshape(rows, KV, groups, HD)
    row_delta = jnp.sum(attn_grad_heads.astype(F32) * attended, axis=-1).transpose(1, 2, 0)

    def backward_step(carry_state, parts, first_row):
        query_grad, key_grad, value_grad = carry_state
        key_part, value_part, anchors = parts
        count = key_part.shape[0]
        key_heads = key_part.reshape(count, KV, HD)
        value_heads = value_part.reshape(count, KV, HD)
        scores, allowed = masked_scores(key_heads, anchors)
        probs = jnp.where(allowed, jnp.exp(scores - log_total[..., None]), 0.0)
        value_piece = jnp.einsum(
            "kgts,tkgd->skd", probs.astype(BF), attn_grad_heads, preferred_element_type=F32
        )
        prob_grad = jnp.einsum(
            "tkgd,skd->kgts", attn_grad_heads, value_heads, preferred_element_type=F32
        )
        score_grad = (probs * (prob_grad - row_delta[..., None]) * score_scale).astype(BF)
        query_grad = query_grad + jnp.einsum(
            "kgts,skd->tkgd", score_grad, key_heads, preferred_element_type=F32
        )
        key_piece = jnp.einsum("kgts,tkgd->skd", score_grad, queries, preferred_element_type=F32)
        key_grad = lax.dynamic_update_slice_in_dim(
            key_grad, key_piece.reshape(count, kv_width), first_row, 0
        )
        value_grad = lax.dynamic_update_slice_in_dim(
            value_grad, value_piece.reshape(count, kv_width), first_row, 0
        )
        return (query_grad, key_grad, value_grad)

    start_grads = (
        jnp.zeros((rows, KV, groups, HD), F32),
        jnp.zeros((seq_rows, kv_width), F32),
        jnp.zeros((seq_rows, kv_width), F32),
    )
    query_grad, key_grad_all, value_grad_all = sweep_keys(
        backward_step, start_grads, (key_all, value_all, key_anchor)
    )
    pair_grads = jnp.concatenate([key_grad_all, value_grad_all], axis=1)
    pair_own = sum_over_ctx(
        lambda offset: pair_grads[order.index(offset) * rows : (order.index(offset) + 1) * rows]
    )
    key_grad_own, value_grad_own = pair_own[:, :kv_width], pair_own[:, kv_width:]
    query_part = rotate(query_grad.reshape(rows, H, HD), -token_places).reshape(rows, H * HD)
    key_part = rotate(key_grad_own.reshape(rows, KV, HD), -token_places).reshape(rows, kv_width)
    pair_part = jnp.concatenate([key_part, value_grad_own], axis=1).astype(BF)
    query_part = query_part.astype(BF)
    normed_one_grad = nt(query_part, qkv_full[:, : H * HD]) + nt(pair_part, qkv_full[:, H * HD :])

    rows_one = gather_rows(normed_one)
    qkv_grad = jnp.concatenate(
        [
            rows_to_owner(token_product(rows_one, columns_to_owner(part)).astype(BF)).astype(F32)
            for part in (query_part, pair_part)
        ],
        axis=1,
    )

    unit_one = inputs * scale_one
    attn_gain_term = jnp.sum(normed_one_grad * unit_one, axis=0)
    scaled_one = attn_gain * normed_one_grad
    input_grad = residual_grad + scale_one * (
        scaled_one - unit_one * jnp.mean(scaled_one * unit_one, axis=-1, keepdims=True)
    )
    return (
        output[None],
        input_grad[None],
        qkv_grad,
        out_weight_grad,
        ffn_weight_grad,
        sum_all(attn_gain_term),
        sum_all(ffn_gain_term),
    )


def solution(mesh):
    return jax.shard_map(
        body,
        mesh=mesh,
        in_specs=(
            P("fsdp", "ctx", None),
            P("fsdp", "ctx", None),
            P("fsdp", "ctx"),
            P(),
            P(),
            P(),
            P("fsdp", None),
            P("fsdp", None),
            P(None, None, "fsdp"),
        ),
        out_specs=(
            P("fsdp", "ctx", None),
            P("fsdp", "ctx", None),
            P(("ctx", "fsdp"), None),
            P(("ctx", "fsdp"), None),
            P("ctx", None, "fsdp"),
            P(("ctx", "fsdp")),
            P(("ctx", "fsdp")),
        ),
        check_vma=False,
    )
```

```python
import math

import jax
import jax.numpy as jnp
from jax import lax
from jax.experimental import pallas as pl
from jax.experimental.pallas import tpu as pltpu
from jax.sharding import PartitionSpec as P

H = 32
KV = 8
HD = 64

NORM_EPS = 1e-05
ROPE_BASE = 500000.0
KEY_STEP = 512


BF = jnp.bfloat16
F32 = jnp.float32


def mm(a, b, dims):
    return lax.dot_general(a, b, (dims, ((), ())), preferred_element_type=F32)


def nn(a, b):
    return mm(a, b, ((1,), (0,)))


def nt(a, b):
    return mm(a, b, ((1,), (1,)))


def tn(a, b):
    return mm(a, b, ((0,), (0,)))


def swap(value, axis, offset):
    count = lax.axis_size(axis)
    return lax.ppermute(value, axis, [(i, i ^ offset) for i in range(count)])


def rotate(values, token_places):
    head_dim = values.shape[-1]
    half_dim = head_dim // 2
    frequency = jnp.power(ROPE_BASE, -(jnp.arange(half_dim, dtype=F32) * 2.0 / head_dim))
    angles = token_places.astype(F32)[:, None] * frequency[None, :]
    cosine = jnp.concatenate([jnp.cos(angles), jnp.cos(angles)], axis=-1)[:, None, :]
    sine_part = jnp.concatenate([jnp.sin(angles), jnp.sin(angles)], axis=-1)[:, None, :]
    turned = jnp.concatenate([-values[..., half_dim:], values[..., :half_dim]], axis=-1)
    return values * cosine + turned * sine_part


def norm_scale(values):
    return lax.rsqrt(jnp.mean(values * values, axis=-1, keepdims=True) + NORM_EPS)


def lookup(entries, row_ids):
    matches = row_ids[:, None] == jnp.arange(entries.shape[0], dtype=jnp.int32)[None, :]
    return jnp.sum(jnp.where(matches, entries[None, :], 0), axis=1)


def anchors_of(block_order, owner, row_count):
    block_len = row_count // 2
    row_ids = owner * row_count + jnp.arange(row_count, dtype=jnp.int32)
    return lookup(block_order, row_ids // block_len) * block_len + row_ids % block_len


def after(value, *earlier):
    return lax.optimization_barrier((value, *earlier))[0]


def ids():
    return lax.axis_index("ctx"), lax.axis_index("fsdp")


def gather_pieces(weight):
    ctx_count, fsdp_count = lax.axis_size("ctx"), lax.axis_size("fsdp")
    rows, columns = weight.shape
    share = columns // ctx_count
    mine = lax.dynamic_slice(weight, (0, lax.axis_index("ctx") * share), (rows, share))
    planes = {}
    if fsdp_count == 4:
        planes[1] = swap(mine, "fsdp", 1)
        planes[3] = swap(mine, "fsdp", 3)
        planes[2] = swap(planes[3], "fsdp", 1)
    else:
        for away in range(1, fsdp_count):
            planes[away] = swap(mine, "fsdp", away)
    pieces = []
    half = rows // 2
    for away, first in planes.items():
        along_x, along_y = swap(first, "ctx", 2), swap(first, "ctx", 4)
        parts = [(0, 0, first), (2, 0, along_x), (4, 0, along_y)]
        parts.append((6, 0, swap(along_y[:half], "ctx", 2)))
        parts.append((6, half, swap(along_x[half:], "ctx", 4)))
        for offset, start, part in parts:
            pieces.append((away, offset, start, part))
            pieces.append((away, offset + 1, start, swap(part, "ctx", 1)))
    return pieces


def pieces_kernel(places, rows_in, share, back, ids_ref, x_ref, own_ref, *refs):
    count = len(places)
    piece_refs, y_ref = refs[:count], refs[count]
    own_buf, bufs, sems = refs[count + 1], refs[count + 2 : -1], refs[-1]
    me, plane = ids_ref[0], ids_ref[1]
    copies = [pltpu.make_async_copy(own_ref, own_buf, sems.at[count])]
    for i in range(count):
        copies.append(pltpu.make_async_copy(piece_refs[i], bufs[i], sems.at[i]))
    for copy in copies:
        copy.start()

    def tokens(start, size):
        return x_ref[:, pl.ds(pl.multiple_of(start, 128), size)]

    copies[0].wait()
    if back:
        y_ref[...] = jnp.zeros_like(y_ref)
        y_ref[:, pl.ds(pl.multiple_of(plane * rows_in, 128), rows_in)] = nt(
            x_ref[...], own_buf[...]
        )
    else:
        y_ref[...] = nn(tokens(plane * rows_in, rows_in), own_buf[...])
    for i, (away, offset, start, height) in enumerate(places):
        copies[i + 1].wait()
        inner = (plane ^ away) * rows_in + start
        outer = (me ^ offset) * share
        if back:
            at = pl.ds(pl.multiple_of(inner, 128), height)
            y_ref[:, at] += nt(tokens(outer, share), bufs[i][...])
        else:
            at = pl.ds(pl.multiple_of(outer, 128), share)
            y_ref[:, at] += nn(tokens(inner, height), bufs[i][...])


def pieces_matmul(x, own, pieces, back):
    me, plane = ids()
    rows_in, columns = own.shape
    share = columns // lax.axis_size("ctx")
    width = rows_in * lax.axis_size("fsdp") if back else columns
    places = tuple((away, offset, start, part.shape[0]) for away, offset, start, part in pieces)
    arrays = [part for _, _, _, part in pieces]
    hbm = pl.BlockSpec(memory_space=pl.ANY)
    return pl.pallas_call(
        lambda *refs: pieces_kernel(places, rows_in, share, back, *refs),
        out_shape=jax.ShapeDtypeStruct((x.shape[0], width), F32),
        in_specs=[
            pl.BlockSpec(memory_space=pltpu.SMEM),
            pl.BlockSpec(memory_space=pltpu.VMEM),
            hbm,
        ]
        + [hbm] * len(arrays),
        out_specs=pl.BlockSpec(memory_space=pltpu.VMEM),
        scratch_shapes=[pltpu.VMEM(own.shape, own.dtype)]
        + [pltpu.VMEM(part.shape, part.dtype) for part in arrays]
        + [pltpu.SemaphoreType.DMA((len(arrays) + 1,))],
        compiler_params=pltpu.CompilerParams(vmem_limit_bytes=40 << 20),
        cost_estimate=pl.CostEstimate(
            flops=2 * x.shape[0] * rows_in * lax.axis_size("fsdp") * columns,
            bytes_accessed=2 * rows_in * lax.axis_size("fsdp") * columns,
            transcendentals=0,
        ),
        name="pieces_back" if back else "pieces_forward",
    )(jnp.stack([me, plane]), x, own, *arrays)


def gather_blocks(weight):
    rows, columns = weight.shape
    share = columns // lax.axis_size("ctx")
    mine = lax.dynamic_slice(weight, (0, lax.axis_index("ctx") * share), (rows, share))
    return lax.all_gather(lax.all_gather(mine, "fsdp"), "ctx")


def whole_of(blocks):
    ctx_count, fsdp_count, rows, share = blocks.shape
    return blocks.transpose(1, 2, 0, 3).reshape(fsdp_count * rows, ctx_count * share)


def out_forward_kernel(x_ref, w_ref, hidden_ref, gain_ref, residual_ref, normed_ref):
    step = pl.program_id(0)

    @pl.when(step == 0)
    def _():
        residual_ref[...] = hidden_ref[...].astype(F32)

    rows = w_ref.shape[2]
    for plane in range(w_ref.shape[1]):
        residual_ref[:, plane * rows : (plane + 1) * rows] += nt(x_ref[...], w_ref[0, plane])

    @pl.when(step == pl.num_programs(0) - 1)
    def _():
        residual = residual_ref[...]
        normed_ref[...] = (residual * norm_scale(residual) * gain_ref[...]).astype(BF)


def out_forward(attn_rows, blocks, hidden, gain):
    rows, width = hidden.shape
    ctx_count, fsdp_count, height, share = blocks.shape
    if share % 128:
        residual = hidden.astype(F32) + nt(attn_rows, whole_of(blocks))
        return residual, (residual * norm_scale(residual) * gain).astype(BF)
    return pl.pallas_call(
        out_forward_kernel,
        grid=(ctx_count,),
        out_shape=(
            jax.ShapeDtypeStruct((rows, width), F32),
            jax.ShapeDtypeStruct((rows, width), BF),
        ),
        in_specs=[
            pl.BlockSpec((rows, share), lambda c: (0, c)),
            pl.BlockSpec((1, fsdp_count, height, share), lambda c: (c, 0, 0, 0)),
            pl.BlockSpec((rows, width), lambda c: (0, 0)),
            pl.BlockSpec((1, width), lambda c: (0, 0)),
        ],
        out_specs=(
            pl.BlockSpec((rows, width), lambda c: (0, 0)),
            pl.BlockSpec((rows, width), lambda c: (0, 0)),
        ),
        compiler_params=pltpu.CompilerParams(vmem_limit_bytes=24 << 20),
        cost_estimate=pl.CostEstimate(
            flops=2 * rows * width * ctx_count * share,
            bytes_accessed=2 * width * ctx_count * share,
            transcendentals=0,
        ),
        name="out_forward",
    )(attn_rows, blocks, hidden, gain[None])


def out_back_kernel(x_ref, w_ref, y_ref):
    rows = w_ref.shape[2]
    total = nn(x_ref[:, :rows], w_ref[0, 0])
    for plane in range(1, w_ref.shape[1]):
        total += nn(x_ref[:, plane * rows : (plane + 1) * rows], w_ref[0, plane])
    y_ref[...] = total.astype(BF)


def out_back(x, blocks):
    rows, width = x.shape
    ctx_count, fsdp_count, height, share = blocks.shape
    if share % 128:
        return nn(x, whole_of(blocks)).astype(BF)
    return pl.pallas_call(
        out_back_kernel,
        grid=(ctx_count,),
        out_shape=jax.ShapeDtypeStruct((rows, ctx_count * share), BF),
        in_specs=[
            pl.BlockSpec((rows, width), lambda c: (0, 0)),
            pl.BlockSpec((1, fsdp_count, height, share), lambda c: (c, 0, 0, 0)),
        ],
        out_specs=pl.BlockSpec((rows, share), lambda c: (0, c)),
        compiler_params=pltpu.CompilerParams(vmem_limit_bytes=24 << 20),
        cost_estimate=pl.CostEstimate(
            flops=2 * rows * width * ctx_count * share,
            bytes_accessed=2 * width * ctx_count * share,
            transcendentals=0,
        ),
        name="out_back",
    )(x, blocks)


def gather_rows(values):
    count = lax.axis_size("fsdp")
    planes = {0: values}
    if count == 4:
        planes[1] = swap(values, "fsdp", 1)
        planes[3] = swap(values, "fsdp", 3)
        planes[2] = swap(planes[3], "fsdp", 1)
    else:
        for away in range(1, count):
            planes[away] = swap(values, "fsdp", away)
    return jnp.concatenate([planes[away] for away in range(count)], axis=0)


def sum_rows(values):
    count = lax.axis_size("fsdp")
    rows = values.shape[0] // count
    parts = [values[away * rows : (away + 1) * rows] for away in range(count)]
    if count == 4:
        third = parts[3] + swap(parts[2].astype(BF), "fsdp", 1).astype(F32)
        first = swap(parts[1].astype(BF), "fsdp", 1).astype(F32)
        return parts[0] + first + swap(third.astype(BF), "fsdp", 3).astype(F32)
    total = parts[0]
    for away in range(1, count):
        total = total + swap(parts[away].astype(BF), "fsdp", away).astype(F32)
    return total


def gather_planes(values):
    count = lax.axis_size("fsdp")
    rows, columns = values.shape
    copies = jnp.broadcast_to(values[None], (count, rows, columns)).reshape(count * rows, columns)
    return lax.all_to_all(copies, "fsdp", split_axis=0, concat_axis=0, tiled=True)


def columns_to_owner(values):
    return lax.all_to_all(values, "fsdp", split_axis=1, concat_axis=0, tiled=True)


def rows_to_owner(values):
    count = lax.axis_size("fsdp")
    rows, columns = values.shape
    out = lax.all_to_all(values, "fsdp", split_axis=0, concat_axis=0, tiled=True)
    return out.reshape(count, rows // count, columns)


def joined(parts):
    return jnp.concatenate([parts[i] for i in range(parts.shape[0])], axis=1)


def sum_over_ctx(part_for):
    pairs = lax.axis_size("ctx") // 2
    sent = jnp.stack([part_for(2 * pair + 1).astype(BF) for pair in range(pairs)])
    got = swap(sent, "ctx", 1)
    sums = [part_for(2 * pair).astype(F32) + got[pair].astype(F32) for pair in range(pairs)]
    total = sums[0]
    for pair in range(1, pairs):
        total = total + swap(sums[pair].astype(BF), "ctx", 2 * pair).astype(F32)
    return total


def ctx_rows_sum(values):
    height = values.shape[0] // lax.axis_size("ctx")
    me = lax.axis_index("ctx")

    def part(offset):
        return lax.dynamic_slice(
            values, ((me ^ offset) * height, 0), (height, values.shape[1])
        )

    return sum_over_ctx(part)


def gather_keys(piece):
    pairs = lax.axis_size("ctx") // 2
    same = [piece] + [swap(piece, "ctx", 2 * pair) for pair in range(1, pairs)]
    mine = jnp.stack(same)
    other = swap(mine, "ctx", 1)
    return jnp.concatenate([mine[:, None], other[:, None]], axis=1).reshape(
        2 * pairs * piece.shape[0], piece.shape[1]
    )


def sweep_keys(step_fn, carried, pieces):
    row_count = pieces[0].shape[0]

    def loop_step(index, state):
        parts = tuple(lax.dynamic_slice_in_dim(p, index * KEY_STEP, KEY_STEP, 0) for p in pieces)
        return step_fn(state, parts, index * KEY_STEP)

    return lax.fori_loop(0, row_count // KEY_STEP, loop_step, carried)


def body(
    hidden_in,
    out_grad,
    positions,
    block_order,
    attn_gain,
    ffn_gain,
    qkv_weight,
    out_weight,
    ffn_weight,
):
    ctx_count, fsdp_count = lax.axis_size("ctx"), lax.axis_size("fsdp")
    me = lax.axis_index("ctx")
    rows, width = hidden_in.shape[1], hidden_in.shape[2]
    seq_rows = rows * ctx_count
    groups = H // KV
    kv_width = KV * HD
    score_scale = 1.0 / math.sqrt(HD)
    gate_weight, up_weight, down_weight = (ffn_weight[:, k, :] for k in range(3))

    own_anchor = anchors_of(block_order, me, rows)
    key_anchor = jnp.concatenate(
        [anchors_of(block_order, me ^ offset, rows) for offset in range(ctx_count)]
    )

    inputs = hidden_in[0].astype(F32)
    grad_in = out_grad[0]
    token_places = positions[0]
    scale_one = norm_scale(inputs)
    normed_one = (inputs * scale_one * attn_gain).astype(BF)

    fast = ctx_count == 8 and (qkv_weight.shape[1] // ctx_count) % 128 == 0
    out_blocks = gather_blocks(out_weight)
    if fast:
        qkv_pieces = gather_pieces(qkv_weight)
        projected = pieces_matmul(normed_one, qkv_weight, qkv_pieces, False)
    else:
        qkv_full = whole_of(gather_blocks(qkv_weight))
        projected = nn(normed_one, qkv_full)
    plane = lax.axis_index("fsdp")
    grad_planes = lax.all_gather(after(grad_in, out_blocks), "fsdp")
    rows_out = jnp.concatenate(
        [
            lax.dynamic_index_in_dim(grad_planes, plane ^ away, 0, keepdims=False)
            for away in range(fsdp_count)
        ],
        axis=0,
    )
    act_grad = nn(rows_out, down_weight)

    queries = rotate(projected[:, : H * HD].reshape(rows, H, HD), token_places).astype(BF)
    queries = queries.reshape(rows, KV, groups, HD)
    key_local = rotate(
        projected[:, H * HD : (H + KV) * HD].reshape(rows, KV, HD), token_places
    ).astype(BF)
    value_local = projected[:, (H + KV) * HD :].astype(BF)
    keys_values = gather_keys(
        jnp.concatenate([key_local.reshape(rows, kv_width), value_local], axis=1)
    )
    key_all, value_all = keys_values[:, :kv_width], keys_values[:, kv_width:]

    def masked_scores(key_heads, anchors):
        scores = (
            jnp.einsum("tkgd,skd->kgts", queries, key_heads, preferred_element_type=F32)
            * score_scale
        )
        allowed = (anchors[None, :] <= own_anchor[:, None])[None, None]
        return (jnp.where(allowed, scores, -1e30), allowed)

    def forward_step(carry_state, parts, first_row):
        top_old, total_old, summed = carry_state
        key_part, value_part, anchors = parts
        count = key_part.shape[0]
        key_heads = key_part.reshape(count, KV, HD)
        value_heads = value_part.reshape(count, KV, HD)
        scores, allowed = masked_scores(key_heads, anchors)
        top_new = jnp.maximum(top_old, jnp.max(scores, axis=-1))
        weights = jnp.where(allowed, jnp.exp(scores - top_new[..., None]), 0.0)
        rescale = jnp.exp(top_old - top_new)
        total_new = total_old * rescale + jnp.sum(weights, axis=-1)
        summed = summed * rescale[..., None] + jnp.einsum(
            "kgts,skd->kgtd", weights.astype(BF), value_heads, preferred_element_type=F32
        )
        return (top_new, total_new, summed)

    start_state = (
        jnp.full((KV, groups, rows), -1e30, F32),
        jnp.zeros((KV, groups, rows), F32),
        jnp.zeros((KV, groups, rows, HD), F32),
    )
    row_top, row_total, summed = sweep_keys(
        forward_step, start_state, (key_all, value_all, key_anchor)
    )
    log_total = row_top + jnp.log(row_total)
    attended = (summed / row_total[..., None]).transpose(2, 0, 1, 3)
    attn_rows = attended.reshape(rows, H * HD).astype(BF)

    residual, normed_two = out_forward(attn_rows, out_blocks, hidden_in[0], ffn_gain)
    scale_two = norm_scale(residual)
    rows_in = gather_rows(normed_two)

    gate_pre = nn(rows_in, gate_weight)
    up_pre = nn(rows_in, up_weight)
    sig = jax.nn.sigmoid(gate_pre)
    activated = (gate_pre * sig * up_pre).astype(BF)
    gate_grad = (act_grad * up_pre * sig * (1.0 + gate_pre * (1.0 - sig))).astype(BF)
    up_grad = (act_grad * gate_pre * sig).astype(BF)
    sum_grad = sum_rows(nt(gate_grad, gate_weight) + nt(up_grad, up_weight))
    out_sum = sum_rows(after(nt(activated, down_weight), sum_grad))
    output = (residual + out_sum).astype(BF)
    ffn_weight_grad = jnp.stack(
        [
            lax.psum_scatter(tn(left, right).astype(BF), "ctx", scatter_dimension=0, tiled=True)
            for left, right in ((rows_in, gate_grad), (rows_in, up_grad), (rows_out, activated))
        ],
        axis=1,
    ).astype(F32)

    unit_two = residual * scale_two
    ffn_gain_term = jnp.sum(sum_grad * unit_two, axis=0)
    scaled_two = ffn_gain * sum_grad
    residual_grad = grad_in.astype(F32) + scale_two * (
        scaled_two - unit_two * jnp.mean(scaled_two * unit_two, axis=-1, keepdims=True)
    )
    residual_bf = residual_grad.astype(BF)
    attn_grad = out_back(residual_bf, out_blocks)
    residual_planes = gather_planes(residual_bf)
    out_share = tn(residual_planes, columns_to_owner(attn_rows)).astype(BF)

    attn_grad_heads = attn_grad.reshape(rows, KV, groups, HD)
    row_delta = jnp.sum(attn_grad_heads.astype(F32) * attended, axis=-1).transpose(1, 2, 0)

    def backward_step(carry_state, parts, first_row):
        query_grad, key_grad, value_grad = carry_state
        key_part, value_part, anchors = parts
        count = key_part.shape[0]
        key_heads = key_part.reshape(count, KV, HD)
        value_heads = value_part.reshape(count, KV, HD)
        scores, allowed = masked_scores(key_heads, anchors)
        probs = jnp.where(allowed, jnp.exp(scores - log_total[..., None]), 0.0)
        value_piece = jnp.einsum(
            "kgts,tkgd->skd", probs.astype(BF), attn_grad_heads, preferred_element_type=F32
        )
        prob_grad = jnp.einsum(
            "tkgd,skd->kgts", attn_grad_heads, value_heads, preferred_element_type=F32
        )
        score_grad = (probs * (prob_grad - row_delta[..., None]) * score_scale).astype(BF)
        query_grad = query_grad + jnp.einsum(
            "kgts,skd->tkgd", score_grad, key_heads, preferred_element_type=F32
        )
        key_piece = jnp.einsum("kgts,tkgd->skd", score_grad, queries, preferred_element_type=F32)
        key_grad = lax.dynamic_update_slice_in_dim(
            key_grad, key_piece.reshape(count, kv_width), first_row, 0
        )
        value_grad = lax.dynamic_update_slice_in_dim(
            value_grad, value_piece.reshape(count, kv_width), first_row, 0
        )
        return (query_grad, key_grad, value_grad)

    start_grads = (
        jnp.zeros((rows, KV, groups, HD), F32),
        jnp.zeros((seq_rows, kv_width), F32),
        jnp.zeros((seq_rows, kv_width), F32),
    )
    query_grad, key_grad_all, value_grad_all = sweep_keys(
        backward_step, start_grads, (key_all, value_all, key_anchor)
    )
    pair_grads = jnp.concatenate([key_grad_all, value_grad_all], axis=1)
    pair_own = sum_over_ctx(lambda offset: pair_grads[offset * rows : (offset + 1) * rows])
    key_grad_own, value_grad_own = pair_own[:, :kv_width], pair_own[:, kv_width:]
    query_part = rotate(query_grad.reshape(rows, H, HD), -token_places).reshape(rows, H * HD)
    query_part = query_part.astype(BF)
    key_part = rotate(key_grad_own.reshape(rows, KV, HD), -token_places).reshape(rows, kv_width)
    pair_part = jnp.concatenate([key_part, value_grad_own], axis=1).astype(BF)
    projected_grad = jnp.concatenate([query_part, pair_part], axis=1)
    if fast:
        normed_one_grad = pieces_matmul(projected_grad, qkv_weight, qkv_pieces, True)
    else:
        normed_one_grad = nt(projected_grad, qkv_full)

    rows_one = gather_planes(normed_one)
    query_share = tn(rows_one, columns_to_owner(query_part)).astype(BF)
    first_sums = ctx_rows_sum(jnp.concatenate([out_share, query_share], axis=1))
    first_sums = rows_to_owner(first_sums.astype(BF)).astype(F32)

    unit_one = inputs * scale_one
    attn_gain_term = jnp.sum(normed_one_grad * unit_one, axis=0)
    scaled_one = attn_gain * normed_one_grad
    input_grad = residual_grad + scale_one * (
        scaled_one - unit_one * jnp.mean(scaled_one * unit_one, axis=-1, keepdims=True)
    )

    pair_share = tn(rows_one, columns_to_owner(pair_part)).astype(BF)
    gain_terms = jnp.concatenate(
        [
            jnp.broadcast_to(term[:, None], (width, 64))
            for term in (attn_gain_term, ffn_gain_term)
        ],
        axis=1,
    ).astype(BF)
    last_sums = ctx_rows_sum(jnp.concatenate([pair_share, gain_terms], axis=1))
    last_sums = rows_to_owner(last_sums.astype(BF)).astype(F32)

    out_columns, query_columns = out_share.shape[1], query_share.shape[1]
    pair_columns = pair_share.shape[1]
    out_weight_grad = joined(first_sums[:, :, :out_columns])
    qkv_grad = jnp.concatenate(
        [joined(first_sums[:, :, out_columns:]), joined(last_sums[:, :, :pair_columns])], axis=1
    )
    gain_grads = jnp.sum(last_sums[:, :, pair_columns:], axis=0)
    return (
        output[None],
        input_grad[None],
        qkv_grad,
        out_weight_grad,
        ffn_weight_grad,
        gain_grads[:, 0],
        gain_grads[:, 64],
    )


def solution(mesh):
    return jax.shard_map(
        body,
        mesh=mesh,
        in_specs=(
            P("fsdp", "ctx", None),
            P("fsdp", "ctx", None),
            P("fsdp", "ctx"),
            P(),
            P(),
            P(),
            P("fsdp", None),
            P("fsdp", None),
            P(None, None, "fsdp"),
        ),
        out_specs=(
            P("fsdp", "ctx", None),
            P("fsdp", "ctx", None),
            P(("ctx", "fsdp"), None),
            P(("ctx", "fsdp"), None),
            P("ctx", None, "fsdp"),
            P(("ctx", "fsdp")),
            P(("ctx", "fsdp")),
        ),
        check_vma=False,
    )
```

```python
import math

import jax
import jax.numpy as jnp
from jax import lax
from jax.experimental import pallas as pl
from jax.experimental.pallas import tpu as pltpu
from jax.sharding import PartitionSpec as P


H = 32
KV = 8
HD = 64

NORM_EPS = 1e-05
ROPE_BASE = 500000.0
FFN_TILE = 512


BF = jnp.bfloat16
F32 = jnp.float32


def mm(a, b, dims):
    return lax.dot_general(a, b, (dims, ((), ())), preferred_element_type=F32)


def nn(a, b):
    return mm(a, b, ((1,), (0,)))


def nt(a, b):
    return mm(a, b, ((1,), (1,)))


def tn(a, b):
    return mm(a, b, ((0,), (0,)))


def swap(value, axis, offset):
    count = lax.axis_size(axis)
    return lax.ppermute(value, axis, [(i, i ^ offset) for i in range(count)])


def rotate(values, token_places):
    head_dim = values.shape[-1]
    half_dim = head_dim // 2
    frequency = jnp.power(ROPE_BASE, -(jnp.arange(half_dim, dtype=F32) * 2.0 / head_dim))
    angles = token_places.astype(F32)[:, None] * frequency[None, :]
    cosine = jnp.concatenate([jnp.cos(angles), jnp.cos(angles)], axis=-1)[:, None, :]
    sine_part = jnp.concatenate([jnp.sin(angles), jnp.sin(angles)], axis=-1)[:, None, :]
    turned = jnp.concatenate([-values[..., half_dim:], values[..., :half_dim]], axis=-1)
    return values * cosine + turned * sine_part


def norm_scale(values):
    return lax.rsqrt(jnp.mean(values * values, axis=-1, keepdims=True) + NORM_EPS)


def lookup(entries, row_ids):
    matches = row_ids[:, None] == jnp.arange(entries.shape[0], dtype=jnp.int32)[None, :]
    return jnp.sum(jnp.where(matches, entries[None, :], 0), axis=1)


def anchors_of(block_order, owner, row_count):
    block_len = row_count // 2
    row_ids = owner * row_count + jnp.arange(row_count, dtype=jnp.int32)
    return lookup(block_order, row_ids // block_len) * block_len + row_ids % block_len


def after(value, *earlier):
    return lax.optimization_barrier((value, earlier))[0]


def ids():
    return lax.axis_index("ctx"), lax.axis_index("fsdp")


def gather_pieces(weight):
    rows, columns = weight.shape
    share = columns // lax.axis_size("ctx")
    half = rows // 2
    mine = lax.dynamic_slice(weight, (0, lax.axis_index("ctx") * share), (rows, share))
    planes = {}
    planes[3] = swap(mine, "fsdp", 3)
    planes[1] = swap(mine, "fsdp", 1)
    planes[2] = swap(planes[3], "fsdp", 1)
    pieces = []
    for away in (1, 3, 2):
        first = planes[away]
        along_x, along_y = swap(first, "ctx", 2), swap(first, "ctx", 4)
        top, low = swap(along_y[:half], "ctx", 2), swap(along_x[half:], "ctx", 4)
        parts = [(0, 0, first), (2, 0, along_x), (4, 0, along_y), (6, 0, top), (6, half, low)]
        for offset, start, part in parts:
            pieces.append((away, offset, start, part))
            pieces.append((away, offset + 1, start, swap(part, "ctx", 1)))
    return pieces, (planes[1], (pieces[-4][3], pieces[-2][3]))


def pieces_kernel(places, rows_in, share, back, ids_ref, x_ref, own_ref, *refs):
    count = len(places)
    piece_refs, refs = refs[:count], refs[count:]
    if back:
        y_ref, refs = refs[0], refs[1:]
    else:
        (cos_ref, sin_ref, q_ref, pair_ref, y_ref), refs = refs[:5], refs[5:]
    own_buf, bufs, sems = refs[0], refs[1:-1], refs[-1]
    me, plane = ids_ref[0], ids_ref[1]
    copies = [pltpu.make_async_copy(own_ref, own_buf, sems.at[count])]
    for i in range(count):
        copies.append(pltpu.make_async_copy(piece_refs[i], bufs[i], sems.at[i]))
    for copy in copies:
        copy.start()

    def tokens(start, size):
        return x_ref[:, pl.ds(pl.multiple_of(start, 128), size)]

    copies[0].wait()
    if back:
        y_ref[...] = jnp.zeros_like(y_ref)
        y_ref[:, pl.ds(pl.multiple_of(plane * rows_in, 128), rows_in)] = nt(
            x_ref[...], own_buf[...]
        )
    else:
        y_ref[...] = nn(tokens(plane * rows_in, rows_in), own_buf[...])
    for i, (away, offset, start, height) in enumerate(places):
        copies[i + 1].wait()
        inner = (plane ^ away) * rows_in + start
        outer = (me ^ offset) * share
        if back:
            at = pl.ds(pl.multiple_of(inner, 128), height)
            y_ref[:, at] += nt(tokens(outer, share), bufs[i][...])
        else:
            at = pl.ds(pl.multiple_of(outer, 128), share)
            y_ref[:, at] += nn(tokens(inner, height), bufs[i][...])
    if not back:
        cosine, sine = cos_ref[...], sin_ref[...]
        queries, keys = H * HD, KV * HD
        for start in range(0, queries + keys, 128):
            tile = turn(y_ref[:, start : start + 128], cosine, sine)
            if start < queries:
                q_ref[:, start : start + 128] = (tile * (1.0 / math.sqrt(HD))).astype(BF)
            else:
                pair_ref[:, start - queries : start - queries + 128] = tile.astype(BF)
        pair_ref[:, keys:] = y_ref[:, queries + keys :].astype(BF)


def pieces_call(x, own, pieces, extra, out_shape, scratch, back):
    me, plane = ids()
    rows_in, columns = own.shape
    share = columns // lax.axis_size("ctx")
    places = tuple((away, offset, start, part.shape[0]) for away, offset, start, part in pieces)
    arrays = [part for _, _, _, part in pieces]
    hbm, vmem = pl.BlockSpec(memory_space=pl.ANY), pl.BlockSpec(memory_space=pltpu.VMEM)
    return pl.pallas_call(
        lambda *refs: pieces_kernel(places, rows_in, share, back, *refs),
        out_shape=out_shape,
        in_specs=[pl.BlockSpec(memory_space=pltpu.SMEM), vmem, hbm]
        + [hbm] * len(arrays)
        + [vmem] * len(extra),
        out_specs=jax.tree.map(lambda _: vmem, out_shape),
        scratch_shapes=scratch
        + [pltpu.VMEM(own.shape, own.dtype)]
        + [pltpu.VMEM(part.shape, part.dtype) for part in arrays]
        + [pltpu.SemaphoreType.DMA((len(arrays) + 1,))],
        compiler_params=pltpu.CompilerParams(vmem_limit_bytes=32 << 20),
        cost_estimate=pl.CostEstimate(
            flops=2 * x.shape[0] * rows_in * lax.axis_size("fsdp") * columns,
            bytes_accessed=2 * rows_in * lax.axis_size("fsdp") * columns,
            transcendentals=0,
        ),
        name="pieces_back" if back else "pieces_forward",
    )(jnp.stack([me, plane]), x, own, *arrays, *extra)


def pieces_forward(x, own, pieces, cosine, sine):
    rows, columns = x.shape[0], own.shape[1]
    out_shape = (
        jax.ShapeDtypeStruct((rows, H * HD), BF),
        jax.ShapeDtypeStruct((rows, 2 * KV * HD), BF),
    )
    scratch = [pltpu.VMEM((rows, columns), F32)]
    return pieces_call(x, own, pieces, [cosine, sine], out_shape, scratch, False)


def pieces_back(x, own, pieces):
    out_shape = jax.ShapeDtypeStruct((x.shape[0], own.shape[0] * lax.axis_size("fsdp")), F32)
    return pieces_call(x, own, pieces, [], out_shape, [], True)


def gather_blocks(weight, before_fsdp, before_ctx):
    rows, columns = weight.shape
    share = columns // lax.axis_size("ctx")
    mine = lax.dynamic_slice(weight, (0, lax.axis_index("ctx") * share), (rows, share))
    planes = lax.all_gather(after(mine, before_fsdp), "fsdp")
    return lax.all_gather(after(planes, before_ctx), "ctx")


def whole_of(blocks):
    ctx_count, fsdp_count, rows, share = blocks.shape
    return blocks.transpose(1, 2, 0, 3).reshape(fsdp_count * rows, ctx_count * share)


def out_forward_kernel(x_ref, w_ref, hidden_ref, gain_ref, residual_ref, normed_ref):
    step = pl.program_id(0)

    @pl.when(step == 0)
    def _():
        residual_ref[...] = hidden_ref[...].astype(F32)

    rows = w_ref.shape[2]
    for plane in range(w_ref.shape[1]):
        residual_ref[:, plane * rows : (plane + 1) * rows] += nt(x_ref[...], w_ref[0, plane])

    @pl.when(step == pl.num_programs(0) - 1)
    def _():
        residual = residual_ref[...]
        normed_ref[...] = (residual * norm_scale(residual) * gain_ref[...]).astype(BF)


def out_forward(attn_rows, blocks, hidden, gain):
    rows, width = hidden.shape
    ctx_count, fsdp_count, height, share = blocks.shape
    if share % 128:
        residual = hidden.astype(F32) + nt(attn_rows, whole_of(blocks))
        return residual, (residual * norm_scale(residual) * gain).astype(BF)
    return pl.pallas_call(
        out_forward_kernel,
        grid=(ctx_count,),
        out_shape=(
            jax.ShapeDtypeStruct((rows, width), F32),
            jax.ShapeDtypeStruct((rows, width), BF),
        ),
        in_specs=[
            pl.BlockSpec((rows, share), lambda c: (0, c)),
            pl.BlockSpec((1, fsdp_count, height, share), lambda c: (c, 0, 0, 0)),
            pl.BlockSpec((rows, width), lambda c: (0, 0)),
            pl.BlockSpec((1, width), lambda c: (0, 0)),
        ],
        out_specs=(
            pl.BlockSpec((rows, width), lambda c: (0, 0)),
            pl.BlockSpec((rows, width), lambda c: (0, 0)),
        ),
        compiler_params=pltpu.CompilerParams(vmem_limit_bytes=24 << 20),
        cost_estimate=pl.CostEstimate(
            flops=2 * rows * width * ctx_count * share,
            bytes_accessed=2 * width * ctx_count * share,
            transcendentals=0,
        ),
        name="out_forward",
    )(attn_rows, blocks, hidden, gain[None])


def out_back_kernel(x_ref, w_ref, y_ref):
    rows = w_ref.shape[2]
    total = nn(x_ref[:, :rows], w_ref[0, 0])
    for plane in range(1, w_ref.shape[1]):
        total += nn(x_ref[:, plane * rows : (plane + 1) * rows], w_ref[0, plane])
    y_ref[...] = total.astype(BF)


def out_back(x, blocks):
    rows, width = x.shape
    ctx_count, fsdp_count, height, share = blocks.shape
    if share % 128:
        return nn(x, whole_of(blocks)).astype(BF)
    return pl.pallas_call(
        out_back_kernel,
        grid=(ctx_count,),
        out_shape=jax.ShapeDtypeStruct((rows, ctx_count * share), BF),
        in_specs=[
            pl.BlockSpec((rows, width), lambda c: (0, 0)),
            pl.BlockSpec((1, fsdp_count, height, share), lambda c: (c, 0, 0, 0)),
        ],
        out_specs=pl.BlockSpec((rows, share), lambda c: (0, c)),
        compiler_params=pltpu.CompilerParams(vmem_limit_bytes=24 << 20),
        cost_estimate=pl.CostEstimate(
            flops=2 * rows * width * ctx_count * share,
            bytes_accessed=2 * width * ctx_count * share,
            transcendentals=0,
        ),
        name="out_back",
    )(x, blocks)


def gather_rows(values, label=None):
    count = lax.axis_size("fsdp")
    planes = {0: values}
    if count == 4 and label:
        planes[3] = swap(values, "fsdp", 3)
        planes[1] = swap(values, "fsdp", 1)
        planes[2] = swap(planes[3], "fsdp", 1)
    else:
        for away in range(1, count):
            planes[away] = swap(values, "fsdp", away)
    half = count // 2
    return tuple(
        jnp.concatenate([planes[away] for away in group], axis=0)
        for group in (range(half), range(half, count))
    )


def sum_rows(halves):
    count = lax.axis_size("fsdp")
    half = count // 2
    rows = halves[0].shape[0] // half
    parts = [
        halves[away // half][away % half * rows : (away % half + 1) * rows] for away in range(count)
    ]
    if count == 4:
        passed = swap(parts[2].astype(BF), "fsdp", 1).astype(F32)
        one = swap(parts[1].astype(BF), "fsdp", 1).astype(F32)
        third = swap((parts[3] + passed).astype(BF), "fsdp", 3).astype(F32)
        return parts[0] + one + third
    total = parts[0]
    for away in range(1, count):
        total = total + swap(parts[away].astype(BF), "fsdp", away).astype(F32)
    return total


def by_offset(values):
    count, plane = lax.axis_size("fsdp"), lax.axis_index("fsdp")
    rows = values.shape[0] // count
    return jnp.concatenate(
        [
            lax.dynamic_slice(values, ((plane ^ away) * rows, 0), (rows, values.shape[1]))
            for away in range(count)
        ],
        axis=0,
    )


def columns_to_owner(values):
    return lax.all_to_all(values, "fsdp", split_axis=1, concat_axis=0, tiled=True)


def rows_to_owner(values):
    count = lax.axis_size("fsdp")
    rows, columns = values.shape
    out = lax.all_to_all(values, "fsdp", split_axis=0, concat_axis=0, tiled=True)
    return out.reshape(count, rows // count, columns)


def joined(parts):
    return jnp.concatenate([parts[i] for i in range(parts.shape[0])], axis=1)


def sum_over_ctx(part_for):
    pairs = lax.axis_size("ctx") // 2
    sent = jnp.stack([part_for(2 * pair + 1).astype(BF) for pair in range(pairs)])
    got = swap(sent, "ctx", 1)
    sums = [part_for(2 * pair).astype(F32) + got[pair].astype(F32) for pair in range(pairs)]
    total = sums[0]
    for pair in range(1, pairs):
        total = total + swap(sums[pair].astype(BF), "ctx", 2 * pair).astype(F32)
    return total


def ctx_rows_sum(values):
    height = values.shape[0] // lax.axis_size("ctx")
    me = lax.axis_index("ctx")

    def part(offset):
        return lax.dynamic_slice(
            values, ((me ^ offset) * height, 0), (height, values.shape[1])
        )

    return sum_over_ctx(part)


def key_offsets():
    count = lax.axis_size("ctx")
    return list(range(0, count, 2)) + list(range(1, count, 2))


def gather_keys(piece):
    same = [piece] + [swap(piece, "ctx", far) for far in range(2, lax.axis_size("ctx"), 2)]
    mine = jnp.concatenate(same, axis=0)
    other = swap(mine, "ctx", 1)
    return jnp.concatenate([mine, other], axis=0)


def sum_pairs(parts, cosine, sine):
    _, count, width = parts.shape
    pairs = lax.axis_size("ctx") // 2
    parts = parts.reshape(2, 2, pairs, count // (2 * pairs), width)
    got = swap(parts[:, 1], "ctx", 1)
    sums = parts[:, 0].astype(F32) + got.astype(F32)
    far = [swap(sums[:, pair].astype(BF), "ctx", 2 * pair) for pair in range(1, pairs)]
    return pair_turn(sums[:, 0], far, cosine, sine)


def half_mask(shape):
    return lax.broadcasted_iota(jnp.int32, shape, len(shape) - 1) % 128 < HD


def turn(values, cosine, sine):
    lanes = lax.broadcasted_iota(jnp.int32, values.shape, 1) % HD
    turned = jnp.where(
        lanes < HD // 2, pltpu.roll(values, 128 - HD // 2, 1), pltpu.roll(values, HD // 2, 1)
    )
    return values * cosine + turned * sine


def doubled(tile, odd):
    wide = tile.astype(F32)
    other = pltpu.roll(wide, HD, 1)
    return jnp.where(half_mask(tile.shape) == (odd == 0), wide, other).astype(BF)


def split_heads(tile_pair):
    zero = jnp.zeros((), tile_pair.dtype)
    parts = []
    for j in range(2):
        tile = tile_pair[:, j * 128 : (j + 1) * 128]
        mask = half_mask(tile.shape)
        parts += [jnp.where(mask, tile, zero), jnp.where(mask, zero, tile)]
    return jnp.concatenate(parts, axis=0)


def merge_heads(stacked):
    rows = stacked.shape[0] // 4
    tiles = []
    for j in range(2):
        even = stacked[2 * j * rows : (2 * j + 1) * rows]
        odd = stacked[(2 * j + 1) * rows : (2 * j + 2) * rows]
        tiles.append(jnp.where(half_mask(even.shape), even, odd))
    return jnp.concatenate(tiles, axis=1)


def attend_kernel(q_ref, k_ref, v_ref, key_ref, own_ref, rows_ref, attended_ref, log_ref):
    odd = pl.program_id(0) % 2
    rows = q_ref.shape[0]
    queries = split_heads(q_ref[...])
    keys, values = doubled(k_ref[...], odd), doubled(v_ref[...], odd)
    allowed = key_ref[:, :1] <= own_ref[...]
    bias = jnp.where(allowed, 0.0, -1e30).astype(F32)
    bias = jnp.concatenate([bias] * 4, axis=1)
    scores = nt(keys, queries) + bias
    top = jnp.max(scores, axis=0, keepdims=True)
    weights = jnp.exp(scores - top)
    total = jnp.sum(weights, axis=0, keepdims=True)
    summed = tn(weights.astype(BF), values)
    log_ref[0] = top + jnp.log(total)
    attended = merge_heads(summed / jnp.transpose(jnp.broadcast_to(total, (128, 4 * rows))))
    attended_ref[...] = attended
    rows_ref[...] = attended.astype(BF)


def attend(queries, keys_values, key_anchor, own_anchor):
    rows, width = queries.shape
    count, both = keys_values.shape
    tiles = both // 256
    return pl.pallas_call(
        attend_kernel,
        grid=(KV,),
        out_shape=(
            jax.ShapeDtypeStruct((rows, width), BF),
            jax.ShapeDtypeStruct((rows, width), F32),
            jax.ShapeDtypeStruct((KV, 1, 4 * rows), F32),
        ),
        in_specs=[
            pl.BlockSpec((rows, 256), lambda g: (0, g)),
            pl.BlockSpec((count, 128), lambda g: (0, g // 2)),
            pl.BlockSpec((count, 128), lambda g: (0, tiles + g // 2)),
            pl.BlockSpec((count, 128), lambda g: (0, 0)),
            pl.BlockSpec((1, rows), lambda g: (0, 0)),
        ],
        out_specs=(
            pl.BlockSpec((rows, 256), lambda g: (0, g)),
            pl.BlockSpec((rows, 256), lambda g: (0, g)),
            pl.BlockSpec((1, 1, 4 * rows), lambda g: (g, 0, 0)),
        ),
        compiler_params=pltpu.CompilerParams(vmem_limit_bytes=48 << 20),
        cost_estimate=pl.CostEstimate(
            flops=4 * rows * width * count,
            bytes_accessed=2 * count * both,
            transcendentals=rows * H * count,
        ),
        name="attend",
    )(queries, keys_values, keys_values, key_anchor, own_anchor)


def attend_back_kernel(
    chunk, q_ref, grad_ref, attended_ref, k_ref, v_ref, key_ref, own_ref, log_ref, cos_ref, sin_ref,
    dq_ref, pair_ref,
):
    odd = pl.program_id(0) % 2
    rows = q_ref.shape[0]
    count = k_ref.shape[0]
    queries, grads = split_heads(q_ref[...]), split_heads(grad_ref[...])
    product = grads.astype(F32) * split_heads(attended_ref[...])
    delta = jnp.sum(jnp.transpose(product), axis=0, keepdims=True)
    log_total = log_ref[0]
    total = jnp.zeros((4 * rows, 128), F32)
    keep = half_mask((chunk, 128)) == (odd == 0)
    for start in range(0, count, chunk):
        at = slice(start, start + chunk)
        keys, values = doubled(k_ref[at, :], odd), doubled(v_ref[at, :], odd)
        allowed = key_ref[at, :1] <= own_ref[...]
        bias = jnp.where(allowed, 0.0, -1e30).astype(F32)
        bias = jnp.concatenate([bias] * 4, axis=1)
        probs = jnp.exp(nt(keys, queries) + bias - log_total)
        value_grad = nn(probs.astype(BF), grads)
        score_grad = (probs * (nt(values, grads) - delta)).astype(BF)
        key_grad = nn(score_grad, queries)
        total += tn(score_grad, keys)
        for part, value in enumerate((key_grad, value_grad)):
            value = (value + pltpu.roll(value, HD, 1)).astype(BF)
            pair_ref[part, at, :] = jnp.where(keep, value, pair_ref[part, at, :])
    merged = merge_heads(total) * (1.0 / math.sqrt(HD))
    cosine, sine = cos_ref[...], sin_ref[...]
    for j in range(2):
        tile = slice(j * 128, (j + 1) * 128)
        dq_ref[:, tile] = turn(merged[:, tile], cosine, -sine).astype(BF)


def attend_back(queries, grads, attended, keys_values, key_anchor, own_anchor, logs, cosine, sine):
    rows, width = queries.shape
    count, both = keys_values.shape
    tiles = both // 256
    wide = pl.BlockSpec((rows, 256), lambda g: (0, g))
    small = pl.BlockSpec((rows, 128), lambda g: (0, 0))
    return pl.pallas_call(
        lambda *refs: attend_back_kernel(256, *refs),
        grid=(KV,),
        out_shape=(
            jax.ShapeDtypeStruct((rows, width), BF),
            jax.ShapeDtypeStruct((2, count, both // 2), BF),
        ),
        in_specs=[
            wide,
            wide,
            wide,
            pl.BlockSpec((count, 128), lambda g: (0, g // 2)),
            pl.BlockSpec((count, 128), lambda g: (0, tiles + g // 2)),
            pl.BlockSpec((count, 128), lambda g: (0, 0)),
            pl.BlockSpec((1, rows), lambda g: (0, 0)),
            pl.BlockSpec((1, 1, 4 * rows), lambda g: (g, 0, 0)),
            small,
            small,
        ],
        out_specs=(
            wide,
            pl.BlockSpec((2, count, 128), lambda g: (0, 0, g // 2)),
        ),
        compiler_params=pltpu.CompilerParams(vmem_limit_bytes=48 << 20),
        cost_estimate=pl.CostEstimate(
            flops=10 * rows * width * count,
            bytes_accessed=4 * count * both,
            transcendentals=rows * H * count,
        ),
        name="attend_back",
    )(queries, grads, attended, keys_values, keys_values, key_anchor, own_anchor, logs, cosine, sine)


def pair_turn_kernel(own_ref, *refs):
    got, (cos_ref, sin_ref, y_ref) = refs[:-3], refs[-3:]
    total = own_ref[...]
    for ref in got:
        total = total + ref[...].astype(F32)
    cosine, sine = cos_ref[...], sin_ref[...]
    width = total.shape[2]
    for start in range(0, width, 128):
        tile = slice(start, start + 128)
        y_ref[:, tile] = turn(total[0, :, tile], cosine, -sine).astype(BF)
    y_ref[:, width:] = total[1].astype(BF)


def pair_turn(own, got, cosine, sine):
    _, rows, width = own.shape
    return pl.pallas_call(
        pair_turn_kernel,
        out_shape=jax.ShapeDtypeStruct((rows, 2 * width), BF),
        name="pair_turn",
    )(own, *got, cosine, sine)


def ffn_kernel(x_ref, act_ref, w_ref, out_ref, sum_ref):
    step = pl.program_id(0)
    gate_w, up_w = w_ref[0], w_ref[1]
    x = x_ref[...]
    gate, up = nn(x, gate_w), nn(x, up_w)
    act_grad = act_ref[...]
    sig = jax.nn.sigmoid(gate)
    silu = gate * sig
    gate_grad = (act_grad * up * sig * (1.0 + gate * (1.0 - sig))).astype(BF)
    up_grad = (act_grad * silu).astype(BF)
    out_ref[0], out_ref[1], out_ref[2] = gate_grad, up_grad, (silu * up).astype(BF)
    part = nt(gate_grad, gate_w) + nt(up_grad, up_w)

    @pl.when(step == 0)
    def _():
        sum_ref[...] = part

    @pl.when(step > 0)
    def _():
        sum_ref[...] += part


def ffn_middle(rows_in, act_grad, weights):
    rows, width = rows_in.shape
    hidden = weights.shape[2]
    tile = FFN_TILE
    return pl.pallas_call(
        ffn_kernel,
        grid=(hidden // tile,),
        out_shape=(
            jax.ShapeDtypeStruct((3, rows, hidden), BF),
            jax.ShapeDtypeStruct((rows, width), F32),
        ),
        in_specs=[
            pl.BlockSpec((rows, width), lambda j: (0, 0)),
            pl.BlockSpec((rows, tile), lambda j: (0, j)),
            pl.BlockSpec((2, width, tile), lambda j: (0, 0, j)),
        ],
        out_specs=(
            pl.BlockSpec((3, rows, tile), lambda j: (0, 0, j)),
            pl.BlockSpec((rows, width), lambda j: (0, 0)),
        ),
        compiler_params=pltpu.CompilerParams(vmem_limit_bytes=40 << 20),
        cost_estimate=pl.CostEstimate(
            flops=8 * rows * width * hidden,
            bytes_accessed=4 * width * hidden,
            transcendentals=rows * hidden,
        ),
        name="ffn_middle",
    )(rows_in, act_grad, weights)


def products_kernel(in_a, in_b, grad_a, grad_b, right_a, right_b, out_ref):
    def emit(left_a, left_b):
        out_ref[0] = (tn(left_a[...], right_a[0]) + tn(left_b[...], right_b[0])).astype(BF)

    @pl.when(pl.program_id(0) < 2)
    def _():
        emit(in_a, in_b)

    @pl.when(pl.program_id(0) == 2)
    def _():
        emit(grad_a, grad_b)


def ffn_products(rows_in, rows_out, parts):
    rows, width = rows_in[0].shape
    hidden = parts[0].shape[2]
    tile = FFN_TILE
    last = width // tile - 1
    left = pl.BlockSpec((rows, tile), lambda k, i: (0, jnp.where(k < 2, i, last)))
    grad = pl.BlockSpec((rows, tile), lambda k, i: (0, jnp.where(k == 2, i, 0)))
    right = pl.BlockSpec((1, rows, hidden), lambda k, i: (k, 0, 0))
    return pl.pallas_call(
        products_kernel,
        grid=(3, width // tile),
        out_shape=jax.ShapeDtypeStruct((3, width, hidden), BF),
        in_specs=[left, left, grad, grad, right, right],
        out_specs=pl.BlockSpec((1, tile, hidden), lambda k, i: (k, i, 0)),
        compiler_params=pltpu.CompilerParams(vmem_limit_bytes=32 << 20),
        cost_estimate=pl.CostEstimate(
            flops=12 * rows * width * hidden,
            bytes_accessed=6 * width * hidden,
            transcendentals=0,
        ),
        name="ffn_products",
    )(*rows_in, *rows_out, *parts)


def simple_kernel(x_ref, w_ref, y_ref):
    y_ref[...] = nn(x_ref[...], w_ref[0])


def down_back(x, weights):
    rows, width = x.shape
    hidden = weights.shape[2]
    tile = FFN_TILE
    return pl.pallas_call(
        simple_kernel,
        grid=(hidden // tile,),
        out_shape=jax.ShapeDtypeStruct((rows, hidden), F32),
        in_specs=[
            pl.BlockSpec((rows, width), lambda j: (0, 0)),
            pl.BlockSpec((1, width, tile), lambda j: (2, 0, j)),
        ],
        out_specs=pl.BlockSpec((rows, tile), lambda j: (0, j)),
        compiler_params=pltpu.CompilerParams(vmem_limit_bytes=24 << 20),
        cost_estimate=pl.CostEstimate(
            flops=2 * rows * width * hidden,
            bytes_accessed=2 * width * hidden,
            transcendentals=0,
        ),
        name="down_back",
    )(x, weights)


def share_kernel(count, pairs, ids_ref, *refs):
    lefts, rights = refs[:count], refs[count : 2 * count]
    rest = refs[2 * count :]
    step = pl.program_id(0)
    terms, (sent_ref, kept_ref) = rest[:-2], rest[-2:]
    parts = [tn(left[...], right[...]) for left, right in zip(lefts, rights)]
    if terms:
        tall = [jnp.broadcast_to(term[...], (64, term.shape[1])) for term in terms]
        parts.append(jnp.transpose(jnp.concatenate(tall, axis=0)))
    block = jnp.concatenate(parts, axis=1).astype(BF)

    @pl.when(step < pairs)
    def _():
        sent_ref[0] = block

    @pl.when(step >= pairs)
    def _():
        kept_ref[0] = block


def share_products(lefts, rights, terms):
    ctx_count = lax.axis_size("ctx")
    pairs = ctx_count // 2
    rows, width = lefts[0].shape
    height = width // ctx_count
    columns = sum(right.shape[1] for right in rights) + 64 * len(terms)

    def place(i, ids_ref):
        offset = jnp.where(i < pairs, 2 * i + 1, 2 * (i - pairs))
        return (0, ids_ref[0] ^ offset)

    shape = jax.ShapeDtypeStruct((pairs, height, columns), BF)
    return pl.pallas_call(
        lambda *refs: share_kernel(len(lefts), pairs, *refs),
        grid_spec=pltpu.PrefetchScalarGridSpec(
            num_scalar_prefetch=1,
            grid=(ctx_count,),
            in_specs=[pl.BlockSpec((rows, height), place) for _ in lefts]
            + [pl.BlockSpec(right.shape, lambda i, ids_ref: (0, 0)) for right in rights]
            + [pl.BlockSpec((1, height), place) for _ in terms],
            out_specs=(
                pl.BlockSpec(
                    (1, height, columns), lambda i, ids_ref: (jnp.minimum(i, pairs - 1), 0, 0)
                ),
                pl.BlockSpec(
                    (1, height, columns), lambda i, ids_ref: (jnp.maximum(i - pairs, 0), 0, 0)
                ),
            ),
        ),
        out_shape=(shape, shape),
        compiler_params=pltpu.CompilerParams(vmem_limit_bytes=24 << 20),
        cost_estimate=pl.CostEstimate(
            flops=2 * rows * width * columns,
            bytes_accessed=2 * (rows + columns) * width,
            transcendentals=0,
        ),
        name="share_terms" if terms else "share_products",
    )(jnp.stack(ids()), *lefts, *rights, *[term[None] for term in terms])


def share_sum(lefts, rights, terms):
    pairs = lax.axis_size("ctx") // 2
    if (lefts[0].shape[1] // (2 * pairs)) % 128:
        values = [tn(left, right) for left, right in zip(lefts, rights)]
        values += [jnp.broadcast_to(term[:, None], (term.shape[0], 64)) for term in terms]
        return ctx_rows_sum(jnp.concatenate(values, axis=1)).astype(BF)
    sent, kept = share_products(lefts, rights, terms)
    got = swap(sent, "ctx", 1)
    total = kept[0].astype(F32) + got[0].astype(F32)
    for pair in range(1, pairs):
        part = (kept[pair].astype(F32) + got[pair].astype(F32)).astype(BF)
        total = total + swap(part, "ctx", 2 * pair).astype(F32)
    return total.astype(BF)


def layer(
    hidden_in,
    out_grad,
    positions,
    block_order,
    attn_gain,
    ffn_gain,
    qkv_weight,
    out_weight,
    ffn_weight,
):
    ctx_count = lax.axis_size("ctx")
    me, _ = ids()
    rows = hidden_in.shape[1]
    queries_width, kv_width = H * HD, KV * HD
    ffn_parts = ffn_weight.transpose(1, 0, 2)

    frequency = jnp.power(ROPE_BASE, -(jnp.arange(HD // 2, dtype=F32) * 2.0 / HD))
    angles = positions[0].astype(F32)[:, None] * frequency[None, :]
    cosine = jnp.tile(jnp.cos(angles), (1, 4))
    sine = jnp.tile(jnp.concatenate([-jnp.sin(angles), jnp.sin(angles)], axis=1), (1, 2))
    own_anchor = anchors_of(block_order, me, rows)[None]
    key_anchor = jnp.concatenate(
        [anchors_of(block_order, me ^ offset, rows) for offset in key_offsets()]
    )
    key_anchor = jnp.broadcast_to(key_anchor[:, None], (rows * ctx_count, 128))

    inputs = hidden_in[0].astype(F32)
    grad_in = out_grad[0]
    scale_one = norm_scale(inputs)
    normed_one = (inputs * scale_one * attn_gain).astype(BF)

    fast = ctx_count == 8 and (qkv_weight.shape[1] // ctx_count) % 128 == 0
    if fast:
        qkv_pieces, marks = gather_pieces(qkv_weight)
        out_blocks = gather_blocks(out_weight, *marks)
        queries, pair = pieces_forward(normed_one, qkv_weight, qkv_pieces, cosine, sine)
    else:
        out_blocks = gather_blocks(out_weight, normed_one, normed_one)
        qkv_full = whole_of(gather_blocks(qkv_weight, normed_one, normed_one))
        projected = nn(normed_one, qkv_full)
        turned = rotate(
            projected[:, : queries_width + kv_width].reshape(rows, H + KV, HD), positions[0]
        ).reshape(rows, queries_width + kv_width)
        queries = (turned[:, :queries_width] * (1.0 / math.sqrt(HD))).astype(BF)
        pair = jnp.concatenate(
            [turned[:, queries_width:], projected[:, queries_width + kv_width :]], axis=1
        ).astype(BF)
    keys_values = gather_keys(pair)
    rows_out = gather_rows(after(grad_in, pair))
    act_grad = []
    for half in rows_out:
        act_grad.append(down_back(half, ffn_parts))

    attn_rows, attended, logs = attend(queries, keys_values, key_anchor, own_anchor)
    residual, normed_two = out_forward(attn_rows, out_blocks, hidden_in[0], ffn_gain)
    scale_two = norm_scale(residual)
    rows_in = gather_rows(normed_two, "normed")

    attn_share = by_offset(columns_to_owner(after(attn_rows, rows_in[1])))
    middle = []
    for half, act in zip(rows_in, act_grad):
        middle.append(ffn_middle(half, act, ffn_parts))
    parts, partial = [m[0] for m in middle], [m[1] for m in middle]
    sum_grad = sum_rows(partial)
    rows_one = lax.all_gather(after(normed_one, rows_in), "fsdp", tiled=True)
    products = ffn_products(rows_in, rows_out, parts).transpose(1, 0, 2)
    ffn_weight_grad = lax.psum_scatter(products, "ctx", scatter_dimension=0, tiled=True)
    ffn_weight_grad = ffn_weight_grad.astype(F32)
    out_partial = [nt(part[2], ffn_parts[2]) for part in parts]

    unit_two = residual * scale_two
    ffn_gain_term = jnp.sum(sum_grad * unit_two, axis=0)
    scaled_two = ffn_gain * sum_grad
    residual_grad = grad_in.astype(F32) + scale_two * (
        scaled_two - unit_two * jnp.mean(scaled_two * unit_two, axis=-1, keepdims=True)
    )
    residual_bf = residual_grad.astype(BF)
    residual_planes = jnp.concatenate(gather_rows(residual_bf), axis=0)
    attn_grad = out_back(residual_bf, out_blocks)
    query_part, pair_grads = attend_back(
        queries, attn_grad, attended, keys_values, key_anchor, own_anchor, logs, cosine, sine
    )
    query_owned = columns_to_owner(query_part)
    pair_part = sum_pairs(pair_grads, cosine, sine)
    pair_owned = columns_to_owner(pair_part)
    first_sums = share_sum(
        [residual_planes, after(rows_one, pair_part)], [attn_share, query_owned], []
    )
    first_sums = rows_to_owner(first_sums).astype(F32)

    projected_grad = jnp.concatenate([query_part, pair_part], axis=1)
    if fast:
        normed_one_grad = pieces_back(projected_grad, qkv_weight, qkv_pieces)
    else:
        normed_one_grad = nt(projected_grad, qkv_full)
    unit_one = inputs * scale_one
    attn_gain_term = jnp.sum(normed_one_grad * unit_one, axis=0)
    scaled_one = attn_gain * normed_one_grad
    input_grad = residual_grad + scale_one * (
        scaled_one - unit_one * jnp.mean(scaled_one * unit_one, axis=-1, keepdims=True)
    )

    last_sums = share_sum([rows_one], [pair_owned], [attn_gain_term, ffn_gain_term])
    last_sums = rows_to_owner(last_sums).astype(F32)

    out_sum = sum_rows([after(half, pair_part) for half in out_partial])
    output = (residual + out_sum).astype(BF)

    out_columns, pair_columns = attn_share.shape[1], pair_owned.shape[1]
    out_weight_grad = joined(first_sums[:, :, :out_columns])
    qkv_grad = jnp.concatenate(
        [joined(first_sums[:, :, out_columns:]), joined(last_sums[:, :, :pair_columns])], axis=1
    )
    gain_grads = jnp.sum(last_sums[:, :, pair_columns:], axis=0)
    return (
        output[None],
        input_grad[None],
        qkv_grad,
        out_weight_grad,
        ffn_weight_grad,
        gain_grads[:, 0],
        gain_grads[:, 64],
    )


def solution(mesh):
    step = sharded(mesh)
    return step


def sharded(mesh):
    return jax.shard_map(
        layer,
        mesh=mesh,
        in_specs=(
            P("fsdp", "ctx", None),
            P("fsdp", "ctx", None),
            P("fsdp", "ctx"),
            P(),
            P(),
            P(),
            P("fsdp", None),
            P("fsdp", None),
            P(None, None, "fsdp"),
        ),
        out_specs=(
            P("fsdp", "ctx", None),
            P("fsdp", "ctx", None),
            P(("ctx", "fsdp"), None),
            P(("ctx", "fsdp"), None),
            P("ctx", None, "fsdp"),
            P(("ctx", "fsdp")),
            P(("ctx", "fsdp")),
        ),
        check_vma=False,
    )
```

```python
import math

import jax
import jax.numpy as jnp
from jax import lax
from jax.experimental import pallas as pl
from jax.experimental.pallas import tpu as pltpu
from jax.sharding import PartitionSpec as P


H = 32
KV = 8
HD = 64

NORM_EPS = 1e-05
ROPE_BASE = 500000.0
FFN_TILE = 512


BF = jnp.bfloat16
F32 = jnp.float32


def mm(a, b, dims):
    return lax.dot_general(a, b, (dims, ((), ())), preferred_element_type=F32)


def nn(a, b):
    return mm(a, b, ((1,), (0,)))


def nt(a, b):
    return mm(a, b, ((1,), (1,)))


def tn(a, b):
    return mm(a, b, ((0,), (0,)))


def swap(value, axis, offset):
    count = lax.axis_size(axis)
    return lax.ppermute(value, axis, [(i, i ^ offset) for i in range(count)])


def rotate(values, token_places):
    head_dim = values.shape[-1]
    half_dim = head_dim // 2
    frequency = jnp.power(ROPE_BASE, -(jnp.arange(half_dim, dtype=F32) * 2.0 / head_dim))
    angles = token_places.astype(F32)[:, None] * frequency[None, :]
    cosine = jnp.concatenate([jnp.cos(angles), jnp.cos(angles)], axis=-1)[:, None, :]
    sine_part = jnp.concatenate([jnp.sin(angles), jnp.sin(angles)], axis=-1)[:, None, :]
    turned = jnp.concatenate([-values[..., half_dim:], values[..., :half_dim]], axis=-1)
    return values * cosine + turned * sine_part


def norm_scale(values):
    return lax.rsqrt(jnp.mean(values * values, axis=-1, keepdims=True) + NORM_EPS)


def lookup(entries, row_ids):
    matches = row_ids[:, None] == jnp.arange(entries.shape[0], dtype=jnp.int32)[None, :]
    return jnp.sum(jnp.where(matches, entries[None, :], 0), axis=1)


def anchors_of(block_order, owner, row_count):
    block_len = row_count // 2
    row_ids = owner * row_count + jnp.arange(row_count, dtype=jnp.int32)
    return lookup(block_order, row_ids // block_len) * block_len + row_ids % block_len


def after(value, *earlier):
    return lax.optimization_barrier((value, earlier))[0]


def ids():
    return lax.axis_index("ctx"), lax.axis_index("fsdp")


def gather_pieces(weight, early, ones):
    rows, columns = weight.shape
    share = columns // lax.axis_size("ctx")
    half = rows // 2
    mine = lax.dynamic_slice(weight, (0, lax.axis_index("ctx") * share), (rows, share))
    planes = {}
    planes[3] = swap(mine, "fsdp", 3)
    planes[1] = swap(mine, "fsdp", 1)
    planes[2] = swap(after(planes[3], early), "fsdp", 1)
    rows_one = gather_rows(ones)
    pieces = []
    for away in (1, 3, 2):
        first = planes[away]
        along_x, along_y = swap(first, "ctx", 2), swap(first, "ctx", 4)
        top, low = swap(along_y[:half], "ctx", 2), swap(along_x[half:], "ctx", 4)
        parts = [(0, 0, first), (2, 0, along_x), (4, 0, along_y), (6, 0, top), (6, half, low)]
        for offset, start, part in parts:
            pieces.append((away, offset, start, part))
            pieces.append((away, offset + 1, start, swap(part, "ctx", 1)))
    return pieces, (planes[1], (pieces[-4][3], pieces[-2][3])), rows_one


def pieces_kernel(places, rows_in, share, ids_ref, x_ref, own_ref, *refs):
    count = len(places)
    piece_refs, refs = refs[:count], refs[count:]
    cos_ref, sin_ref, q_ref, pair_ref, full_ref, y_ref, buf, in_sems, out_sems = refs
    me, plane = ids_ref[0], ids_ref[1]

    def block(away):
        return pl.ds(pl.multiple_of((plane ^ away) * rows_in, 128), rows_in)

    own_copy = pltpu.make_async_copy(own_ref, buf.at[block(0)], in_sems.at[count])
    own_copy.start()
    copies = []
    for i, (away, offset, start, height) in enumerate(places):
        at = pl.ds(pl.multiple_of((plane ^ away) * rows_in + start, 128), height)
        columns = pl.ds(pl.multiple_of((me ^ offset) * share, 128), share)
        copies.append(pltpu.make_async_copy(piece_refs[i], buf.at[at, columns], in_sems.at[i]))
        copies[-1].start()
    outs = []
    order = [0] + list(dict.fromkeys(away for away, _, _, _ in places))
    for away in order:
        if away:
            for copy, place in zip(copies, places):
                if place[0] == away:
                    copy.wait()
        else:
            own_copy.wait()
        outs.append(
            pltpu.make_async_copy(buf.at[block(away)], full_ref.at[block(away)], out_sems.at[away])
        )
        outs[-1].start()
        part = nn(x_ref[:, block(away)], buf[block(away)])
        y_ref[...] = part if away == 0 else y_ref[...] + part
    cosine, sine = cos_ref[...], sin_ref[...]
    queries, keys = H * HD, KV * HD
    for start in range(0, queries + keys, 128):
        tile = turn(y_ref[:, start : start + 128], cosine, sine)
        if start < queries:
            q_ref[:, start : start + 128] = (tile * (1.0 / math.sqrt(HD))).astype(BF)
        else:
            pair_ref[:, start - queries : start - queries + 128] = tile.astype(BF)
    pair_ref[:, keys:] = y_ref[:, queries + keys :].astype(BF)
    for copy in outs:
        copy.wait()


def pieces_forward(x, own, pieces, cosine, sine):
    me, plane = ids()
    rows_in, columns = own.shape
    rows, width = x.shape
    share = columns // lax.axis_size("ctx")
    places = tuple((away, offset, start, part.shape[0]) for away, offset, start, part in pieces)
    arrays = [part for _, _, _, part in pieces]
    hbm, vmem = pl.BlockSpec(memory_space=pltpu.HBM), pl.BlockSpec(memory_space=pltpu.VMEM)
    return pl.pallas_call(
        lambda *refs: pieces_kernel(places, rows_in, share, *refs),
        out_shape=(
            jax.ShapeDtypeStruct((rows, H * HD), BF),
            jax.ShapeDtypeStruct((rows, 2 * KV * HD), BF),
            jax.ShapeDtypeStruct((width, columns), BF),
        ),
        in_specs=[pl.BlockSpec(memory_space=pltpu.SMEM), vmem, hbm]
        + [hbm] * len(arrays)
        + [vmem, vmem],
        out_specs=(vmem, vmem, hbm),
        scratch_shapes=[
            pltpu.VMEM((rows, columns), F32),
            pltpu.VMEM((width, columns), BF),
            pltpu.SemaphoreType.DMA((len(arrays) + 1,)),
            pltpu.SemaphoreType.DMA((width // rows_in,)),
        ],
        compiler_params=pltpu.CompilerParams(vmem_limit_bytes=32 << 20),
        cost_estimate=pl.CostEstimate(
            flops=2 * rows * width * columns, bytes_accessed=4 * width * columns, transcendentals=0
        ),
        name="pieces_forward",
    )(jnp.stack([me, plane]), x, own, *arrays, cosine, sine)


def gather_blocks(weight, before_fsdp, before_ctx):
    rows, columns = weight.shape
    me, plane = ids()
    share = columns // lax.axis_size("ctx")
    mine = lax.dynamic_slice(weight, (0, me * share), (rows, share))
    planes = lax.all_gather(after(mine, before_fsdp), "fsdp")
    others = jnp.stack(
        [
            lax.dynamic_index_in_dim(planes, plane ^ away, 0, keepdims=False)
            for away in range(1, planes.shape[0])
        ]
    )
    return lax.all_gather(after(others, before_ctx), "ctx")


def whole_of(own, blocks):
    ctx_count, others, rows, share = blocks.shape
    plane = lax.axis_index("fsdp")
    columns = ctx_count * share
    full = jnp.zeros(((others + 1) * rows, columns), own.dtype)
    full = lax.dynamic_update_slice(full, own, (plane * rows, 0))
    for away in range(1, others + 1):
        part = blocks[:, away - 1].transpose(1, 0, 2).reshape(rows, columns)
        full = lax.dynamic_update_slice(full, part, ((plane ^ away) * rows, 0))
    return full


def in_hbm(value):
    return pltpu.with_memory_space_constraint(value, pltpu.HBM)


def out_forward_kernel(
    ids_ref, x_ref, own_ref, w_ref, hidden_ref, gain_ref, residual_ref, normed_ref
):
    step = pl.program_id(0)

    @pl.when(step == 0)
    def _():
        residual_ref[...] = hidden_ref[...].astype(F32)

    rows = w_ref.shape[2]
    plane = ids_ref[1]
    for away in range(w_ref.shape[1] + 1):
        at = pl.ds(pl.multiple_of((plane ^ away) * rows, 128), rows)
        residual_ref[:, at] += nt(x_ref[...], w_ref[0, away - 1] if away else own_ref[...])

    @pl.when(step == pl.num_programs(0) - 1)
    def _():
        residual = residual_ref[...]
        normed_ref[...] = (residual * norm_scale(residual) * gain_ref[...]).astype(BF)


def out_specs_of(blocks):
    _, others, height, share = blocks.shape
    return [
        pl.BlockSpec((height, share), lambda c, ids_ref: (0, c)),
        pl.BlockSpec((1, others, height, share), lambda c, ids_ref: (c, 0, 0, 0)),
    ]


def out_forward(attn_rows, own, blocks, hidden, gain):
    rows, width = hidden.shape
    ctx_count, _, _, share = blocks.shape
    if share % 128:
        residual = hidden.astype(F32) + nt(attn_rows, whole_of(own, blocks))
        return residual, (residual * norm_scale(residual) * gain).astype(BF)
    whole = pl.BlockSpec((rows, width), lambda c, ids_ref: (0, 0))
    return pl.pallas_call(
        out_forward_kernel,
        grid_spec=pltpu.PrefetchScalarGridSpec(
            num_scalar_prefetch=1,
            grid=(ctx_count,),
            in_specs=[pl.BlockSpec((rows, share), lambda c, ids_ref: (0, c))]
            + out_specs_of(blocks)
            + [whole, pl.BlockSpec((1, width), lambda c, ids_ref: (0, 0))],
            out_specs=(whole, whole),
        ),
        out_shape=(
            jax.ShapeDtypeStruct((rows, width), F32),
            jax.ShapeDtypeStruct((rows, width), BF),
        ),
        compiler_params=pltpu.CompilerParams(vmem_limit_bytes=24 << 20),
        cost_estimate=pl.CostEstimate(
            flops=2 * rows * width * ctx_count * share,
            bytes_accessed=2 * width * ctx_count * share,
            transcendentals=0,
        ),
        name="out_forward",
    )(jnp.stack(ids()), attn_rows, in_hbm(own), in_hbm(blocks), hidden, gain[None])


def out_back_kernel(ids_ref, x_ref, own_ref, w_ref, y_ref):
    rows = w_ref.shape[2]
    plane = ids_ref[1]
    total = None
    for away in range(w_ref.shape[1] + 1):
        at = pl.ds(pl.multiple_of((plane ^ away) * rows, 128), rows)
        part = nn(x_ref[:, at], w_ref[0, away - 1] if away else own_ref[...])
        total = part if total is None else total + part
    y_ref[...] = total.astype(BF)


def out_back(x, own, blocks):
    rows, width = x.shape
    ctx_count, _, _, share = blocks.shape
    if share % 128:
        return nn(x, whole_of(own, blocks)).astype(BF)
    return pl.pallas_call(
        out_back_kernel,
        grid_spec=pltpu.PrefetchScalarGridSpec(
            num_scalar_prefetch=1,
            grid=(ctx_count,),
            in_specs=[pl.BlockSpec((rows, width), lambda c, ids_ref: (0, 0))]
            + out_specs_of(blocks),
            out_specs=pl.BlockSpec((rows, share), lambda c, ids_ref: (0, c)),
        ),
        out_shape=jax.ShapeDtypeStruct((rows, ctx_count * share), BF),
        compiler_params=pltpu.CompilerParams(vmem_limit_bytes=24 << 20),
        cost_estimate=pl.CostEstimate(
            flops=2 * rows * width * ctx_count * share,
            bytes_accessed=2 * width * ctx_count * share,
            transcendentals=0,
        ),
        name="out_back",
    )(jnp.stack(ids()), x, in_hbm(own), in_hbm(blocks))


def gather_rows(values, label=None):
    count = lax.axis_size("fsdp")
    planes = {0: values}
    if count == 4 and label:
        planes[3] = swap(values, "fsdp", 3)
        planes[1] = swap(values, "fsdp", 1)
        planes[2] = swap(planes[3], "fsdp", 1)
    else:
        for away in range(1, count):
            planes[away] = swap(values, "fsdp", away)
    return halves_of([planes[away] for away in range(count)])


def fetch_rows(values):
    count = lax.axis_size("fsdp")
    return [values] + [swap(values, "fsdp", away) for away in range(1, count)]


def halves_of(planes):
    half = len(planes) // 2
    return (jnp.concatenate(planes[:half], axis=0), jnp.concatenate(planes[half:], axis=0))


def sum_rows(halves):
    count = lax.axis_size("fsdp")
    half = count // 2
    rows = halves[0].shape[0] // half
    parts = [
        halves[away // half][away % half * rows : (away % half + 1) * rows] for away in range(count)
    ]
    if count == 4:
        passed = swap(parts[2].astype(BF), "fsdp", 1).astype(F32)
        one = swap(parts[1].astype(BF), "fsdp", 1).astype(F32)
        third = swap((parts[3] + passed).astype(BF), "fsdp", 3).astype(F32)
        return parts[0] + one + third
    total = parts[0]
    for away in range(1, count):
        total = total + swap(parts[away].astype(BF), "fsdp", away).astype(F32)
    return total


def by_offset(values):
    count, plane = lax.axis_size("fsdp"), lax.axis_index("fsdp")
    rows = values.shape[0] // count
    return jnp.concatenate(
        [
            lax.dynamic_slice(values, ((plane ^ away) * rows, 0), (rows, values.shape[1]))
            for away in range(count)
        ],
        axis=0,
    )


def columns_to_owner(values):
    return lax.all_to_all(values, "fsdp", split_axis=1, concat_axis=0, tiled=True)


def rows_to_owner(values):
    count = lax.axis_size("fsdp")
    rows, columns = values.shape
    out = lax.all_to_all(values, "fsdp", split_axis=0, concat_axis=0, tiled=True)
    return out.reshape(count, rows // count, columns)


def joined(parts):
    return jnp.concatenate([parts[i] for i in range(parts.shape[0])], axis=1)


def sum_over_ctx(part_for):
    pairs = lax.axis_size("ctx") // 2
    sent = jnp.stack([part_for(2 * pair + 1).astype(BF) for pair in range(pairs)])
    got = swap(sent, "ctx", 1)
    sums = [part_for(2 * pair).astype(F32) + got[pair].astype(F32) for pair in range(pairs)]
    total = sums[0]
    for pair in range(1, pairs):
        total = total + swap(sums[pair].astype(BF), "ctx", 2 * pair).astype(F32)
    return total


def ctx_rows_sum(values):
    height = values.shape[0] // lax.axis_size("ctx")
    me = lax.axis_index("ctx")

    def part(offset):
        return lax.dynamic_slice(
            values, ((me ^ offset) * height, 0), (height, values.shape[1])
        )

    return sum_over_ctx(part)


def key_offsets():
    count = lax.axis_size("ctx")
    return list(range(0, count, 2)) + list(range(1, count, 2))


def gather_keys(piece):
    same = [piece] + [swap(piece, "ctx", far) for far in range(2, lax.axis_size("ctx"), 2)]
    mine = jnp.concatenate(same, axis=0)
    other = swap(mine, "ctx", 1)
    return jnp.concatenate([mine, other], axis=0)


def sum_pairs(parts, cosine, sine):
    _, count, width = parts.shape
    pairs = lax.axis_size("ctx") // 2
    parts = parts.reshape(2, 2, pairs, count // (2 * pairs), width)
    got = swap(parts[:, 1], "ctx", 1)
    sums = parts[:, 0].astype(F32) + got.astype(F32)
    far = [swap(sums[:, pair].astype(BF), "ctx", 2 * pair) for pair in range(1, pairs)]
    return pair_turn(sums[:, 0], far, cosine, sine)


def half_mask(shape):
    return lax.broadcasted_iota(jnp.int32, shape, len(shape) - 1) % 128 < HD


def turn(values, cosine, sine):
    lanes = lax.broadcasted_iota(jnp.int32, values.shape, 1) % HD
    turned = jnp.where(
        lanes < HD // 2, pltpu.roll(values, 128 - HD // 2, 1), pltpu.roll(values, HD // 2, 1)
    )
    return values * cosine + turned * sine


def doubled(tile, odd):
    wide = tile.astype(F32)
    other = pltpu.roll(wide, HD, 1)
    return jnp.where(half_mask(tile.shape) == (odd == 0), wide, other).astype(BF)


def split_heads(tile_pair):
    zero = jnp.zeros((), tile_pair.dtype)
    parts = []
    for j in range(2):
        tile = tile_pair[:, j * 128 : (j + 1) * 128]
        mask = half_mask(tile.shape)
        parts += [jnp.where(mask, tile, zero), jnp.where(mask, zero, tile)]
    return jnp.concatenate(parts, axis=0)


def merge_heads(stacked):
    rows = stacked.shape[0] // 4
    tiles = []
    for j in range(2):
        even = stacked[2 * j * rows : (2 * j + 1) * rows]
        odd = stacked[(2 * j + 1) * rows : (2 * j + 2) * rows]
        tiles.append(jnp.where(half_mask(even.shape), even, odd))
    return jnp.concatenate(tiles, axis=1)


def attend_kernel(q_ref, k_ref, v_ref, key_ref, own_ref, rows_ref, attended_ref, log_ref):
    odd = pl.program_id(0) % 2
    rows = q_ref.shape[0]
    queries = split_heads(q_ref[...])
    keys, values = doubled(k_ref[...], odd), doubled(v_ref[...], odd)
    allowed = key_ref[:, :1] <= own_ref[...]
    bias = jnp.where(allowed, 0.0, -1e30).astype(F32)
    bias = jnp.concatenate([bias] * 4, axis=1)
    scores = nt(keys, queries) + bias
    top = jnp.max(scores, axis=0, keepdims=True)
    weights = jnp.exp(scores - top)
    total = jnp.sum(weights, axis=0, keepdims=True)
    summed = tn(weights.astype(BF), values)
    log_ref[0] = top + jnp.log(total)
    attended = merge_heads(summed / jnp.transpose(jnp.broadcast_to(total, (128, 4 * rows))))
    attended_ref[...] = attended
    rows_ref[...] = attended.astype(BF)


def attend(queries, keys_values, key_anchor, own_anchor):
    rows, width = queries.shape
    count, both = keys_values.shape
    tiles = both // 256
    return pl.pallas_call(
        attend_kernel,
        grid=(KV,),
        out_shape=(
            jax.ShapeDtypeStruct((rows, width), BF),
            jax.ShapeDtypeStruct((rows, width), F32),
            jax.ShapeDtypeStruct((KV, 1, 4 * rows), F32),
        ),
        in_specs=[
            pl.BlockSpec((rows, 256), lambda g: (0, g)),
            pl.BlockSpec((count, 128), lambda g: (0, g // 2)),
            pl.BlockSpec((count, 128), lambda g: (0, tiles + g // 2)),
            pl.BlockSpec((count, 128), lambda g: (0, 0)),
            pl.BlockSpec((1, rows), lambda g: (0, 0)),
        ],
        out_specs=(
            pl.BlockSpec((rows, 256), lambda g: (0, g)),
            pl.BlockSpec((rows, 256), lambda g: (0, g)),
            pl.BlockSpec((1, 1, 4 * rows), lambda g: (g, 0, 0)),
        ),
        compiler_params=pltpu.CompilerParams(vmem_limit_bytes=48 << 20),
        cost_estimate=pl.CostEstimate(
            flops=4 * rows * width * count,
            bytes_accessed=2 * count * both,
            transcendentals=rows * H * count,
        ),
        name="attend",
    )(queries, keys_values, keys_values, key_anchor, own_anchor)


def attend_back_kernel(
    chunk, q_ref, grad_ref, attended_ref, k_ref, v_ref, key_ref, own_ref, log_ref, cos_ref, sin_ref,
    dq_ref, pair_ref,
):
    odd = pl.program_id(0) % 2
    rows = q_ref.shape[0]
    count = k_ref.shape[0]
    queries, grads = split_heads(q_ref[...]), split_heads(grad_ref[...])
    product = grads.astype(F32) * split_heads(attended_ref[...])
    delta = jnp.sum(jnp.transpose(product), axis=0, keepdims=True)
    log_total = log_ref[0]
    total = jnp.zeros((4 * rows, 128), F32)
    keep = half_mask((chunk, 128)) == (odd == 0)
    for start in range(0, count, chunk):
        at = slice(start, start + chunk)
        keys, values = doubled(k_ref[at, :], odd), doubled(v_ref[at, :], odd)
        allowed = key_ref[at, :1] <= own_ref[...]
        bias = jnp.where(allowed, 0.0, -1e30).astype(F32)
        bias = jnp.concatenate([bias] * 4, axis=1)
        probs = jnp.exp(nt(keys, queries) + bias - log_total)
        value_grad = nn(probs.astype(BF), grads)
        score_grad = (probs * (nt(values, grads) - delta)).astype(BF)
        key_grad = nn(score_grad, queries)
        total += tn(score_grad, keys)
        for part, value in enumerate((key_grad, value_grad)):
            value = (value + pltpu.roll(value, HD, 1)).astype(BF)
            pair_ref[part, at, :] = jnp.where(keep, value, pair_ref[part, at, :])
    merged = merge_heads(total) * (1.0 / math.sqrt(HD))
    cosine, sine = cos_ref[...], sin_ref[...]
    for j in range(2):
        tile = slice(j * 128, (j + 1) * 128)
        dq_ref[:, tile] = turn(merged[:, tile], cosine, -sine).astype(BF)


def attend_back(queries, grads, attended, keys_values, key_anchor, own_anchor, logs, cosine, sine):
    rows, width = queries.shape
    count, both = keys_values.shape
    tiles = both // 256
    wide = pl.BlockSpec((rows, 256), lambda g: (0, g))
    small = pl.BlockSpec((rows, 128), lambda g: (0, 0))
    return pl.pallas_call(
        lambda *refs: attend_back_kernel(256, *refs),
        grid=(KV,),
        out_shape=(
            jax.ShapeDtypeStruct((rows, width), BF),
            jax.ShapeDtypeStruct((2, count, both // 2), BF),
        ),
        in_specs=[
            wide,
            wide,
            wide,
            pl.BlockSpec((count, 128), lambda g: (0, g // 2)),
            pl.BlockSpec((count, 128), lambda g: (0, tiles + g // 2)),
            pl.BlockSpec((count, 128), lambda g: (0, 0)),
            pl.BlockSpec((1, rows), lambda g: (0, 0)),
            pl.BlockSpec((1, 1, 4 * rows), lambda g: (g, 0, 0)),
            small,
            small,
        ],
        out_specs=(
            wide,
            pl.BlockSpec((2, count, 128), lambda g: (0, 0, g // 2)),
        ),
        compiler_params=pltpu.CompilerParams(vmem_limit_bytes=48 << 20),
        cost_estimate=pl.CostEstimate(
            flops=10 * rows * width * count,
            bytes_accessed=4 * count * both,
            transcendentals=rows * H * count,
        ),
        name="attend_back",
    )(queries, grads, attended, keys_values, keys_values, key_anchor, own_anchor, logs, cosine, sine)


def pair_turn_kernel(own_ref, *refs):
    got, (cos_ref, sin_ref, y_ref) = refs[:-3], refs[-3:]
    total = own_ref[...]
    for ref in got:
        total = total + ref[...].astype(F32)
    cosine, sine = cos_ref[...], sin_ref[...]
    width = total.shape[2]
    for start in range(0, width, 128):
        tile = slice(start, start + 128)
        y_ref[:, tile] = turn(total[0, :, tile], cosine, -sine).astype(BF)
    y_ref[:, width:] = total[1].astype(BF)


def pair_turn(own, got, cosine, sine):
    _, rows, width = own.shape
    return pl.pallas_call(
        pair_turn_kernel,
        out_shape=jax.ShapeDtypeStruct((rows, 2 * width), BF),
        name="pair_turn",
    )(own, *got, cosine, sine)


def ffn_kernel(x_ref, act_ref, w_ref, out_ref, sum_ref):
    step = pl.program_id(0)
    gate_w, up_w = w_ref[0], w_ref[1]
    x = x_ref[...]
    gate, up = nn(x, gate_w), nn(x, up_w)
    act_grad = act_ref[...]
    sig = jax.nn.sigmoid(gate)
    silu = gate * sig
    gate_grad = (act_grad * up * sig * (1.0 + gate * (1.0 - sig))).astype(BF)
    up_grad = (act_grad * silu).astype(BF)
    out_ref[0], out_ref[1], out_ref[2] = gate_grad, up_grad, (silu * up).astype(BF)
    part = nt(gate_grad, gate_w) + nt(up_grad, up_w)

    @pl.when(step == 0)
    def _():
        sum_ref[...] = part

    @pl.when(step > 0)
    def _():
        sum_ref[...] += part


def ffn_middle(rows_in, act_grad, weights):
    rows, width = rows_in.shape
    hidden = weights.shape[2]
    tile = FFN_TILE
    return pl.pallas_call(
        ffn_kernel,
        grid=(hidden // tile,),
        out_shape=(
            jax.ShapeDtypeStruct((3, rows, hidden), BF),
            jax.ShapeDtypeStruct((rows, width), F32),
        ),
        in_specs=[
            pl.BlockSpec((rows, width), lambda j: (0, 0)),
            pl.BlockSpec((rows, tile), lambda j: (0, j)),
            pl.BlockSpec((2, width, tile), lambda j: (0, 0, j)),
        ],
        out_specs=(
            pl.BlockSpec((3, rows, tile), lambda j: (0, 0, j)),
            pl.BlockSpec((rows, width), lambda j: (0, 0)),
        ),
        compiler_params=pltpu.CompilerParams(vmem_limit_bytes=40 << 20),
        cost_estimate=pl.CostEstimate(
            flops=8 * rows * width * hidden,
            bytes_accessed=4 * width * hidden,
            transcendentals=rows * hidden,
        ),
        name="ffn_middle",
    )(rows_in, act_grad, weights)


def products_kernel(in_a, in_b, grad_a, grad_b, right_a, right_b, out_ref):
    def emit(left_a, left_b):
        out_ref[0] = (tn(left_a[...], right_a[0]) + tn(left_b[...], right_b[0])).astype(BF)

    @pl.when(pl.program_id(0) < 2)
    def _():
        emit(in_a, in_b)

    @pl.when(pl.program_id(0) == 2)
    def _():
        emit(grad_a, grad_b)


def ffn_products(rows_in, rows_out, parts):
    rows, width = rows_in[0].shape
    hidden = parts[0].shape[2]
    tile = FFN_TILE
    last = width // tile - 1
    left = pl.BlockSpec((rows, tile), lambda k, i: (0, jnp.where(k < 2, i, last)))
    grad = pl.BlockSpec((rows, tile), lambda k, i: (0, jnp.where(k == 2, i, 0)))
    right = pl.BlockSpec((1, rows, hidden), lambda k, i: (k, 0, 0))
    return pl.pallas_call(
        products_kernel,
        grid=(3, width // tile),
        out_shape=jax.ShapeDtypeStruct((3, width, hidden), BF),
        in_specs=[left, left, grad, grad, right, right],
        out_specs=pl.BlockSpec((1, tile, hidden), lambda k, i: (k, i, 0)),
        compiler_params=pltpu.CompilerParams(vmem_limit_bytes=32 << 20),
        cost_estimate=pl.CostEstimate(
            flops=12 * rows * width * hidden,
            bytes_accessed=6 * width * hidden,
            transcendentals=0,
        ),
        name="ffn_products",
    )(*rows_in, *rows_out, *parts)


def simple_kernel(x_ref, w_ref, y_ref):
    y_ref[...] = nn(x_ref[...], w_ref[0])


def down_back(x, weights):
    rows, width = x.shape
    hidden = weights.shape[2]
    tile = FFN_TILE
    return pl.pallas_call(
        simple_kernel,
        grid=(hidden // tile,),
        out_shape=jax.ShapeDtypeStruct((rows, hidden), F32),
        in_specs=[
            pl.BlockSpec((rows, width), lambda j: (0, 0)),
            pl.BlockSpec((1, width, tile), lambda j: (2, 0, j)),
        ],
        out_specs=pl.BlockSpec((rows, tile), lambda j: (0, j)),
        compiler_params=pltpu.CompilerParams(vmem_limit_bytes=24 << 20),
        cost_estimate=pl.CostEstimate(
            flops=2 * rows * width * hidden,
            bytes_accessed=2 * width * hidden,
            transcendentals=0,
        ),
        name="down_back",
    )(x, weights)


def down_kernel(a_ref, b_ref, w_ref, y_ref):
    rows = a_ref.shape[1]
    for half, ref in enumerate((a_ref, b_ref)):
        y_ref[half * rows : (half + 1) * rows] = nt(ref[0], w_ref[0])


def down_forward(parts, weights):
    _, rows, hidden = parts[0].shape
    width = weights.shape[1]
    tile = FFN_TILE
    left = pl.BlockSpec((1, rows, hidden), lambda j: (2, 0, 0))
    total = pl.pallas_call(
        down_kernel,
        grid=(width // tile,),
        out_shape=jax.ShapeDtypeStruct((2 * rows, width), F32),
        in_specs=[left, left, pl.BlockSpec((1, tile, hidden), lambda j: (2, j, 0))],
        out_specs=pl.BlockSpec((2 * rows, tile), lambda j: (0, j)),
        compiler_params=pltpu.CompilerParams(vmem_limit_bytes=24 << 20),
        cost_estimate=pl.CostEstimate(
            flops=4 * rows * width * hidden,
            bytes_accessed=2 * width * hidden,
            transcendentals=0,
        ),
        name="down_forward",
    )(*parts, weights)
    return total[:rows], total[rows:]


def share_kernel(count, pairs, ids_ref, *refs):
    lefts, rights = refs[:count], refs[count : 2 * count]
    rest = refs[2 * count :]
    step = pl.program_id(0)
    terms, (sent_ref, kept_ref) = rest[:-2], rest[-2:]
    parts = [tn(left[...], right[...]) for left, right in zip(lefts, rights)]
    if terms:
        tall = [jnp.broadcast_to(term[...], (64, term.shape[1])) for term in terms]
        parts.append(jnp.transpose(jnp.concatenate(tall, axis=0)))
    block = jnp.concatenate(parts, axis=1).astype(BF)

    @pl.when(step < pairs)
    def _():
        sent_ref[0] = block

    @pl.when(step >= pairs)
    def _():
        kept_ref[0] = block


def share_products(lefts, rights, terms):
    ctx_count = lax.axis_size("ctx")
    pairs = ctx_count // 2
    rows, width = lefts[0].shape
    height = width // ctx_count
    columns = sum(right.shape[1] for right in rights) + 64 * len(terms)

    def place(i, ids_ref):
        offset = jnp.where(i < pairs, 2 * i + 1, 2 * (i - pairs))
        return (0, ids_ref[0] ^ offset)

    shape = jax.ShapeDtypeStruct((pairs, height, columns), BF)
    return pl.pallas_call(
        lambda *refs: share_kernel(len(lefts), pairs, *refs),
        grid_spec=pltpu.PrefetchScalarGridSpec(
            num_scalar_prefetch=1,
            grid=(ctx_count,),
            in_specs=[pl.BlockSpec((rows, height), place) for _ in lefts]
            + [pl.BlockSpec(right.shape, lambda i, ids_ref: (0, 0)) for right in rights]
            + [pl.BlockSpec((1, height), place) for _ in terms],
            out_specs=(
                pl.BlockSpec(
                    (1, height, columns), lambda i, ids_ref: (jnp.minimum(i, pairs - 1), 0, 0)
                ),
                pl.BlockSpec(
                    (1, height, columns), lambda i, ids_ref: (jnp.maximum(i - pairs, 0), 0, 0)
                ),
            ),
        ),
        out_shape=(shape, shape),
        compiler_params=pltpu.CompilerParams(vmem_limit_bytes=24 << 20),
        cost_estimate=pl.CostEstimate(
            flops=2 * rows * width * columns,
            bytes_accessed=2 * (rows + columns) * width,
            transcendentals=0,
        ),
        name="share_terms" if terms else "share_products",
    )(jnp.stack(ids()), *lefts, *rights, *[term[None] for term in terms])


def share_sum(lefts, rights, terms):
    pairs = lax.axis_size("ctx") // 2
    if (lefts[0].shape[1] // (2 * pairs)) % 128:
        values = [tn(left, right) for left, right in zip(lefts, rights)]
        values += [jnp.broadcast_to(term[:, None], (term.shape[0], 64)) for term in terms]
        return ctx_rows_sum(jnp.concatenate(values, axis=1)).astype(BF)
    sent, kept = share_products(lefts, rights, terms)
    got = swap(sent, "ctx", 1)
    total = kept[0].astype(F32) + got[0].astype(F32)
    for pair in range(1, pairs):
        part = (kept[pair].astype(F32) + got[pair].astype(F32)).astype(BF)
        total = total + swap(part, "ctx", 2 * pair).astype(F32)
    return total.astype(BF)


def layer(
    hidden_in,
    out_grad,
    positions,
    block_order,
    attn_gain,
    ffn_gain,
    qkv_weight,
    out_weight,
    ffn_weight,
):
    ctx_count = lax.axis_size("ctx")
    me, _ = ids()
    rows = hidden_in.shape[1]
    queries_width, kv_width = H * HD, KV * HD
    ffn_parts = in_hbm(ffn_weight.transpose(1, 0, 2))

    frequency = jnp.power(ROPE_BASE, -(jnp.arange(HD // 2, dtype=F32) * 2.0 / HD))
    angles = positions[0].astype(F32)[:, None] * frequency[None, :]
    cosine = jnp.tile(jnp.cos(angles), (1, 4))
    sine = jnp.tile(jnp.concatenate([-jnp.sin(angles), jnp.sin(angles)], axis=1), (1, 2))
    own_anchor = anchors_of(block_order, me, rows)[None]
    key_anchor = jnp.concatenate(
        [anchors_of(block_order, me ^ offset, rows) for offset in key_offsets()]
    )
    key_anchor = jnp.broadcast_to(key_anchor[:, None], (rows * ctx_count, 128))

    inputs = hidden_in[0].astype(F32)
    grad_in = out_grad[0]
    scale_one = norm_scale(inputs)
    normed_one = (inputs * scale_one * attn_gain).astype(BF)

    fast = ctx_count == 8 and (qkv_weight.shape[1] // ctx_count) % 128 == 0
    if fast:
        early = (cosine, sine, own_anchor, key_anchor)
        qkv_pieces, marks, rows_one = gather_pieces(qkv_weight, early, normed_one)
        out_blocks = gather_blocks(out_weight, *marks)
        queries, pair, qkv_full = pieces_forward(
            normed_one, qkv_weight, qkv_pieces, cosine, sine
        )
    else:
        out_blocks = gather_blocks(out_weight, normed_one, normed_one)
        rows_one = gather_rows(normed_one)
        qkv_full = whole_of(qkv_weight, gather_blocks(qkv_weight, normed_one, normed_one))
        projected = nn(normed_one, qkv_full)
        turned = rotate(
            projected[:, : queries_width + kv_width].reshape(rows, H + KV, HD), positions[0]
        ).reshape(rows, queries_width + kv_width)
        queries = (turned[:, :queries_width] * (1.0 / math.sqrt(HD))).astype(BF)
        pair = jnp.concatenate(
            [turned[:, queries_width:], projected[:, queries_width + kv_width :]], axis=1
        ).astype(BF)
    rows_one = by_offset(jnp.concatenate(rows_one, axis=0))
    keys_values = gather_keys(pair)
    rows_out = fetch_rows(after(grad_in, pair))
    attn_rows, attended, logs = attend(queries, keys_values, key_anchor, own_anchor)
    residual, normed_two = out_forward(
        attn_rows, out_weight, out_blocks, hidden_in[0], ffn_gain
    )
    scale_two = norm_scale(residual)
    rows_in = gather_rows(normed_two, "normed")
    rows_out = halves_of(after(rows_out, normed_two))
    act_grad = []
    for half in rows_out:
        act_grad.append(down_back(half, ffn_parts))

    attn_share = by_offset(columns_to_owner(after(attn_rows, rows_in[1])))
    middle = []
    for half, act in zip(rows_in, act_grad):
        middle.append(ffn_middle(half, act, ffn_parts))
    parts, partial = [m[0] for m in middle], [m[1] for m in middle]
    sum_grad = sum_rows(partial)
    products = ffn_products(rows_in, rows_out, parts).transpose(1, 0, 2)
    ffn_weight_grad = lax.psum_scatter(products, "ctx", scatter_dimension=0, tiled=True)
    ffn_weight_grad = ffn_weight_grad.astype(F32)
    out_partial = down_forward(parts, ffn_parts)

    unit_two = residual * scale_two
    ffn_gain_term = jnp.sum(sum_grad * unit_two, axis=0)
    scaled_two = ffn_gain * sum_grad
    residual_grad = grad_in.astype(F32) + scale_two * (
        scaled_two - unit_two * jnp.mean(scaled_two * unit_two, axis=-1, keepdims=True)
    )
    residual_bf = residual_grad.astype(BF)
    residual_planes = fetch_rows(residual_bf)
    attn_grad = out_back(residual_bf, out_weight, out_blocks)
    query_part, pair_grads = attend_back(
        queries, attn_grad, attended, keys_values, key_anchor, own_anchor, logs, cosine, sine
    )
    query_owned = columns_to_owner(query_part)
    pair_part = sum_pairs(pair_grads, cosine, sine)
    pair_owned = columns_to_owner(pair_part)
    residual_planes = jnp.concatenate(after(residual_planes, pair_part), axis=0)
    first_sums = share_sum(
        [residual_planes, after(rows_one, pair_part)], [attn_share, query_owned], []
    )
    first_sums = rows_to_owner(first_sums).astype(F32)

    projected_grad = jnp.concatenate([query_part, pair_part], axis=1)
    normed_one_grad = nt(projected_grad, qkv_full)
    unit_one = inputs * scale_one
    attn_gain_term = jnp.sum(normed_one_grad * unit_one, axis=0)
    scaled_one = attn_gain * normed_one_grad
    input_grad = residual_grad + scale_one * (
        scaled_one - unit_one * jnp.mean(scaled_one * unit_one, axis=-1, keepdims=True)
    )

    last_sums = share_sum([rows_one], [pair_owned], [attn_gain_term, ffn_gain_term])
    last_sums = rows_to_owner(last_sums).astype(F32)

    out_sum = sum_rows([after(half, pair_part) for half in out_partial])
    output = (residual + out_sum).astype(BF)

    out_columns, pair_columns = attn_share.shape[1], pair_owned.shape[1]
    out_weight_grad = joined(first_sums[:, :, :out_columns])
    qkv_grad = jnp.concatenate(
        [joined(first_sums[:, :, out_columns:]), joined(last_sums[:, :, :pair_columns])], axis=1
    )
    gain_grads = jnp.sum(last_sums[:, :, pair_columns:], axis=0)
    return (
        output[None],
        input_grad[None],
        qkv_grad,
        out_weight_grad,
        ffn_weight_grad,
        gain_grads[:, 0],
        gain_grads[:, 64],
    )


def solution(mesh):
    step = sharded(mesh)
    return step


def sharded(mesh):
    return jax.shard_map(
        layer,
        mesh=mesh,
        in_specs=(
            P("fsdp", "ctx", None),
            P("fsdp", "ctx", None),
            P("fsdp", "ctx"),
            P(),
            P(),
            P(),
            P("fsdp", None),
            P("fsdp", None),
            P(None, None, "fsdp"),
        ),
        out_specs=(
            P("fsdp", "ctx", None),
            P("fsdp", "ctx", None),
            P(("ctx", "fsdp"), None),
            P(("ctx", "fsdp"), None),
            P("ctx", None, "fsdp"),
            P(("ctx", "fsdp")),
            P(("ctx", "fsdp")),
        ),
        check_vma=False,
    )
```

```python
import math

import jax
import jax.numpy as jnp
from jax import lax
from jax.experimental import pallas as pl
from jax.experimental.pallas import tpu as pltpu
from jax.sharding import PartitionSpec as P


H = 32
KV = 8
HD = 64

NORM_EPS = 1e-05
ROPE_BASE = 500000.0
FFN_TILE = 512


BF = jnp.bfloat16
F32 = jnp.float32


def mm(a, b, dims):
    return lax.dot_general(a, b, (dims, ((), ())), preferred_element_type=F32)


def nn(a, b):
    return mm(a, b, ((1,), (0,)))


def nt(a, b):
    return mm(a, b, ((1,), (1,)))


def tn(a, b):
    return mm(a, b, ((0,), (0,)))


def swap(value, axis, offset):
    count = lax.axis_size(axis)
    return lax.ppermute(value, axis, [(i, i ^ offset) for i in range(count)])


def rotate(values, token_places):
    head_dim = values.shape[-1]
    half_dim = head_dim // 2
    frequency = jnp.power(ROPE_BASE, -(jnp.arange(half_dim, dtype=F32) * 2.0 / head_dim))
    angles = token_places.astype(F32)[:, None] * frequency[None, :]
    cosine = jnp.concatenate([jnp.cos(angles), jnp.cos(angles)], axis=-1)[:, None, :]
    sine_part = jnp.concatenate([jnp.sin(angles), jnp.sin(angles)], axis=-1)[:, None, :]
    turned = jnp.concatenate([-values[..., half_dim:], values[..., :half_dim]], axis=-1)
    return values * cosine + turned * sine_part


def norm_scale(values):
    return lax.rsqrt(jnp.mean(values * values, axis=-1, keepdims=True) + NORM_EPS)


def lookup(entries, row_ids):
    matches = row_ids[:, None] == jnp.arange(entries.shape[0], dtype=jnp.int32)[None, :]
    return jnp.sum(jnp.where(matches, entries[None, :], 0), axis=1)


def anchors_of(block_order, owner, row_count):
    block_len = row_count // 2
    row_ids = owner * row_count + jnp.arange(row_count, dtype=jnp.int32)
    return lookup(block_order, row_ids // block_len) * block_len + row_ids % block_len


def after(value, *earlier):
    return lax.optimization_barrier((value, earlier))[0]


def ids():
    return lax.axis_index("ctx"), lax.axis_index("fsdp")


def gather_pieces(weight, early):
    rows, columns = weight.shape
    share = columns // lax.axis_size("ctx")
    half = rows // 2
    mine = lax.dynamic_slice(weight, (0, lax.axis_index("ctx") * share), (rows, share))
    planes = {}
    planes[3] = swap(mine, "fsdp", 3)
    planes[1] = swap(mine, "fsdp", 1)
    planes[2] = swap(after(planes[3], early), "fsdp", 1)
    pieces = []
    for away in (1, 3, 2):
        first = planes[away]
        along_x, along_y = swap(first, "ctx", 2), swap(first, "ctx", 4)
        top, low = swap(along_y[:half], "ctx", 2), swap(along_x[half:], "ctx", 4)
        parts = [(0, 0, first), (2, 0, along_x), (4, 0, along_y), (6, 0, top), (6, half, low)]
        for offset, start, part in parts:
            pieces.append((away, offset, start, part))
            pieces.append((away, offset + 1, start, swap(part, "ctx", 1)))
    return pieces, (planes[2], (pieces[-4][3], pieces[-2][3]))


def pieces_kernel(places, rows_in, share, ids_ref, x_ref, own_ref, *refs):
    count = len(places)
    piece_refs, refs = refs[:count], refs[count:]
    cos_ref, sin_ref, q_ref, pair_ref, full_ref, y_ref, buf, in_sems, out_sems = refs
    me, plane = ids_ref[0], ids_ref[1]

    def block(away):
        return pl.ds(pl.multiple_of((plane ^ away) * rows_in, 128), rows_in)

    own_copy = pltpu.make_async_copy(own_ref, buf.at[block(0)], in_sems.at[count])
    own_copy.start()
    copies = []
    for i, (away, offset, start, height) in enumerate(places):
        at = pl.ds(pl.multiple_of((plane ^ away) * rows_in + start, 128), height)
        columns = pl.ds(pl.multiple_of((me ^ offset) * share, 128), share)
        copies.append(pltpu.make_async_copy(piece_refs[i], buf.at[at, columns], in_sems.at[i]))
        copies[-1].start()
    outs = []
    order = [0] + list(dict.fromkeys(away for away, _, _, _ in places))
    for away in order:
        if away:
            for copy, place in zip(copies, places):
                if place[0] == away:
                    copy.wait()
        else:
            own_copy.wait()
        outs.append(
            pltpu.make_async_copy(buf.at[block(away)], full_ref.at[block(away)], out_sems.at[away])
        )
        outs[-1].start()
        part = nn(x_ref[:, block(away)], buf[block(away)])
        y_ref[...] = part if away == 0 else y_ref[...] + part
    cosine, sine = cos_ref[...], sin_ref[...]
    queries, keys = H * HD, KV * HD
    for start in range(0, queries + keys, 128):
        tile = turn(y_ref[:, start : start + 128], cosine, sine)
        if start < queries:
            q_ref[:, start : start + 128] = (tile * (1.0 / math.sqrt(HD))).astype(BF)
        else:
            pair_ref[:, start - queries : start - queries + 128] = tile.astype(BF)
    pair_ref[:, keys:] = y_ref[:, queries + keys :].astype(BF)
    for copy in outs:
        copy.wait()


def pieces_forward(x, own, pieces, cosine, sine):
    me, plane = ids()
    rows_in, columns = own.shape
    rows, width = x.shape
    share = columns // lax.axis_size("ctx")
    places = tuple((away, offset, start, part.shape[0]) for away, offset, start, part in pieces)
    arrays = [part for _, _, _, part in pieces]
    hbm, vmem = pl.BlockSpec(memory_space=pltpu.HBM), pl.BlockSpec(memory_space=pltpu.VMEM)
    return pl.pallas_call(
        lambda *refs: pieces_kernel(places, rows_in, share, *refs),
        out_shape=(
            jax.ShapeDtypeStruct((rows, H * HD), BF),
            jax.ShapeDtypeStruct((rows, 2 * KV * HD), BF),
            jax.ShapeDtypeStruct((width, columns), BF),
        ),
        in_specs=[pl.BlockSpec(memory_space=pltpu.SMEM), vmem, hbm]
        + [hbm] * len(arrays)
        + [vmem, vmem],
        out_specs=(vmem, vmem, hbm),
        scratch_shapes=[
            pltpu.VMEM((rows, columns), F32),
            pltpu.VMEM((width, columns), BF),
            pltpu.SemaphoreType.DMA((len(arrays) + 1,)),
            pltpu.SemaphoreType.DMA((width // rows_in,)),
        ],
        compiler_params=pltpu.CompilerParams(vmem_limit_bytes=32 << 20),
        cost_estimate=pl.CostEstimate(
            flops=2 * rows * width * columns, bytes_accessed=4 * width * columns, transcendentals=0
        ),
        name="pieces_forward",
    )(jnp.stack([me, plane]), x, in_hbm(own), *[in_hbm(part) for part in arrays], cosine, sine)


def gather_blocks(weight, before_fsdp, before_ctx):
    rows, columns = weight.shape
    me, plane = ids()
    share = columns // lax.axis_size("ctx")
    mine = lax.dynamic_slice(weight, (0, me * share), (rows, share))
    planes = lax.all_gather(after(mine, before_fsdp), "fsdp")
    others = jnp.stack(
        [
            lax.dynamic_index_in_dim(planes, plane ^ away, 0, keepdims=False)
            for away in range(1, planes.shape[0])
        ]
    )
    return lax.all_gather(after(others, before_ctx), "ctx")


def whole_of(own, blocks):
    ctx_count, others, rows, share = blocks.shape
    plane = lax.axis_index("fsdp")
    columns = ctx_count * share
    full = jnp.zeros(((others + 1) * rows, columns), own.dtype)
    full = lax.dynamic_update_slice(full, own, (plane * rows, 0))
    for away in range(1, others + 1):
        part = blocks[:, away - 1].transpose(1, 0, 2).reshape(rows, columns)
        full = lax.dynamic_update_slice(full, part, ((plane ^ away) * rows, 0))
    return full


def in_hbm(value):
    return pltpu.with_memory_space_constraint(value, pltpu.HBM)


def out_kernel(back, ids_ref, x_ref, own_ref, blocks_ref, *refs):
    hidden_ref, gain_ref = (None, None) if back else refs[:2]
    outs = refs if back else refs[2:]
    own_buf, buf, sems = outs[-3:]
    ctx_count, others, rows, share = buf.shape
    plane = ids_ref[1]
    copies = [pltpu.make_async_copy(own_ref, own_buf, sems.at[ctx_count])]
    for c in range(ctx_count):
        copies.append(pltpu.make_async_copy(blocks_ref.at[c], buf.at[c], sems.at[c]))
    for copy in copies:
        copy.start()

    def features(away):
        return pl.ds(pl.multiple_of((plane ^ away) * rows, 128), rows)

    copies[0].wait()
    if back:
        y_ref = outs[0]
        own_part = nn(x_ref[:, features(0)], own_buf[...])
        for c in range(ctx_count):
            copies[c + 1].wait()
            at = slice(c * share, (c + 1) * share)
            total = own_part[:, at]
            for away in range(1, others + 1):
                total += nn(x_ref[:, features(away)], buf[c, away - 1])
            y_ref[:, at] = total.astype(BF)
        return
    residual_ref, normed_ref = outs[:2]
    residual_ref[...] = hidden_ref[...].astype(F32)
    residual_ref[:, features(0)] += nt(x_ref[...], own_buf[...])
    for c in range(ctx_count):
        copies[c + 1].wait()
        x = x_ref[:, c * share : (c + 1) * share]
        for away in range(1, others + 1):
            residual_ref[:, features(away)] += nt(x, buf[c, away - 1])
    residual = residual_ref[...]
    normed_ref[...] = (residual * norm_scale(residual) * gain_ref[...]).astype(BF)


def out_call(back, x, own, blocks, extra, out_shape):
    vmem, hbm = pl.BlockSpec(memory_space=pltpu.VMEM), pl.BlockSpec(memory_space=pltpu.HBM)
    return pl.pallas_call(
        lambda *refs: out_kernel(back, *refs),
        out_shape=out_shape,
        in_specs=[pl.BlockSpec(memory_space=pltpu.SMEM), vmem, hbm, hbm] + [vmem] * len(extra),
        out_specs=jax.tree.map(lambda _: vmem, out_shape),
        scratch_shapes=[
            pltpu.VMEM(own.shape, own.dtype),
            pltpu.VMEM(blocks.shape, blocks.dtype),
            pltpu.SemaphoreType.DMA((blocks.shape[0] + 1,)),
        ],
        compiler_params=pltpu.CompilerParams(vmem_limit_bytes=24 << 20),
        cost_estimate=pl.CostEstimate(
            flops=2 * x.shape[0] * own.size * (blocks.shape[1] + 1),
            bytes_accessed=2 * own.size * (blocks.shape[1] + 1),
            transcendentals=0,
        ),
        name="out_back" if back else "out_forward",
    )(jnp.stack(ids()), x, in_hbm(own), in_hbm(blocks), *extra)


def out_forward(attn_rows, own, blocks, hidden, gain):
    if blocks.shape[3] % 128:
        residual = hidden.astype(F32) + nt(attn_rows, whole_of(own, blocks))
        return residual, (residual * norm_scale(residual) * gain).astype(BF)
    out_shape = (
        jax.ShapeDtypeStruct(hidden.shape, F32),
        jax.ShapeDtypeStruct(hidden.shape, BF),
    )
    return out_call(False, attn_rows, own, blocks, [hidden, gain[None]], out_shape)


def out_back(x, own, blocks):
    if blocks.shape[3] % 128:
        return nn(x, whole_of(own, blocks)).astype(BF)
    out_shape = jax.ShapeDtypeStruct((x.shape[0], own.shape[1]), BF)
    return out_call(True, x, own, blocks, [], out_shape)


def one_back_kernel(
    query_ref, pair_ref, w_ref, hidden_ref, gain_ref, residual_ref, y_ref, term_ref
):
    step = pl.program_id(0)
    rows = w_ref.shape[0]
    split = query_ref.shape[1]
    y_ref[:, pl.ds(pl.multiple_of(step * rows, 128), rows)] = nt(
        query_ref[...], w_ref[:, :split]
    ) + nt(pair_ref[...], w_ref[:, split:])

    @pl.when(step == pl.num_programs(0) - 1)
    def _():
        grad = y_ref[...]
        inputs = hidden_ref[...].astype(F32)
        scale = norm_scale(inputs)
        unit = inputs * scale
        term_ref[...] = jnp.sum(grad * unit, axis=0, keepdims=True)
        scaled = gain_ref[...] * grad
        y_ref[...] = residual_ref[...] + scale * (
            scaled - unit * jnp.mean(scaled * unit, axis=-1, keepdims=True)
        )


def one_back(query_part, pair_part, weight, hidden, gain, residual_grad):
    rows, width = hidden.shape
    columns = weight.shape[1]
    tile = FFN_TILE

    def whole(array):
        return pl.BlockSpec(array.shape, lambda j: (0, 0))

    gain = gain[None]
    return pl.pallas_call(
        one_back_kernel,
        grid=(width // tile,),
        out_shape=(
            jax.ShapeDtypeStruct((rows, width), F32),
            jax.ShapeDtypeStruct((1, width), F32),
        ),
        in_specs=[
            whole(query_part),
            whole(pair_part),
            pl.BlockSpec((tile, columns), lambda j: (j, 0)),
            whole(hidden),
            whole(gain),
            whole(residual_grad),
        ],
        out_specs=(
            pl.BlockSpec((rows, width), lambda j: (0, 0)),
            pl.BlockSpec((1, width), lambda j: (0, 0)),
        ),
        compiler_params=pltpu.CompilerParams(vmem_limit_bytes=24 << 20),
        cost_estimate=pl.CostEstimate(
            flops=2 * rows * width * columns,
            bytes_accessed=2 * width * columns,
            transcendentals=0,
        ),
        name="one_back",
    )(query_part, pair_part, in_hbm(weight), hidden, gain, residual_grad)


def gather_rows(values, label=None):
    count = lax.axis_size("fsdp")
    planes = {0: values}
    if count == 4 and label:
        planes[3] = swap(values, "fsdp", 3)
        planes[1] = swap(values, "fsdp", 1)
        planes[2] = swap(planes[3], "fsdp", 1)
    else:
        for away in range(1, count):
            planes[away] = swap(values, "fsdp", away)
    return halves_of([planes[away] for away in range(count)])


def fetch_rows(values):
    count = lax.axis_size("fsdp")
    return [values] + [swap(values, "fsdp", away) for away in range(1, count)]


def halves_of(planes):
    half = len(planes) // 2
    return (jnp.concatenate(planes[:half], axis=0), jnp.concatenate(planes[half:], axis=0))


def sum_rows(halves):
    count = lax.axis_size("fsdp")
    half = count // 2
    rows = halves[0].shape[0] // half
    parts = [
        halves[away // half][away % half * rows : (away % half + 1) * rows] for away in range(count)
    ]
    if count == 4:
        passed = swap(parts[2].astype(BF), "fsdp", 1).astype(F32)
        one = swap(parts[1].astype(BF), "fsdp", 1).astype(F32)
        third = swap((parts[3] + passed).astype(BF), "fsdp", 3).astype(F32)
        return parts[0] + one + third
    total = parts[0]
    for away in range(1, count):
        total = total + swap(parts[away].astype(BF), "fsdp", away).astype(F32)
    return total


def by_feature(values):
    rows, width = values.shape
    ctx_count, fsdp_count = lax.axis_size("ctx"), lax.axis_size("fsdp")
    blocks = values.reshape(rows, ctx_count, fsdp_count, width // (ctx_count * fsdp_count))
    return blocks.transpose(0, 2, 1, 3).reshape(rows, width)


def gather_planes(values):
    count = lax.axis_size("fsdp")
    rows, columns = values.shape
    copies = jnp.broadcast_to(values[None], (count, rows, columns)).reshape(count * rows, columns)
    return lax.all_to_all(copies, "fsdp", split_axis=0, concat_axis=0, tiled=True)


def columns_to_owner(values):
    return lax.all_to_all(values, "fsdp", split_axis=1, concat_axis=0, tiled=True)


def sum_over_ctx(part_for):
    pairs = lax.axis_size("ctx") // 2
    sent = jnp.stack([part_for(2 * pair + 1).astype(BF) for pair in range(pairs)])
    got = swap(sent, "ctx", 1)
    sums = [part_for(2 * pair).astype(F32) + got[pair].astype(F32) for pair in range(pairs)]
    total = sums[0]
    for pair in range(1, pairs):
        total = total + swap(sums[pair].astype(BF), "ctx", 2 * pair).astype(F32)
    return total


def ctx_rows_sum(values):
    height = values.shape[0] // lax.axis_size("ctx")
    me = lax.axis_index("ctx")

    def part(offset):
        return lax.dynamic_slice(
            values, ((me ^ offset) * height, 0), (height, values.shape[1])
        )

    return sum_over_ctx(part)


def key_offsets():
    count = lax.axis_size("ctx")
    return list(range(0, count, 2)) + list(range(1, count, 2))


def gather_keys(piece):
    same = [piece] + [swap(piece, "ctx", far) for far in range(2, lax.axis_size("ctx"), 2)]
    mine = jnp.concatenate(same, axis=0)
    other = swap(mine, "ctx", 1)
    return jnp.concatenate([mine, other], axis=0)


def sum_pairs(kept, sent, cosine, sine):
    _, count, width = kept.shape
    pairs = lax.axis_size("ctx") // 2
    got = swap(sent, "ctx", 1)
    sums = (kept.astype(F32) + got.astype(F32)).reshape(2, pairs, count // pairs, width)
    far = [swap(sums[:, pair].astype(BF), "ctx", 2 * pair) for pair in range(1, pairs)]
    return pair_turn(sums[:, 0], far, cosine, sine)


def half_mask(shape):
    return lax.broadcasted_iota(jnp.int32, shape, len(shape) - 1) % 128 < HD


def turn(values, cosine, sine):
    lanes = lax.broadcasted_iota(jnp.int32, values.shape, 1) % HD
    turned = jnp.where(
        lanes < HD // 2, pltpu.roll(values, 128 - HD // 2, 1), pltpu.roll(values, HD // 2, 1)
    )
    return values * cosine + turned * sine


def doubled(tile, odd):
    wide = tile.astype(F32)
    other = pltpu.roll(wide, HD, 1)
    return jnp.where(half_mask(tile.shape) == (odd == 0), wide, other).astype(BF)


def split_heads(tile_pair):
    zero = jnp.zeros((), tile_pair.dtype)
    parts = []
    for j in range(2):
        tile = tile_pair[:, j * 128 : (j + 1) * 128]
        mask = half_mask(tile.shape)
        parts += [jnp.where(mask, tile, zero), jnp.where(mask, zero, tile)]
    return jnp.concatenate(parts, axis=0)


def merge_heads(stacked):
    rows = stacked.shape[0] // 4
    tiles = []
    for j in range(2):
        even = stacked[2 * j * rows : (2 * j + 1) * rows]
        odd = stacked[(2 * j + 1) * rows : (2 * j + 2) * rows]
        tiles.append(jnp.where(half_mask(even.shape), even, odd))
    return jnp.concatenate(tiles, axis=1)


def attend_kernel(q_ref, k_ref, v_ref, key_ref, own_ref, rows_ref, attended_ref, log_ref):
    odd = pl.program_id(0) % 2
    rows = q_ref.shape[0]
    queries = split_heads(q_ref[...])
    keys, values = doubled(k_ref[...], odd), doubled(v_ref[...], odd)
    allowed = key_ref[:, :1] <= own_ref[...]
    bias = jnp.where(allowed, 0.0, -1e30).astype(F32)
    bias = jnp.concatenate([bias] * 4, axis=1)
    scores = nt(keys, queries) + bias
    top = jnp.max(scores, axis=0, keepdims=True)
    weights = jnp.exp(scores - top)
    total = jnp.sum(weights, axis=0, keepdims=True)
    summed = tn(weights.astype(BF), values)
    log_ref[0] = top + jnp.log(total)
    attended = merge_heads(summed / jnp.transpose(jnp.broadcast_to(total, (128, 4 * rows))))
    attended_ref[...] = attended
    rows_ref[...] = attended.astype(BF)


def attend(queries, keys_values, key_anchor, own_anchor):
    rows, width = queries.shape
    count, both = keys_values.shape
    tiles = both // 256
    return pl.pallas_call(
        attend_kernel,
        grid=(KV,),
        out_shape=(
            jax.ShapeDtypeStruct((rows, width), BF),
            jax.ShapeDtypeStruct((rows, width), F32),
            jax.ShapeDtypeStruct((KV, 1, 4 * rows), F32),
        ),
        in_specs=[
            pl.BlockSpec((rows, 256), lambda g: (0, g)),
            pl.BlockSpec((count, 128), lambda g: (0, g // 2)),
            pl.BlockSpec((count, 128), lambda g: (0, tiles + g // 2)),
            pl.BlockSpec((count, 128), lambda g: (0, 0)),
            pl.BlockSpec((1, rows), lambda g: (0, 0)),
        ],
        out_specs=(
            pl.BlockSpec((rows, 256), lambda g: (0, g)),
            pl.BlockSpec((rows, 256), lambda g: (0, g)),
            pl.BlockSpec((1, 1, 4 * rows), lambda g: (g, 0, 0)),
        ),
        compiler_params=pltpu.CompilerParams(vmem_limit_bytes=48 << 20),
        cost_estimate=pl.CostEstimate(
            flops=4 * rows * width * count,
            bytes_accessed=2 * count * both,
            transcendentals=rows * H * count,
        ),
        name="attend",
    )(queries, keys_values, keys_values, key_anchor, own_anchor)


def attend_back_kernel(
    chunk, q_ref, grad_ref, attended_ref, k_ref, v_ref, key_ref, own_ref, log_ref, cos_ref, sin_ref,
    dq_ref, kept_ref, sent_ref,
):
    odd = pl.program_id(0) % 2
    rows = q_ref.shape[0]
    count = k_ref.shape[0]
    queries, grads = split_heads(q_ref[...]), split_heads(grad_ref[...])
    product = grads.astype(F32) * split_heads(attended_ref[...])
    delta = jnp.sum(jnp.transpose(product), axis=0, keepdims=True)
    log_total = log_ref[0]
    total = jnp.zeros((4 * rows, 128), F32)
    keep = half_mask((chunk, 128)) == (odd == 0)
    for start in range(0, count, chunk):
        at = slice(start, start + chunk)
        keys, values = doubled(k_ref[at, :], odd), doubled(v_ref[at, :], odd)
        allowed = key_ref[at, :1] <= own_ref[...]
        bias = jnp.where(allowed, 0.0, -1e30).astype(F32)
        bias = jnp.concatenate([bias] * 4, axis=1)
        probs = jnp.exp(nt(keys, queries) + bias - log_total)
        value_grad = nn(probs.astype(BF), grads)
        score_grad = (probs * (nt(values, grads) - delta)).astype(BF)
        key_grad = nn(score_grad, queries)
        total += tn(score_grad, keys)
        far = start >= count // 2
        out_ref, at = (sent_ref if far else kept_ref), slice(
            start - far * (count // 2), start - far * (count // 2) + chunk
        )
        for part, value in enumerate((key_grad, value_grad)):
            value = (value + pltpu.roll(value, HD, 1)).astype(BF)
            out_ref[part, at, :] = jnp.where(keep, value, out_ref[part, at, :])
    merged = merge_heads(total) * (1.0 / math.sqrt(HD))
    cosine, sine = cos_ref[...], sin_ref[...]
    for j in range(2):
        tile = slice(j * 128, (j + 1) * 128)
        dq_ref[:, tile] = turn(merged[:, tile], cosine, -sine).astype(BF)


def attend_back(queries, grads, attended, keys_values, key_anchor, own_anchor, logs, cosine, sine):
    rows, width = queries.shape
    count, both = keys_values.shape
    tiles = both // 256
    wide = pl.BlockSpec((rows, 256), lambda g: (0, g))
    small = pl.BlockSpec((rows, 128), lambda g: (0, 0))
    return pl.pallas_call(
        lambda *refs: attend_back_kernel(256, *refs),
        grid=(KV,),
        out_shape=(
            jax.ShapeDtypeStruct((rows, width), BF),
            jax.ShapeDtypeStruct((2, count // 2, both // 2), BF),
            jax.ShapeDtypeStruct((2, count // 2, both // 2), BF),
        ),
        in_specs=[
            wide,
            wide,
            wide,
            pl.BlockSpec((count, 128), lambda g: (0, g // 2)),
            pl.BlockSpec((count, 128), lambda g: (0, tiles + g // 2)),
            pl.BlockSpec((count, 128), lambda g: (0, 0)),
            pl.BlockSpec((1, rows), lambda g: (0, 0)),
            pl.BlockSpec((1, 1, 4 * rows), lambda g: (g, 0, 0)),
            small,
            small,
        ],
        out_specs=(
            wide,
            pl.BlockSpec((2, count // 2, 128), lambda g: (0, 0, g // 2)),
            pl.BlockSpec((2, count // 2, 128), lambda g: (0, 0, g // 2)),
        ),
        compiler_params=pltpu.CompilerParams(vmem_limit_bytes=48 << 20),
        cost_estimate=pl.CostEstimate(
            flops=10 * rows * width * count,
            bytes_accessed=4 * count * both,
            transcendentals=rows * H * count,
        ),
        name="attend_back",
    )(queries, grads, attended, keys_values, keys_values, key_anchor, own_anchor, logs, cosine, sine)


def pair_turn_kernel(own_ref, *refs):
    got, (cos_ref, sin_ref, y_ref) = refs[:-3], refs[-3:]
    total = own_ref[...]
    for ref in got:
        total = total + ref[...].astype(F32)
    cosine, sine = cos_ref[...], sin_ref[...]
    width = total.shape[2]
    for start in range(0, width, 128):
        tile = slice(start, start + 128)
        y_ref[:, tile] = turn(total[0, :, tile], cosine, -sine).astype(BF)
    y_ref[:, width:] = total[1].astype(BF)


def pair_turn(own, got, cosine, sine):
    _, rows, width = own.shape
    return pl.pallas_call(
        pair_turn_kernel,
        out_shape=jax.ShapeDtypeStruct((rows, 2 * width), BF),
        name="pair_turn",
    )(own, *got, cosine, sine)


def ffn_kernel(x_ref, act_ref, w_ref, out_ref, sum_ref):
    step = pl.program_id(0)
    gate_w, up_w = w_ref[0], w_ref[1]
    x = x_ref[...]
    gate, up = nn(x, gate_w), nn(x, up_w)
    act_grad = act_ref[...]
    sig = jax.nn.sigmoid(gate)
    silu = gate * sig
    gate_grad = (act_grad * up * sig * (1.0 + gate * (1.0 - sig))).astype(BF)
    up_grad = (act_grad * silu).astype(BF)
    out_ref[0], out_ref[1], out_ref[2] = gate_grad, up_grad, (silu * up).astype(BF)
    part = nt(gate_grad, gate_w) + nt(up_grad, up_w)

    @pl.when(step == 0)
    def _():
        sum_ref[...] = part

    @pl.when(step > 0)
    def _():
        sum_ref[...] += part


def ffn_middle(rows_in, act_grad, weights):
    rows, width = rows_in.shape
    hidden = weights.shape[2]
    tile = FFN_TILE
    return pl.pallas_call(
        ffn_kernel,
        grid=(hidden // tile,),
        out_shape=(
            jax.ShapeDtypeStruct((3, rows, hidden), BF),
            jax.ShapeDtypeStruct((rows, width), F32),
        ),
        in_specs=[
            pl.BlockSpec((rows, width), lambda j: (0, 0)),
            pl.BlockSpec((rows, tile), lambda j: (0, j)),
            pl.BlockSpec((2, width, tile), lambda j: (0, 0, j)),
        ],
        out_specs=(
            pl.BlockSpec((3, rows, tile), lambda j: (0, 0, j)),
            pl.BlockSpec((rows, width), lambda j: (0, 0)),
        ),
        compiler_params=pltpu.CompilerParams(vmem_limit_bytes=40 << 20),
        cost_estimate=pl.CostEstimate(
            flops=8 * rows * width * hidden,
            bytes_accessed=4 * width * hidden,
            transcendentals=rows * hidden,
        ),
        name="ffn_middle",
    )(rows_in, act_grad, weights)


def products_kernel(in_a, in_b, grad_a, grad_b, right_a, right_b, out_ref):
    def emit(left_a, left_b):
        out_ref[0] = (tn(left_a[...], right_a[0]) + tn(left_b[...], right_b[0])).astype(BF)

    @pl.when(pl.program_id(0) < 2)
    def _():
        emit(in_a, in_b)

    @pl.when(pl.program_id(0) == 2)
    def _():
        emit(grad_a, grad_b)


def ffn_products(rows_in, rows_out, parts):
    rows, width = rows_in[0].shape
    hidden = parts[0].shape[2]
    tile = FFN_TILE
    last = width // tile - 1
    left = pl.BlockSpec((rows, tile), lambda k, i: (0, jnp.where(k < 2, i, last)))
    grad = pl.BlockSpec((rows, tile), lambda k, i: (0, jnp.where(k == 2, i, 0)))
    right = pl.BlockSpec((1, rows, hidden), lambda k, i: (k, 0, 0))
    return pl.pallas_call(
        products_kernel,
        grid=(3, width // tile),
        out_shape=jax.ShapeDtypeStruct((3, width, hidden), BF),
        in_specs=[left, left, grad, grad, right, right],
        out_specs=pl.BlockSpec((1, tile, hidden), lambda k, i: (k, i, 0)),
        compiler_params=pltpu.CompilerParams(vmem_limit_bytes=32 << 20),
        cost_estimate=pl.CostEstimate(
            flops=12 * rows * width * hidden,
            bytes_accessed=6 * width * hidden,
            transcendentals=0,
        ),
        name="ffn_products",
    )(*rows_in, *rows_out, *parts)


def simple_kernel(x_ref, w_ref, y_ref):
    y_ref[...] = nn(x_ref[...], w_ref[0])


def down_back(x, weights):
    rows, width = x.shape
    hidden = weights.shape[2]
    tile = FFN_TILE
    return pl.pallas_call(
        simple_kernel,
        grid=(hidden // tile,),
        out_shape=jax.ShapeDtypeStruct((rows, hidden), F32),
        in_specs=[
            pl.BlockSpec((rows, width), lambda j: (0, 0)),
            pl.BlockSpec((1, width, tile), lambda j: (2, 0, j)),
        ],
        out_specs=pl.BlockSpec((rows, tile), lambda j: (0, j)),
        compiler_params=pltpu.CompilerParams(vmem_limit_bytes=24 << 20),
        cost_estimate=pl.CostEstimate(
            flops=2 * rows * width * hidden,
            bytes_accessed=2 * width * hidden,
            transcendentals=0,
        ),
        name="down_back",
    )(x, weights)


def down_kernel(a_ref, b_ref, w_ref, y_ref):
    rows = a_ref.shape[1]
    for half, ref in enumerate((a_ref, b_ref)):
        y_ref[half * rows : (half + 1) * rows] = nt(ref[0], w_ref[0])


def down_forward(parts, weights):
    _, rows, hidden = parts[0].shape
    width = weights.shape[1]
    tile = FFN_TILE
    left = pl.BlockSpec((1, rows, hidden), lambda j: (2, 0, 0))
    total = pl.pallas_call(
        down_kernel,
        grid=(width // tile,),
        out_shape=jax.ShapeDtypeStruct((2 * rows, width), F32),
        in_specs=[left, left, pl.BlockSpec((1, tile, hidden), lambda j: (2, j, 0))],
        out_specs=pl.BlockSpec((2 * rows, tile), lambda j: (0, j)),
        compiler_params=pltpu.CompilerParams(vmem_limit_bytes=24 << 20),
        cost_estimate=pl.CostEstimate(
            flops=4 * rows * width * hidden,
            bytes_accessed=2 * width * hidden,
            transcendentals=0,
        ),
        name="down_forward",
    )(*parts, weights)
    return total[:rows], total[rows:]


def share_kernel(count, ids_ref, *refs):
    lefts, rights = refs[:count], refs[count : 2 * count]
    terms, (kept_ref, sent_ref) = refs[2 * count : -2], refs[-2:]
    half = kept_ref.shape[1]
    own = ids_ref[0] % 2 == 0
    column = 0
    for left, right in zip(lefts, rights):
        width = right.shape[1]
        part = tn(left[...], right[...]).astype(BF)
        at = slice(column, column + width)
        kept_ref[0, :, at] = jnp.where(own, part[:half], part[half:])
        sent_ref[0, :, at] = jnp.where(own, part[half:], part[:half])
        column += width
    if terms:
        tall = jnp.concatenate(
            [jnp.broadcast_to(term[...], (64, term.shape[1])) for term in terms], axis=0
        )
        part = jnp.transpose(tall).astype(BF)
        kept_ref[0, :, column:] = jnp.where(own, part[:half], part[half:])
        sent_ref[0, :, column:] = jnp.where(own, part[half:], part[:half])


def share_products(lefts, rights, terms):
    ctx_count = lax.axis_size("ctx")
    pairs = ctx_count // 2
    rows, width = lefts[0].shape
    height = width // ctx_count
    columns = sum(right.shape[1] for right in rights) + 64 * len(terms)

    def place(j, ids_ref):
        return (0, (ids_ref[0] // 2) ^ j)

    shape = jax.ShapeDtypeStruct((pairs, height, columns), BF)
    out = pl.BlockSpec((1, height, columns), lambda j, ids_ref: (j, 0, 0))
    return pl.pallas_call(
        lambda *refs: share_kernel(len(lefts), *refs),
        grid_spec=pltpu.PrefetchScalarGridSpec(
            num_scalar_prefetch=1,
            grid=(pairs,),
            in_specs=[pl.BlockSpec((rows, 2 * height), place) for _ in lefts]
            + [pl.BlockSpec(right.shape, lambda j, ids_ref: (0, 0)) for right in rights]
            + [pl.BlockSpec((1, 2 * height), place) for _ in terms],
            out_specs=(out, out),
        ),
        out_shape=(shape, shape),
        compiler_params=pltpu.CompilerParams(vmem_limit_bytes=24 << 20),
        cost_estimate=pl.CostEstimate(
            flops=2 * rows * width * columns,
            bytes_accessed=2 * (rows + columns) * width,
            transcendentals=0,
        ),
        name="share_terms" if terms else "share_products",
    )(jnp.stack(ids()), *lefts, *rights, *[term[None] for term in terms])


def share_sum(lefts, rights, terms):
    pairs = lax.axis_size("ctx") // 2
    if (lefts[0].shape[1] // pairs) % 128:
        values = [tn(left, right) for left, right in zip(lefts, rights)]
        values += [jnp.broadcast_to(term[:, None], (term.shape[0], 64)) for term in terms]
        return ctx_rows_sum(jnp.concatenate(values, axis=1))
    kept, sent = share_products(lefts, rights, terms)
    got = swap(sent, "ctx", 1)
    total = kept[0].astype(F32) + got[0].astype(F32)
    for pair in range(1, pairs):
        part = (kept[pair].astype(F32) + got[pair].astype(F32)).astype(BF)
        total = total + swap(part, "ctx", 2 * pair).astype(F32)
    return total


def own_features(terms):
    ctx_count, fsdp_count = lax.axis_size("ctx"), lax.axis_size("fsdp")
    total = jnp.stack(terms)
    away = 1
    while away < fsdp_count:
        total = total + swap(total, "fsdp", away)
        away *= 2
    blocks = total.reshape(len(terms), ctx_count, fsdp_count, -1)
    own = lax.dynamic_index_in_dim(blocks, lax.axis_index("fsdp"), 2, keepdims=False)
    own = own.reshape(len(terms), -1)
    return [own[i] for i in range(len(terms))]


def layer(
    hidden_in,
    out_grad,
    positions,
    block_order,
    attn_gain,
    ffn_gain,
    qkv_weight,
    out_weight,
    ffn_weight,
):
    ctx_count = lax.axis_size("ctx")
    me, _ = ids()
    rows = hidden_in.shape[1]
    queries_width, kv_width = H * HD, KV * HD
    ffn_parts = in_hbm(ffn_weight.transpose(1, 0, 2))

    frequency = jnp.power(ROPE_BASE, -(jnp.arange(HD // 2, dtype=F32) * 2.0 / HD))
    angles = positions[0].astype(F32)[:, None] * frequency[None, :]
    cosine = jnp.tile(jnp.cos(angles), (1, 4))
    sine = jnp.tile(jnp.concatenate([-jnp.sin(angles), jnp.sin(angles)], axis=1), (1, 2))
    own_anchor = anchors_of(block_order, me, rows)[None]
    key_anchor = jnp.concatenate(
        [anchors_of(block_order, me ^ offset, rows) for offset in key_offsets()]
    )
    key_anchor = jnp.broadcast_to(key_anchor[:, None], (rows * ctx_count, 128))

    inputs = hidden_in[0].astype(F32)
    grad_in = out_grad[0]
    scale_one = norm_scale(inputs)
    normed_one = (inputs * scale_one * attn_gain).astype(BF)

    fast = ctx_count == 8 and (qkv_weight.shape[1] // ctx_count) % 128 == 0
    if fast:
        early = (cosine, sine, own_anchor, key_anchor)
        qkv_pieces, marks = gather_pieces(qkv_weight, early)
        out_blocks = gather_blocks(out_weight, *marks)
        queries, pair, qkv_full = pieces_forward(
            normed_one, qkv_weight, qkv_pieces, cosine, sine
        )
    else:
        marks = (normed_one, normed_one)
        out_blocks = gather_blocks(out_weight, *marks)
        qkv_full = whole_of(qkv_weight, gather_blocks(qkv_weight, normed_one, normed_one))
        projected = nn(normed_one, qkv_full)
        turned = rotate(
            projected[:, : queries_width + kv_width].reshape(rows, H + KV, HD), positions[0]
        ).reshape(rows, queries_width + kv_width)
        queries = (turned[:, :queries_width] * (1.0 / math.sqrt(HD))).astype(BF)
        pair = jnp.concatenate(
            [turned[:, queries_width:], projected[:, queries_width + kv_width :]], axis=1
        ).astype(BF)
    own_one = columns_to_owner(by_feature(after(normed_one, marks[0])))
    keys_values = gather_keys(pair)
    rows_out = fetch_rows(after(grad_in, pair))
    attn_rows, attended, logs = attend(queries, keys_values, key_anchor, own_anchor)
    residual, normed_two = out_forward(
        attn_rows, out_weight, out_blocks, hidden_in[0], ffn_gain
    )
    scale_two = norm_scale(residual)
    rows_in = gather_rows(normed_two, "normed")
    rows_out = halves_of(after(rows_out, normed_two))
    act_grad = []
    for half in rows_out:
        act_grad.append(down_back(half, ffn_parts))

    all_attn = gather_planes(after(attn_rows, rows_in[1]))
    middle = []
    for half, act in zip(rows_in, act_grad):
        middle.append(ffn_middle(half, in_hbm(act), ffn_parts))
    parts, partial = [in_hbm(m[0]) for m in middle], [m[1] for m in middle]
    sum_grad = sum_rows(partial)
    products = ffn_products(rows_in, rows_out, parts).transpose(1, 0, 2)
    ffn_weight_grad = lax.psum_scatter(products, "ctx", scatter_dimension=0, tiled=True)
    ffn_weight_grad = ffn_weight_grad.astype(F32)
    out_partial = down_forward(parts, ffn_parts)

    unit_two = residual * scale_two
    ffn_gain_term = jnp.sum(sum_grad * unit_two, axis=0)
    scaled_two = ffn_gain * sum_grad
    residual_grad = grad_in.astype(F32) + scale_two * (
        scaled_two - unit_two * jnp.mean(scaled_two * unit_two, axis=-1, keepdims=True)
    )
    residual_bf = residual_grad.astype(BF)
    own_residual = columns_to_owner(by_feature(residual_bf))
    attn_grad = out_back(residual_bf, out_weight, out_blocks)
    query_part, kept, sent = attend_back(
        queries, attn_grad, attended, keys_values, key_anchor, own_anchor, logs, cosine, sine
    )
    all_query = gather_planes(query_part)
    pair_part = sum_pairs(kept, sent, cosine, sine)
    all_pair = gather_planes(pair_part)
    first_sums = share_sum([own_residual, own_one], [after(all_attn, pair_part), all_query], [])
    input_grad, attn_gain_term = one_back(
        query_part, pair_part, qkv_full, hidden_in[0], attn_gain, residual_grad
    )
    terms = own_features([attn_gain_term[0], ffn_gain_term])
    last_sums = share_sum([own_one], [all_pair], terms)

    out_sum = sum_rows([after(half, pair_part) for half in out_partial])
    output = (residual + out_sum).astype(BF)

    pairs_width = 2 * kv_width
    out_weight_grad = first_sums[:, :queries_width]
    qkv_grad = jnp.concatenate(
        [first_sums[:, queries_width:], last_sums[:, :pairs_width]], axis=1
    )
    return (
        output[None],
        input_grad[None],
        qkv_grad,
        out_weight_grad,
        ffn_weight_grad,
        last_sums[:, pairs_width],
        last_sums[:, pairs_width + 64],
    )


def solution(mesh):
    step = sharded(mesh)
    return step


def sharded(mesh):
    return jax.shard_map(
        layer,
        mesh=mesh,
        in_specs=(
            P("fsdp", "ctx", None),
            P("fsdp", "ctx", None),
            P("fsdp", "ctx"),
            P(),
            P(),
            P(),
            P("fsdp", None),
            P("fsdp", None),
            P(None, None, "fsdp"),
        ),
        out_specs=(
            P("fsdp", "ctx", None),
            P("fsdp", "ctx", None),
            P(("ctx", "fsdp"), None),
            P(("ctx", "fsdp"), None),
            P("ctx", None, "fsdp"),
            P(("ctx", "fsdp")),
            P(("ctx", "fsdp")),
        ),
        check_vma=False,
    )
```

```python
import math

import jax
import jax.numpy as jnp
from jax import lax
from jax.experimental import pallas as pl
from jax.experimental.pallas import tpu as pltpu
from jax.sharding import PartitionSpec as P


H = 32
KV = 8
HD = 64

NORM_EPS = 1e-05
ROPE_BASE = 500000.0
FFN_TILE = 512


BF = jnp.bfloat16
F32 = jnp.float32


def mm(a, b, dims):
    return lax.dot_general(a, b, (dims, ((), ())), preferred_element_type=F32)


def nn(a, b):
    return mm(a, b, ((1,), (0,)))


def nt(a, b):
    return mm(a, b, ((1,), (1,)))


def tn(a, b):
    return mm(a, b, ((0,), (0,)))


def swap(value, axis, offset):
    count = lax.axis_size(axis)
    return lax.ppermute(value, axis, [(i, i ^ offset) for i in range(count)])


def rotate(values, token_places):
    head_dim = values.shape[-1]
    half_dim = head_dim // 2
    frequency = jnp.power(ROPE_BASE, -(jnp.arange(half_dim, dtype=F32) * 2.0 / head_dim))
    angles = token_places.astype(F32)[:, None] * frequency[None, :]
    cosine = jnp.concatenate([jnp.cos(angles), jnp.cos(angles)], axis=-1)[:, None, :]
    sine_part = jnp.concatenate([jnp.sin(angles), jnp.sin(angles)], axis=-1)[:, None, :]
    turned = jnp.concatenate([-values[..., half_dim:], values[..., :half_dim]], axis=-1)
    return values * cosine + turned * sine_part


def norm_scale(values):
    return lax.rsqrt(jnp.mean(values * values, axis=-1, keepdims=True) + NORM_EPS)


def lookup(entries, row_ids):
    matches = row_ids[:, None] == jnp.arange(entries.shape[0], dtype=jnp.int32)[None, :]
    return jnp.sum(jnp.where(matches, entries[None, :], 0), axis=1)


def anchors_of(block_order, owner, row_count):
    block_len = row_count // 2
    row_ids = owner * row_count + jnp.arange(row_count, dtype=jnp.int32)
    return lookup(block_order, row_ids // block_len) * block_len + row_ids % block_len


def after(value, *earlier):
    return lax.optimization_barrier((value, earlier))[0]


def ids():
    return lax.axis_index("ctx"), lax.axis_index("fsdp")


def gather_pieces(weight, early):
    rows, columns = weight.shape
    share = columns // lax.axis_size("ctx")
    half = rows // 2
    mine = lax.dynamic_slice(weight, (0, lax.axis_index("ctx") * share), (rows, share))
    planes = {}
    planes[3] = swap(mine, "fsdp", 3)
    planes[1] = swap(mine, "fsdp", 1)
    planes[2] = swap(after(planes[3], early), "fsdp", 1)
    pieces = []
    for away in (1, 3, 2):
        first = planes[away]
        along_x, along_y = swap(first, "ctx", 2), swap(first, "ctx", 4)
        top, low = swap(along_y[:half], "ctx", 2), swap(along_x[half:], "ctx", 4)
        parts = [(0, 0, first), (2, 0, along_x), (4, 0, along_y), (6, 0, top), (6, half, low)]
        for offset, start, part in parts:
            pieces.append((away, offset, start, part))
            pieces.append((away, offset + 1, start, swap(part, "ctx", 1)))
    return pieces, (planes[2], (pieces[-4][3], pieces[-2][3]))


def pieces_kernel(places, rows_in, share, ids_ref, x_ref, own_ref, *refs):
    count = len(places)
    piece_refs, refs = refs[:count], refs[count:]
    cos_ref, sin_ref, q_ref, pair_ref, full_ref, y_ref, buf, in_sems, out_sems = refs
    me, plane = ids_ref[0], ids_ref[1]

    def block(away):
        return pl.ds(pl.multiple_of((plane ^ away) * rows_in, 128), rows_in)

    own_copy = pltpu.make_async_copy(own_ref, buf.at[block(0)], in_sems.at[count])
    own_copy.start()
    copies = []
    for i, (away, offset, start, height) in enumerate(places):
        at = pl.ds(pl.multiple_of((plane ^ away) * rows_in + start, 128), height)
        columns = pl.ds(pl.multiple_of((me ^ offset) * share, 128), share)
        copies.append(pltpu.make_async_copy(piece_refs[i], buf.at[at, columns], in_sems.at[i]))
        copies[-1].start()
    outs = []
    order = [0] + list(dict.fromkeys(away for away, _, _, _ in places))
    for away in order:
        if away:
            for copy, place in zip(copies, places):
                if place[0] == away:
                    copy.wait()
        else:
            own_copy.wait()
        outs.append(
            pltpu.make_async_copy(buf.at[block(away)], full_ref.at[block(away)], out_sems.at[away])
        )
        outs[-1].start()
        part = nn(x_ref[:, block(away)], buf[block(away)])
        y_ref[...] = part if away == 0 else y_ref[...] + part
    cosine, sine = cos_ref[...], sin_ref[...]
    queries, keys = H * HD, KV * HD
    for start in range(0, queries + keys, 128):
        tile = turn(y_ref[:, start : start + 128], cosine, sine)
        if start < queries:
            q_ref[:, start : start + 128] = (tile * (1.0 / math.sqrt(HD))).astype(BF)
        else:
            pair_ref[:, start - queries : start - queries + 128] = tile.astype(BF)
    pair_ref[:, keys:] = y_ref[:, queries + keys :].astype(BF)
    for copy in outs:
        copy.wait()


def pieces_forward(x, own, pieces, cosine, sine):
    me, plane = ids()
    rows_in, columns = own.shape
    rows, width = x.shape
    share = columns // lax.axis_size("ctx")
    places = tuple((away, offset, start, part.shape[0]) for away, offset, start, part in pieces)
    arrays = [part for _, _, _, part in pieces]
    hbm, vmem = pl.BlockSpec(memory_space=pltpu.HBM), pl.BlockSpec(memory_space=pltpu.VMEM)
    return pl.pallas_call(
        lambda *refs: pieces_kernel(places, rows_in, share, *refs),
        out_shape=(
            jax.ShapeDtypeStruct((rows, H * HD), BF),
            jax.ShapeDtypeStruct((rows, 2 * KV * HD), BF),
            pltpu.HBM((width, columns), BF),
        ),
        in_specs=[pl.BlockSpec(memory_space=pltpu.SMEM), vmem, hbm]
        + [hbm] * len(arrays)
        + [vmem, vmem],
        out_specs=(vmem, vmem, hbm),
        scratch_shapes=[
            pltpu.VMEM((rows, columns), F32),
            pltpu.VMEM((width, columns), BF),
            pltpu.SemaphoreType.DMA((len(arrays) + 1,)),
            pltpu.SemaphoreType.DMA((width // rows_in,)),
        ],
        compiler_params=pltpu.CompilerParams(vmem_limit_bytes=32 << 20),
        cost_estimate=pl.CostEstimate(
            flops=2 * rows * width * columns, bytes_accessed=4 * width * columns, transcendentals=0
        ),
        name="pieces_forward",
    )(jnp.stack([me, plane]), x, in_hbm(own), *[in_hbm(part) for part in arrays], cosine, sine)


def gather_blocks(weight, before_fsdp, before_ctx):
    rows, columns = weight.shape
    me, plane = ids()
    share = columns // lax.axis_size("ctx")
    mine = lax.dynamic_slice(weight, (0, me * share), (rows, share))
    planes = lax.all_gather(after(mine, before_fsdp), "fsdp")
    others = jnp.stack(
        [
            lax.dynamic_index_in_dim(planes, plane ^ away, 0, keepdims=False)
            for away in range(1, planes.shape[0])
        ]
    )
    return lax.all_gather(after(others, before_ctx), "ctx")


def whole_of(own, blocks):
    ctx_count, others, rows, share = blocks.shape
    plane = lax.axis_index("fsdp")
    columns = ctx_count * share
    full = jnp.zeros(((others + 1) * rows, columns), own.dtype)
    full = lax.dynamic_update_slice(full, own, (plane * rows, 0))
    for away in range(1, others + 1):
        part = blocks[:, away - 1].transpose(1, 0, 2).reshape(rows, columns)
        full = lax.dynamic_update_slice(full, part, ((plane ^ away) * rows, 0))
    return full


def in_hbm(value):
    return pltpu.with_memory_space_constraint(value, pltpu.HBM)


def out_kernel(back, ids_ref, x_ref, own_ref, blocks_ref, *refs):
    hidden_ref, gain_ref = (None, None) if back else refs[:2]
    outs = refs if back else refs[2:]
    own_buf, buf, sems = outs[-3:]
    ctx_count, others, rows, share = buf.shape
    plane = ids_ref[1]
    copies = [pltpu.make_async_copy(own_ref, own_buf, sems.at[ctx_count])]
    for c in range(ctx_count):
        copies.append(pltpu.make_async_copy(blocks_ref.at[c], buf.at[c], sems.at[c]))
    for copy in copies:
        copy.start()

    def features(away):
        return pl.ds(pl.multiple_of((plane ^ away) * rows, 128), rows)

    copies[0].wait()
    if back:
        y_ref = outs[0]
        own_part = nn(x_ref[:, features(0)], own_buf[...])
        for c in range(ctx_count):
            copies[c + 1].wait()
            at = slice(c * share, (c + 1) * share)
            total = own_part[:, at]
            for away in range(1, others + 1):
                total += nn(x_ref[:, features(away)], buf[c, away - 1])
            y_ref[:, at] = total.astype(BF)
        return
    residual_ref, normed_ref = outs[:2]
    residual_ref[...] = hidden_ref[...].astype(F32)
    residual_ref[:, features(0)] += nt(x_ref[...], own_buf[...])
    for c in range(ctx_count):
        copies[c + 1].wait()
        x = x_ref[:, c * share : (c + 1) * share]
        for away in range(1, others + 1):
            residual_ref[:, features(away)] += nt(x, buf[c, away - 1])
    residual = residual_ref[...]
    normed_ref[...] = (residual * norm_scale(residual) * gain_ref[...]).astype(BF)


def out_call(back, x, own, blocks, extra, out_shape):
    vmem, hbm = pl.BlockSpec(memory_space=pltpu.VMEM), pl.BlockSpec(memory_space=pltpu.HBM)
    return pl.pallas_call(
        lambda *refs: out_kernel(back, *refs),
        out_shape=out_shape,
        in_specs=[pl.BlockSpec(memory_space=pltpu.SMEM), vmem, hbm, hbm] + [vmem] * len(extra),
        out_specs=jax.tree.map(lambda _: vmem, out_shape),
        scratch_shapes=[
            pltpu.VMEM(own.shape, own.dtype),
            pltpu.VMEM(blocks.shape, blocks.dtype),
            pltpu.SemaphoreType.DMA((blocks.shape[0] + 1,)),
        ],
        compiler_params=pltpu.CompilerParams(vmem_limit_bytes=24 << 20),
        cost_estimate=pl.CostEstimate(
            flops=2 * x.shape[0] * own.size * (blocks.shape[1] + 1),
            bytes_accessed=2 * own.size * (blocks.shape[1] + 1),
            transcendentals=0,
        ),
        name="out_back" if back else "out_forward",
    )(jnp.stack(ids()), x, in_hbm(own), in_hbm(blocks), *extra)


def out_forward(attn_rows, own, blocks, hidden, gain):
    if blocks.shape[3] % 128:
        residual = hidden.astype(F32) + nt(attn_rows, whole_of(own, blocks))
        return residual, (residual * norm_scale(residual) * gain).astype(BF)
    out_shape = (
        jax.ShapeDtypeStruct(hidden.shape, F32),
        jax.ShapeDtypeStruct(hidden.shape, BF),
    )
    return out_call(False, attn_rows, own, blocks, [hidden, gain[None]], out_shape)


def out_back(x, own, blocks):
    if blocks.shape[3] % 128:
        return nn(x, whole_of(own, blocks)).astype(BF)
    out_shape = jax.ShapeDtypeStruct((x.shape[0], own.shape[1]), BF)
    return out_call(True, x, own, blocks, [], out_shape)


def one_back_kernel(
    query_ref, pair_ref, w_ref, hidden_ref, gain_ref, residual_ref, y_ref, term_ref
):
    step = pl.program_id(0)
    rows = w_ref.shape[0]
    split = query_ref.shape[1]
    y_ref[:, pl.ds(pl.multiple_of(step * rows, 128), rows)] = nt(
        query_ref[...], w_ref[:, :split]
    ) + nt(pair_ref[...], w_ref[:, split:])

    @pl.when(step == pl.num_programs(0) - 1)
    def _():
        grad = y_ref[...]
        inputs = hidden_ref[...].astype(F32)
        scale = norm_scale(inputs)
        unit = inputs * scale
        term_ref[...] = jnp.sum(grad * unit, axis=0, keepdims=True)
        scaled = gain_ref[...] * grad
        y_ref[...] = residual_ref[...] + scale * (
            scaled - unit * jnp.mean(scaled * unit, axis=-1, keepdims=True)
        )


def one_back(query_part, pair_part, weight, hidden, gain, residual_grad):
    rows, width = hidden.shape
    columns = weight.shape[1]
    tile = FFN_TILE

    def whole(array):
        return pl.BlockSpec(array.shape, lambda j: (0, 0))

    gain = gain[None]
    return pl.pallas_call(
        one_back_kernel,
        grid=(width // tile,),
        out_shape=(
            jax.ShapeDtypeStruct((rows, width), F32),
            jax.ShapeDtypeStruct((1, width), F32),
        ),
        in_specs=[
            whole(query_part),
            whole(pair_part),
            pl.BlockSpec((tile, columns), lambda j: (j, 0)),
            whole(hidden),
            whole(gain),
            whole(residual_grad),
        ],
        out_specs=(
            pl.BlockSpec((rows, width), lambda j: (0, 0)),
            pl.BlockSpec((1, width), lambda j: (0, 0)),
        ),
        compiler_params=pltpu.CompilerParams(vmem_limit_bytes=24 << 20),
        cost_estimate=pl.CostEstimate(
            flops=2 * rows * width * columns,
            bytes_accessed=2 * width * columns,
            transcendentals=0,
        ),
        name="one_back",
    )(query_part, pair_part, in_hbm(weight), hidden, gain, residual_grad)


def pass_rows(values):
    if lax.axis_size("fsdp") != 4:
        return fetch_rows(values)
    third = swap(values, "fsdp", 3)
    first = swap(values, "fsdp", 1)
    second = swap(third, "fsdp", 1)
    return [values, first, second, third]


def fetch_rows(values):
    count = lax.axis_size("fsdp")
    return [values] + [swap(values, "fsdp", away) for away in range(1, count)]


def halves_of(planes):
    half = len(planes) // 2
    return (jnp.concatenate(planes[:half], axis=0), jnp.concatenate(planes[half:], axis=0))


def sum_rows(halves):
    count = lax.axis_size("fsdp")
    half = count // 2
    rows = halves[0].shape[0] // half
    parts = [
        halves[away // half][away % half * rows : (away % half + 1) * rows] for away in range(count)
    ]
    if count == 4:
        passed = swap(parts[2].astype(BF), "fsdp", 1).astype(F32)
        one = swap(parts[1].astype(BF), "fsdp", 1).astype(F32)
        third = swap((parts[3] + passed).astype(BF), "fsdp", 3).astype(F32)
        return parts[0] + one + third
    total = parts[0]
    for away in range(1, count):
        total = total + swap(parts[away].astype(BF), "fsdp", away).astype(F32)
    return total


def by_feature(values):
    rows, width = values.shape
    ctx_count, fsdp_count = lax.axis_size("ctx"), lax.axis_size("fsdp")
    blocks = values.reshape(rows, ctx_count, fsdp_count, width // (ctx_count * fsdp_count))
    return blocks.transpose(0, 2, 1, 3).reshape(rows, width)


def by_offset(planes):
    count, plane = len(planes), lax.axis_index("fsdp")
    joined = planes
    bit = 1
    while bit < count:
        odd = (plane & bit) != 0
        joined = [jnp.where(odd, joined[i ^ bit], joined[i]) for i in range(count)]
        bit *= 2
    return jnp.concatenate(joined, axis=0)


def gather_planes(values):
    count = lax.axis_size("fsdp")
    rows, columns = values.shape
    copies = jnp.broadcast_to(values[None], (count, rows, columns)).reshape(count * rows, columns)
    return lax.all_to_all(copies, "fsdp", split_axis=0, concat_axis=0, tiled=True)


def columns_to_owner(values):
    return lax.all_to_all(values, "fsdp", split_axis=1, concat_axis=0, tiled=True)


def sum_over_ctx(part_for):
    pairs = lax.axis_size("ctx") // 2
    sent = jnp.stack([part_for(2 * pair + 1).astype(BF) for pair in range(pairs)])
    got = swap(sent, "ctx", 1)
    sums = [part_for(2 * pair).astype(F32) + got[pair].astype(F32) for pair in range(pairs)]
    total = sums[0]
    for pair in range(1, pairs):
        total = total + swap(sums[pair].astype(BF), "ctx", 2 * pair).astype(F32)
    return total


def ctx_rows_sum(values):
    height = values.shape[0] // lax.axis_size("ctx")
    me = lax.axis_index("ctx")

    def part(offset):
        return lax.dynamic_slice(
            values, ((me ^ offset) * height, 0), (height, values.shape[1])
        )

    return sum_over_ctx(part)


def key_offsets():
    count = lax.axis_size("ctx")
    return list(range(0, count, 2)) + list(range(1, count, 2))


def gather_keys(piece):
    same = [piece] + [swap(piece, "ctx", far) for far in range(2, lax.axis_size("ctx"), 2)]
    mine = jnp.concatenate(same, axis=0)
    other = swap(mine, "ctx", 1)
    return jnp.concatenate([mine, other], axis=0)


def sum_pairs(kept, sent, cosine, sine):
    _, count, width = kept.shape
    pairs = lax.axis_size("ctx") // 2
    got = swap(sent, "ctx", 1)
    sums = (kept.astype(F32) + got.astype(F32)).reshape(2, pairs, count // pairs, width)
    far = [swap(sums[:, pair].astype(BF), "ctx", 2 * pair) for pair in range(1, pairs)]
    return pair_turn(sums[:, 0], far, cosine, sine)


def half_mask(shape):
    return lax.broadcasted_iota(jnp.int32, shape, len(shape) - 1) % 128 < HD


def turn(values, cosine, sine):
    lanes = lax.broadcasted_iota(jnp.int32, values.shape, 1) % HD
    turned = jnp.where(
        lanes < HD // 2, pltpu.roll(values, 128 - HD // 2, 1), pltpu.roll(values, HD // 2, 1)
    )
    return values * cosine + turned * sine


def doubled(tile, odd):
    wide = tile.astype(F32)
    other = pltpu.roll(wide, HD, 1)
    return jnp.where(half_mask(tile.shape) == (odd == 0), wide, other).astype(BF)


def split_heads(tile_pair):
    zero = jnp.zeros((), tile_pair.dtype)
    parts = []
    for j in range(2):
        tile = tile_pair[:, j * 128 : (j + 1) * 128]
        mask = half_mask(tile.shape)
        parts += [jnp.where(mask, tile, zero), jnp.where(mask, zero, tile)]
    return jnp.concatenate(parts, axis=0)


def merge_heads(stacked):
    rows = stacked.shape[0] // 4
    tiles = []
    for j in range(2):
        even = stacked[2 * j * rows : (2 * j + 1) * rows]
        odd = stacked[(2 * j + 1) * rows : (2 * j + 2) * rows]
        tiles.append(jnp.where(half_mask(even.shape), even, odd))
    return jnp.concatenate(tiles, axis=1)


def attend_kernel(q_ref, k_ref, v_ref, key_ref, own_ref, rows_ref, attended_ref, log_ref):
    odd = pl.program_id(0) % 2
    rows = q_ref.shape[0]
    queries = split_heads(q_ref[...])
    keys, values = doubled(k_ref[...], odd), doubled(v_ref[...], odd)
    allowed = key_ref[:, :1] <= own_ref[...]
    bias = jnp.where(allowed, 0.0, -1e30).astype(F32)
    bias = jnp.concatenate([bias] * 4, axis=1)
    scores = nt(keys, queries) + bias
    top = jnp.max(scores, axis=0, keepdims=True)
    weights = jnp.exp(scores - top)
    total = jnp.sum(weights, axis=0, keepdims=True)
    summed = tn(weights.astype(BF), values)
    log_ref[0] = top + jnp.log(total)
    attended = merge_heads(summed / jnp.transpose(jnp.broadcast_to(total, (128, 4 * rows))))
    attended_ref[...] = attended
    rows_ref[...] = attended.astype(BF)


def attend(queries, keys_values, key_anchor, own_anchor):
    rows, width = queries.shape
    count, both = keys_values.shape
    tiles = both // 256
    return pl.pallas_call(
        attend_kernel,
        grid=(KV,),
        out_shape=(
            jax.ShapeDtypeStruct((rows, width), BF),
            jax.ShapeDtypeStruct((rows, width), F32),
            jax.ShapeDtypeStruct((KV, 1, 4 * rows), F32),
        ),
        in_specs=[
            pl.BlockSpec((rows, 256), lambda g: (0, g)),
            pl.BlockSpec((count, 128), lambda g: (0, g // 2)),
            pl.BlockSpec((count, 128), lambda g: (0, tiles + g // 2)),
            pl.BlockSpec((count, 128), lambda g: (0, 0)),
            pl.BlockSpec((1, rows), lambda g: (0, 0)),
        ],
        out_specs=(
            pl.BlockSpec((rows, 256), lambda g: (0, g)),
            pl.BlockSpec((rows, 256), lambda g: (0, g)),
            pl.BlockSpec((1, 1, 4 * rows), lambda g: (g, 0, 0)),
        ),
        compiler_params=pltpu.CompilerParams(vmem_limit_bytes=48 << 20),
        cost_estimate=pl.CostEstimate(
            flops=4 * rows * width * count,
            bytes_accessed=2 * count * both,
            transcendentals=rows * H * count,
        ),
        name="attend",
    )(queries, keys_values, keys_values, key_anchor, own_anchor)


def attend_back_kernel(
    chunk, q_ref, grad_ref, attended_ref, k_ref, v_ref, key_ref, own_ref, log_ref, cos_ref, sin_ref,
    dq_ref, kept_ref, sent_ref,
):
    odd = pl.program_id(0) % 2
    rows = q_ref.shape[0]
    count = k_ref.shape[0]
    queries, grads = split_heads(q_ref[...]), split_heads(grad_ref[...])
    product = grads.astype(F32) * split_heads(attended_ref[...])
    delta = jnp.sum(jnp.transpose(product), axis=0, keepdims=True)
    log_total = log_ref[0]
    total = jnp.zeros((4 * rows, 128), F32)
    keep = half_mask((chunk, 128)) == (odd == 0)
    for start in range(0, count, chunk):
        at = slice(start, start + chunk)
        keys, values = doubled(k_ref[at, :], odd), doubled(v_ref[at, :], odd)
        allowed = key_ref[at, :1] <= own_ref[...]
        bias = jnp.where(allowed, 0.0, -1e30).astype(F32)
        bias = jnp.concatenate([bias] * 4, axis=1)
        probs = jnp.exp(nt(keys, queries) + bias - log_total)
        value_grad = nn(probs.astype(BF), grads)
        score_grad = (probs * (nt(values, grads) - delta)).astype(BF)
        key_grad = nn(score_grad, queries)
        total += tn(score_grad, keys)
        far = start >= count // 2
        out_ref, at = (sent_ref if far else kept_ref), slice(
            start - far * (count // 2), start - far * (count // 2) + chunk
        )
        for part, value in enumerate((key_grad, value_grad)):
            value = (value + pltpu.roll(value, HD, 1)).astype(BF)
            out_ref[part, at, :] = jnp.where(keep, value, out_ref[part, at, :])
    merged = merge_heads(total) * (1.0 / math.sqrt(HD))
    cosine, sine = cos_ref[...], sin_ref[...]
    for j in range(2):
        tile = slice(j * 128, (j + 1) * 128)
        dq_ref[:, tile] = turn(merged[:, tile], cosine, -sine).astype(BF)


def attend_back(queries, grads, attended, keys_values, key_anchor, own_anchor, logs, cosine, sine):
    rows, width = queries.shape
    count, both = keys_values.shape
    tiles = both // 256
    wide = pl.BlockSpec((rows, 256), lambda g: (0, g))
    small = pl.BlockSpec((rows, 128), lambda g: (0, 0))
    return pl.pallas_call(
        lambda *refs: attend_back_kernel(256, *refs),
        grid=(KV,),
        out_shape=(
            jax.ShapeDtypeStruct((rows, width), BF),
            jax.ShapeDtypeStruct((2, count // 2, both // 2), BF),
            jax.ShapeDtypeStruct((2, count // 2, both // 2), BF),
        ),
        in_specs=[
            wide,
            wide,
            wide,
            pl.BlockSpec((count, 128), lambda g: (0, g // 2)),
            pl.BlockSpec((count, 128), lambda g: (0, tiles + g // 2)),
            pl.BlockSpec((count, 128), lambda g: (0, 0)),
            pl.BlockSpec((1, rows), lambda g: (0, 0)),
            pl.BlockSpec((1, 1, 4 * rows), lambda g: (g, 0, 0)),
            small,
            small,
        ],
        out_specs=(
            wide,
            pl.BlockSpec((2, count // 2, 128), lambda g: (0, 0, g // 2)),
            pl.BlockSpec((2, count // 2, 128), lambda g: (0, 0, g // 2)),
        ),
        compiler_params=pltpu.CompilerParams(vmem_limit_bytes=48 << 20),
        cost_estimate=pl.CostEstimate(
            flops=10 * rows * width * count,
            bytes_accessed=4 * count * both,
            transcendentals=rows * H * count,
        ),
        name="attend_back",
    )(queries, grads, attended, keys_values, keys_values, key_anchor, own_anchor, logs, cosine, sine)


def pair_turn_kernel(own_ref, *refs):
    got, (cos_ref, sin_ref, y_ref) = refs[:-3], refs[-3:]
    total = own_ref[...]
    for ref in got:
        total = total + ref[...].astype(F32)
    cosine, sine = cos_ref[...], sin_ref[...]
    width = total.shape[2]
    for start in range(0, width, 128):
        tile = slice(start, start + 128)
        y_ref[:, tile] = turn(total[0, :, tile], cosine, -sine).astype(BF)
    y_ref[:, width:] = total[1].astype(BF)


def pair_turn(own, got, cosine, sine):
    _, rows, width = own.shape
    return pl.pallas_call(
        pair_turn_kernel,
        out_shape=jax.ShapeDtypeStruct((rows, 2 * width), BF),
        name="pair_turn",
    )(own, *got, cosine, sine)


def ffn_kernel(x_ref, act_ref, w_ref, out_ref, sum_ref):
    step = pl.program_id(0)
    gate_w, up_w = w_ref[0], w_ref[1]
    x = x_ref[...]
    gate, up = nn(x, gate_w), nn(x, up_w)
    act_grad = act_ref[...]
    sig = jax.nn.sigmoid(gate)
    silu = gate * sig
    gate_grad = (act_grad * up * sig * (1.0 + gate * (1.0 - sig))).astype(BF)
    up_grad = (act_grad * silu).astype(BF)
    out_ref[0], out_ref[1], out_ref[2] = gate_grad, up_grad, (silu * up).astype(BF)
    part = nt(gate_grad, gate_w) + nt(up_grad, up_w)

    @pl.when(step == 0)
    def _():
        sum_ref[...] = part

    @pl.when(step > 0)
    def _():
        sum_ref[...] += part


def ffn_middle(rows_in, act_grad, weights):
    rows, width = rows_in.shape
    hidden = weights.shape[2]
    tile = FFN_TILE
    return pl.pallas_call(
        ffn_kernel,
        grid=(hidden // tile,),
        out_shape=(
            pltpu.HBM((3, rows, hidden), BF),
            jax.ShapeDtypeStruct((rows, width), F32),
        ),
        in_specs=[
            pl.BlockSpec((rows, width), lambda j: (0, 0)),
            pl.BlockSpec((rows, tile), lambda j: (0, j)),
            pl.BlockSpec((2, width, tile), lambda j: (0, 0, j)),
        ],
        out_specs=(
            pl.BlockSpec((3, rows, tile), lambda j: (0, 0, j)),
            pl.BlockSpec((rows, width), lambda j: (0, 0)),
        ),
        compiler_params=pltpu.CompilerParams(vmem_limit_bytes=40 << 20),
        cost_estimate=pl.CostEstimate(
            flops=8 * rows * width * hidden,
            bytes_accessed=4 * width * hidden,
            transcendentals=rows * hidden,
        ),
        name="ffn_middle",
    )(rows_in, act_grad, weights)


def products_kernel(in_a, in_b, grad_a, grad_b, right_a, right_b, out_ref):
    def emit(left_a, left_b):
        out_ref[0] = (tn(left_a[...], right_a[0]) + tn(left_b[...], right_b[0])).astype(BF)

    @pl.when(pl.program_id(0) < 2)
    def _():
        emit(in_a, in_b)

    @pl.when(pl.program_id(0) == 2)
    def _():
        emit(grad_a, grad_b)


def ffn_products(rows_in, rows_out, parts):
    rows, width = rows_in[0].shape
    hidden = parts[0].shape[2]
    tile = FFN_TILE
    last = width // tile - 1
    left = pl.BlockSpec((rows, tile), lambda k, i: (0, jnp.where(k < 2, i, last)))
    grad = pl.BlockSpec((rows, tile), lambda k, i: (0, jnp.where(k == 2, i, 0)))
    right = pl.BlockSpec((1, rows, hidden), lambda k, i: (k, 0, 0))
    return pl.pallas_call(
        products_kernel,
        grid=(3, width // tile),
        out_shape=pltpu.HBM((3, width, hidden), BF),
        in_specs=[left, left, grad, grad, right, right],
        out_specs=pl.BlockSpec((1, tile, hidden), lambda k, i: (k, i, 0)),
        compiler_params=pltpu.CompilerParams(vmem_limit_bytes=32 << 20),
        cost_estimate=pl.CostEstimate(
            flops=12 * rows * width * hidden,
            bytes_accessed=6 * width * hidden,
            transcendentals=0,
        ),
        name="ffn_products",
    )(*rows_in, *rows_out, *parts)


def simple_kernel(x_ref, w_ref, y_ref):
    y_ref[...] = nn(x_ref[...], w_ref[0])


def down_back(x, weights):
    rows, width = x.shape
    hidden = weights.shape[2]
    tile = FFN_TILE
    return pl.pallas_call(
        simple_kernel,
        grid=(hidden // tile,),
        out_shape=pltpu.HBM((rows, hidden), F32),
        in_specs=[
            pl.BlockSpec((rows, width), lambda j: (0, 0)),
            pl.BlockSpec((1, width, tile), lambda j: (2, 0, j)),
        ],
        out_specs=pl.BlockSpec((rows, tile), lambda j: (0, j)),
        compiler_params=pltpu.CompilerParams(vmem_limit_bytes=24 << 20),
        cost_estimate=pl.CostEstimate(
            flops=2 * rows * width * hidden,
            bytes_accessed=2 * width * hidden,
            transcendentals=0,
        ),
        name="down_back",
    )(x, weights)


def down_kernel(a_ref, b_ref, w_ref, y_ref):
    rows = a_ref.shape[1]
    for half, ref in enumerate((a_ref, b_ref)):
        y_ref[half * rows : (half + 1) * rows] = nt(ref[0], w_ref[0])


def down_forward(parts, weights):
    _, rows, hidden = parts[0].shape
    width = weights.shape[1]
    tile = FFN_TILE
    left = pl.BlockSpec((1, rows, hidden), lambda j: (2, 0, 0))
    total = pl.pallas_call(
        down_kernel,
        grid=(width // tile,),
        out_shape=jax.ShapeDtypeStruct((2 * rows, width), F32),
        in_specs=[left, left, pl.BlockSpec((1, tile, hidden), lambda j: (2, j, 0))],
        out_specs=pl.BlockSpec((2 * rows, tile), lambda j: (0, j)),
        compiler_params=pltpu.CompilerParams(vmem_limit_bytes=24 << 20),
        cost_estimate=pl.CostEstimate(
            flops=4 * rows * width * hidden,
            bytes_accessed=2 * width * hidden,
            transcendentals=0,
        ),
        name="down_forward",
    )(*parts, weights)
    return total[:rows], total[rows:]


def share_kernel(count, ids_ref, *refs):
    lefts, rights = refs[:count], refs[count : 2 * count]
    terms, (kept_ref, sent_ref) = refs[2 * count : -2], refs[-2:]
    half = kept_ref.shape[1]
    own = ids_ref[0] % 2 == 0
    column = 0
    for left, right in zip(lefts, rights):
        width = right.shape[1]
        part = tn(left[...], right[...]).astype(BF)
        at = slice(column, column + width)
        kept_ref[0, :, at] = jnp.where(own, part[:half], part[half:])
        sent_ref[0, :, at] = jnp.where(own, part[half:], part[:half])
        column += width
    if terms:
        tall = jnp.concatenate(
            [jnp.broadcast_to(term[...], (64, term.shape[1])) for term in terms], axis=0
        )
        part = jnp.transpose(tall).astype(BF)
        kept_ref[0, :, column:] = jnp.where(own, part[:half], part[half:])
        sent_ref[0, :, column:] = jnp.where(own, part[half:], part[:half])


def share_products(lefts, rights, terms):
    ctx_count = lax.axis_size("ctx")
    pairs = ctx_count // 2
    rows, width = lefts[0].shape
    height = width // ctx_count
    columns = sum(right.shape[1] for right in rights) + 64 * len(terms)

    def place(j, ids_ref):
        return (0, (ids_ref[0] // 2) ^ j)

    shape = jax.ShapeDtypeStruct((pairs, height, columns), BF)
    out = pl.BlockSpec((1, height, columns), lambda j, ids_ref: (j, 0, 0))
    return pl.pallas_call(
        lambda *refs: share_kernel(len(lefts), *refs),
        grid_spec=pltpu.PrefetchScalarGridSpec(
            num_scalar_prefetch=1,
            grid=(pairs,),
            in_specs=[pl.BlockSpec((rows, 2 * height), place) for _ in lefts]
            + [pl.BlockSpec(right.shape, lambda j, ids_ref: (0, 0)) for right in rights]
            + [pl.BlockSpec((1, 2 * height), place) for _ in terms],
            out_specs=(out, out),
        ),
        out_shape=(shape, shape),
        compiler_params=pltpu.CompilerParams(vmem_limit_bytes=24 << 20),
        cost_estimate=pl.CostEstimate(
            flops=2 * rows * width * columns,
            bytes_accessed=2 * (rows + columns) * width,
            transcendentals=0,
        ),
        name="share_terms" if terms else "share_products",
    )(jnp.stack(ids()), *lefts, *rights, *[term[None] for term in terms])


def share_start(lefts, rights, terms):
    pairs = lax.axis_size("ctx") // 2
    if (lefts[0].shape[1] // pairs) % 128:
        values = [tn(left, right) for left, right in zip(lefts, rights)]
        values += [jnp.broadcast_to(term[:, None], (term.shape[0], 64)) for term in terms]
        return [ctx_rows_sum(jnp.concatenate(values, axis=1))]
    kept, sent = share_products(lefts, rights, terms)
    got = swap(sent, "ctx", 1)
    parts = [kept[0], got[0]]
    for pair in range(1, pairs):
        part = (kept[pair].astype(F32) + got[pair].astype(F32)).astype(BF)
        parts.append(swap(part, "ctx", 2 * pair))
    return parts


def share_finish(parts):
    total = parts[0].astype(F32)
    for part in parts[1:]:
        total = total + part.astype(F32)
    return total


def own_features(terms):
    ctx_count, fsdp_count = lax.axis_size("ctx"), lax.axis_size("fsdp")
    total = jnp.stack(terms)
    away = 1
    while away < fsdp_count:
        total = total + swap(total, "fsdp", away)
        away *= 2
    blocks = total.reshape(len(terms), ctx_count, fsdp_count, -1)
    own = lax.dynamic_index_in_dim(blocks, lax.axis_index("fsdp"), 2, keepdims=False)
    own = own.reshape(len(terms), -1)
    return [own[i] for i in range(len(terms))]


def layer(
    hidden_in,
    out_grad,
    positions,
    block_order,
    attn_gain,
    ffn_gain,
    qkv_weight,
    out_weight,
    ffn_weight,
):
    ctx_count = lax.axis_size("ctx")
    me, _ = ids()
    rows = hidden_in.shape[1]
    queries_width, kv_width = H * HD, KV * HD
    ffn_parts = in_hbm(ffn_weight.transpose(1, 0, 2))

    frequency = jnp.power(ROPE_BASE, -(jnp.arange(HD // 2, dtype=F32) * 2.0 / HD))
    angles = positions[0].astype(F32)[:, None] * frequency[None, :]
    cosine = jnp.tile(jnp.cos(angles), (1, 4))
    sine = jnp.tile(jnp.concatenate([-jnp.sin(angles), jnp.sin(angles)], axis=1), (1, 2))
    own_anchor = anchors_of(block_order, me, rows)[None]
    key_anchor = jnp.concatenate(
        [anchors_of(block_order, me ^ offset, rows) for offset in key_offsets()]
    )
    key_anchor = jnp.broadcast_to(key_anchor[:, None], (rows * ctx_count, 128))

    inputs = hidden_in[0].astype(F32)
    grad_in = out_grad[0]
    scale_one = norm_scale(inputs)
    normed_one = (inputs * scale_one * attn_gain).astype(BF)

    fast = ctx_count == 8 and (qkv_weight.shape[1] // ctx_count) % 128 == 0
    if fast:
        early = (cosine, sine, own_anchor, key_anchor)
        qkv_pieces, marks = gather_pieces(qkv_weight, early)
        out_blocks = gather_blocks(out_weight, *marks)
        queries, pair, qkv_full = pieces_forward(
            normed_one, qkv_weight, qkv_pieces, cosine, sine
        )
    else:
        marks = (normed_one, normed_one)
        out_blocks = gather_blocks(out_weight, *marks)
        qkv_full = whole_of(qkv_weight, gather_blocks(qkv_weight, normed_one, normed_one))
        projected = nn(normed_one, qkv_full)
        turned = rotate(
            projected[:, : queries_width + kv_width].reshape(rows, H + KV, HD), positions[0]
        ).reshape(rows, queries_width + kv_width)
        queries = (turned[:, :queries_width] * (1.0 / math.sqrt(HD))).astype(BF)
        pair = jnp.concatenate(
            [turned[:, queries_width:], projected[:, queries_width + kv_width :]], axis=1
        ).astype(BF)
    own_one = columns_to_owner(by_feature(after(normed_one, pair)))
    keys_values = gather_keys(pair)
    rows_out = fetch_rows(after(grad_in, marks[0]))
    attn_rows, attended, logs = attend(queries, keys_values, key_anchor, own_anchor)
    residual, normed_two = out_forward(
        attn_rows, out_weight, out_blocks, hidden_in[0], ffn_gain
    )
    scale_two = norm_scale(residual)
    rows_in = halves_of(pass_rows(normed_two))
    rows_out = halves_of(after(rows_out, normed_two))
    act_grad = []
    for half in rows_out:
        act_grad.append(down_back(half, ffn_parts))

    all_attn = gather_planes(after(attn_rows, rows_in[1]))
    middle = []
    for half, act in zip(rows_in, act_grad):
        middle.append(ffn_middle(half, in_hbm(act), ffn_parts))
    parts, partial = [in_hbm(m[0]) for m in middle], [m[1] for m in middle]
    sum_grad = sum_rows(partial)
    products = ffn_products(rows_in, rows_out, parts).transpose(1, 0, 2)
    ffn_weight_grad = lax.psum_scatter(products, "ctx", scatter_dimension=0, tiled=True)
    ffn_weight_grad = ffn_weight_grad.astype(F32)
    out_partial = down_forward(parts, ffn_parts)

    unit_two = residual * scale_two
    ffn_gain_term = jnp.sum(sum_grad * unit_two, axis=0)
    scaled_two = ffn_gain * sum_grad
    residual_grad = grad_in.astype(F32) + scale_two * (
        scaled_two - unit_two * jnp.mean(scaled_two * unit_two, axis=-1, keepdims=True)
    )
    residual_bf = residual_grad.astype(BF)
    own_residual = columns_to_owner(by_feature(residual_bf))
    attn_grad = out_back(residual_bf, out_weight, out_blocks)
    query_part, kept, sent = attend_back(
        queries, attn_grad, attended, keys_values, key_anchor, own_anchor, logs, cosine, sine
    )
    query_planes = pass_rows(query_part)
    pair_part = sum_pairs(kept, sent, cosine, sine)
    all_pair = gather_planes(pair_part)
    all_query = by_offset(after(query_planes, pair_part))
    first_sums = share_start([own_residual, own_one], [after(all_attn, pair_part), all_query], [])
    input_grad, attn_gain_term = one_back(
        query_part, pair_part, qkv_full, hidden_in[0], attn_gain, residual_grad
    )
    terms = own_features([attn_gain_term[0], ffn_gain_term])
    last_sums = share_finish(share_start([own_one], [all_pair], terms))
    first_sums = share_finish(after(first_sums, last_sums))

    out_sum = sum_rows([after(half, pair_part) for half in out_partial])
    output = (residual + out_sum).astype(BF)

    pairs_width = 2 * kv_width
    out_weight_grad = first_sums[:, :queries_width]
    qkv_grad = jnp.concatenate(
        [first_sums[:, queries_width:], last_sums[:, :pairs_width]], axis=1
    )
    return (
        output[None],
        input_grad[None],
        qkv_grad,
        out_weight_grad,
        ffn_weight_grad,
        last_sums[:, pairs_width],
        last_sums[:, pairs_width + 64],
    )


def solution(mesh):
    step = sharded(mesh)
    return step


def sharded(mesh):
    return jax.shard_map(
        layer,
        mesh=mesh,
        in_specs=(
            P("fsdp", "ctx", None),
            P("fsdp", "ctx", None),
            P("fsdp", "ctx"),
            P(),
            P(),
            P(),
            P("fsdp", None),
            P("fsdp", None),
            P(None, None, "fsdp"),
        ),
        out_specs=(
            P("fsdp", "ctx", None),
            P("fsdp", "ctx", None),
            P(("ctx", "fsdp"), None),
            P(("ctx", "fsdp"), None),
            P("ctx", None, "fsdp"),
            P(("ctx", "fsdp")),
            P(("ctx", "fsdp")),
        ),
        check_vma=False,
    )
```

```python
import math

import jax
import jax.numpy as jnp
from jax import lax
from jax.experimental import pallas as pl
from jax.experimental.pallas import tpu as pltpu
from jax.sharding import PartitionSpec as P


H = 32
KV = 8
HD = 64

NORM_EPS = 1e-05
ROPE_BASE = 500000.0
FFN_TILE = 512
KEY_CHUNK = 256


BF = jnp.bfloat16
F32 = jnp.float32


def mm(a, b, dims):
    return lax.dot_general(a, b, (dims, ((), ())), preferred_element_type=F32)


def nn(a, b):
    return mm(a, b, ((1,), (0,)))


def nt(a, b):
    return mm(a, b, ((1,), (1,)))


def tn(a, b):
    return mm(a, b, ((0,), (0,)))


def swap(value, axis, offset):
    count = lax.axis_size(axis)
    return lax.ppermute(value, axis, [(i, i ^ offset) for i in range(count)])


def rotate(values, token_places):
    head_dim = values.shape[-1]
    half_dim = head_dim // 2
    frequency = jnp.power(ROPE_BASE, -(jnp.arange(half_dim, dtype=F32) * 2.0 / head_dim))
    angles = token_places.astype(F32)[:, None] * frequency[None, :]
    cosine = jnp.concatenate([jnp.cos(angles), jnp.cos(angles)], axis=-1)[:, None, :]
    sine_part = jnp.concatenate([jnp.sin(angles), jnp.sin(angles)], axis=-1)[:, None, :]
    turned = jnp.concatenate([-values[..., half_dim:], values[..., :half_dim]], axis=-1)
    return values * cosine + turned * sine_part


def norm_scale(values):
    return lax.rsqrt(jnp.mean(values * values, axis=-1, keepdims=True) + NORM_EPS)


def lookup(entries, row_ids):
    matches = row_ids[:, None] == jnp.arange(entries.shape[0], dtype=jnp.int32)[None, :]
    return jnp.sum(jnp.where(matches, entries[None, :], 0), axis=1)


def anchors_of(block_order, owner, row_count):
    block_len = row_count // 2
    row_ids = owner * row_count + jnp.arange(row_count, dtype=jnp.int32)
    return lookup(block_order, row_ids // block_len) * block_len + row_ids % block_len


def after(value, *earlier):
    return lax.optimization_barrier((value, earlier))[0]


def ids():
    return lax.axis_index("ctx"), lax.axis_index("fsdp")


def gather_pieces(weight, early):
    rows, columns = weight.shape
    share = columns // lax.axis_size("ctx")
    half = rows // 2
    mine = lax.dynamic_slice(weight, (0, lax.axis_index("ctx") * share), (rows, share))
    planes = {}
    planes[3] = swap(mine, "fsdp", 3)
    planes[1] = swap(mine, "fsdp", 1)
    planes[2] = swap(after(planes[3], early), "fsdp", 1)
    pieces = []
    for away in (1, 3, 2):
        first = planes[away]
        along_x, along_y = swap(first, "ctx", 2), swap(first, "ctx", 4)
        top, low = swap(along_y[:half], "ctx", 2), swap(along_x[half:], "ctx", 4)
        parts = [(0, 0, first), (2, 0, along_x), (4, 0, along_y), (6, 0, top), (6, half, low)]
        for offset, start, part in parts:
            pieces.append((away, offset, start, part))
            pieces.append((away, offset + 1, start, swap(part, "ctx", 1)))
    return pieces, (planes[2], (pieces[-4][3], pieces[-2][3]))


def pieces_kernel(places, rows_in, share, ids_ref, x_ref, own_ref, *refs):
    count = len(places)
    piece_refs, refs = refs[:count], refs[count:]
    cos_ref, sin_ref, q_ref, pair_ref, full_ref, y_ref, buf, in_sems, out_sems = refs
    me, plane = ids_ref[0], ids_ref[1]

    def block(away):
        return pl.ds(pl.multiple_of((plane ^ away) * rows_in, 128), rows_in)

    own_copy = pltpu.make_async_copy(own_ref, buf.at[block(0)], in_sems.at[count])
    own_copy.start()
    copies = []
    for i, (away, offset, start, height) in enumerate(places):
        at = pl.ds(pl.multiple_of((plane ^ away) * rows_in + start, 128), height)
        columns = pl.ds(pl.multiple_of((me ^ offset) * share, 128), share)
        copies.append(pltpu.make_async_copy(piece_refs[i], buf.at[at, columns], in_sems.at[i]))
        copies[-1].start()
    outs = []
    order = [0] + list(dict.fromkeys(away for away, _, _, _ in places))
    for away in order:
        if away:
            for copy, place in zip(copies, places):
                if place[0] == away:
                    copy.wait()
        else:
            own_copy.wait()
        outs.append(
            pltpu.make_async_copy(buf.at[block(away)], full_ref.at[block(away)], out_sems.at[away])
        )
        outs[-1].start()
        part = nn(x_ref[:, block(away)], buf[block(away)])
        y_ref[...] = part if away == 0 else y_ref[...] + part
    cosine, sine = cos_ref[...], sin_ref[...]
    queries, keys = H * HD, KV * HD
    for start in range(0, queries + keys, 128):
        tile = turn(y_ref[:, start : start + 128], cosine, sine)
        if start < queries:
            q_ref[:, start : start + 128] = (tile * (1.0 / math.sqrt(HD))).astype(BF)
        else:
            pair_ref[:, start - queries : start - queries + 128] = tile.astype(BF)
    pair_ref[:, keys:] = y_ref[:, queries + keys :].astype(BF)
    for copy in outs:
        copy.wait()


def pieces_forward(x, own, pieces, cosine, sine):
    me, plane = ids()
    rows_in, columns = own.shape
    rows, width = x.shape
    share = columns // lax.axis_size("ctx")
    places = tuple((away, offset, start, part.shape[0]) for away, offset, start, part in pieces)
    arrays = [part for _, _, _, part in pieces]
    hbm, vmem = pl.BlockSpec(memory_space=pltpu.HBM), pl.BlockSpec(memory_space=pltpu.VMEM)
    return pl.pallas_call(
        lambda *refs: pieces_kernel(places, rows_in, share, *refs),
        out_shape=(
            jax.ShapeDtypeStruct((rows, H * HD), BF),
            jax.ShapeDtypeStruct((rows, 2 * KV * HD), BF),
            pltpu.HBM((width, columns), BF),
        ),
        in_specs=[pl.BlockSpec(memory_space=pltpu.SMEM), vmem, hbm]
        + [hbm] * len(arrays)
        + [vmem, vmem],
        out_specs=(vmem, vmem, hbm),
        scratch_shapes=[
            pltpu.VMEM((rows, columns), F32),
            pltpu.VMEM((width, columns), BF),
            pltpu.SemaphoreType.DMA((len(arrays) + 1,)),
            pltpu.SemaphoreType.DMA((width // rows_in,)),
        ],
        compiler_params=pltpu.CompilerParams(vmem_limit_bytes=32 << 20),
        cost_estimate=pl.CostEstimate(
            flops=2 * rows * width * columns, bytes_accessed=4 * width * columns, transcendentals=0
        ),
        name="pieces_forward",
    )(jnp.stack([me, plane]), x, in_hbm(own), *[in_hbm(part) for part in arrays], cosine, sine)


def gather_blocks(weight, before_fsdp, before_ctx):
    rows, columns = weight.shape
    me, plane = ids()
    share = columns // lax.axis_size("ctx")
    mine = lax.dynamic_slice(weight, (0, me * share), (rows, share))
    planes = lax.all_gather(after(mine, before_fsdp), "fsdp")
    others = jnp.stack(
        [
            lax.dynamic_index_in_dim(planes, plane ^ away, 0, keepdims=False)
            for away in range(1, planes.shape[0])
        ]
    )
    return lax.all_gather(after(others, before_ctx), "ctx")


def whole_of(own, blocks):
    ctx_count, others, rows, share = blocks.shape
    plane = lax.axis_index("fsdp")
    columns = ctx_count * share
    full = jnp.zeros(((others + 1) * rows, columns), own.dtype)
    full = lax.dynamic_update_slice(full, own, (plane * rows, 0))
    for away in range(1, others + 1):
        part = blocks[:, away - 1].transpose(1, 0, 2).reshape(rows, columns)
        full = lax.dynamic_update_slice(full, part, ((plane ^ away) * rows, 0))
    return full


def in_hbm(value):
    return pltpu.with_memory_space_constraint(value, pltpu.HBM)


def out_kernel(back, ids_ref, x_ref, own_ref, blocks_ref, *refs):
    hidden_ref, gain_ref = (None, None) if back else refs[:2]
    outs = refs if back else refs[2:]
    own_buf, buf, sems = outs[-3:]
    ctx_count, others, rows, share = buf.shape
    plane = ids_ref[1]
    copies = [pltpu.make_async_copy(own_ref, own_buf, sems.at[ctx_count])]
    for c in range(ctx_count):
        copies.append(pltpu.make_async_copy(blocks_ref.at[c], buf.at[c], sems.at[c]))
    for copy in copies:
        copy.start()

    def features(away):
        return pl.ds(pl.multiple_of((plane ^ away) * rows, 128), rows)

    copies[0].wait()
    if back:
        y_ref = outs[0]
        own_part = nn(x_ref[:, features(0)], own_buf[...])
        for c in range(ctx_count):
            copies[c + 1].wait()
            at = slice(c * share, (c + 1) * share)
            total = own_part[:, at]
            for away in range(1, others + 1):
                total += nn(x_ref[:, features(away)], buf[c, away - 1])
            y_ref[:, at] = total.astype(BF)
        return
    residual_ref, normed_ref = outs[:2]
    residual_ref[...] = hidden_ref[...].astype(F32)
    residual_ref[:, features(0)] += nt(x_ref[...], own_buf[...])
    for c in range(ctx_count):
        copies[c + 1].wait()
        x = x_ref[:, c * share : (c + 1) * share]
        for away in range(1, others + 1):
            residual_ref[:, features(away)] += nt(x, buf[c, away - 1])
    residual = residual_ref[...]
    normed_ref[...] = (residual * norm_scale(residual) * gain_ref[...]).astype(BF)


def out_call(back, x, own, blocks, extra, out_shape):
    vmem, hbm = pl.BlockSpec(memory_space=pltpu.VMEM), pl.BlockSpec(memory_space=pltpu.HBM)
    return pl.pallas_call(
        lambda *refs: out_kernel(back, *refs),
        out_shape=out_shape,
        in_specs=[pl.BlockSpec(memory_space=pltpu.SMEM), vmem, hbm, hbm] + [vmem] * len(extra),
        out_specs=jax.tree.map(lambda _: vmem, out_shape),
        scratch_shapes=[
            pltpu.VMEM(own.shape, own.dtype),
            pltpu.VMEM(blocks.shape, blocks.dtype),
            pltpu.SemaphoreType.DMA((blocks.shape[0] + 1,)),
        ],
        compiler_params=pltpu.CompilerParams(vmem_limit_bytes=24 << 20),
        cost_estimate=pl.CostEstimate(
            flops=2 * x.shape[0] * own.size * (blocks.shape[1] + 1),
            bytes_accessed=2 * own.size * (blocks.shape[1] + 1),
            transcendentals=0,
        ),
        name="out_back" if back else "out_forward",
    )(jnp.stack(ids()), x, in_hbm(own), in_hbm(blocks), *extra)


def out_forward(attn_rows, own, blocks, hidden, gain):
    if blocks.shape[3] % 128:
        residual = hidden.astype(F32) + nt(attn_rows, whole_of(own, blocks))
        return residual, (residual * norm_scale(residual) * gain).astype(BF)
    out_shape = (
        jax.ShapeDtypeStruct(hidden.shape, F32),
        jax.ShapeDtypeStruct(hidden.shape, BF),
    )
    return out_call(False, attn_rows, own, blocks, [hidden, gain[None]], out_shape)


def out_back(x, own, blocks):
    if blocks.shape[3] % 128:
        return nn(x, whole_of(own, blocks)).astype(BF)
    out_shape = jax.ShapeDtypeStruct((x.shape[0], own.shape[1]), BF)
    return out_call(True, x, own, blocks, [], out_shape)


def one_back_kernel(
    query_ref, pair_ref, w_ref, hidden_ref, gain_ref, residual_ref, y_ref
):
    step = pl.program_id(0)
    rows = w_ref.shape[0]
    split = query_ref.shape[1]
    y_ref[:, pl.ds(pl.multiple_of(step * rows, 128), rows)] = nt(
        query_ref[...], w_ref[:, :split]
    ) + nt(pair_ref[...], w_ref[:, split:])

    @pl.when(step == pl.num_programs(0) - 1)
    def _():
        grad = y_ref[...]
        inputs = hidden_ref[...].astype(F32)
        scale = norm_scale(inputs)
        unit = inputs * scale
        scaled = gain_ref[...] * grad
        y_ref[...] = residual_ref[...] + scale * (
            scaled - unit * jnp.mean(scaled * unit, axis=-1, keepdims=True)
        )


def one_back(query_part, pair_part, weight, hidden, gain, residual_grad):
    rows, width = hidden.shape
    columns = weight.shape[1]
    tile = FFN_TILE

    def whole(array):
        return pl.BlockSpec(array.shape, lambda j: (0, 0))

    gain = gain[None]
    return pl.pallas_call(
        one_back_kernel,
        grid=(width // tile,),
        out_shape=jax.ShapeDtypeStruct((rows, width), F32),
        in_specs=[
            whole(query_part),
            whole(pair_part),
            pl.BlockSpec((tile, columns), lambda j: (j, 0)),
            whole(hidden),
            whole(gain),
            whole(residual_grad),
        ],
        out_specs=pl.BlockSpec((rows, width), lambda j: (0, 0)),
        compiler_params=pltpu.CompilerParams(vmem_limit_bytes=24 << 20),
        cost_estimate=pl.CostEstimate(
            flops=2 * rows * width * columns,
            bytes_accessed=2 * width * columns,
            transcendentals=0,
        ),
        name="one_back",
    )(query_part, pair_part, in_hbm(weight), hidden, gain, residual_grad)


def pass_rows(values):
    if lax.axis_size("fsdp") != 4:
        return fetch_rows(values)
    third = swap(values, "fsdp", 3)
    first = swap(values, "fsdp", 1)
    second = swap(third, "fsdp", 1)
    return [values, first, second, third]


def fetch_rows(values):
    count = lax.axis_size("fsdp")
    return [values] + [swap(values, "fsdp", away) for away in range(1, count)]


def sum_rows(halves):
    count = lax.axis_size("fsdp")
    half = count // 2
    rows = halves[0].shape[0] // half
    parts = [
        halves[away // half][away % half * rows : (away % half + 1) * rows] for away in range(count)
    ]
    if count == 4:
        passed = swap(parts[2].astype(BF), "fsdp", 1).astype(F32)
        one = swap(parts[1].astype(BF), "fsdp", 1).astype(F32)
        third = swap((parts[3] + passed).astype(BF), "fsdp", 3).astype(F32)
        return parts[0] + one + third
    total = parts[0]
    for away in range(1, count):
        total = total + swap(parts[away].astype(BF), "fsdp", away).astype(F32)
    return total


def by_feature(values):
    rows, width = values.shape
    ctx_count, fsdp_count = lax.axis_size("ctx"), lax.axis_size("fsdp")
    blocks = values.reshape(rows, ctx_count, fsdp_count, width // (ctx_count * fsdp_count))
    return blocks.transpose(0, 2, 1, 3).reshape(rows, width)


def by_offset(planes):
    count, plane = len(planes), lax.axis_index("fsdp")
    joined = planes
    bit = 1
    while bit < count:
        odd = (plane & bit) != 0
        joined = [jnp.where(odd, joined[i ^ bit], joined[i]) for i in range(count)]
        bit *= 2
    return jnp.concatenate(joined, axis=0)


def gather_planes(values):
    count = lax.axis_size("fsdp")
    rows, columns = values.shape
    copies = jnp.broadcast_to(values[None], (count, rows, columns)).reshape(count * rows, columns)
    return lax.all_to_all(copies, "fsdp", split_axis=0, concat_axis=0, tiled=True)


def columns_to_owner(values):
    return lax.all_to_all(values, "fsdp", split_axis=1, concat_axis=0, tiled=True)


def sum_over_ctx(part_for):
    pairs = lax.axis_size("ctx") // 2
    sent = jnp.stack([part_for(2 * pair + 1).astype(BF) for pair in range(pairs)])
    got = swap(sent, "ctx", 1)
    sums = [part_for(2 * pair).astype(F32) + got[pair].astype(F32) for pair in range(pairs)]
    total = sums[0]
    for pair in range(1, pairs):
        total = total + swap(sums[pair].astype(BF), "ctx", 2 * pair).astype(F32)
    return total


def ctx_rows_sum(values):
    height = values.shape[0] // lax.axis_size("ctx")
    me = lax.axis_index("ctx")

    def part(offset):
        return lax.dynamic_slice(
            values, ((me ^ offset) * height, 0), (height, values.shape[1])
        )

    return sum_over_ctx(part)


def key_offsets():
    count = lax.axis_size("ctx")
    return list(range(0, count, 2)) + list(range(1, count, 2))


def gather_keys(piece):
    same = [piece] + [swap(piece, "ctx", far) for far in range(2, lax.axis_size("ctx"), 2)]
    mine = jnp.concatenate(same, axis=0)
    return mine, swap(mine, "ctx", 1)


def sum_pairs(kept, sent, cosine, sine):
    _, count, width = kept.shape
    pairs = lax.axis_size("ctx") // 2
    got = swap(sent, "ctx", 1)
    sums = (kept.astype(F32) + got.astype(F32)).reshape(2, pairs, count // pairs, width)
    far = [swap(sums[:, pair].astype(BF), "ctx", 2 * pair) for pair in range(1, pairs)]
    return pair_turn(sums[:, 0], far, cosine, sine)


def half_mask(shape):
    return lax.broadcasted_iota(jnp.int32, shape, len(shape) - 1) % 128 < HD


def turn(values, cosine, sine):
    lanes = lax.broadcasted_iota(jnp.int32, values.shape, 1) % HD
    turned = jnp.where(
        lanes < HD // 2, pltpu.roll(values, 128 - HD // 2, 1), pltpu.roll(values, HD // 2, 1)
    )
    return values * cosine + turned * sine


def doubled(tile, odd):
    wide = tile.astype(F32)
    other = pltpu.roll(wide, HD, 1)
    return jnp.where(half_mask(tile.shape) == (odd == 0), wide, other).astype(BF)


def split_heads(tile_pair):
    zero = jnp.zeros((), tile_pair.dtype)
    parts = []
    for j in range(2):
        tile = tile_pair[:, j * 128 : (j + 1) * 128]
        mask = half_mask(tile.shape)
        parts += [jnp.where(mask, tile, zero), jnp.where(mask, zero, tile)]
    return jnp.concatenate(parts, axis=0)


def merge_heads(stacked):
    rows = stacked.shape[0] // 4
    tiles = []
    for j in range(2):
        even = stacked[2 * j * rows : (2 * j + 1) * rows]
        odd = stacked[(2 * j + 1) * rows : (2 * j + 2) * rows]
        tiles.append(jnp.where(half_mask(even.shape), even, odd))
    return jnp.concatenate(tiles, axis=1)


def key_chunks(refs, chunk):
    first = 0
    for k_ref, v_ref in refs:
        for start in range(0, k_ref.shape[0], chunk):
            at = slice(start, start + chunk)
            yield first + start, k_ref.at[at, :], v_ref.at[at, :]
        first += k_ref.shape[0]


def masked_scores(keys, queries, key_ref, own_ref, start):
    allowed = key_ref[start : start + keys.shape[0], :1] <= own_ref[...]
    bias = jnp.where(allowed, 0.0, -1e30).astype(F32)
    return nt(keys, queries) + jnp.concatenate([bias] * 4, axis=1)


def attend_kernel(
    chunk, q_ref, ka_ref, va_ref, kb_ref, vb_ref, key_ref, own_ref, rows_ref, attended_ref, log_ref
):
    odd = pl.program_id(0) % 2
    rows = q_ref.shape[0]
    queries = split_heads(q_ref[...])
    parts = list(key_chunks(((ka_ref, va_ref), (kb_ref, vb_ref)), chunk))
    scores = [
        masked_scores(doubled(k_ref[...], odd), queries, key_ref, own_ref, start)
        for start, k_ref, _ in parts
    ]
    top = jnp.max(scores[0], axis=0, keepdims=True)
    for score in scores[1:]:
        top = jnp.maximum(top, jnp.max(score, axis=0, keepdims=True))
    total = jnp.zeros_like(top)
    summed = jnp.zeros((4 * rows, 128), F32)
    for score, (_, _, v_ref) in zip(scores, parts):
        weights = jnp.exp(score - top)
        total += jnp.sum(weights, axis=0, keepdims=True)
        summed += tn(weights.astype(BF), doubled(v_ref[...], odd))
    log_ref[0] = top + jnp.log(total)
    attended = merge_heads(summed / jnp.transpose(jnp.broadcast_to(total, (128, 4 * rows))))
    attended_ref[...] = attended
    rows_ref[...] = attended.astype(BF)


def key_specs(parts):
    tiles = parts[0].shape[1] // 256
    specs, arrays = [], []
    for part in parts:
        specs.append(pl.BlockSpec((part.shape[0], 128), lambda g: (0, g // 2)))
        specs.append(pl.BlockSpec((part.shape[0], 128), lambda g: (0, tiles + g // 2)))
        arrays += [part, part]
    return specs, arrays


def attend(queries, keys_values, key_anchor, own_anchor):
    rows, width = queries.shape
    count = key_anchor.shape[0]
    specs, arrays = key_specs(keys_values)
    wide = pl.BlockSpec((rows, 256), lambda g: (0, g))
    return pl.pallas_call(
        lambda *refs: attend_kernel(KEY_CHUNK, *refs),
        grid=(KV,),
        out_shape=(
            jax.ShapeDtypeStruct((rows, width), BF),
            jax.ShapeDtypeStruct((rows, width), F32),
            jax.ShapeDtypeStruct((KV, 1, 4 * rows), F32),
        ),
        in_specs=[wide]
        + specs
        + [
            pl.BlockSpec((count, 128), lambda g: (0, 0)),
            pl.BlockSpec((1, rows), lambda g: (0, 0)),
        ],
        out_specs=(wide, wide, pl.BlockSpec((1, 1, 4 * rows), lambda g: (g, 0, 0))),
        compiler_params=pltpu.CompilerParams(vmem_limit_bytes=48 << 20),
        cost_estimate=pl.CostEstimate(
            flops=4 * rows * width * count,
            bytes_accessed=4 * count * KV * HD,
            transcendentals=rows * H * count,
        ),
        name="attend",
    )(queries, *arrays, key_anchor, own_anchor)


def attend_back_kernel(
    chunk, q_ref, grad_ref, attended_ref, ka_ref, va_ref, kb_ref, vb_ref, key_ref, own_ref, log_ref,
    cos_ref, sin_ref, dq_ref, kept_ref, sent_ref,
):
    odd = pl.program_id(0) % 2
    rows = q_ref.shape[0]
    half = ka_ref.shape[0]
    queries, grads = split_heads(q_ref[...]), split_heads(grad_ref[...])
    product = grads.astype(F32) * split_heads(attended_ref[...])
    delta = jnp.sum(jnp.transpose(product), axis=0, keepdims=True)
    log_total = log_ref[0]
    total = jnp.zeros((4 * rows, 128), F32)
    keep = half_mask((chunk, 128)) == (odd == 0)
    for start, k_ref, v_ref in key_chunks(((ka_ref, va_ref), (kb_ref, vb_ref)), chunk):
        keys, values = doubled(k_ref[...], odd), doubled(v_ref[...], odd)
        scores = masked_scores(keys, queries, key_ref, own_ref, start)
        probs = jnp.exp(scores - log_total)
        value_grad = nn(probs.astype(BF), grads)
        score_grad = (probs * (nt(values, grads) - delta)).astype(BF)
        key_grad = nn(score_grad, queries)
        total += tn(score_grad, keys)
        out_ref = kept_ref if start < half else sent_ref
        at = slice(start % half, start % half + chunk)
        for part, value in enumerate((key_grad, value_grad)):
            value = (value + pltpu.roll(value, HD, 1)).astype(BF)
            out_ref[part, at, :] = jnp.where(keep, value, out_ref[part, at, :])
    merged = merge_heads(total) * (1.0 / math.sqrt(HD))
    cosine, sine = cos_ref[...], sin_ref[...]
    for j in range(2):
        tile = slice(j * 128, (j + 1) * 128)
        dq_ref[:, tile] = turn(merged[:, tile], cosine, -sine).astype(BF)


def attend_back(queries, grads, attended, keys_values, key_anchor, own_anchor, logs, cosine, sine):
    rows, width = queries.shape
    count = key_anchor.shape[0]
    specs, arrays = key_specs(keys_values)
    wide = pl.BlockSpec((rows, 256), lambda g: (0, g))
    small = pl.BlockSpec((rows, 128), lambda g: (0, 0))
    pair = pl.BlockSpec((2, count // 2, 128), lambda g: (0, 0, g // 2))
    return pl.pallas_call(
        lambda *refs: attend_back_kernel(KEY_CHUNK, *refs),
        grid=(KV,),
        out_shape=(
            jax.ShapeDtypeStruct((rows, width), BF),
            jax.ShapeDtypeStruct((2, count // 2, KV * HD), BF),
            jax.ShapeDtypeStruct((2, count // 2, KV * HD), BF),
        ),
        in_specs=[wide, wide, wide]
        + specs
        + [
            pl.BlockSpec((count, 128), lambda g: (0, 0)),
            pl.BlockSpec((1, rows), lambda g: (0, 0)),
            pl.BlockSpec((1, 1, 4 * rows), lambda g: (g, 0, 0)),
            small,
            small,
        ],
        out_specs=(wide, pair, pair),
        compiler_params=pltpu.CompilerParams(vmem_limit_bytes=48 << 20),
        cost_estimate=pl.CostEstimate(
            flops=10 * rows * width * count,
            bytes_accessed=8 * count * KV * HD,
            transcendentals=rows * H * count,
        ),
        name="attend_back",
    )(queries, grads, attended, *arrays, key_anchor, own_anchor, logs, cosine, sine)


def pair_turn_kernel(own_ref, *refs):
    got, (cos_ref, sin_ref, y_ref) = refs[:-3], refs[-3:]
    total = own_ref[...]
    for ref in got:
        total = total + ref[...].astype(F32)
    cosine, sine = cos_ref[...], sin_ref[...]
    width = total.shape[2]
    for start in range(0, width, 128):
        tile = slice(start, start + 128)
        y_ref[:, tile] = turn(total[0, :, tile], cosine, -sine).astype(BF)
    y_ref[:, width:] = total[1].astype(BF)


def pair_turn(own, got, cosine, sine):
    _, rows, width = own.shape
    return pl.pallas_call(
        pair_turn_kernel,
        out_shape=jax.ShapeDtypeStruct((rows, 2 * width), BF),
        name="pair_turn",
    )(own, *got, cosine, sine)


def join_rows(x_buf, refs):
    @pl.when((pl.program_id(0) == 0))
    def _():
        rows = refs[0].shape[0]
        for i, ref in enumerate(refs):
            x_buf[i * rows : (i + 1) * rows] = ref[...]


def ffn_kernel(count, *refs):
    rows_refs, (act_ref, w_ref, out_ref, sum_ref, x_buf) = refs[:count], refs[count:]
    join_rows(x_buf, rows_refs)
    step = pl.program_id(0)
    gate_w, up_w = w_ref[0], w_ref[1]
    x = x_buf[...]
    gate, up = nn(x, gate_w), nn(x, up_w)
    act_grad = act_ref[...]
    sig = jax.nn.sigmoid(gate)
    silu = gate * sig
    gate_grad = (act_grad * up * sig * (1.0 + gate * (1.0 - sig))).astype(BF)
    up_grad = (act_grad * silu).astype(BF)
    out_ref[0], out_ref[1], out_ref[2] = gate_grad, up_grad, (silu * up).astype(BF)
    part = nt(gate_grad, gate_w) + nt(up_grad, up_w)

    @pl.when(step == 0)
    def _():
        sum_ref[...] = part

    @pl.when(step > 0)
    def _():
        sum_ref[...] += part


def ffn_middle(blocks, act_grad, half, weights):
    width = blocks[0].shape[1]
    rows = blocks[0].shape[0] * len(blocks)
    hidden = weights.shape[2]
    tile = FFN_TILE
    return pl.pallas_call(
        lambda *refs: ffn_kernel(len(blocks), *refs),
        grid=(hidden // tile,),
        out_shape=(
            pltpu.HBM((3, rows, hidden), BF),
            jax.ShapeDtypeStruct((rows, width), F32),
        ),
        in_specs=[pl.BlockSpec(block.shape, lambda j: (0, 0)) for block in blocks]
        + [
            pl.BlockSpec((rows, tile), lambda j: (half, j)),
            pl.BlockSpec((2, width, tile), lambda j: (0, 0, j)),
        ],
        out_specs=(
            pl.BlockSpec((3, rows, tile), lambda j: (0, 0, j)),
            pl.BlockSpec((rows, width), lambda j: (0, 0)),
        ),
        scratch_shapes=[pltpu.VMEM((rows, width), BF)],
        compiler_params=pltpu.CompilerParams(vmem_limit_bytes=40 << 20),
        cost_estimate=pl.CostEstimate(
            flops=8 * rows * width * hidden,
            bytes_accessed=4 * width * hidden,
            transcendentals=rows * hidden,
        ),
        name="ffn_middle",
    )(*blocks, act_grad, weights)


def products_kernel(count, *refs):
    in_refs, grad_refs = refs[:count], refs[count : 2 * count]
    right_a, right_b, out_ref = refs[2 * count :]
    half = count // 2

    def emit(lefts):
        left_a = jnp.concatenate([ref[...] for ref in lefts[:half]], axis=0)
        left_b = jnp.concatenate([ref[...] for ref in lefts[half:]], axis=0)
        out_ref[0] = (tn(left_a, right_a[0]) + tn(left_b, right_b[0])).astype(BF)

    @pl.when(pl.program_id(0) < 2)
    def _():
        emit(in_refs)

    @pl.when(pl.program_id(0) == 2)
    def _():
        emit(grad_refs)


def ffn_products(rows_in, rows_out, parts):
    count = len(rows_in)
    rows, width = rows_in[0].shape
    hidden = parts[0].shape[2]
    tile = FFN_TILE
    last = width // tile - 1
    left = pl.BlockSpec((rows, tile), lambda k, i: (0, jnp.where(k < 2, i, last)))
    grad = pl.BlockSpec((rows, tile), lambda k, i: (0, jnp.where(k == 2, i, 0)))
    right = pl.BlockSpec((1, rows * count // 2, hidden), lambda k, i: (k, 0, 0))
    return pl.pallas_call(
        lambda *refs: products_kernel(count, *refs),
        grid=(3, width // tile),
        out_shape=pltpu.HBM((3, width, hidden), BF),
        in_specs=[left] * count + [grad] * count + [right, right],
        out_specs=pl.BlockSpec((1, tile, hidden), lambda k, i: (k, i, 0)),
        compiler_params=pltpu.CompilerParams(vmem_limit_bytes=32 << 20),
        cost_estimate=pl.CostEstimate(
            flops=6 * count * rows * width * hidden,
            bytes_accessed=6 * width * hidden,
            transcendentals=0,
        ),
        name="ffn_products",
    )(*rows_in, *rows_out, *parts)


def down_back_kernel(count, *refs):
    rows_refs, (w_ref, y_ref, x_buf) = refs[:count], refs[count:]
    join_rows(x_buf, rows_refs)
    y_ref[...] = nn(x_buf[...], w_ref[0])


def down_back(blocks, weights):
    width = blocks[0].shape[1]
    rows = blocks[0].shape[0] * len(blocks)
    hidden = weights.shape[2]
    tile = FFN_TILE
    return pl.pallas_call(
        lambda *refs: down_back_kernel(len(blocks), *refs),
        grid=(hidden // tile,),
        out_shape=pltpu.HBM((rows, hidden), F32),
        in_specs=[pl.BlockSpec(block.shape, lambda j: (0, 0)) for block in blocks]
        + [pl.BlockSpec((1, width, tile), lambda j: (2, 0, j))],
        out_specs=pl.BlockSpec((rows, tile), lambda j: (0, j)),
        scratch_shapes=[pltpu.VMEM((rows, width), BF)],
        compiler_params=pltpu.CompilerParams(vmem_limit_bytes=24 << 20),
        cost_estimate=pl.CostEstimate(
            flops=2 * rows * width * hidden,
            bytes_accessed=2 * width * hidden,
            transcendentals=0,
        ),
        name="down_back",
    )(*blocks, weights)


def down_kernel(a_ref, b_ref, w_ref, y_ref):
    rows = a_ref.shape[1]
    for half, ref in enumerate((a_ref, b_ref)):
        y_ref[half * rows : (half + 1) * rows] = nt(ref[0], w_ref[0])


def down_forward(parts, weights):
    _, rows, hidden = parts[0].shape
    width = weights.shape[1]
    tile = FFN_TILE
    left = pl.BlockSpec((1, rows, hidden), lambda j: (2, 0, 0))
    total = pl.pallas_call(
        down_kernel,
        grid=(width // tile,),
        out_shape=jax.ShapeDtypeStruct((2 * rows, width), F32),
        in_specs=[left, left, pl.BlockSpec((1, tile, hidden), lambda j: (2, j, 0))],
        out_specs=pl.BlockSpec((2 * rows, tile), lambda j: (0, j)),
        compiler_params=pltpu.CompilerParams(vmem_limit_bytes=24 << 20),
        cost_estimate=pl.CostEstimate(
            flops=4 * rows * width * hidden,
            bytes_accessed=2 * width * hidden,
            transcendentals=0,
        ),
        name="down_forward",
    )(*parts, weights)
    return total[:rows], total[rows:]


def share_kernel(count, ids_ref, *refs):
    lefts, rights = refs[:count], refs[count : 2 * count]
    terms, (kept_ref, sent_ref) = refs[2 * count : -2], refs[-2:]
    half = kept_ref.shape[1]
    own = ids_ref[0] % 2 == 0
    column = 0
    for left, right in zip(lefts, rights):
        width = right.shape[1]
        part = tn(left[...], right[...]).astype(BF)
        at = slice(column, column + width)
        kept_ref[0, :, at] = jnp.where(own, part[:half], part[half:])
        sent_ref[0, :, at] = jnp.where(own, part[half:], part[:half])
        column += width
    if terms:
        tall = jnp.concatenate(
            [jnp.broadcast_to(term[...], (128, term.shape[1])) for term in terms], axis=0
        )
        part = jnp.transpose(tall).astype(BF)
        kept_ref[0, :, column:] = jnp.where(own, part[:half], part[half:])
        sent_ref[0, :, column:] = jnp.where(own, part[half:], part[:half])


def share_products(lefts, rights, terms):
    ctx_count = lax.axis_size("ctx")
    pairs = ctx_count // 2
    rows, width = lefts[0].shape
    height = width // ctx_count
    columns = sum(right.shape[1] for right in rights) + 128 * len(terms)

    def place(j, ids_ref):
        return (0, (ids_ref[0] // 2) ^ j)

    shape = jax.ShapeDtypeStruct((pairs, height, columns), BF)
    out = pl.BlockSpec((1, height, columns), lambda j, ids_ref: (j, 0, 0))
    return pl.pallas_call(
        lambda *refs: share_kernel(len(lefts), *refs),
        grid_spec=pltpu.PrefetchScalarGridSpec(
            num_scalar_prefetch=1,
            grid=(pairs,),
            in_specs=[pl.BlockSpec((rows, 2 * height), place) for _ in lefts]
            + [pl.BlockSpec(right.shape, lambda j, ids_ref: (0, 0)) for right in rights]
            + [pl.BlockSpec((1, 2 * height), place) for _ in terms],
            out_specs=(out, out),
        ),
        out_shape=(shape, shape),
        compiler_params=pltpu.CompilerParams(vmem_limit_bytes=24 << 20),
        cost_estimate=pl.CostEstimate(
            flops=2 * rows * width * columns,
            bytes_accessed=2 * (rows + columns) * width,
            transcendentals=0,
        ),
        name="share_terms" if terms else "share_products",
    )(jnp.stack(ids()), *lefts, *rights, *[term[None] for term in terms])


def share_start(lefts, rights, terms):
    pairs = lax.axis_size("ctx") // 2
    if (lefts[0].shape[1] // pairs) % 128:
        values = [tn(left, right) for left, right in zip(lefts, rights)]
        values += [jnp.broadcast_to(term[:, None], (term.shape[0], 128)) for term in terms]
        return [ctx_rows_sum(jnp.concatenate(values, axis=1))], values[0]
    kept, sent = share_products(lefts, rights, terms)
    got = swap(sent, "ctx", 1)
    parts = [kept[0], got[0]]
    for pair in range(1, pairs):
        part = (kept[pair].astype(F32) + got[pair].astype(F32)).astype(BF)
        parts.append(swap(part, "ctx", 2 * pair))
    return parts, sent


def share_finish(parts):
    total = parts[0].astype(F32)
    for part in parts[1:]:
        total = total + part.astype(F32)
    return total


def own_rows_of(values, height):
    index = lax.axis_index("ctx") * lax.axis_size("fsdp") + lax.axis_index("fsdp")
    return lax.dynamic_slice_in_dim(values, index * height, height, 0)


def feature_rows(values):
    count, plane = lax.axis_size("fsdp"), lax.axis_index("fsdp")
    values = by_feature(values)
    rows, width = values.shape
    width //= count
    out = []
    for away in range(count):
        part = lax.dynamic_slice(values, (0, (plane ^ away) * width), (rows, width))
        out.append(swap(part, "fsdp", away) if away else part)
    return out


def own_features(terms):
    ctx_count, fsdp_count = lax.axis_size("ctx"), lax.axis_size("fsdp")
    total = jnp.stack(terms)
    away = 1
    while away < fsdp_count:
        total = total + swap(total, "fsdp", away)
        away *= 2
    blocks = total.reshape(len(terms), ctx_count, fsdp_count, -1)
    own = lax.dynamic_index_in_dim(blocks, lax.axis_index("fsdp"), 2, keepdims=False)
    own = own.reshape(len(terms), -1)
    return [own[i] for i in range(len(terms))]


def layer(
    hidden_in,
    out_grad,
    positions,
    block_order,
    attn_gain,
    ffn_gain,
    qkv_weight,
    out_weight,
    ffn_weight,
):
    ctx_count, fsdp_count = lax.axis_size("ctx"), lax.axis_size("fsdp")
    me, _ = ids()
    rows = hidden_in.shape[1]
    queries_width, kv_width = H * HD, KV * HD
    ffn_parts = in_hbm(ffn_weight.transpose(1, 0, 2))

    frequency = jnp.power(ROPE_BASE, -(jnp.arange(HD // 2, dtype=F32) * 2.0 / HD))
    angles = positions[0].astype(F32)[:, None] * frequency[None, :]
    cosine = jnp.tile(jnp.cos(angles), (1, 4))
    sine = jnp.tile(jnp.concatenate([-jnp.sin(angles), jnp.sin(angles)], axis=1), (1, 2))
    own_anchor = anchors_of(block_order, me, rows)[None]
    key_anchor = jnp.concatenate(
        [anchors_of(block_order, me ^ offset, rows) for offset in key_offsets()]
    )
    key_anchor = jnp.broadcast_to(key_anchor[:, None], (rows * ctx_count, 128))

    inputs = hidden_in[0].astype(F32)
    grad_in = out_grad[0]
    scale_one = norm_scale(inputs)
    normed_one = (inputs * scale_one * attn_gain).astype(BF)

    fast = ctx_count == 8 and (qkv_weight.shape[1] // ctx_count) % 128 == 0
    if fast:
        early = (cosine, sine, own_anchor, key_anchor)
        qkv_pieces, marks = gather_pieces(qkv_weight, early)
        out_blocks = gather_blocks(out_weight, *marks)
        queries, pair, qkv_full = pieces_forward(
            normed_one, qkv_weight, qkv_pieces, cosine, sine
        )
    else:
        marks = (normed_one, normed_one)
        out_blocks = gather_blocks(out_weight, *marks)
        qkv_full = whole_of(qkv_weight, gather_blocks(qkv_weight, normed_one, normed_one))
        projected = nn(normed_one, qkv_full)
        turned = rotate(
            projected[:, : queries_width + kv_width].reshape(rows, H + KV, HD), positions[0]
        ).reshape(rows, queries_width + kv_width)
        queries = (turned[:, :queries_width] * (1.0 / math.sqrt(HD))).astype(BF)
        pair = jnp.concatenate(
            [turned[:, queries_width:], projected[:, queries_width + kv_width :]], axis=1
        ).astype(BF)
    own_one = columns_to_owner(by_feature(after(normed_one, pair)))
    keys_values = gather_keys(pair)
    rows_out = fetch_rows(after(grad_in, marks[0]))
    attn_rows, attended, logs = attend(queries, keys_values, key_anchor, own_anchor)
    residual, normed_two = out_forward(
        attn_rows, out_weight, out_blocks, hidden_in[0], ffn_gain
    )
    scale_two = norm_scale(residual)
    rows_in = pass_rows(normed_two)
    rows_out = after(rows_out, normed_two)
    act_grad = down_back(rows_out, ffn_parts)

    all_attn = lax.all_gather(after(attn_rows, rows_in[2]), "fsdp", tiled=True)
    middle = []
    half = fsdp_count // 2
    for index in range(2):
        blocks = rows_in[index * half : (index + 1) * half]
        middle.append(ffn_middle(blocks, act_grad, index, ffn_parts))
    parts, partial = [m[0] for m in middle], [m[1] for m in middle]
    sum_grad = sum_rows(partial)
    products = ffn_products(rows_in, rows_out, parts).transpose(1, 0, 2)
    ffn_weight_grad = lax.psum_scatter(products, "ctx", scatter_dimension=0, tiled=True)
    ffn_weight_grad = ffn_weight_grad.astype(F32)
    out_partial = down_forward(parts, ffn_parts)

    unit_two = residual * scale_two
    ffn_gain_term = jnp.sum(sum_grad * unit_two, axis=0)
    scaled_two = ffn_gain * sum_grad
    residual_grad = grad_in.astype(F32) + scale_two * (
        scaled_two - unit_two * jnp.mean(scaled_two * unit_two, axis=-1, keepdims=True)
    )
    residual_bf = residual_grad.astype(BF)
    out_sum = sum_rows([after(part, residual_bf) for part in out_partial])
    output = (residual + out_sum).astype(BF)
    (ffn_term,) = own_features([ffn_gain_term])
    attn_grad = out_back(residual_bf, out_weight, out_blocks)
    query_part, kept, sent = attend_back(
        queries, attn_grad, attended, keys_values, key_anchor, own_anchor, logs, cosine, sine
    )
    query_planes = pass_rows(query_part)
    pair_part = sum_pairs(kept, sent, cosine, sine)
    own_residual = by_offset(feature_rows(after(residual_bf, sent)))
    all_pair = gather_planes(pair_part)
    input_grad = one_back(
        query_part, pair_part, qkv_full, hidden_in[0], attn_gain, residual_grad
    )
    last_sums, last_sent = share_start([own_one], [all_pair], [ffn_term])
    all_query = by_offset(after(query_planes, last_sent))
    first_sums, _ = share_start(
        [own_residual, own_one], [after(all_attn, last_sent), all_query], []
    )
    last_sums = share_finish(last_sums)
    first_sums = share_finish(after(first_sums, last_sums))

    pairs_width = 2 * kv_width
    out_weight_grad = first_sums[:, :queries_width]
    qkv_grad = jnp.concatenate(
        [first_sums[:, queries_width:], last_sums[:, :pairs_width]], axis=1
    )
    features = own_rows_of(attn_gain, qkv_grad.shape[0])
    gain_grad = jnp.sum(own_rows_of(qkv_full, qkv_grad.shape[0]).astype(F32) * qkv_grad, axis=1)
    return (
        output[None],
        input_grad[None],
        qkv_grad,
        out_weight_grad,
        ffn_weight_grad,
        gain_grad / features,
        last_sums[:, pairs_width],
    )


def solution(mesh):
    step = sharded(mesh)
    return step


def sharded(mesh):
    return jax.shard_map(
        layer,
        mesh=mesh,
        in_specs=(
            P("fsdp", "ctx", None),
            P("fsdp", "ctx", None),
            P("fsdp", "ctx"),
            P(),
            P(),
            P(),
            P("fsdp", None),
            P("fsdp", None),
            P(None, None, "fsdp"),
        ),
        out_specs=(
            P("fsdp", "ctx", None),
            P("fsdp", "ctx", None),
            P(("ctx", "fsdp"), None),
            P(("ctx", "fsdp"), None),
            P("ctx", None, "fsdp"),
            P(("ctx", "fsdp")),
            P(("ctx", "fsdp")),
        ),
        check_vma=False,
    )
```

```python
import math

import jax
import jax.numpy as jnp
from jax import lax
from jax.experimental import pallas as pl
from jax.experimental.pallas import tpu as pltpu
from jax.sharding import PartitionSpec as P


H = 32
KV = 8
HD = 64

NORM_EPS = 1e-05
ROPE_BASE = 500000.0
FFN_TILE = 512
KEY_CHUNK = 256


BF = jnp.bfloat16
F32 = jnp.float32


def mm(a, b, dims):
    return lax.dot_general(a, b, (dims, ((), ())), preferred_element_type=F32)


def nn(a, b):
    return mm(a, b, ((1,), (0,)))


def nt(a, b):
    return mm(a, b, ((1,), (1,)))


def tn(a, b):
    return mm(a, b, ((0,), (0,)))


def swap(value, axis, offset):
    count = lax.axis_size(axis)
    return lax.ppermute(value, axis, [(i, i ^ offset) for i in range(count)])


def rotate(values, token_places):
    head_dim = values.shape[-1]
    half_dim = head_dim // 2
    frequency = jnp.power(ROPE_BASE, -(jnp.arange(half_dim, dtype=F32) * 2.0 / head_dim))
    angles = token_places.astype(F32)[:, None] * frequency[None, :]
    cosine = jnp.concatenate([jnp.cos(angles), jnp.cos(angles)], axis=-1)[:, None, :]
    sine_part = jnp.concatenate([jnp.sin(angles), jnp.sin(angles)], axis=-1)[:, None, :]
    turned = jnp.concatenate([-values[..., half_dim:], values[..., :half_dim]], axis=-1)
    return values * cosine + turned * sine_part


def norm_scale(values):
    return lax.rsqrt(jnp.mean(values * values, axis=-1, keepdims=True) + NORM_EPS)


def lookup(entries, row_ids):
    matches = row_ids[:, None] == jnp.arange(entries.shape[0], dtype=jnp.int32)[None, :]
    return jnp.sum(jnp.where(matches, entries[None, :], 0), axis=1)


def anchors_of(block_order, owner, row_count):
    block_len = row_count // 2
    row_ids = owner * row_count + jnp.arange(row_count, dtype=jnp.int32)
    return lookup(block_order, row_ids // block_len) * block_len + row_ids % block_len


def after(value, *earlier):
    return lax.optimization_barrier((value, earlier))[0]


def ids():
    return lax.axis_index("ctx"), lax.axis_index("fsdp")


def gather_pieces(weight, early):
    rows, columns = weight.shape
    share = columns // lax.axis_size("ctx")
    half = rows // 2
    mine = lax.dynamic_slice(weight, (0, lax.axis_index("ctx") * share), (rows, share))
    planes = {}
    planes[3] = swap(mine, "fsdp", 3)
    planes[1] = swap(mine, "fsdp", 1)
    planes[2] = swap(after(planes[3], early), "fsdp", 1)
    pieces = []
    for away in (1, 3, 2):
        first = planes[away]
        along_x, along_y = swap(first, "ctx", 2), swap(first, "ctx", 4)
        top, low = swap(along_y[:half], "ctx", 2), swap(along_x[half:], "ctx", 4)
        parts = [(0, 0, first), (2, 0, along_x), (4, 0, along_y), (6, 0, top), (6, half, low)]
        for offset, start, part in parts:
            pieces.append((away, offset, start, part))
            pieces.append((away, offset + 1, start, swap(part, "ctx", 1)))
    return pieces, (planes[2], (pieces[-4][3], pieces[-2][3]))


def pieces_kernel(places, rows_in, share, ids_ref, x_ref, own_ref, *refs):
    count = len(places)
    piece_refs, refs = refs[:count], refs[count:]
    cos_ref, sin_ref, q_ref, pair_ref, full_ref, y_ref, buf, in_sems, out_sems = refs
    me, plane = ids_ref[0], ids_ref[1]

    def block(away):
        return pl.ds(pl.multiple_of((plane ^ away) * rows_in, 128), rows_in)

    own_copy = pltpu.make_async_copy(own_ref, buf.at[block(0)], in_sems.at[count])
    own_copy.start()
    copies = []
    for i, (away, offset, start, height) in enumerate(places):
        at = pl.ds(pl.multiple_of((plane ^ away) * rows_in + start, 128), height)
        columns = pl.ds(pl.multiple_of((me ^ offset) * share, 128), share)
        copies.append(pltpu.make_async_copy(piece_refs[i], buf.at[at, columns], in_sems.at[i]))
        copies[-1].start()
    outs = []
    order = [0] + list(dict.fromkeys(away for away, _, _, _ in places))
    for away in order:
        if away:
            for copy, place in zip(copies, places):
                if place[0] == away:
                    copy.wait()
        else:
            own_copy.wait()
        outs.append(
            pltpu.make_async_copy(buf.at[block(away)], full_ref.at[block(away)], out_sems.at[away])
        )
        outs[-1].start()
        part = nn(x_ref[:, block(away)], buf[block(away)])
        y_ref[...] = part if away == 0 else y_ref[...] + part
    cosine, sine = cos_ref[...], sin_ref[...]
    queries, keys = H * HD, KV * HD
    for start in range(0, queries + keys, 128):
        tile = turn(y_ref[:, start : start + 128], cosine, sine)
        if start < queries:
            q_ref[:, start : start + 128] = (tile * (1.0 / math.sqrt(HD))).astype(BF)
        else:
            pair_ref[:, start - queries : start - queries + 128] = tile.astype(BF)
    pair_ref[:, keys:] = y_ref[:, queries + keys :].astype(BF)
    for copy in outs:
        copy.wait()


def pieces_forward(x, own, pieces, cosine, sine):
    me, plane = ids()
    rows_in, columns = own.shape
    rows, width = x.shape
    share = columns // lax.axis_size("ctx")
    places = tuple((away, offset, start, part.shape[0]) for away, offset, start, part in pieces)
    arrays = [part for _, _, _, part in pieces]
    hbm, vmem = pl.BlockSpec(memory_space=pltpu.HBM), pl.BlockSpec(memory_space=pltpu.VMEM)
    return pl.pallas_call(
        lambda *refs: pieces_kernel(places, rows_in, share, *refs),
        out_shape=(
            jax.ShapeDtypeStruct((rows, H * HD), BF),
            jax.ShapeDtypeStruct((rows, 2 * KV * HD), BF),
            pltpu.HBM((width, columns), BF),
        ),
        in_specs=[pl.BlockSpec(memory_space=pltpu.SMEM), vmem, hbm]
        + [hbm] * len(arrays)
        + [vmem, vmem],
        out_specs=(vmem, vmem, hbm),
        scratch_shapes=[
            pltpu.VMEM((rows, columns), F32),
            pltpu.VMEM((width, columns), BF),
            pltpu.SemaphoreType.DMA((len(arrays) + 1,)),
            pltpu.SemaphoreType.DMA((width // rows_in,)),
        ],
        compiler_params=pltpu.CompilerParams(vmem_limit_bytes=32 << 20),
        cost_estimate=pl.CostEstimate(
            flops=2 * rows * width * columns, bytes_accessed=4 * width * columns, transcendentals=0
        ),
        name="pieces_forward",
    )(jnp.stack([me, plane]), x, in_hbm(own), *[in_hbm(part) for part in arrays], cosine, sine)


def gather_blocks(weight, before_fsdp, before_ctx):
    rows, columns = weight.shape
    me, plane = ids()
    share = columns // lax.axis_size("ctx")
    mine = lax.dynamic_slice(weight, (0, me * share), (rows, share))
    planes = lax.all_gather(after(mine, before_fsdp), "fsdp")
    others = jnp.stack(
        [
            lax.dynamic_index_in_dim(planes, plane ^ away, 0, keepdims=False)
            for away in range(1, planes.shape[0])
        ]
    )
    return lax.all_gather(after(others, before_ctx), "ctx")


def whole_of(own, blocks):
    ctx_count, others, rows, share = blocks.shape
    plane = lax.axis_index("fsdp")
    columns = ctx_count * share
    full = jnp.zeros(((others + 1) * rows, columns), own.dtype)
    full = lax.dynamic_update_slice(full, own, (plane * rows, 0))
    for away in range(1, others + 1):
        part = blocks[:, away - 1].transpose(1, 0, 2).reshape(rows, columns)
        full = lax.dynamic_update_slice(full, part, ((plane ^ away) * rows, 0))
    return full


def in_hbm(value):
    return pltpu.with_memory_space_constraint(value, pltpu.HBM)


def out_kernel(back, ids_ref, x_ref, own_ref, blocks_ref, *refs):
    hidden_ref, gain_ref = (None, None) if back else refs[:2]
    outs = refs if back else refs[2:]
    own_buf, buf, sems = outs[-3:]
    ctx_count, others, rows, share = buf.shape
    plane = ids_ref[1]
    copies = [pltpu.make_async_copy(own_ref, own_buf, sems.at[ctx_count])]
    for c in range(ctx_count):
        copies.append(pltpu.make_async_copy(blocks_ref.at[c], buf.at[c], sems.at[c]))
    for copy in copies:
        copy.start()

    def features(away):
        return pl.ds(pl.multiple_of((plane ^ away) * rows, 128), rows)

    copies[0].wait()
    if back:
        y_ref = outs[0]
        own_part = nn(x_ref[:, features(0)], own_buf[...])
        for c in range(ctx_count):
            copies[c + 1].wait()
            at = slice(c * share, (c + 1) * share)
            total = own_part[:, at]
            for away in range(1, others + 1):
                total += nn(x_ref[:, features(away)], buf[c, away - 1])
            y_ref[:, at] = total.astype(BF)
        return
    residual_ref, normed_ref = outs[:2]
    residual_ref[...] = hidden_ref[...].astype(F32)
    residual_ref[:, features(0)] += nt(x_ref[...], own_buf[...])
    for c in range(ctx_count):
        copies[c + 1].wait()
        x = x_ref[:, c * share : (c + 1) * share]
        for away in range(1, others + 1):
            residual_ref[:, features(away)] += nt(x, buf[c, away - 1])
    residual = residual_ref[...]
    normed_ref[...] = (residual * norm_scale(residual) * gain_ref[...]).astype(BF)


def out_call(back, x, own, blocks, extra, out_shape):
    vmem, hbm = pl.BlockSpec(memory_space=pltpu.VMEM), pl.BlockSpec(memory_space=pltpu.HBM)
    return pl.pallas_call(
        lambda *refs: out_kernel(back, *refs),
        out_shape=out_shape,
        in_specs=[pl.BlockSpec(memory_space=pltpu.SMEM), vmem, hbm, hbm] + [vmem] * len(extra),
        out_specs=jax.tree.map(lambda _: vmem, out_shape),
        scratch_shapes=[
            pltpu.VMEM(own.shape, own.dtype),
            pltpu.VMEM(blocks.shape, blocks.dtype),
            pltpu.SemaphoreType.DMA((blocks.shape[0] + 1,)),
        ],
        compiler_params=pltpu.CompilerParams(vmem_limit_bytes=24 << 20),
        cost_estimate=pl.CostEstimate(
            flops=2 * x.shape[0] * own.size * (blocks.shape[1] + 1),
            bytes_accessed=2 * own.size * (blocks.shape[1] + 1),
            transcendentals=0,
        ),
        name="out_back" if back else "out_forward",
    )(jnp.stack(ids()), x, in_hbm(own), in_hbm(blocks), *extra)


def out_forward(attn_rows, own, blocks, hidden, gain):
    if blocks.shape[3] % 128:
        residual = hidden.astype(F32) + nt(attn_rows, whole_of(own, blocks))
        return residual, (residual * norm_scale(residual) * gain).astype(BF)
    out_shape = (
        jax.ShapeDtypeStruct(hidden.shape, F32),
        jax.ShapeDtypeStruct(hidden.shape, BF),
    )
    return out_call(False, attn_rows, own, blocks, [hidden, gain[None]], out_shape)


def out_back(x, own, blocks):
    if blocks.shape[3] % 128:
        return nn(x, whole_of(own, blocks)).astype(BF)
    out_shape = jax.ShapeDtypeStruct((x.shape[0], own.shape[1]), BF)
    return out_call(True, x, own, blocks, [], out_shape)


def one_back_kernel(
    query_ref, pair_ref, w_ref, hidden_ref, gain_ref, residual_ref, y_ref
):
    step = pl.program_id(0)
    rows = w_ref.shape[0]
    split = query_ref.shape[1]
    y_ref[:, pl.ds(pl.multiple_of(step * rows, 128), rows)] = nt(
        query_ref[...], w_ref[:, :split]
    ) + nt(pair_ref[...], w_ref[:, split:])

    @pl.when(step == pl.num_programs(0) - 1)
    def _():
        grad = y_ref[...]
        inputs = hidden_ref[...].astype(F32)
        scale = norm_scale(inputs)
        unit = inputs * scale
        scaled = gain_ref[...] * grad
        y_ref[...] = residual_ref[...] + scale * (
            scaled - unit * jnp.mean(scaled * unit, axis=-1, keepdims=True)
        )


def one_back(query_part, pair_part, weight, hidden, gain, residual_grad):
    rows, width = hidden.shape
    columns = weight.shape[1]
    tile = FFN_TILE

    def whole(array):
        return pl.BlockSpec(array.shape, lambda j: (0, 0))

    gain = gain[None]
    return pl.pallas_call(
        one_back_kernel,
        grid=(width // tile,),
        out_shape=jax.ShapeDtypeStruct((rows, width), F32),
        in_specs=[
            whole(query_part),
            whole(pair_part),
            pl.BlockSpec((tile, columns), lambda j: (j, 0)),
            whole(hidden),
            whole(gain),
            whole(residual_grad),
        ],
        out_specs=pl.BlockSpec((rows, width), lambda j: (0, 0)),
        compiler_params=pltpu.CompilerParams(vmem_limit_bytes=24 << 20),
        cost_estimate=pl.CostEstimate(
            flops=2 * rows * width * columns,
            bytes_accessed=2 * width * columns,
            transcendentals=0,
        ),
        name="one_back",
    )(query_part, pair_part, in_hbm(weight), hidden, gain, residual_grad)


def pass_rows(values):
    if lax.axis_size("fsdp") != 4:
        return fetch_rows(values)
    third = swap(values, "fsdp", 3)
    first = swap(values, "fsdp", 1)
    second = swap(third, "fsdp", 1)
    return [values, first, second, third]


def fetch_rows(values):
    count = lax.axis_size("fsdp")
    return [values] + [swap(values, "fsdp", away) for away in range(1, count)]


def sum_rows(halves, forward):
    count = lax.axis_size("fsdp")
    half = count // 2
    rows = halves[0].shape[0] // half
    parts = [
        halves[away // half][away % half * rows : (away % half + 1) * rows] for away in range(count)
    ]
    if count == 4 and forward:
        passed = swap(parts[2].astype(BF), "fsdp", 1).astype(F32)
        one = swap(parts[1].astype(BF), "fsdp", 1).astype(F32)
        third = swap((parts[3] + passed).astype(BF), "fsdp", 3).astype(F32)
        return parts[0] + one + third
    total = parts[0]
    for away in range(1, count):
        total = total + swap(parts[away].astype(BF), "fsdp", away).astype(F32)
    return total


def by_feature(values):
    rows, width = values.shape
    ctx_count, fsdp_count = lax.axis_size("ctx"), lax.axis_size("fsdp")
    blocks = values.reshape(rows, ctx_count, fsdp_count, width // (ctx_count * fsdp_count))
    return blocks.transpose(0, 2, 1, 3).reshape(rows, width)


def gather_planes(values):
    count = lax.axis_size("fsdp")
    rows, columns = values.shape
    copies = jnp.broadcast_to(values[None], (count, rows, columns)).reshape(count * rows, columns)
    return lax.all_to_all(copies, "fsdp", split_axis=0, concat_axis=0, tiled=True)


def sum_over_ctx(part_for):
    pairs = lax.axis_size("ctx") // 2
    sent = jnp.stack([part_for(2 * pair + 1).astype(BF) for pair in range(pairs)])
    got = swap(sent, "ctx", 1)
    sums = [part_for(2 * pair).astype(F32) + got[pair].astype(F32) for pair in range(pairs)]
    total = sums[0]
    for pair in range(1, pairs):
        total = total + swap(sums[pair].astype(BF), "ctx", 2 * pair).astype(F32)
    return total


def ctx_rows_sum(values):
    height = values.shape[0] // lax.axis_size("ctx")
    me = lax.axis_index("ctx")

    def part(offset):
        return lax.dynamic_slice(
            values, ((me ^ offset) * height, 0), (height, values.shape[1])
        )

    return sum_over_ctx(part)


def key_offsets():
    count = lax.axis_size("ctx")
    return list(range(0, count, 2)) + list(range(1, count, 2))


def gather_keys(piece):
    same = [piece] + [swap(piece, "ctx", far) for far in range(2, lax.axis_size("ctx"), 2)]
    mine = jnp.concatenate(same, axis=0)
    return mine, swap(mine, "ctx", 1)


def sum_pairs(kept, sent, cosine, sine):
    _, count, width = kept.shape
    pairs = lax.axis_size("ctx") // 2
    got = swap(sent, "ctx", 1)
    sums = (kept.astype(F32) + got.astype(F32)).reshape(2, pairs, count // pairs, width)
    far = [swap(sums[:, pair].astype(BF), "ctx", 2 * pair) for pair in range(1, pairs)]
    return pair_turn(sums[:, 0], far, cosine, sine), far[0]


def half_mask(shape):
    return lax.broadcasted_iota(jnp.int32, shape, len(shape) - 1) % 128 < HD


def turn(values, cosine, sine):
    lanes = lax.broadcasted_iota(jnp.int32, values.shape, 1) % HD
    turned = jnp.where(
        lanes < HD // 2, pltpu.roll(values, 128 - HD // 2, 1), pltpu.roll(values, HD // 2, 1)
    )
    return values * cosine + turned * sine


def doubled(tile, odd):
    wide = tile.astype(F32)
    other = pltpu.roll(wide, HD, 1)
    return jnp.where(half_mask(tile.shape) == (odd == 0), wide, other).astype(BF)


def split_heads(tile_pair):
    zero = jnp.zeros((), tile_pair.dtype)
    parts = []
    for j in range(2):
        tile = tile_pair[:, j * 128 : (j + 1) * 128]
        mask = half_mask(tile.shape)
        parts += [jnp.where(mask, tile, zero), jnp.where(mask, zero, tile)]
    return jnp.concatenate(parts, axis=0)


def merge_heads(stacked):
    rows = stacked.shape[0] // 4
    tiles = []
    for j in range(2):
        even = stacked[2 * j * rows : (2 * j + 1) * rows]
        odd = stacked[(2 * j + 1) * rows : (2 * j + 2) * rows]
        tiles.append(jnp.where(half_mask(even.shape), even, odd))
    return jnp.concatenate(tiles, axis=1)


def key_chunks(refs, chunk):
    first = 0
    for k_ref, v_ref in refs:
        for start in range(0, k_ref.shape[0], chunk):
            at = slice(start, start + chunk)
            yield first + start, k_ref.at[at, :], v_ref.at[at, :]
        first += k_ref.shape[0]


def masked_scores(keys, queries, key_ref, own_ref, start):
    allowed = key_ref[start : start + keys.shape[0], :1] <= own_ref[...]
    bias = jnp.where(allowed, 0.0, -1e30).astype(F32)
    return nt(keys, queries) + jnp.concatenate([bias] * 4, axis=1)


def attend_kernel(
    chunk, q_ref, ka_ref, va_ref, kb_ref, vb_ref, key_ref, own_ref, rows_ref, attended_ref, log_ref
):
    odd = pl.program_id(0) % 2
    rows = q_ref.shape[0]
    queries = split_heads(q_ref[...])
    parts = list(key_chunks(((ka_ref, va_ref), (kb_ref, vb_ref)), chunk))
    scores = [
        masked_scores(doubled(k_ref[...], odd), queries, key_ref, own_ref, start)
        for start, k_ref, _ in parts
    ]
    top = jnp.max(scores[0], axis=0, keepdims=True)
    for score in scores[1:]:
        top = jnp.maximum(top, jnp.max(score, axis=0, keepdims=True))
    total = jnp.zeros_like(top)
    summed = jnp.zeros((4 * rows, 128), F32)
    for score, (_, _, v_ref) in zip(scores, parts):
        weights = jnp.exp(score - top)
        total += jnp.sum(weights, axis=0, keepdims=True)
        summed += tn(weights.astype(BF), doubled(v_ref[...], odd))
    log_ref[0] = top + jnp.log(total)
    attended = merge_heads(summed / jnp.transpose(jnp.broadcast_to(total, (128, 4 * rows))))
    attended_ref[...] = attended
    rows_ref[...] = attended.astype(BF)


def key_specs(parts):
    tiles = parts[0].shape[1] // 256
    specs, arrays = [], []
    for part in parts:
        specs.append(pl.BlockSpec((part.shape[0], 128), lambda g: (0, g // 2)))
        specs.append(pl.BlockSpec((part.shape[0], 128), lambda g: (0, tiles + g // 2)))
        arrays += [part, part]
    return specs, arrays


def attend(queries, keys_values, key_anchor, own_anchor):
    rows, width = queries.shape
    count = key_anchor.shape[0]
    specs, arrays = key_specs(keys_values)
    wide = pl.BlockSpec((rows, 256), lambda g: (0, g))
    return pl.pallas_call(
        lambda *refs: attend_kernel(KEY_CHUNK, *refs),
        grid=(KV,),
        out_shape=(
            jax.ShapeDtypeStruct((rows, width), BF),
            jax.ShapeDtypeStruct((rows, width), F32),
            jax.ShapeDtypeStruct((KV, 1, 4 * rows), F32),
        ),
        in_specs=[wide]
        + specs
        + [
            pl.BlockSpec((count, 128), lambda g: (0, 0)),
            pl.BlockSpec((1, rows), lambda g: (0, 0)),
        ],
        out_specs=(wide, wide, pl.BlockSpec((1, 1, 4 * rows), lambda g: (g, 0, 0))),
        compiler_params=pltpu.CompilerParams(vmem_limit_bytes=48 << 20),
        cost_estimate=pl.CostEstimate(
            flops=4 * rows * width * count,
            bytes_accessed=4 * count * KV * HD,
            transcendentals=rows * H * count,
        ),
        name="attend",
    )(queries, *arrays, key_anchor, own_anchor)


def attend_back_kernel(
    chunk, q_ref, grad_ref, attended_ref, ka_ref, va_ref, kb_ref, vb_ref, key_ref, own_ref, log_ref,
    cos_ref, sin_ref, dq_ref, kept_ref, sent_ref,
):
    odd = pl.program_id(0) % 2
    rows = q_ref.shape[0]
    half = ka_ref.shape[0]
    queries, grads = split_heads(q_ref[...]), split_heads(grad_ref[...])
    product = grads.astype(F32) * split_heads(attended_ref[...])
    delta = jnp.sum(jnp.transpose(product), axis=0, keepdims=True)
    log_total = log_ref[0]
    total = jnp.zeros((4 * rows, 128), F32)
    keep = half_mask((chunk, 128)) == (odd == 0)
    for start, k_ref, v_ref in key_chunks(((ka_ref, va_ref), (kb_ref, vb_ref)), chunk):
        keys, values = doubled(k_ref[...], odd), doubled(v_ref[...], odd)
        scores = masked_scores(keys, queries, key_ref, own_ref, start)
        probs = jnp.exp(scores - log_total)
        value_grad = nn(probs.astype(BF), grads)
        score_grad = (probs * (nt(values, grads) - delta)).astype(BF)
        key_grad = nn(score_grad, queries)
        total += tn(score_grad, keys)
        out_ref = kept_ref if start < half else sent_ref
        at = slice(start % half, start % half + chunk)
        for part, value in enumerate((key_grad, value_grad)):
            value = (value + pltpu.roll(value, HD, 1)).astype(BF)
            out_ref[part, at, :] = jnp.where(keep, value, out_ref[part, at, :])
    merged = merge_heads(total) * (1.0 / math.sqrt(HD))
    cosine, sine = cos_ref[...], sin_ref[...]
    for j in range(2):
        tile = slice(j * 128, (j + 1) * 128)
        dq_ref[:, tile] = turn(merged[:, tile], cosine, -sine).astype(BF)


def attend_back(queries, grads, attended, keys_values, key_anchor, own_anchor, logs, cosine, sine):
    rows, width = queries.shape
    count = key_anchor.shape[0]
    specs, arrays = key_specs(keys_values)
    wide = pl.BlockSpec((rows, 256), lambda g: (0, g))
    small = pl.BlockSpec((rows, 128), lambda g: (0, 0))
    pair = pl.BlockSpec((2, count // 2, 128), lambda g: (0, 0, g // 2))
    return pl.pallas_call(
        lambda *refs: attend_back_kernel(KEY_CHUNK, *refs),
        grid=(KV,),
        out_shape=(
            jax.ShapeDtypeStruct((rows, width), BF),
            jax.ShapeDtypeStruct((2, count // 2, KV * HD), BF),
            jax.ShapeDtypeStruct((2, count // 2, KV * HD), BF),
        ),
        in_specs=[wide, wide, wide]
        + specs
        + [
            pl.BlockSpec((count, 128), lambda g: (0, 0)),
            pl.BlockSpec((1, rows), lambda g: (0, 0)),
            pl.BlockSpec((1, 1, 4 * rows), lambda g: (g, 0, 0)),
            small,
            small,
        ],
        out_specs=(wide, pair, pair),
        compiler_params=pltpu.CompilerParams(vmem_limit_bytes=48 << 20),
        cost_estimate=pl.CostEstimate(
            flops=10 * rows * width * count,
            bytes_accessed=8 * count * KV * HD,
            transcendentals=rows * H * count,
        ),
        name="attend_back",
    )(queries, grads, attended, *arrays, key_anchor, own_anchor, logs, cosine, sine)


def pair_turn_kernel(own_ref, *refs):
    got, (cos_ref, sin_ref, y_ref) = refs[:-3], refs[-3:]
    total = own_ref[...]
    for ref in got:
        total = total + ref[...].astype(F32)
    cosine, sine = cos_ref[...], sin_ref[...]
    width = total.shape[2]
    for start in range(0, width, 128):
        tile = slice(start, start + 128)
        y_ref[:, tile] = turn(total[0, :, tile], cosine, -sine).astype(BF)
    y_ref[:, width:] = total[1].astype(BF)


def pair_turn(own, got, cosine, sine):
    _, rows, width = own.shape
    return pl.pallas_call(
        pair_turn_kernel,
        out_shape=jax.ShapeDtypeStruct((rows, 2 * width), BF),
        name="pair_turn",
    )(own, *got, cosine, sine)


def join_rows(x_buf, refs):
    @pl.when((pl.program_id(0) == 0))
    def _():
        rows = refs[0].shape[0]
        for i, ref in enumerate(refs):
            x_buf[i * rows : (i + 1) * rows] = ref[...]


def ffn_kernel(count, *refs):
    rows_refs, (act_ref, w_ref, out_ref, sum_ref, x_buf) = refs[:count], refs[count:]
    join_rows(x_buf, rows_refs)
    step = pl.program_id(0)
    gate_w, up_w = w_ref[0], w_ref[1]
    x = x_buf[...]
    gate, up = nn(x, gate_w), nn(x, up_w)
    act_grad = act_ref[...]
    sig = jax.nn.sigmoid(gate)
    silu = gate * sig
    gate_grad = (act_grad * up * sig * (1.0 + gate * (1.0 - sig))).astype(BF)
    up_grad = (act_grad * silu).astype(BF)
    out_ref[0], out_ref[1], out_ref[2] = gate_grad, up_grad, (silu * up).astype(BF)
    part = nt(gate_grad, gate_w) + nt(up_grad, up_w)

    @pl.when(step == 0)
    def _():
        sum_ref[...] = part

    @pl.when(step > 0)
    def _():
        sum_ref[...] += part


def ffn_middle(blocks, act_grad, half, weights):
    width = blocks[0].shape[1]
    rows = blocks[0].shape[0] * len(blocks)
    hidden = weights.shape[2]
    tile = FFN_TILE
    return pl.pallas_call(
        lambda *refs: ffn_kernel(len(blocks), *refs),
        grid=(hidden // tile,),
        out_shape=(
            pltpu.HBM((3, rows, hidden), BF),
            jax.ShapeDtypeStruct((rows, width), F32),
        ),
        in_specs=[pl.BlockSpec(block.shape, lambda j: (0, 0)) for block in blocks]
        + [
            pl.BlockSpec((rows, tile), lambda j: (half, j)),
            pl.BlockSpec((2, width, tile), lambda j: (0, 0, j)),
        ],
        out_specs=(
            pl.BlockSpec((3, rows, tile), lambda j: (0, 0, j)),
            pl.BlockSpec((rows, width), lambda j: (0, 0)),
        ),
        scratch_shapes=[pltpu.VMEM((rows, width), BF)],
        compiler_params=pltpu.CompilerParams(vmem_limit_bytes=40 << 20),
        cost_estimate=pl.CostEstimate(
            flops=8 * rows * width * hidden,
            bytes_accessed=4 * width * hidden,
            transcendentals=rows * hidden,
        ),
        name="ffn_middle",
    )(*blocks, act_grad, weights)


def products_kernel(count, *refs):
    in_refs, grad_refs = refs[:count], refs[count : 2 * count]
    right_a, right_b, out_ref = refs[2 * count :]
    half = count // 2

    def emit(lefts):
        left_a = jnp.concatenate([ref[...] for ref in lefts[:half]], axis=0)
        left_b = jnp.concatenate([ref[...] for ref in lefts[half:]], axis=0)
        out_ref[0] = (tn(left_a, right_a[0]) + tn(left_b, right_b[0])).astype(BF)

    @pl.when(pl.program_id(0) < 2)
    def _():
        emit(in_refs)

    @pl.when(pl.program_id(0) == 2)
    def _():
        emit(grad_refs)


def ffn_products(rows_in, rows_out, parts):
    count = len(rows_in)
    rows, width = rows_in[0].shape
    hidden = parts[0].shape[2]
    tile = FFN_TILE
    last = width // tile - 1
    left = pl.BlockSpec((rows, tile), lambda k, i: (0, jnp.where(k < 2, i, last)))
    grad = pl.BlockSpec((rows, tile), lambda k, i: (0, jnp.where(k == 2, i, 0)))
    right = pl.BlockSpec((1, rows * count // 2, hidden), lambda k, i: (k, 0, 0))
    return pl.pallas_call(
        lambda *refs: products_kernel(count, *refs),
        grid=(3, width // tile),
        out_shape=pltpu.HBM((3, width, hidden), BF),
        in_specs=[left] * count + [grad] * count + [right, right],
        out_specs=pl.BlockSpec((1, tile, hidden), lambda k, i: (k, i, 0)),
        compiler_params=pltpu.CompilerParams(vmem_limit_bytes=32 << 20),
        cost_estimate=pl.CostEstimate(
            flops=6 * count * rows * width * hidden,
            bytes_accessed=6 * width * hidden,
            transcendentals=0,
        ),
        name="ffn_products",
    )(*rows_in, *rows_out, *parts)


def down_back_kernel(count, *refs):
    rows_refs, (w_ref, y_ref, x_buf) = refs[:count], refs[count:]
    join_rows(x_buf, rows_refs)
    y_ref[...] = nn(x_buf[...], w_ref[0])


def down_back(blocks, weights):
    width = blocks[0].shape[1]
    rows = blocks[0].shape[0] * len(blocks)
    hidden = weights.shape[2]
    tile = FFN_TILE
    return pl.pallas_call(
        lambda *refs: down_back_kernel(len(blocks), *refs),
        grid=(hidden // tile,),
        out_shape=pltpu.HBM((rows, hidden), F32),
        in_specs=[pl.BlockSpec(block.shape, lambda j: (0, 0)) for block in blocks]
        + [pl.BlockSpec((1, width, tile), lambda j: (2, 0, j))],
        out_specs=pl.BlockSpec((rows, tile), lambda j: (0, j)),
        scratch_shapes=[pltpu.VMEM((rows, width), BF)],
        compiler_params=pltpu.CompilerParams(vmem_limit_bytes=24 << 20),
        cost_estimate=pl.CostEstimate(
            flops=2 * rows * width * hidden,
            bytes_accessed=2 * width * hidden,
            transcendentals=0,
        ),
        name="down_back",
    )(*blocks, weights)


def down_kernel(a_ref, b_ref, w_ref, y_ref):
    rows = a_ref.shape[1]
    for half, ref in enumerate((a_ref, b_ref)):
        y_ref[half * rows : (half + 1) * rows] = nt(ref[0], w_ref[0])


def down_forward(parts, weights):
    _, rows, hidden = parts[0].shape
    width = weights.shape[1]
    tile = FFN_TILE
    left = pl.BlockSpec((1, rows, hidden), lambda j: (2, 0, 0))
    total = pl.pallas_call(
        down_kernel,
        grid=(width // tile,),
        out_shape=jax.ShapeDtypeStruct((2 * rows, width), F32),
        in_specs=[left, left, pl.BlockSpec((1, tile, hidden), lambda j: (2, j, 0))],
        out_specs=pl.BlockSpec((2 * rows, tile), lambda j: (0, j)),
        compiler_params=pltpu.CompilerParams(vmem_limit_bytes=24 << 20),
        cost_estimate=pl.CostEstimate(
            flops=4 * rows * width * hidden,
            bytes_accessed=2 * width * hidden,
            transcendentals=0,
        ),
        name="down_forward",
    )(*parts, weights)
    return total[:rows], total[rows:]


def share_kernel(count, sizes, ids_ref, *refs):
    products = len(sizes)
    lefts = [refs[i * count : (i + 1) * count] for i in range(products)]
    rest = refs[products * count :]
    rights = []
    for size in sizes:
        rights.append(rest[:size])
        rest = rest[size:]
    bufs = rest[len(rest) - products :]
    terms, (kept_ref, sent_ref) = rest[: -products - 2], rest[-products - 2 : -products]
    half = kept_ref.shape[1]
    own = ids_ref[0] % 2 == 0

    @pl.when(pl.program_id(0) == 0)
    def _():
        for parts, buf in zip(rights, bufs):
            rows = buf.shape[0] // count
            for away in range(count):
                if len(parts) > 1:
                    block = parts[away][...]
                else:
                    start = (ids_ref[1] ^ away) * rows
                    block = parts[0][pl.ds(pl.multiple_of(start, 16), rows), :]
                buf[away * rows : (away + 1) * rows] = block

    def emit(part, column):
        at = slice(column, column + part.shape[1])
        kept_ref[0, :, at] = jnp.where(own, part[:half], part[half:])
        sent_ref[0, :, at] = jnp.where(own, part[half:], part[:half])

    column = 0
    for left, buf in zip(lefts, bufs):
        joined = jnp.concatenate([ref[...] for ref in left], axis=0)
        emit(tn(joined, buf[...]).astype(BF), column)
        column += buf.shape[1]
    for term in terms:
        tall = jnp.broadcast_to(term[...], (128, term.shape[1]))
        emit(jnp.transpose(tall).astype(BF), column)
        column += 128


def share_products(lefts, rights, terms):
    ctx_count = lax.axis_size("ctx")
    pairs = ctx_count // 2
    count = len(lefts[0])
    rows, width = lefts[0][0].shape
    height = width // ctx_count
    groups = [right if isinstance(right, list) else [right] for right in rights]
    widths = [group[0].shape[1] for group in groups]
    columns = sum(widths) + 128 * len(terms)

    def place(j, ids_ref):
        return (0, (ids_ref[0] // 2) ^ j)

    def whole(array):
        return pl.BlockSpec(array.shape, lambda j, ids_ref: (0, 0))

    shape = jax.ShapeDtypeStruct((pairs, height, columns), BF)
    out = pl.BlockSpec((1, height, columns), lambda j, ids_ref: (j, 0, 0))
    flat_lefts = [block for left in lefts for block in left]
    flat_rights = [block for group in groups for block in group]
    return pl.pallas_call(
        lambda *refs: share_kernel(count, [len(group) for group in groups], *refs),
        grid_spec=pltpu.PrefetchScalarGridSpec(
            num_scalar_prefetch=1,
            grid=(pairs,),
            in_specs=[pl.BlockSpec((rows, 2 * height), place) for _ in flat_lefts]
            + [whole(block) for block in flat_rights]
            + [pl.BlockSpec((1, 2 * height), place) for _ in terms],
            out_specs=(out, out),
            scratch_shapes=[pltpu.VMEM((count * rows, size), BF) for size in widths],
        ),
        out_shape=(shape, shape),
        compiler_params=pltpu.CompilerParams(vmem_limit_bytes=32 << 20),
        cost_estimate=pl.CostEstimate(
            flops=2 * count * rows * width * columns,
            bytes_accessed=2 * (count * rows + columns) * width,
            transcendentals=0,
        ),
        name="share_terms" if terms else "share_products",
    )(jnp.stack(ids()), *flat_lefts, *flat_rights, *[term[None] for term in terms])


def in_fsdp_order(value):
    if not isinstance(value, list):
        return value
    plane = lax.axis_index("fsdp")
    stacked = jnp.stack(value)
    parts = [
        lax.dynamic_index_in_dim(stacked, plane ^ away, 0, keepdims=False)
        for away in range(len(value))
    ]
    return jnp.concatenate(parts, axis=0)


def share_start(lefts, rights, terms):
    pairs = lax.axis_size("ctx") // 2
    if (lefts[0][0].shape[1] // pairs) % 128:
        values = [tn(in_fsdp_order(a), in_fsdp_order(b)) for a, b in zip(lefts, rights)]
        values += [jnp.broadcast_to(term[:, None], (term.shape[0], 128)) for term in terms]
        return [ctx_rows_sum(jnp.concatenate(values, axis=1))]
    kept, sent = share_products(lefts, rights, terms)
    got = swap(sent, "ctx", 1)
    parts = [kept[0], got[0]]
    for pair in range(1, pairs):
        part = (kept[pair].astype(F32) + got[pair].astype(F32)).astype(BF)
        parts.append(swap(part, "ctx", 2 * pair))
    return parts


def share_finish(parts):
    total = parts[0].astype(F32)
    for part in parts[1:]:
        total = total + part.astype(F32)
    return total


def own_rows_of(values, height):
    index = lax.axis_index("ctx") * lax.axis_size("fsdp") + lax.axis_index("fsdp")
    return lax.dynamic_slice_in_dim(values, index * height, height, 0)


def feature_rows(values):
    count, plane = lax.axis_size("fsdp"), lax.axis_index("fsdp")
    values = by_feature(values)
    rows, width = values.shape
    width //= count
    out = []
    for away in range(count):
        part = lax.dynamic_slice(values, (0, (plane ^ away) * width), (rows, width))
        out.append(swap(part, "fsdp", away) if away else part)
    return out


def own_features(terms):
    ctx_count, fsdp_count = lax.axis_size("ctx"), lax.axis_size("fsdp")
    total = jnp.stack(terms)
    away = 1
    while away < fsdp_count:
        total = total + swap(total, "fsdp", away)
        away *= 2
    blocks = total.reshape(len(terms), ctx_count, fsdp_count, -1)
    own = lax.dynamic_index_in_dim(blocks, lax.axis_index("fsdp"), 2, keepdims=False)
    own = own.reshape(len(terms), -1)
    return [own[i] for i in range(len(terms))]


def layer(
    hidden_in,
    out_grad,
    positions,
    block_order,
    attn_gain,
    ffn_gain,
    qkv_weight,
    out_weight,
    ffn_weight,
):
    ctx_count, fsdp_count = lax.axis_size("ctx"), lax.axis_size("fsdp")
    me, _ = ids()
    rows = hidden_in.shape[1]
    queries_width, kv_width = H * HD, KV * HD
    ffn_parts = in_hbm(ffn_weight.transpose(1, 0, 2))

    frequency = jnp.power(ROPE_BASE, -(jnp.arange(HD // 2, dtype=F32) * 2.0 / HD))
    angles = positions[0].astype(F32)[:, None] * frequency[None, :]
    cosine = jnp.tile(jnp.cos(angles), (1, 4))
    sine = jnp.tile(jnp.concatenate([-jnp.sin(angles), jnp.sin(angles)], axis=1), (1, 2))
    own_anchor = anchors_of(block_order, me, rows)[None]
    key_anchor = jnp.concatenate(
        [anchors_of(block_order, me ^ offset, rows) for offset in key_offsets()]
    )
    key_anchor = jnp.broadcast_to(key_anchor[:, None], (rows * ctx_count, 128))

    inputs = hidden_in[0].astype(F32)
    grad_in = out_grad[0]
    scale_one = norm_scale(inputs)
    normed_one = (inputs * scale_one * attn_gain).astype(BF)

    fast = ctx_count == 8 and (qkv_weight.shape[1] // ctx_count) % 128 == 0
    if fast:
        early = (cosine, sine, own_anchor, key_anchor)
        qkv_pieces, marks = gather_pieces(qkv_weight, early)
        out_blocks = gather_blocks(out_weight, *marks)
        queries, pair, qkv_full = pieces_forward(
            normed_one, qkv_weight, qkv_pieces, cosine, sine
        )
    else:
        marks = (normed_one, normed_one)
        out_blocks = gather_blocks(out_weight, *marks)
        qkv_full = whole_of(qkv_weight, gather_blocks(qkv_weight, normed_one, normed_one))
        projected = nn(normed_one, qkv_full)
        turned = rotate(
            projected[:, : queries_width + kv_width].reshape(rows, H + KV, HD), positions[0]
        ).reshape(rows, queries_width + kv_width)
        queries = (turned[:, :queries_width] * (1.0 / math.sqrt(HD))).astype(BF)
        pair = jnp.concatenate(
            [turned[:, queries_width:], projected[:, queries_width + kv_width :]], axis=1
        ).astype(BF)
    own_one = feature_rows(after(normed_one, marks[1]))
    keys_values = gather_keys(pair)
    rows_out = fetch_rows(after(grad_in, pair))
    attn_rows, attended, logs = attend(queries, keys_values, key_anchor, own_anchor)
    residual, normed_two = out_forward(
        attn_rows, out_weight, out_blocks, hidden_in[0], ffn_gain
    )
    scale_two = norm_scale(residual)
    rows_in = pass_rows(normed_two)
    rows_out = after(rows_out, normed_two)
    act_grad = down_back(rows_out, ffn_parts)

    all_attn = pass_rows(after(attn_rows, rows_in[2]))
    middle = []
    half = fsdp_count // 2
    for index in range(2):
        blocks = rows_in[index * half : (index + 1) * half]
        middle.append(ffn_middle(blocks, in_hbm(act_grad), index, ffn_parts))
    parts, partial = [m[0] for m in middle], [m[1] for m in middle]
    sum_grad = sum_rows(partial, True)
    products = ffn_products(rows_in, rows_out, parts).transpose(1, 0, 2)
    ffn_weight_grad = lax.psum_scatter(products, "ctx", scatter_dimension=0, tiled=True)
    ffn_weight_grad = ffn_weight_grad.astype(F32)
    out_partial = down_forward(parts, ffn_parts)

    unit_two = residual * scale_two
    ffn_gain_term = jnp.sum(sum_grad * unit_two, axis=0)
    scaled_two = ffn_gain * sum_grad
    residual_grad = grad_in.astype(F32) + scale_two * (
        scaled_two - unit_two * jnp.mean(scaled_two * unit_two, axis=-1, keepdims=True)
    )
    residual_bf = residual_grad.astype(BF)
    out_sum = sum_rows([after(part, residual_bf) for part in out_partial], False)
    output = (residual + out_sum).astype(BF)
    (ffn_term,) = own_features([ffn_gain_term])
    attn_grad = out_back(residual_bf, out_weight, out_blocks)
    query_part, kept, sent = attend_back(
        queries, attn_grad, attended, keys_values, key_anchor, own_anchor, logs, cosine, sine
    )
    query_planes = pass_rows(query_part)
    pair_part, far = sum_pairs(kept, sent, cosine, sine)
    own_residual = feature_rows(after(residual_bf, far))
    all_pair = gather_planes(pair_part)
    input_grad = one_back(
        query_part, pair_part, qkv_full, hidden_in[0], attn_gain, residual_grad
    )
    first_sums = share_start(
        [own_residual, own_one], [after(all_attn, input_grad), after(query_planes, input_grad)], []
    )
    last_sums = share_start([own_one], [all_pair], [ffn_term])
    last_sums = share_finish(last_sums)
    first_sums = share_finish(after(first_sums, last_sums))

    pairs_width = 2 * kv_width
    out_weight_grad = first_sums[:, :queries_width]
    qkv_grad = jnp.concatenate(
        [first_sums[:, queries_width:], last_sums[:, :pairs_width]], axis=1
    )
    features = own_rows_of(attn_gain, qkv_grad.shape[0])
    gain_grad = jnp.sum(own_rows_of(qkv_full, qkv_grad.shape[0]).astype(F32) * qkv_grad, axis=1)
    return (
        output[None],
        input_grad[None],
        qkv_grad,
        out_weight_grad,
        ffn_weight_grad,
        gain_grad / features,
        last_sums[:, pairs_width],
    )


def solution(mesh):
    step = sharded(mesh)
    return step


def sharded(mesh):
    return jax.shard_map(
        layer,
        mesh=mesh,
        in_specs=(
            P("fsdp", "ctx", None),
            P("fsdp", "ctx", None),
            P("fsdp", "ctx"),
            P(),
            P(),
            P(),
            P("fsdp", None),
            P("fsdp", None),
            P(None, None, "fsdp"),
        ),
        out_specs=(
            P("fsdp", "ctx", None),
            P("fsdp", "ctx", None),
            P(("ctx", "fsdp"), None),
            P(("ctx", "fsdp"), None),
            P("ctx", None, "fsdp"),
            P(("ctx", "fsdp")),
            P(("ctx", "fsdp")),
        ),
        check_vma=False,
    )
```

```python
import math

import jax
import jax.numpy as jnp
from jax import lax
from jax.experimental import pallas as pl
from jax.experimental.pallas import tpu as pltpu
from jax.sharding import PartitionSpec as P


H = 32
KV = 8
HD = 64

NORM_EPS = 1e-05
ROPE_BASE = 500000.0
FFN_TILE = 512
KEY_CHUNK = 256


BF = jnp.bfloat16
F32 = jnp.float32


def mm(a, b, dims):
    return lax.dot_general(a, b, (dims, ((), ())), preferred_element_type=F32)


def nn(a, b):
    return mm(a, b, ((1,), (0,)))


def nt(a, b):
    return mm(a, b, ((1,), (1,)))


def tn(a, b):
    return mm(a, b, ((0,), (0,)))


def swap(value, axis, offset):
    count = lax.axis_size(axis)
    return lax.ppermute(value, axis, [(i, i ^ offset) for i in range(count)])


def rotate(values, token_places):
    head_dim = values.shape[-1]
    half_dim = head_dim // 2
    frequency = jnp.power(ROPE_BASE, -(jnp.arange(half_dim, dtype=F32) * 2.0 / head_dim))
    angles = token_places.astype(F32)[:, None] * frequency[None, :]
    cosine = jnp.concatenate([jnp.cos(angles), jnp.cos(angles)], axis=-1)[:, None, :]
    sine_part = jnp.concatenate([jnp.sin(angles), jnp.sin(angles)], axis=-1)[:, None, :]
    turned = jnp.concatenate([-values[..., half_dim:], values[..., :half_dim]], axis=-1)
    return values * cosine + turned * sine_part


def norm_scale(values):
    return lax.rsqrt(jnp.mean(values * values, axis=-1, keepdims=True) + NORM_EPS)


def lookup(entries, row_ids):
    matches = row_ids[:, None] == jnp.arange(entries.shape[0], dtype=jnp.int32)[None, :]
    return jnp.sum(jnp.where(matches, entries[None, :], 0), axis=1)


def anchors_of(block_order, owner, row_count):
    block_len = row_count // 2
    row_ids = owner * row_count + jnp.arange(row_count, dtype=jnp.int32)
    return lookup(block_order, row_ids // block_len) * block_len + row_ids % block_len


def after(value, *earlier):
    return lax.optimization_barrier((value, earlier))[0]


def ids():
    return lax.axis_index("ctx"), lax.axis_index("fsdp")


def gather_pieces(weight, early):
    rows, columns = weight.shape
    share = columns // lax.axis_size("ctx")
    half = rows // 2
    mine = lax.dynamic_slice(weight, (0, lax.axis_index("ctx") * share), (rows, share))
    planes = {}
    planes[3] = swap(mine, "fsdp", 3)
    planes[1] = swap(mine, "fsdp", 1)
    planes[2] = swap(after(planes[3], early), "fsdp", 1)
    pieces = []
    for away in (1, 3, 2):
        first = planes[away]
        along_x, along_y = swap(first, "ctx", 2), swap(first, "ctx", 4)
        top, low = swap(along_y[:half], "ctx", 2), swap(along_x[half:], "ctx", 4)
        parts = [(0, 0, first), (2, 0, along_x), (4, 0, along_y), (6, 0, top), (6, half, low)]
        for offset, start, part in parts:
            pieces.append((away, offset, start, part))
            pieces.append((away, offset + 1, start, swap(part, "ctx", 1)))
    return pieces, (planes[2], (pieces[-4][3], pieces[-2][3]))


def pieces_kernel(places, rows_in, share, ids_ref, x_ref, own_ref, *refs):
    count = len(places)
    piece_refs, refs = refs[:count], refs[count:]
    cos_ref, sin_ref, q_ref, pair_ref, full_ref, y_ref, buf, in_sems, out_sems = refs
    me, plane = ids_ref[0], ids_ref[1]

    def block(away):
        return pl.ds(pl.multiple_of((plane ^ away) * rows_in, 128), rows_in)

    own_copy = pltpu.make_async_copy(own_ref, buf.at[block(0)], in_sems.at[count])
    own_copy.start()
    copies = []
    for i, (away, offset, start, height) in enumerate(places):
        at = pl.ds(pl.multiple_of((plane ^ away) * rows_in + start, 128), height)
        columns = pl.ds(pl.multiple_of((me ^ offset) * share, 128), share)
        copies.append(pltpu.make_async_copy(piece_refs[i], buf.at[at, columns], in_sems.at[i]))
        copies[-1].start()
    outs = []
    order = [0] + list(dict.fromkeys(away for away, _, _, _ in places))
    for away in order:
        if away:
            for copy, place in zip(copies, places):
                if place[0] == away:
                    copy.wait()
        else:
            own_copy.wait()
        outs.append(
            pltpu.make_async_copy(buf.at[block(away)], full_ref.at[block(away)], out_sems.at[away])
        )
        outs[-1].start()
        part = nn(x_ref[:, block(away)], buf[block(away)])
        y_ref[...] = part if away == 0 else y_ref[...] + part
    cosine, sine = cos_ref[...], sin_ref[...]
    queries, keys = H * HD, KV * HD
    for start in range(0, queries + keys, 128):
        tile = turn(y_ref[:, start : start + 128], cosine, sine)
        if start < queries:
            q_ref[:, start : start + 128] = (tile * (1.0 / math.sqrt(HD))).astype(BF)
        else:
            pair_ref[:, start - queries : start - queries + 128] = tile.astype(BF)
    pair_ref[:, keys:] = y_ref[:, queries + keys :].astype(BF)
    for copy in outs:
        copy.wait()


def pieces_forward(x, own, pieces, cosine, sine):
    me, plane = ids()
    rows_in, columns = own.shape
    rows, width = x.shape
    share = columns // lax.axis_size("ctx")
    places = tuple((away, offset, start, part.shape[0]) for away, offset, start, part in pieces)
    arrays = [part for _, _, _, part in pieces]
    hbm, vmem = pl.BlockSpec(memory_space=pltpu.HBM), pl.BlockSpec(memory_space=pltpu.VMEM)
    return pl.pallas_call(
        lambda *refs: pieces_kernel(places, rows_in, share, *refs),
        out_shape=(
            jax.ShapeDtypeStruct((rows, H * HD), BF),
            jax.ShapeDtypeStruct((rows, 2 * KV * HD), BF),
            pltpu.HBM((width, columns), BF),
        ),
        in_specs=[pl.BlockSpec(memory_space=pltpu.SMEM), vmem, hbm]
        + [hbm] * len(arrays)
        + [vmem, vmem],
        out_specs=(vmem, vmem, hbm),
        scratch_shapes=[
            pltpu.VMEM((rows, columns), F32),
            pltpu.VMEM((width, columns), BF),
            pltpu.SemaphoreType.DMA((len(arrays) + 1,)),
            pltpu.SemaphoreType.DMA((width // rows_in,)),
        ],
        compiler_params=pltpu.CompilerParams(vmem_limit_bytes=32 << 20),
        cost_estimate=pl.CostEstimate(
            flops=2 * rows * width * columns, bytes_accessed=4 * width * columns, transcendentals=0
        ),
        name="pieces_forward",
    )(jnp.stack([me, plane]), x, in_hbm(own), *[in_hbm(part) for part in arrays], cosine, sine)


def gather_blocks(weight, before_fsdp, before_ctx):
    rows, columns = weight.shape
    me, plane = ids()
    share = columns // lax.axis_size("ctx")
    mine = lax.dynamic_slice(weight, (0, me * share), (rows, share))
    planes = lax.all_gather(after(mine, before_fsdp), "fsdp")
    others = jnp.stack(
        [
            lax.dynamic_index_in_dim(planes, plane ^ away, 0, keepdims=False)
            for away in range(1, planes.shape[0])
        ]
    )
    return lax.all_gather(after(others, before_ctx), "ctx")


def whole_of(own, blocks):
    ctx_count, others, rows, share = blocks.shape
    plane = lax.axis_index("fsdp")
    columns = ctx_count * share
    full = jnp.zeros(((others + 1) * rows, columns), own.dtype)
    full = lax.dynamic_update_slice(full, own, (plane * rows, 0))
    for away in range(1, others + 1):
        part = blocks[:, away - 1].transpose(1, 0, 2).reshape(rows, columns)
        full = lax.dynamic_update_slice(full, part, ((plane ^ away) * rows, 0))
    return full


def in_hbm(value):
    return pltpu.with_memory_space_constraint(value, pltpu.HBM)


def out_kernel(back, ids_ref, x_ref, own_ref, blocks_ref, *refs):
    hidden_ref, gain_ref = (None, None) if back else refs[:2]
    outs = refs if back else refs[2:]
    own_buf, buf, sems = outs[-3:]
    ctx_count, others, rows, share = buf.shape
    plane = ids_ref[1]
    copies = [pltpu.make_async_copy(own_ref, own_buf, sems.at[ctx_count])]
    for c in range(ctx_count):
        copies.append(pltpu.make_async_copy(blocks_ref.at[c], buf.at[c], sems.at[c]))
    for copy in copies:
        copy.start()

    def features(away):
        return pl.ds(pl.multiple_of((plane ^ away) * rows, 128), rows)

    copies[0].wait()
    if back:
        y_ref = outs[0]
        own_part = nn(x_ref[:, features(0)], own_buf[...])
        for c in range(ctx_count):
            copies[c + 1].wait()
            at = slice(c * share, (c + 1) * share)
            total = own_part[:, at]
            for away in range(1, others + 1):
                total += nn(x_ref[:, features(away)], buf[c, away - 1])
            y_ref[:, at] = total.astype(BF)
        return
    residual_ref, normed_ref = outs[:2]
    residual_ref[...] = hidden_ref[...].astype(F32)
    residual_ref[:, features(0)] += nt(x_ref[...], own_buf[...])
    for c in range(ctx_count):
        copies[c + 1].wait()
        x = x_ref[:, c * share : (c + 1) * share]
        for away in range(1, others + 1):
            residual_ref[:, features(away)] += nt(x, buf[c, away - 1])
    residual = residual_ref[...]
    normed_ref[...] = (residual * norm_scale(residual) * gain_ref[...]).astype(BF)


def out_call(back, x, own, blocks, extra, out_shape):
    vmem, hbm = pl.BlockSpec(memory_space=pltpu.VMEM), pl.BlockSpec(memory_space=pltpu.HBM)
    return pl.pallas_call(
        lambda *refs: out_kernel(back, *refs),
        out_shape=out_shape,
        in_specs=[pl.BlockSpec(memory_space=pltpu.SMEM), vmem, hbm, hbm] + [vmem] * len(extra),
        out_specs=jax.tree.map(lambda _: vmem, out_shape),
        scratch_shapes=[
            pltpu.VMEM(own.shape, own.dtype),
            pltpu.VMEM(blocks.shape, blocks.dtype),
            pltpu.SemaphoreType.DMA((blocks.shape[0] + 1,)),
        ],
        compiler_params=pltpu.CompilerParams(vmem_limit_bytes=24 << 20),
        cost_estimate=pl.CostEstimate(
            flops=2 * x.shape[0] * own.size * (blocks.shape[1] + 1),
            bytes_accessed=2 * own.size * (blocks.shape[1] + 1),
            transcendentals=0,
        ),
        name="out_back" if back else "out_forward",
    )(jnp.stack(ids()), x, in_hbm(own), in_hbm(blocks), *extra)


def out_forward(attn_rows, own, blocks, hidden, gain):
    if blocks.shape[3] % 128:
        residual = hidden.astype(F32) + nt(attn_rows, whole_of(own, blocks))
        return residual, (residual * norm_scale(residual) * gain).astype(BF)
    out_shape = (
        jax.ShapeDtypeStruct(hidden.shape, F32),
        jax.ShapeDtypeStruct(hidden.shape, BF),
    )
    return out_call(False, attn_rows, own, blocks, [hidden, gain[None]], out_shape)


def out_back(x, own, blocks):
    if blocks.shape[3] % 128:
        return nn(x, whole_of(own, blocks)).astype(BF)
    out_shape = jax.ShapeDtypeStruct((x.shape[0], own.shape[1]), BF)
    return out_call(True, x, own, blocks, [], out_shape)


def one_back_kernel(
    query_ref, pair_ref, w_ref, hidden_ref, gain_ref, residual_ref, y_ref
):
    step = pl.program_id(0)
    rows = w_ref.shape[0]
    split = query_ref.shape[1]
    y_ref[:, pl.ds(pl.multiple_of(step * rows, 128), rows)] = nt(
        query_ref[...], w_ref[:, :split]
    ) + nt(pair_ref[...], w_ref[:, split:])

    @pl.when(step == pl.num_programs(0) - 1)
    def _():
        grad = y_ref[...]
        inputs = hidden_ref[...].astype(F32)
        scale = norm_scale(inputs)
        unit = inputs * scale
        scaled = gain_ref[...] * grad
        y_ref[...] = residual_ref[...] + scale * (
            scaled - unit * jnp.mean(scaled * unit, axis=-1, keepdims=True)
        )


def one_back(query_part, pair_part, weight, hidden, gain, residual_grad):
    rows, width = hidden.shape
    columns = weight.shape[1]
    tile = FFN_TILE

    def whole(array):
        return pl.BlockSpec(array.shape, lambda j: (0, 0))

    gain = gain[None]
    return pl.pallas_call(
        one_back_kernel,
        grid=(width // tile,),
        out_shape=jax.ShapeDtypeStruct((rows, width), F32),
        in_specs=[
            whole(query_part),
            pl.BlockSpec((rows, pair_part.shape[1]), lambda j: (0, 0)),
            pl.BlockSpec((tile, columns), lambda j: (j, 0)),
            whole(hidden),
            whole(gain),
            whole(residual_grad),
        ],
        out_specs=pl.BlockSpec((rows, width), lambda j: (0, 0)),
        compiler_params=pltpu.CompilerParams(vmem_limit_bytes=24 << 20),
        cost_estimate=pl.CostEstimate(
            flops=2 * rows * width * columns,
            bytes_accessed=2 * width * columns,
            transcendentals=0,
        ),
        name="one_back",
    )(query_part, pair_part, in_hbm(weight), hidden, gain, residual_grad)


def send_rows(values):
    if lax.axis_size("fsdp") != 4:
        return fetch_rows(values)
    third = swap(values, "fsdp", 3)
    return [values, swap(values, "fsdp", 1), third]


def relay_rows(planes):
    if lax.axis_size("fsdp") != 4:
        return planes
    values, first, third = planes
    return [values, first, swap(third, "fsdp", 1), third]


def pass_rows(values):
    return relay_rows(send_rows(values))


def fetch_rows(values):
    count = lax.axis_size("fsdp")
    return [values] + [swap(values, "fsdp", away) for away in range(1, count)]


def sum_rows(halves, forward):
    count = lax.axis_size("fsdp")
    half = count // 2
    rows = halves[0].shape[0] // half
    parts = [
        halves[away // half][away % half * rows : (away % half + 1) * rows] for away in range(count)
    ]
    if count == 4 and forward:
        passed = swap(parts[2].astype(BF), "fsdp", 1).astype(F32)
        one = swap(parts[1].astype(BF), "fsdp", 1).astype(F32)
        third = swap((parts[3] + passed).astype(BF), "fsdp", 3).astype(F32)
        return [parts[0], one, third]
    return parts[:1] + [swap(parts[i].astype(BF), "fsdp", i) for i in range(1, count)]


def by_feature(values):
    rows, width = values.shape
    ctx_count, fsdp_count = lax.axis_size("ctx"), lax.axis_size("fsdp")
    blocks = values.reshape(rows, ctx_count, fsdp_count, width // (ctx_count * fsdp_count))
    return blocks.transpose(0, 2, 1, 3).reshape(rows, width)


def sum_over_ctx(part_for):
    pairs = lax.axis_size("ctx") // 2
    sent = jnp.stack([part_for(2 * pair + 1).astype(BF) for pair in range(pairs)])
    got = swap(sent, "ctx", 1)
    sums = [part_for(2 * pair).astype(F32) + got[pair].astype(F32) for pair in range(pairs)]
    total = sums[0]
    for pair in range(1, pairs):
        total = total + swap(sums[pair].astype(BF), "ctx", 2 * pair).astype(F32)
    return total


def ctx_rows_sum(values):
    height = values.shape[0] // lax.axis_size("ctx")
    me = lax.axis_index("ctx")

    def part(offset):
        return lax.dynamic_slice(
            values, ((me ^ offset) * height, 0), (height, values.shape[1])
        )

    return sum_over_ctx(part)


def key_offsets():
    count = lax.axis_size("ctx")
    return list(range(0, count, 2)) + list(range(1, count, 2))


def gather_keys(piece):
    same = [piece] + [swap(piece, "ctx", far) for far in range(2, lax.axis_size("ctx"), 2)]
    mine = jnp.concatenate(same, axis=0)
    return mine, swap(mine, "ctx", 1)


def sum_pairs(kept, sent, cosine, sine):
    _, count, width = kept.shape
    pairs = lax.axis_size("ctx") // 2
    got = swap(sent, "ctx", 1)
    sums = (kept.astype(F32) + got.astype(F32)).reshape(2, pairs, count // pairs, width)
    far = [swap(sums[:, pair].astype(BF), "ctx", 2 * pair) for pair in range(1, pairs)]
    return pair_turn(sums[:, 0], far, cosine, sine), got


def half_mask(shape):
    return lax.broadcasted_iota(jnp.int32, shape, len(shape) - 1) % 128 < HD


def turn(values, cosine, sine):
    lanes = lax.broadcasted_iota(jnp.int32, values.shape, 1) % HD
    turned = jnp.where(
        lanes < HD // 2, pltpu.roll(values, 128 - HD // 2, 1), pltpu.roll(values, HD // 2, 1)
    )
    return values * cosine + turned * sine


def doubled(tile, odd):
    wide = tile.astype(F32)
    other = pltpu.roll(wide, HD, 1)
    return jnp.where(half_mask(tile.shape) == (odd == 0), wide, other).astype(BF)


def split_heads(tile_pair):
    zero = jnp.zeros((), tile_pair.dtype)
    parts = []
    for j in range(2):
        tile = tile_pair[:, j * 128 : (j + 1) * 128]
        mask = half_mask(tile.shape)
        parts += [jnp.where(mask, tile, zero), jnp.where(mask, zero, tile)]
    return jnp.concatenate(parts, axis=0)


def merge_heads(stacked):
    rows = stacked.shape[0] // 4
    tiles = []
    for j in range(2):
        even = stacked[2 * j * rows : (2 * j + 1) * rows]
        odd = stacked[(2 * j + 1) * rows : (2 * j + 2) * rows]
        tiles.append(jnp.where(half_mask(even.shape), even, odd))
    return jnp.concatenate(tiles, axis=1)


def key_chunks(refs, chunk):
    first = 0
    for k_ref, v_ref in refs:
        for start in range(0, k_ref.shape[0], chunk):
            at = slice(start, start + chunk)
            yield first + start, k_ref.at[at, :], v_ref.at[at, :]
        first += k_ref.shape[0]


def masked_scores(keys, queries, key_ref, own_ref, start):
    allowed = key_ref[start : start + keys.shape[0], :1] <= own_ref[...]
    bias = jnp.where(allowed, 0.0, -1e30).astype(F32)
    return nt(keys, queries) + jnp.concatenate([bias] * 4, axis=1)


def attend_kernel(
    chunk, q_ref, ka_ref, va_ref, kb_ref, vb_ref, key_ref, own_ref, rows_ref, attended_ref, log_ref
):
    odd = pl.program_id(0) % 2
    rows = q_ref.shape[0]
    queries = split_heads(q_ref[...])
    parts = list(key_chunks(((ka_ref, va_ref), (kb_ref, vb_ref)), chunk))
    scores = [
        masked_scores(doubled(k_ref[...], odd), queries, key_ref, own_ref, start)
        for start, k_ref, _ in parts
    ]
    top = jnp.max(scores[0], axis=0, keepdims=True)
    for score in scores[1:]:
        top = jnp.maximum(top, jnp.max(score, axis=0, keepdims=True))
    total = jnp.zeros_like(top)
    summed = jnp.zeros((4 * rows, 128), F32)
    for score, (_, _, v_ref) in zip(scores, parts):
        weights = jnp.exp(score - top)
        total += jnp.sum(weights, axis=0, keepdims=True)
        summed += tn(weights.astype(BF), doubled(v_ref[...], odd))
    log_ref[0] = top + jnp.log(total)
    attended = merge_heads(summed / jnp.transpose(jnp.broadcast_to(total, (128, 4 * rows))))
    attended_ref[...] = attended
    rows_ref[...] = attended.astype(BF)


def key_specs(parts):
    tiles = parts[0].shape[1] // 256
    specs, arrays = [], []
    for part in parts:
        specs.append(pl.BlockSpec((part.shape[0], 128), lambda g: (0, g // 2)))
        specs.append(pl.BlockSpec((part.shape[0], 128), lambda g: (0, tiles + g // 2)))
        arrays += [part, part]
    return specs, arrays


def attend(queries, keys_values, key_anchor, own_anchor):
    rows, width = queries.shape
    count = key_anchor.shape[0]
    specs, arrays = key_specs(keys_values)
    wide = pl.BlockSpec((rows, 256), lambda g: (0, g))
    return pl.pallas_call(
        lambda *refs: attend_kernel(KEY_CHUNK, *refs),
        grid=(KV,),
        out_shape=(
            jax.ShapeDtypeStruct((rows, width), BF),
            jax.ShapeDtypeStruct((rows, width), F32),
            jax.ShapeDtypeStruct((KV, 1, 4 * rows), F32),
        ),
        in_specs=[wide]
        + specs
        + [
            pl.BlockSpec((count, 128), lambda g: (0, 0)),
            pl.BlockSpec((1, rows), lambda g: (0, 0)),
        ],
        out_specs=(wide, wide, pl.BlockSpec((1, 1, 4 * rows), lambda g: (g, 0, 0))),
        compiler_params=pltpu.CompilerParams(vmem_limit_bytes=48 << 20),
        cost_estimate=pl.CostEstimate(
            flops=4 * rows * width * count,
            bytes_accessed=4 * count * KV * HD,
            transcendentals=rows * H * count,
        ),
        name="attend",
    )(queries, *arrays, key_anchor, own_anchor)


def attend_back_kernel(
    chunk, q_ref, grad_ref, attended_ref, ka_ref, va_ref, kb_ref, vb_ref, key_ref, own_ref, log_ref,
    cos_ref, sin_ref, dq_ref, kept_ref, sent_ref,
):
    odd = pl.program_id(0) % 2
    rows = q_ref.shape[0]
    half = ka_ref.shape[0]
    queries, grads = split_heads(q_ref[...]), split_heads(grad_ref[...])
    product = grads.astype(F32) * split_heads(attended_ref[...])
    delta = jnp.sum(jnp.transpose(product), axis=0, keepdims=True)
    log_total = log_ref[0]
    total = jnp.zeros((4 * rows, 128), F32)
    keep = half_mask((chunk, 128)) == (odd == 0)
    for start, k_ref, v_ref in key_chunks(((ka_ref, va_ref), (kb_ref, vb_ref)), chunk):
        keys, values = doubled(k_ref[...], odd), doubled(v_ref[...], odd)
        scores = masked_scores(keys, queries, key_ref, own_ref, start)
        probs = jnp.exp(scores - log_total)
        value_grad = nn(probs.astype(BF), grads)
        score_grad = (probs * (nt(values, grads) - delta)).astype(BF)
        key_grad = nn(score_grad, queries)
        total += tn(score_grad, keys)
        out_ref = kept_ref if start < half else sent_ref
        at = slice(start % half, start % half + chunk)
        for part, value in enumerate((key_grad, value_grad)):
            value = (value + pltpu.roll(value, HD, 1)).astype(BF)
            out_ref[part, at, :] = jnp.where(keep, value, out_ref[part, at, :])
    merged = merge_heads(total) * (1.0 / math.sqrt(HD))
    cosine, sine = cos_ref[...], sin_ref[...]
    for j in range(2):
        tile = slice(j * 128, (j + 1) * 128)
        dq_ref[:, tile] = turn(merged[:, tile], cosine, -sine).astype(BF)


def attend_back(queries, grads, attended, keys_values, key_anchor, own_anchor, logs, cosine, sine):
    rows, width = queries.shape
    count = key_anchor.shape[0]
    specs, arrays = key_specs(keys_values)
    wide = pl.BlockSpec((rows, 256), lambda g: (0, g))
    small = pl.BlockSpec((rows, 128), lambda g: (0, 0))
    pair = pl.BlockSpec((2, count // 2, 128), lambda g: (0, 0, g // 2))
    return pl.pallas_call(
        lambda *refs: attend_back_kernel(KEY_CHUNK, *refs),
        grid=(KV,),
        out_shape=(
            jax.ShapeDtypeStruct((rows, width), BF),
            jax.ShapeDtypeStruct((2, count // 2, KV * HD), BF),
            jax.ShapeDtypeStruct((2, count // 2, KV * HD), BF),
        ),
        in_specs=[wide, wide, wide]
        + specs
        + [
            pl.BlockSpec((count, 128), lambda g: (0, 0)),
            pl.BlockSpec((1, rows), lambda g: (0, 0)),
            pl.BlockSpec((1, 1, 4 * rows), lambda g: (g, 0, 0)),
            small,
            small,
        ],
        out_specs=(wide, pair, pair),
        compiler_params=pltpu.CompilerParams(vmem_limit_bytes=48 << 20),
        cost_estimate=pl.CostEstimate(
            flops=10 * rows * width * count,
            bytes_accessed=8 * count * KV * HD,
            transcendentals=rows * H * count,
        ),
        name="attend_back",
    )(queries, grads, attended, *arrays, key_anchor, own_anchor, logs, cosine, sine)


def pair_turn_kernel(copies, own_ref, *refs):
    got, (cos_ref, sin_ref, y_ref) = refs[:-3], refs[-3:]
    total = own_ref[...]
    for ref in got:
        total = total + ref[...].astype(F32)
    cosine, sine = cos_ref[...], sin_ref[...]
    _, rows, width = total.shape
    tiles = [
        turn(total[0, :, start : start + 128], cosine, -sine).astype(BF)
        for start in range(0, width, 128)
    ]
    values = total[1].astype(BF)
    for copy in range(copies):
        at = slice(copy * rows, (copy + 1) * rows)
        for i, tile in enumerate(tiles):
            y_ref[at, i * 128 : (i + 1) * 128] = tile
        y_ref[at, width:] = values


def pair_turn(own, got, cosine, sine):
    _, rows, width = own.shape
    copies = lax.axis_size("fsdp")
    return pl.pallas_call(
        lambda *refs: pair_turn_kernel(copies, *refs),
        out_shape=jax.ShapeDtypeStruct((copies * rows, 2 * width), BF),
        name="pair_turn",
    )(own, *got, cosine, sine)


def join_rows(x_buf, refs):
    @pl.when((pl.program_id(0) == 0))
    def _():
        rows = refs[0].shape[0]
        for i, ref in enumerate(refs):
            x_buf[i * rows : (i + 1) * rows] = ref[...]


def ffn_kernel(count, *refs):
    rows_refs, (act_ref, w_ref, out_ref, sum_ref, x_buf) = refs[:count], refs[count:]
    join_rows(x_buf, rows_refs)
    step = pl.program_id(0)
    gate_w, up_w = w_ref[0], w_ref[1]
    x = x_buf[...]
    gate, up = nn(x, gate_w), nn(x, up_w)
    act_grad = act_ref[...]
    sig = jax.nn.sigmoid(gate)
    silu = gate * sig
    gate_grad = (act_grad * up * sig * (1.0 + gate * (1.0 - sig))).astype(BF)
    up_grad = (act_grad * silu).astype(BF)
    out_ref[0], out_ref[1], out_ref[2] = gate_grad, up_grad, (silu * up).astype(BF)
    part = nt(gate_grad, gate_w) + nt(up_grad, up_w)

    @pl.when(step == 0)
    def _():
        sum_ref[...] = part

    @pl.when(step > 0)
    def _():
        sum_ref[...] += part


def ffn_middle(blocks, act_grad, half, weights):
    width = blocks[0].shape[1]
    rows = blocks[0].shape[0] * len(blocks)
    hidden = weights.shape[2]
    tile = FFN_TILE
    return pl.pallas_call(
        lambda *refs: ffn_kernel(len(blocks), *refs),
        grid=(hidden // tile,),
        out_shape=(
            pltpu.HBM((3, rows, hidden), BF),
            jax.ShapeDtypeStruct((rows, width), F32),
        ),
        in_specs=[pl.BlockSpec(block.shape, lambda j: (0, 0)) for block in blocks]
        + [
            pl.BlockSpec((rows, tile), lambda j: (half, j)),
            pl.BlockSpec((2, width, tile), lambda j: (0, 0, j)),
        ],
        out_specs=(
            pl.BlockSpec((3, rows, tile), lambda j: (0, 0, j)),
            pl.BlockSpec((rows, width), lambda j: (0, 0)),
        ),
        scratch_shapes=[pltpu.VMEM((rows, width), BF)],
        compiler_params=pltpu.CompilerParams(vmem_limit_bytes=40 << 20),
        cost_estimate=pl.CostEstimate(
            flops=8 * rows * width * hidden,
            bytes_accessed=4 * width * hidden,
            transcendentals=rows * hidden,
        ),
        name="ffn_middle",
    )(*blocks, act_grad, weights)


def products_kernel(count, *refs):
    in_refs, grad_refs = refs[:count], refs[count : 2 * count]
    right_a, right_b, out_ref = refs[2 * count :]
    half = count // 2

    def emit(lefts):
        left_a = jnp.concatenate([ref[...] for ref in lefts[:half]], axis=0)
        left_b = jnp.concatenate([ref[...] for ref in lefts[half:]], axis=0)
        out_ref[0] = (tn(left_a, right_a[0]) + tn(left_b, right_b[0])).astype(BF)

    @pl.when(pl.program_id(0) < 2)
    def _():
        emit(in_refs)

    @pl.when(pl.program_id(0) == 2)
    def _():
        emit(grad_refs)


def ffn_products(rows_in, rows_out, parts):
    count = len(rows_in)
    rows, width = rows_in[0].shape
    hidden = parts[0].shape[2]
    tile = FFN_TILE
    last = width // tile - 1
    left = pl.BlockSpec((rows, tile), lambda k, i: (0, jnp.where(k < 2, i, last)))
    grad = pl.BlockSpec((rows, tile), lambda k, i: (0, jnp.where(k == 2, i, 0)))
    right = pl.BlockSpec((1, rows * count // 2, hidden), lambda k, i: (k, 0, 0))
    return pl.pallas_call(
        lambda *refs: products_kernel(count, *refs),
        grid=(3, width // tile),
        out_shape=pltpu.HBM((3, width, hidden), BF),
        in_specs=[left] * count + [grad] * count + [right, right],
        out_specs=pl.BlockSpec((1, tile, hidden), lambda k, i: (k, i, 0)),
        compiler_params=pltpu.CompilerParams(vmem_limit_bytes=32 << 20),
        cost_estimate=pl.CostEstimate(
            flops=6 * count * rows * width * hidden,
            bytes_accessed=6 * width * hidden,
            transcendentals=0,
        ),
        name="ffn_products",
    )(*rows_in, *rows_out, *parts)


def down_back_kernel(count, *refs):
    rows_refs, (w_ref, y_ref, x_buf) = refs[:count], refs[count:]
    join_rows(x_buf, rows_refs)
    y_ref[...] = nn(x_buf[...], w_ref[0])


def down_back(blocks, weights):
    width = blocks[0].shape[1]
    rows = blocks[0].shape[0] * len(blocks)
    hidden = weights.shape[2]
    tile = FFN_TILE
    return pl.pallas_call(
        lambda *refs: down_back_kernel(len(blocks), *refs),
        grid=(hidden // tile,),
        out_shape=pltpu.HBM((rows, hidden), F32),
        in_specs=[pl.BlockSpec(block.shape, lambda j: (0, 0)) for block in blocks]
        + [pl.BlockSpec((1, width, tile), lambda j: (2, 0, j))],
        out_specs=pl.BlockSpec((rows, tile), lambda j: (0, j)),
        scratch_shapes=[pltpu.VMEM((rows, width), BF)],
        compiler_params=pltpu.CompilerParams(vmem_limit_bytes=24 << 20),
        cost_estimate=pl.CostEstimate(
            flops=2 * rows * width * hidden,
            bytes_accessed=2 * width * hidden,
            transcendentals=0,
        ),
        name="down_back",
    )(*blocks, weights)


def down_kernel(a_ref, b_ref, w_ref, y_ref):
    rows = a_ref.shape[1]
    for half, ref in enumerate((a_ref, b_ref)):
        y_ref[half * rows : (half + 1) * rows] = nt(ref[0], w_ref[0])


def down_forward(parts, weights):
    _, rows, hidden = parts[0].shape
    width = weights.shape[1]
    tile = FFN_TILE
    left = pl.BlockSpec((1, rows, hidden), lambda j: (2, 0, 0))
    total = pl.pallas_call(
        down_kernel,
        grid=(width // tile,),
        out_shape=jax.ShapeDtypeStruct((2 * rows, width), F32),
        in_specs=[left, left, pl.BlockSpec((1, tile, hidden), lambda j: (2, j, 0))],
        out_specs=pl.BlockSpec((2 * rows, tile), lambda j: (0, j)),
        compiler_params=pltpu.CompilerParams(vmem_limit_bytes=24 << 20),
        cost_estimate=pl.CostEstimate(
            flops=4 * rows * width * hidden,
            bytes_accessed=2 * width * hidden,
            transcendentals=0,
        ),
        name="down_forward",
    )(*parts, weights)
    return total[:rows], total[rows:]


def share_kernel(count, sizes, ids_ref, *refs):
    products = len(sizes)
    lefts = [refs[i * count : (i + 1) * count] for i in range(products)]
    rest = refs[products * count :]
    rights = []
    for size in sizes:
        rights.append(rest[:size])
        rest = rest[size:]
    bufs = rest[len(rest) - products :]
    terms, (kept_ref, sent_ref) = rest[: -products - 2], rest[-products - 2 : -products]
    half = kept_ref.shape[1]
    own = ids_ref[0] % 2 == 0

    @pl.when(pl.program_id(0) == 0)
    def _():
        for parts, buf in zip(rights, bufs):
            rows = buf.shape[0] // count
            for away in range(count):
                if len(parts) > 1:
                    block = parts[away][...]
                else:
                    start = (ids_ref[1] ^ away) * rows
                    block = parts[0][pl.ds(pl.multiple_of(start, 16), rows), :]
                buf[away * rows : (away + 1) * rows] = block

    def emit(part, column):
        at = slice(column, column + part.shape[1])
        kept_ref[0, :, at] = jnp.where(own, part[:half], part[half:])
        sent_ref[0, :, at] = jnp.where(own, part[half:], part[:half])

    column = 0
    for left, buf in zip(lefts, bufs):
        joined = jnp.concatenate([ref[...] for ref in left], axis=0)
        emit(tn(joined, buf[...]).astype(BF), column)
        column += buf.shape[1]
    for term in terms:
        tall = jnp.broadcast_to(term[...], (128, term.shape[1]))
        emit(jnp.transpose(tall).astype(BF), column)
        column += 128


def share_products(lefts, rights, terms):
    ctx_count = lax.axis_size("ctx")
    pairs = ctx_count // 2
    count = len(lefts[0])
    rows, width = lefts[0][0].shape
    height = width // ctx_count
    groups = [right if isinstance(right, list) else [right] for right in rights]
    widths = [group[0].shape[1] for group in groups]
    columns = sum(widths) + 128 * len(terms)

    def place(j, ids_ref):
        return (0, (ids_ref[0] // 2) ^ j)

    def whole(array):
        return pl.BlockSpec(array.shape, lambda j, ids_ref: (0, 0))

    shape = jax.ShapeDtypeStruct((pairs, height, columns), BF)
    out = pl.BlockSpec((1, height, columns), lambda j, ids_ref: (j, 0, 0))
    flat_lefts = [block for left in lefts for block in left]
    flat_rights = [block for group in groups for block in group]
    return pl.pallas_call(
        lambda *refs: share_kernel(count, [len(group) for group in groups], *refs),
        grid_spec=pltpu.PrefetchScalarGridSpec(
            num_scalar_prefetch=1,
            grid=(pairs,),
            in_specs=[pl.BlockSpec((rows, 2 * height), place) for _ in flat_lefts]
            + [whole(block) for block in flat_rights]
            + [pl.BlockSpec((1, 2 * height), place) for _ in terms],
            out_specs=(out, out),
            scratch_shapes=[pltpu.VMEM((count * rows, size), BF) for size in widths],
        ),
        out_shape=(shape, shape),
        compiler_params=pltpu.CompilerParams(vmem_limit_bytes=32 << 20),
        cost_estimate=pl.CostEstimate(
            flops=2 * count * rows * width * columns,
            bytes_accessed=2 * (count * rows + columns) * width,
            transcendentals=0,
        ),
        name="share_terms" if terms else "share_products",
    )(jnp.stack(ids()), *flat_lefts, *flat_rights, *[term[None] for term in terms])


def in_fsdp_order(value):
    if not isinstance(value, list):
        return value
    plane = lax.axis_index("fsdp")
    stacked = jnp.stack(value)
    parts = [
        lax.dynamic_index_in_dim(stacked, plane ^ away, 0, keepdims=False)
        for away in range(len(value))
    ]
    return jnp.concatenate(parts, axis=0)


def share_start(lefts, rights, terms):
    pairs = lax.axis_size("ctx") // 2
    if (lefts[0][0].shape[1] // pairs) % 128:
        values = [tn(in_fsdp_order(a), in_fsdp_order(b)) for a, b in zip(lefts, rights)]
        values += [jnp.broadcast_to(term[:, None], (term.shape[0], 128)) for term in terms]
        return [ctx_rows_sum(jnp.concatenate(values, axis=1))]
    kept, sent = share_products(lefts, rights, terms)
    got = swap(sent, "ctx", 1)
    parts = [kept[0], got[0]]
    for pair in range(1, pairs):
        part = (kept[pair].astype(F32) + got[pair].astype(F32)).astype(BF)
        parts.append(swap(part, "ctx", 2 * pair))
    return parts


def share_finish(parts):
    total = parts[0].astype(F32)
    for part in parts[1:]:
        total = total + part.astype(F32)
    return total


def own_rows_of(values, height):
    index = lax.axis_index("ctx") * lax.axis_size("fsdp") + lax.axis_index("fsdp")
    return lax.dynamic_slice_in_dim(values, index * height, height, 0)


def feature_parts(values):
    count, plane = lax.axis_size("fsdp"), lax.axis_index("fsdp")
    values = by_feature(values)
    rows, width = values.shape
    width //= count
    return [
        lax.dynamic_slice(values, (0, (plane ^ away) * width), (rows, width))
        for away in range(count)
    ]


def feature_rows(parts):
    return [swap(part, "fsdp", away) if away else part for away, part in enumerate(parts)]


def own_features(terms):
    ctx_count, fsdp_count = lax.axis_size("ctx"), lax.axis_size("fsdp")
    total = jnp.stack(terms)
    away = 1
    while away < fsdp_count:
        total = total + swap(total, "fsdp", away)
        away *= 2
    blocks = total.reshape(len(terms), ctx_count, fsdp_count, -1)
    own = lax.dynamic_index_in_dim(blocks, lax.axis_index("fsdp"), 2, keepdims=False)
    own = own.reshape(len(terms), -1)
    return [own[i] for i in range(len(terms))]


def layer(
    hidden_in,
    out_grad,
    positions,
    block_order,
    attn_gain,
    ffn_gain,
    qkv_weight,
    out_weight,
    ffn_weight,
):
    ctx_count, fsdp_count = lax.axis_size("ctx"), lax.axis_size("fsdp")
    me, _ = ids()
    rows = hidden_in.shape[1]
    queries_width, kv_width = H * HD, KV * HD
    ffn_parts = in_hbm(ffn_weight.transpose(1, 0, 2))

    frequency = jnp.power(ROPE_BASE, -(jnp.arange(HD // 2, dtype=F32) * 2.0 / HD))
    angles = positions[0].astype(F32)[:, None] * frequency[None, :]
    cosine = jnp.tile(jnp.cos(angles), (1, 4))
    sine = jnp.tile(jnp.concatenate([-jnp.sin(angles), jnp.sin(angles)], axis=1), (1, 2))
    own_anchor = anchors_of(block_order, me, rows)[None]
    key_anchor = jnp.concatenate(
        [anchors_of(block_order, me ^ offset, rows) for offset in key_offsets()]
    )
    key_anchor = jnp.broadcast_to(key_anchor[:, None], (rows * ctx_count, 128))

    inputs = hidden_in[0].astype(F32)
    grad_in = out_grad[0]
    scale_one = norm_scale(inputs)
    normed_one = (inputs * scale_one * attn_gain).astype(BF)

    one_parts = feature_parts(normed_one)
    fast = ctx_count == 8 and (qkv_weight.shape[1] // ctx_count) % 128 == 0
    if fast:
        early = (cosine, sine, own_anchor, key_anchor, one_parts)
        qkv_pieces, marks = gather_pieces(qkv_weight, early)
        out_blocks = gather_blocks(out_weight, *marks)
        queries, pair, qkv_full = pieces_forward(
            normed_one, qkv_weight, qkv_pieces, cosine, sine
        )
    else:
        marks = (normed_one, normed_one)
        out_blocks = gather_blocks(out_weight, *marks)
        qkv_full = whole_of(qkv_weight, gather_blocks(qkv_weight, normed_one, normed_one))
        projected = nn(normed_one, qkv_full)
        turned = rotate(
            projected[:, : queries_width + kv_width].reshape(rows, H + KV, HD), positions[0]
        ).reshape(rows, queries_width + kv_width)
        queries = (turned[:, :queries_width] * (1.0 / math.sqrt(HD))).astype(BF)
        pair = jnp.concatenate(
            [turned[:, queries_width:], projected[:, queries_width + kv_width :]], axis=1
        ).astype(BF)
    own_one = feature_rows(after(one_parts, pair))
    keys_values = gather_keys(pair)
    rows_out = send_rows(after(grad_in, pair))
    attn_rows, attended, logs = attend(queries, keys_values, key_anchor, own_anchor)
    rows_out = relay_rows(after(rows_out, attn_rows))
    residual, normed_two = out_forward(
        attn_rows, out_weight, out_blocks, hidden_in[0], ffn_gain
    )
    scale_two = norm_scale(residual)
    rows_in = pass_rows(normed_two)
    rows_out = after(rows_out, normed_two)
    act_grad = down_back(rows_out, ffn_parts)

    all_attn = pass_rows(after(attn_rows, rows_in[2]))
    middle = []
    half = fsdp_count // 2
    for index in range(2):
        blocks = rows_in[index * half : (index + 1) * half]
        middle.append(ffn_middle(blocks, in_hbm(act_grad), index, ffn_parts))
    parts, partial = [in_hbm(m[0]) for m in middle], [m[1] for m in middle]
    sum_grad = share_finish(sum_rows(partial, True))
    products = ffn_products(rows_in, rows_out, parts).transpose(1, 0, 2)
    ffn_weight_grad = lax.psum_scatter(products, "ctx", scatter_dimension=0, tiled=True)
    ffn_weight_grad = ffn_weight_grad.astype(F32)
    out_partial = down_forward(parts, ffn_parts)

    unit_two = residual * scale_two
    ffn_gain_term = jnp.sum(sum_grad * unit_two, axis=0)
    scaled_two = ffn_gain * sum_grad
    residual_grad = grad_in.astype(F32) + scale_two * (
        scaled_two - unit_two * jnp.mean(scaled_two * unit_two, axis=-1, keepdims=True)
    )
    residual_bf = residual_grad.astype(BF)
    (ffn_term,) = own_features([ffn_gain_term])
    attn_grad = out_back(residual_bf, out_weight, out_blocks)
    query_part, kept, sent = attend_back(
        queries, attn_grad, attended, keys_values, key_anchor, own_anchor, logs, cosine, sine
    )
    query_planes = pass_rows(query_part)
    pair_copies, near = sum_pairs(kept, sent, cosine, sine)
    own_residual = feature_rows(feature_parts(after(residual_bf, near)))
    all_pair = lax.all_to_all(pair_copies, "fsdp", split_axis=0, concat_axis=0, tiled=True)
    input_grad = one_back(
        query_part, pair_copies, qkv_full, hidden_in[0], attn_gain, residual_grad
    )
    out_sum = sum_rows([after(part, input_grad) for part in out_partial], False)
    first_sums = share_start(
        [own_residual, own_one], [after(all_attn, input_grad), after(query_planes, input_grad)], []
    )
    last_sums = share_start([own_one], [all_pair], [ffn_term])
    last_sums = share_finish(last_sums)
    first_sums = share_finish(after(first_sums, last_sums))
    output = (residual + share_finish(after(out_sum, last_sums))).astype(BF)

    pairs_width = 2 * kv_width
    out_weight_grad = first_sums[:, :queries_width]
    qkv_grad = jnp.concatenate(
        [first_sums[:, queries_width:], last_sums[:, :pairs_width]], axis=1
    )
    features = own_rows_of(attn_gain, qkv_grad.shape[0])
    gain_grad = jnp.sum(own_rows_of(qkv_full, qkv_grad.shape[0]).astype(F32) * qkv_grad, axis=1)
    return (
        output[None],
        input_grad[None],
        qkv_grad,
        out_weight_grad,
        ffn_weight_grad,
        gain_grad / features,
        last_sums[:, pairs_width],
    )


def solution(mesh):
    step = sharded(mesh)
    return step


def sharded(mesh):
    return jax.shard_map(
        layer,
        mesh=mesh,
        in_specs=(
            P("fsdp", "ctx", None),
            P("fsdp", "ctx", None),
            P("fsdp", "ctx"),
            P(),
            P(),
            P(),
            P("fsdp", None),
            P("fsdp", None),
            P(None, None, "fsdp"),
        ),
        out_specs=(
            P("fsdp", "ctx", None),
            P("fsdp", "ctx", None),
            P(("ctx", "fsdp"), None),
            P(("ctx", "fsdp"), None),
            P("ctx", None, "fsdp"),
            P(("ctx", "fsdp")),
            P(("ctx", "fsdp")),
        ),
        check_vma=False,
    )
```

```python
import math

import jax
import jax.numpy as jnp
from jax import lax
from jax.experimental import pallas as pl
from jax.experimental.pallas import tpu as pltpu
from jax.sharding import PartitionSpec as P


H = 32
KV = 8
HD = 64

NORM_EPS = 1e-05
ROPE_BASE = 500000.0
FFN_TILE = 512
KEY_CHUNK = 256


BF = jnp.bfloat16
F32 = jnp.float32


def mm(a, b, dims):
    return lax.dot_general(a, b, (dims, ((), ())), preferred_element_type=F32)


def nn(a, b):
    return mm(a, b, ((1,), (0,)))


def nt(a, b):
    return mm(a, b, ((1,), (1,)))


def tn(a, b):
    return mm(a, b, ((0,), (0,)))


def swap(value, axis, offset):
    count = lax.axis_size(axis)
    return lax.ppermute(value, axis, [(i, i ^ offset) for i in range(count)])


def rotate(values, token_places):
    head_dim = values.shape[-1]
    half_dim = head_dim // 2
    frequency = jnp.power(ROPE_BASE, -(jnp.arange(half_dim, dtype=F32) * 2.0 / head_dim))
    angles = token_places.astype(F32)[:, None] * frequency[None, :]
    cosine = jnp.concatenate([jnp.cos(angles), jnp.cos(angles)], axis=-1)[:, None, :]
    sine_part = jnp.concatenate([jnp.sin(angles), jnp.sin(angles)], axis=-1)[:, None, :]
    turned = jnp.concatenate([-values[..., half_dim:], values[..., :half_dim]], axis=-1)
    return values * cosine + turned * sine_part


def norm_scale(values):
    return lax.rsqrt(jnp.mean(values * values, axis=-1, keepdims=True) + NORM_EPS)


def lookup(entries, row_ids):
    matches = row_ids[:, None] == jnp.arange(entries.shape[0], dtype=jnp.int32)[None, :]
    return jnp.sum(jnp.where(matches, entries[None, :], 0), axis=1)


def anchors_of(block_order, owner, row_count):
    block_len = row_count // 2
    row_ids = owner * row_count + jnp.arange(row_count, dtype=jnp.int32)
    return lookup(block_order, row_ids // block_len) * block_len + row_ids % block_len


def after(value, *earlier):
    return lax.optimization_barrier((value, earlier))[0]


def ids():
    return lax.axis_index("ctx"), lax.axis_index("fsdp")


def gather_pieces(weight, early):
    rows, columns = weight.shape
    share = columns // lax.axis_size("ctx")
    half = rows // 2
    mine = lax.dynamic_slice(weight, (0, lax.axis_index("ctx") * share), (rows, share))
    planes = {}
    planes[3] = swap(mine, "fsdp", 3)
    planes[1] = swap(mine, "fsdp", 1)
    planes[2] = swap(after(planes[3], early), "fsdp", 1)
    pieces = []
    for away in (1, 3, 2):
        first = planes[away]
        along_x, along_y = swap(first, "ctx", 2), swap(first, "ctx", 4)
        top, low = swap(along_y[:half], "ctx", 2), swap(along_x[half:], "ctx", 4)
        parts = [(0, 0, first), (2, 0, along_x), (4, 0, along_y), (6, 0, top), (6, half, low)]
        for offset, start, part in parts:
            pieces.append((away, offset, start, part))
            pieces.append((away, offset + 1, start, swap(part, "ctx", 1)))
    return pieces, (planes[2], (pieces[-4][3], pieces[-2][3]))


def pieces_kernel(places, rows_in, share, ids_ref, x_ref, own_ref, *refs):
    count = len(places)
    piece_refs, refs = refs[:count], refs[count:]
    cos_ref, sin_ref, q_ref, pair_ref, full_ref, y_ref, buf, in_sems, out_sems = refs
    me, plane = ids_ref[0], ids_ref[1]

    def block(away):
        return pl.ds(pl.multiple_of((plane ^ away) * rows_in, 128), rows_in)

    own_copy = pltpu.make_async_copy(own_ref, buf.at[block(0)], in_sems.at[count])
    own_copy.start()
    copies = []
    for i, (away, offset, start, height) in enumerate(places):
        at = pl.ds(pl.multiple_of((plane ^ away) * rows_in + start, 128), height)
        columns = pl.ds(pl.multiple_of((me ^ offset) * share, 128), share)
        copies.append(pltpu.make_async_copy(piece_refs[i], buf.at[at, columns], in_sems.at[i]))
        copies[-1].start()
    outs = []
    order = [0] + list(dict.fromkeys(away for away, _, _, _ in places))
    for away in order:
        if away:
            for copy, place in zip(copies, places):
                if place[0] == away:
                    copy.wait()
        else:
            own_copy.wait()
        outs.append(
            pltpu.make_async_copy(buf.at[block(away)], full_ref.at[block(away)], out_sems.at[away])
        )
        outs[-1].start()
        part = nn(x_ref[:, block(away)], buf[block(away)])
        y_ref[...] = part if away == 0 else y_ref[...] + part
    cosine, sine = cos_ref[...], sin_ref[...]
    queries, keys = H * HD, KV * HD
    for start in range(0, queries + keys, 128):
        tile = turn(y_ref[:, start : start + 128], cosine, sine)
        if start < queries:
            q_ref[:, start : start + 128] = (tile * (1.0 / math.sqrt(HD))).astype(BF)
        else:
            pair_ref[:, start - queries : start - queries + 128] = tile.astype(BF)
    pair_ref[:, keys:] = y_ref[:, queries + keys :].astype(BF)
    for copy in outs:
        copy.wait()


def pieces_forward(x, own, pieces, cosine, sine):
    me, plane = ids()
    rows_in, columns = own.shape
    rows, width = x.shape
    share = columns // lax.axis_size("ctx")
    places = tuple((away, offset, start, part.shape[0]) for away, offset, start, part in pieces)
    arrays = [part for _, _, _, part in pieces]
    hbm, vmem = pl.BlockSpec(memory_space=pltpu.HBM), pl.BlockSpec(memory_space=pltpu.VMEM)
    return pl.pallas_call(
        lambda *refs: pieces_kernel(places, rows_in, share, *refs),
        out_shape=(
            jax.ShapeDtypeStruct((rows, H * HD), BF),
            jax.ShapeDtypeStruct((rows, 2 * KV * HD), BF),
            pltpu.HBM((width, columns), BF),
        ),
        in_specs=[pl.BlockSpec(memory_space=pltpu.SMEM), vmem, hbm]
        + [hbm] * len(arrays)
        + [vmem, vmem],
        out_specs=(vmem, vmem, hbm),
        scratch_shapes=[
            pltpu.VMEM((rows, columns), F32),
            pltpu.VMEM((width, columns), BF),
            pltpu.SemaphoreType.DMA((len(arrays) + 1,)),
            pltpu.SemaphoreType.DMA((width // rows_in,)),
        ],
        compiler_params=pltpu.CompilerParams(vmem_limit_bytes=32 << 20),
        cost_estimate=pl.CostEstimate(
            flops=2 * rows * width * columns, bytes_accessed=4 * width * columns, transcendentals=0
        ),
        name="pieces_forward",
    )(jnp.stack([me, plane]), x, in_hbm(own), *[in_hbm(part) for part in arrays], cosine, sine)


def gather_blocks(weight, before_fsdp, before_ctx):
    rows, columns = weight.shape
    me, plane = ids()
    share = columns // lax.axis_size("ctx")
    mine = lax.dynamic_slice(weight, (0, me * share), (rows, share))
    planes = lax.all_gather(after(mine, before_fsdp), "fsdp")
    others = jnp.stack(
        [
            lax.dynamic_index_in_dim(planes, plane ^ away, 0, keepdims=False)
            for away in range(1, planes.shape[0])
        ]
    )
    return lax.all_gather(after(others, before_ctx), "ctx")


def whole_of(own, blocks):
    ctx_count, others, rows, share = blocks.shape
    plane = lax.axis_index("fsdp")
    columns = ctx_count * share
    full = jnp.zeros(((others + 1) * rows, columns), own.dtype)
    full = lax.dynamic_update_slice(full, own, (plane * rows, 0))
    for away in range(1, others + 1):
        part = blocks[:, away - 1].transpose(1, 0, 2).reshape(rows, columns)
        full = lax.dynamic_update_slice(full, part, ((plane ^ away) * rows, 0))
    return full


def in_hbm(value):
    return pltpu.with_memory_space_constraint(value, pltpu.HBM)


def out_kernel(back, ids_ref, x_ref, own_ref, blocks_ref, *refs):
    hidden_ref, gain_ref = (None, None) if back else refs[:2]
    outs = refs if back else refs[2:]
    own_buf, buf, sems = outs[-3:]
    ctx_count, others, rows, share = buf.shape
    plane = ids_ref[1]
    copies = [pltpu.make_async_copy(own_ref, own_buf, sems.at[ctx_count])]
    for c in range(ctx_count):
        copies.append(pltpu.make_async_copy(blocks_ref.at[c], buf.at[c], sems.at[c]))
    for copy in copies:
        copy.start()

    def features(away):
        return pl.ds(pl.multiple_of((plane ^ away) * rows, 128), rows)

    copies[0].wait()
    if back:
        y_ref = outs[0]
        own_part = nn(x_ref[:, features(0)], own_buf[...])
        for c in range(ctx_count):
            copies[c + 1].wait()
            at = slice(c * share, (c + 1) * share)
            total = own_part[:, at]
            for away in range(1, others + 1):
                total += nn(x_ref[:, features(away)], buf[c, away - 1])
            y_ref[:, at] = total.astype(BF)
        return
    residual_ref, normed_ref = outs[:2]
    residual_ref[...] = hidden_ref[...].astype(F32)
    residual_ref[:, features(0)] += nt(x_ref[...], own_buf[...])
    for c in range(ctx_count):
        copies[c + 1].wait()
        x = x_ref[:, c * share : (c + 1) * share]
        for away in range(1, others + 1):
            residual_ref[:, features(away)] += nt(x, buf[c, away - 1])
    residual = residual_ref[...]
    normed_ref[...] = (residual * norm_scale(residual) * gain_ref[...]).astype(BF)


def out_call(back, x, own, blocks, extra, out_shape):
    vmem, hbm = pl.BlockSpec(memory_space=pltpu.VMEM), pl.BlockSpec(memory_space=pltpu.HBM)
    return pl.pallas_call(
        lambda *refs: out_kernel(back, *refs),
        out_shape=out_shape,
        in_specs=[pl.BlockSpec(memory_space=pltpu.SMEM), vmem, hbm, hbm] + [vmem] * len(extra),
        out_specs=jax.tree.map(lambda _: vmem, out_shape),
        scratch_shapes=[
            pltpu.VMEM(own.shape, own.dtype),
            pltpu.VMEM(blocks.shape, blocks.dtype),
            pltpu.SemaphoreType.DMA((blocks.shape[0] + 1,)),
        ],
        compiler_params=pltpu.CompilerParams(vmem_limit_bytes=24 << 20),
        cost_estimate=pl.CostEstimate(
            flops=2 * x.shape[0] * own.size * (blocks.shape[1] + 1),
            bytes_accessed=2 * own.size * (blocks.shape[1] + 1),
            transcendentals=0,
        ),
        name="out_back" if back else "out_forward",
    )(jnp.stack(ids()), x, in_hbm(own), in_hbm(blocks), *extra)


def out_forward(attn_rows, own, blocks, hidden, gain):
    if blocks.shape[3] % 128:
        residual = hidden.astype(F32) + nt(attn_rows, whole_of(own, blocks))
        return residual, (residual * norm_scale(residual) * gain).astype(BF)
    out_shape = (
        jax.ShapeDtypeStruct(hidden.shape, F32),
        jax.ShapeDtypeStruct(hidden.shape, BF),
    )
    return out_call(False, attn_rows, own, blocks, [hidden, gain[None]], out_shape)


def out_back(x, own, blocks):
    if blocks.shape[3] % 128:
        return nn(x, whole_of(own, blocks)).astype(BF)
    out_shape = jax.ShapeDtypeStruct((x.shape[0], own.shape[1]), BF)
    return out_call(True, x, own, blocks, [], out_shape)


def one_back_kernel(
    query_ref, pair_ref, w_ref, hidden_ref, gain_ref, residual_ref, y_ref
):
    step = pl.program_id(0)
    rows = w_ref.shape[0]
    split = query_ref.shape[1]
    y_ref[:, pl.ds(pl.multiple_of(step * rows, 128), rows)] = nt(
        query_ref[...], w_ref[:, :split]
    ) + nt(pair_ref[...], w_ref[:, split:])

    @pl.when(step == pl.num_programs(0) - 1)
    def _():
        grad = y_ref[...]
        inputs = hidden_ref[...].astype(F32)
        scale = norm_scale(inputs)
        unit = inputs * scale
        scaled = gain_ref[...] * grad
        y_ref[...] = residual_ref[...] + scale * (
            scaled - unit * jnp.mean(scaled * unit, axis=-1, keepdims=True)
        )


def one_back(query_part, pair_part, weight, hidden, gain, residual_grad):
    rows, width = hidden.shape
    columns = weight.shape[1]
    tile = FFN_TILE

    def whole(array):
        return pl.BlockSpec(array.shape, lambda j: (0, 0))

    gain = gain[None]
    return pl.pallas_call(
        one_back_kernel,
        grid=(width // tile,),
        out_shape=jax.ShapeDtypeStruct((rows, width), F32),
        in_specs=[
            whole(query_part),
            pl.BlockSpec((rows, pair_part.shape[1]), lambda j: (0, 0)),
            pl.BlockSpec((tile, columns), lambda j: (j, 0)),
            whole(hidden),
            whole(gain),
            whole(residual_grad),
        ],
        out_specs=pl.BlockSpec((rows, width), lambda j: (0, 0)),
        compiler_params=pltpu.CompilerParams(vmem_limit_bytes=24 << 20),
        cost_estimate=pl.CostEstimate(
            flops=2 * rows * width * columns,
            bytes_accessed=2 * width * columns,
            transcendentals=0,
        ),
        name="one_back",
    )(query_part, pair_part, in_hbm(weight), hidden, gain, residual_grad)


def send_rows(values):
    if lax.axis_size("fsdp") != 4:
        return fetch_rows(values)
    third = swap(values, "fsdp", 3)
    return [values, swap(values, "fsdp", 1), third]


def relay_rows(planes):
    if lax.axis_size("fsdp") != 4:
        return planes
    values, first, third = planes
    return [values, first, swap(third, "fsdp", 1), third]


def pass_rows(values):
    return relay_rows(send_rows(values))


def fetch_rows(values):
    count = lax.axis_size("fsdp")
    return [values] + [swap(values, "fsdp", away) for away in range(1, count)]


def sum_rows(parts, forward):
    count = len(parts)
    if count == 4 and forward:
        passed = swap(parts[2], "fsdp", 1).astype(F32)
        one = swap(parts[1], "fsdp", 1)
        third = swap((parts[3].astype(F32) + passed).astype(BF), "fsdp", 3)
        return [parts[0], one, third]
    return parts[:1] + [swap(parts[i], "fsdp", i) for i in range(1, count)]


def by_feature(values):
    rows, width = values.shape
    ctx_count, fsdp_count = lax.axis_size("ctx"), lax.axis_size("fsdp")
    blocks = values.reshape(rows, ctx_count, fsdp_count, width // (ctx_count * fsdp_count))
    return blocks.transpose(0, 2, 1, 3).reshape(rows, width)


def sum_over_ctx(part_for):
    pairs = lax.axis_size("ctx") // 2
    sent = jnp.stack([part_for(2 * pair + 1).astype(BF) for pair in range(pairs)])
    got = swap(sent, "ctx", 1)
    sums = [part_for(2 * pair).astype(F32) + got[pair].astype(F32) for pair in range(pairs)]
    total = sums[0]
    for pair in range(1, pairs):
        total = total + swap(sums[pair].astype(BF), "ctx", 2 * pair).astype(F32)
    return total


def ctx_rows_sum(values):
    height = values.shape[0] // lax.axis_size("ctx")
    me = lax.axis_index("ctx")

    def part(offset):
        return lax.dynamic_slice(
            values, ((me ^ offset) * height, 0), (height, values.shape[1])
        )

    return sum_over_ctx(part)


def key_offsets():
    count = lax.axis_size("ctx")
    return list(range(0, count, 2)) + list(range(1, count, 2))


def gather_keys(piece):
    same = [piece] + [swap(piece, "ctx", far) for far in range(2, lax.axis_size("ctx"), 2)]
    mine = jnp.concatenate(same, axis=0)
    return mine, swap(mine, "ctx", 1)


def sum_pairs(kept, sent, cosine, sine):
    _, count, width = kept.shape
    pairs = lax.axis_size("ctx") // 2
    got = swap(sent, "ctx", 1)
    sums = (kept.astype(F32) + got.astype(F32)).reshape(2, pairs, count // pairs, width)
    far = [swap(sums[:, pair].astype(BF), "ctx", 2 * pair) for pair in range(1, pairs)]
    return pair_turn(sums[:, 0], far, cosine, sine), got


def half_mask(shape):
    return lax.broadcasted_iota(jnp.int32, shape, len(shape) - 1) % 128 < HD


def turn(values, cosine, sine):
    lanes = lax.broadcasted_iota(jnp.int32, values.shape, 1) % HD
    turned = jnp.where(
        lanes < HD // 2, pltpu.roll(values, 128 - HD // 2, 1), pltpu.roll(values, HD // 2, 1)
    )
    return values * cosine + turned * sine


def doubled(tile, odd):
    wide = tile.astype(F32)
    other = pltpu.roll(wide, HD, 1)
    return jnp.where(half_mask(tile.shape) == (odd == 0), wide, other).astype(BF)


def split_heads(tile_pair):
    zero = jnp.zeros((), tile_pair.dtype)
    parts = []
    for j in range(2):
        tile = tile_pair[:, j * 128 : (j + 1) * 128]
        mask = half_mask(tile.shape)
        parts += [jnp.where(mask, tile, zero), jnp.where(mask, zero, tile)]
    return jnp.concatenate(parts, axis=0)


def merge_heads(stacked):
    rows = stacked.shape[0] // 4
    tiles = []
    for j in range(2):
        even = stacked[2 * j * rows : (2 * j + 1) * rows]
        odd = stacked[(2 * j + 1) * rows : (2 * j + 2) * rows]
        tiles.append(jnp.where(half_mask(even.shape), even, odd))
    return jnp.concatenate(tiles, axis=1)


def key_chunks(refs, chunk):
    first = 0
    for k_ref, v_ref in refs:
        for start in range(0, k_ref.shape[0], chunk):
            at = slice(start, start + chunk)
            yield first + start, k_ref.at[at, :], v_ref.at[at, :]
        first += k_ref.shape[0]


def masked_scores(keys, queries, key_ref, own_ref, start):
    allowed = key_ref[start : start + keys.shape[0], :1] <= own_ref[...]
    bias = jnp.where(allowed, 0.0, -1e30).astype(F32)
    return nt(keys, queries) + jnp.concatenate([bias] * 4, axis=1)


def attend_kernel(
    chunk, q_ref, ka_ref, va_ref, kb_ref, vb_ref, key_ref, own_ref, rows_ref, attended_ref, log_ref
):
    odd = pl.program_id(0) % 2
    rows = q_ref.shape[0]
    queries = split_heads(q_ref[...])
    parts = list(key_chunks(((ka_ref, va_ref), (kb_ref, vb_ref)), chunk))
    scores = [
        masked_scores(doubled(k_ref[...], odd), queries, key_ref, own_ref, start)
        for start, k_ref, _ in parts
    ]
    top = jnp.max(scores[0], axis=0, keepdims=True)
    for score in scores[1:]:
        top = jnp.maximum(top, jnp.max(score, axis=0, keepdims=True))
    total = jnp.zeros_like(top)
    summed = jnp.zeros((4 * rows, 128), F32)
    for score, (_, _, v_ref) in zip(scores, parts):
        weights = jnp.exp(score - top)
        total += jnp.sum(weights, axis=0, keepdims=True)
        summed += tn(weights.astype(BF), doubled(v_ref[...], odd))
    log_ref[0] = top + jnp.log(total)
    attended = merge_heads(summed / jnp.transpose(jnp.broadcast_to(total, (128, 4 * rows))))
    attended_ref[...] = attended
    rows_ref[...] = attended.astype(BF)


def key_specs(parts):
    tiles = parts[0].shape[1] // 256
    specs, arrays = [], []
    for part in parts:
        specs.append(pl.BlockSpec((part.shape[0], 128), lambda g: (0, g // 2)))
        specs.append(pl.BlockSpec((part.shape[0], 128), lambda g: (0, tiles + g // 2)))
        arrays += [part, part]
    return specs, arrays


def attend(queries, keys_values, key_anchor, own_anchor):
    rows, width = queries.shape
    count = key_anchor.shape[0]
    specs, arrays = key_specs(keys_values)
    wide = pl.BlockSpec((rows, 256), lambda g: (0, g))
    return pl.pallas_call(
        lambda *refs: attend_kernel(KEY_CHUNK, *refs),
        grid=(KV,),
        out_shape=(
            jax.ShapeDtypeStruct((rows, width), BF),
            jax.ShapeDtypeStruct((rows, width), F32),
            jax.ShapeDtypeStruct((KV, 1, 4 * rows), F32),
        ),
        in_specs=[wide]
        + specs
        + [
            pl.BlockSpec((count, 128), lambda g: (0, 0)),
            pl.BlockSpec((1, rows), lambda g: (0, 0)),
        ],
        out_specs=(wide, wide, pl.BlockSpec((1, 1, 4 * rows), lambda g: (g, 0, 0))),
        compiler_params=pltpu.CompilerParams(vmem_limit_bytes=48 << 20),
        cost_estimate=pl.CostEstimate(
            flops=4 * rows * width * count,
            bytes_accessed=4 * count * KV * HD,
            transcendentals=rows * H * count,
        ),
        name="attend",
    )(queries, *arrays, key_anchor, own_anchor)


def attend_back_kernel(
    chunk, q_ref, grad_ref, attended_ref, ka_ref, va_ref, kb_ref, vb_ref, key_ref, own_ref, log_ref,
    cos_ref, sin_ref, dq_ref, kept_ref, sent_ref,
):
    odd = pl.program_id(0) % 2
    rows = q_ref.shape[0]
    half = ka_ref.shape[0]
    queries, grads = split_heads(q_ref[...]), split_heads(grad_ref[...])
    product = grads.astype(F32) * split_heads(attended_ref[...])
    delta = jnp.sum(jnp.transpose(product), axis=0, keepdims=True)
    log_total = log_ref[0]
    total = jnp.zeros((4 * rows, 128), F32)
    keep = half_mask((chunk, 128)) == (odd == 0)
    for start, k_ref, v_ref in key_chunks(((ka_ref, va_ref), (kb_ref, vb_ref)), chunk):
        keys, values = doubled(k_ref[...], odd), doubled(v_ref[...], odd)
        scores = masked_scores(keys, queries, key_ref, own_ref, start)
        probs = jnp.exp(scores - log_total)
        value_grad = nn(probs.astype(BF), grads)
        score_grad = (probs * (nt(values, grads) - delta)).astype(BF)
        key_grad = nn(score_grad, queries)
        total += tn(score_grad, keys)
        out_ref = kept_ref if start < half else sent_ref
        at = slice(start % half, start % half + chunk)
        for part, value in enumerate((key_grad, value_grad)):
            value = (value + pltpu.roll(value, HD, 1)).astype(BF)
            out_ref[part, at, :] = jnp.where(keep, value, out_ref[part, at, :])
    merged = merge_heads(total) * (1.0 / math.sqrt(HD))
    cosine, sine = cos_ref[...], sin_ref[...]
    for j in range(2):
        tile = slice(j * 128, (j + 1) * 128)
        dq_ref[:, tile] = turn(merged[:, tile], cosine, -sine).astype(BF)


def attend_back(queries, grads, attended, keys_values, key_anchor, own_anchor, logs, cosine, sine):
    rows, width = queries.shape
    count = key_anchor.shape[0]
    specs, arrays = key_specs(keys_values)
    wide = pl.BlockSpec((rows, 256), lambda g: (0, g))
    small = pl.BlockSpec((rows, 128), lambda g: (0, 0))
    pair = pl.BlockSpec((2, count // 2, 128), lambda g: (0, 0, g // 2))
    return pl.pallas_call(
        lambda *refs: attend_back_kernel(KEY_CHUNK, *refs),
        grid=(KV,),
        out_shape=(
            jax.ShapeDtypeStruct((rows, width), BF),
            jax.ShapeDtypeStruct((2, count // 2, KV * HD), BF),
            jax.ShapeDtypeStruct((2, count // 2, KV * HD), BF),
        ),
        in_specs=[wide, wide, wide]
        + specs
        + [
            pl.BlockSpec((count, 128), lambda g: (0, 0)),
            pl.BlockSpec((1, rows), lambda g: (0, 0)),
            pl.BlockSpec((1, 1, 4 * rows), lambda g: (g, 0, 0)),
            small,
            small,
        ],
        out_specs=(wide, pair, pair),
        compiler_params=pltpu.CompilerParams(vmem_limit_bytes=48 << 20),
        cost_estimate=pl.CostEstimate(
            flops=10 * rows * width * count,
            bytes_accessed=8 * count * KV * HD,
            transcendentals=rows * H * count,
        ),
        name="attend_back",
    )(queries, grads, attended, *arrays, key_anchor, own_anchor, logs, cosine, sine)


def pair_turn_kernel(copies, own_ref, *refs):
    got, (cos_ref, sin_ref, y_ref) = refs[:-3], refs[-3:]
    total = own_ref[...]
    for ref in got:
        total = total + ref[...].astype(F32)
    cosine, sine = cos_ref[...], sin_ref[...]
    _, rows, width = total.shape
    tiles = [
        turn(total[0, :, start : start + 128], cosine, -sine).astype(BF)
        for start in range(0, width, 128)
    ]
    values = total[1].astype(BF)
    for copy in range(copies):
        at = slice(copy * rows, (copy + 1) * rows)
        for i, tile in enumerate(tiles):
            y_ref[at, i * 128 : (i + 1) * 128] = tile
        y_ref[at, width:] = values


def pair_turn(own, got, cosine, sine):
    _, rows, width = own.shape
    copies = lax.axis_size("fsdp")
    return pl.pallas_call(
        lambda *refs: pair_turn_kernel(copies, *refs),
        out_shape=jax.ShapeDtypeStruct((copies * rows, 2 * width), BF),
        name="pair_turn",
    )(own, *got, cosine, sine)


def join_rows(x_buf, refs):
    @pl.when((pl.program_id(0) == 0))
    def _():
        rows = refs[0].shape[0]
        for i, ref in enumerate(refs):
            x_buf[i * rows : (i + 1) * rows] = ref[...]


def ffn_kernel(count, *refs):
    rows_refs, (act_ref, w_ref, out_ref), refs = refs[:count], refs[count : count + 3], refs[count + 3 :]
    sum_refs, (x_buf, sum_buf) = refs[:count], refs[count:]
    join_rows(x_buf, rows_refs)
    step = pl.program_id(0)
    gate_w, up_w = w_ref[0], w_ref[1]
    x = x_buf[...]
    gate, up = nn(x, gate_w), nn(x, up_w)
    act_grad = act_ref[...]
    sig = jax.nn.sigmoid(gate)
    silu = gate * sig
    gate_grad = (act_grad * up * sig * (1.0 + gate * (1.0 - sig))).astype(BF)
    up_grad = (act_grad * silu).astype(BF)
    out_ref[0], out_ref[1], out_ref[2] = gate_grad, up_grad, (silu * up).astype(BF)
    part = nt(gate_grad, gate_w) + nt(up_grad, up_w)

    @pl.when(step == 0)
    def _():
        sum_buf[...] = part

    @pl.when(step > 0)
    def _():
        sum_buf[...] += part

    @pl.when(step == pl.num_programs(0) - 1)
    def _():
        rows = sum_refs[0].shape[0]
        for i, ref in enumerate(sum_refs):
            ref[...] = sum_buf[i * rows : (i + 1) * rows].astype(ref.dtype)


def ffn_middle(blocks, act_grad, half, weights, kinds):
    width = blocks[0].shape[1]
    rows = blocks[0].shape[0] * len(blocks)
    hidden = weights.shape[2]
    tile = FFN_TILE
    whole = [pl.BlockSpec(block.shape, lambda j: (0, 0)) for block in blocks]
    out = pl.pallas_call(
        lambda *refs: ffn_kernel(len(blocks), *refs),
        grid=(hidden // tile,),
        out_shape=(
            pltpu.HBM((3, rows, hidden), BF),
            *[jax.ShapeDtypeStruct(block.shape, kind) for block, kind in zip(blocks, kinds)],
        ),
        in_specs=whole
        + [
            pl.BlockSpec((rows, tile), lambda j: (half, j)),
            pl.BlockSpec((2, width, tile), lambda j: (0, 0, j)),
        ],
        out_specs=(pl.BlockSpec((3, rows, tile), lambda j: (0, 0, j)), *whole),
        scratch_shapes=[pltpu.VMEM((rows, width), BF), pltpu.VMEM((rows, width), F32)],
        compiler_params=pltpu.CompilerParams(vmem_limit_bytes=40 << 20),
        cost_estimate=pl.CostEstimate(
            flops=8 * rows * width * hidden,
            bytes_accessed=4 * width * hidden,
            transcendentals=rows * hidden,
        ),
        name="ffn_middle",
    )(*blocks, act_grad, weights)
    return out[0], list(out[1:])


def products_kernel(count, *refs):
    in_refs, grad_refs = refs[:count], refs[count : 2 * count]
    right_a, right_b, out_ref = refs[2 * count :]
    half = count // 2

    def emit(lefts):
        left_a = jnp.concatenate([ref[...] for ref in lefts[:half]], axis=0)
        left_b = jnp.concatenate([ref[...] for ref in lefts[half:]], axis=0)
        out_ref[0] = (tn(left_a, right_a[0]) + tn(left_b, right_b[0])).astype(BF)

    @pl.when(pl.program_id(0) < 2)
    def _():
        emit(in_refs)

    @pl.when(pl.program_id(0) == 2)
    def _():
        emit(grad_refs)


def ffn_products(rows_in, rows_out, parts):
    count = len(rows_in)
    rows, width = rows_in[0].shape
    hidden = parts[0].shape[2]
    tile = FFN_TILE
    last = width // tile - 1
    left = pl.BlockSpec((rows, tile), lambda k, i: (0, jnp.where(k < 2, i, last)))
    grad = pl.BlockSpec((rows, tile), lambda k, i: (0, jnp.where(k == 2, i, 0)))
    right = pl.BlockSpec((1, rows * count // 2, hidden), lambda k, i: (k, 0, 0))
    return pl.pallas_call(
        lambda *refs: products_kernel(count, *refs),
        grid=(3, width // tile),
        out_shape=pltpu.HBM((3, width, hidden), BF),
        in_specs=[left] * count + [grad] * count + [right, right],
        out_specs=pl.BlockSpec((1, tile, hidden), lambda k, i: (k, i, 0)),
        compiler_params=pltpu.CompilerParams(vmem_limit_bytes=32 << 20),
        cost_estimate=pl.CostEstimate(
            flops=6 * count * rows * width * hidden,
            bytes_accessed=6 * width * hidden,
            transcendentals=0,
        ),
        name="ffn_products",
    )(*rows_in, *rows_out, *parts)


def half_products_kernel(count, added, ids_ref, *refs):
    in_refs, grad_refs = refs[: 2 * count], refs[2 * count : 4 * count]
    rights, rest = refs[4 * count : 4 * count + 2], refs[4 * count + 2 :]
    out_ref = rest[-1]
    half = count // 2

    def emit(lefts):
        height = lefts[0].shape[1]
        for j in range(2):
            part = None
            for i, right in enumerate(rights):
                group = lefts[j * count + i * half : j * count + (i + 1) * half]
                left = jnp.concatenate([ref[...] for ref in group], axis=0)
                product = tn(left, right[0])
                part = product if part is None else part + product
            at = slice(j * height, (j + 1) * height)
            if added:
                part = part + rest[0][0, at].astype(F32)
            out_ref[0, at] = part.astype(BF)

    @pl.when(pl.program_id(0) < 2)
    def _():
        emit(in_refs)

    @pl.when(pl.program_id(0) == 2)
    def _():
        emit(grad_refs)


def half_products(rows_in, rows_out, parts, got):
    count = len(rows_in)
    rows, width = rows_in[0].shape
    hidden = parts[0].shape[2]
    ctx_count = lax.axis_size("ctx")
    height = width // ctx_count
    last = ctx_count // 4 - 1

    def column(i, j, ids_ref):
        own = ids_ref[0] % 2
        return 2 * (2 * i + j) + (own if got is not None else 1 - own)

    def left(j):
        return pl.BlockSpec(
            (rows, height),
            lambda k, i, ids_ref: (0, column(jnp.where(k < 2, i, last), j, ids_ref)),
        )

    def grad(j):
        return pl.BlockSpec(
            (rows, height),
            lambda k, i, ids_ref: (0, column(jnp.where(k == 2, i, 0), j, ids_ref)),
        )

    right = pl.BlockSpec((1, rows * count // 2, hidden), lambda k, i, ids_ref: (k, 0, 0))
    out = pl.BlockSpec((1, 2 * height, hidden), lambda k, i, ids_ref: (k, i, 0))
    extra = [] if got is None else [in_hbm(got)]
    return pl.pallas_call(
        lambda *refs: half_products_kernel(count, got is not None, *refs),
        grid_spec=pltpu.PrefetchScalarGridSpec(
            num_scalar_prefetch=1,
            grid=(3, ctx_count // 4),
            in_specs=[left(0)] * count
            + [left(1)] * count
            + [grad(0)] * count
            + [grad(1)] * count
            + [right, right]
            + [out] * len(extra),
            out_specs=out,
        ),
        out_shape=pltpu.HBM((3, width // 2, hidden), BF),
        compiler_params=pltpu.CompilerParams(vmem_limit_bytes=40 << 20),
        cost_estimate=pl.CostEstimate(
            flops=3 * count * rows * width * hidden,
            bytes_accessed=3 * width * hidden,
            transcendentals=0,
        ),
        name="kept_products" if extra else "sent_products",
    )(jnp.stack(ids()), *rows_in, *rows_in, *rows_out, *rows_out, *parts, *extra)


def ffn_gradient(rows_in, rows_out, parts):
    count = lax.axis_size("ctx")
    if count % 4 or (rows_in[0].shape[1] // count) % 128:
        products = ffn_products(rows_in, rows_out, parts).transpose(1, 0, 2)
        return lax.psum_scatter(products, "ctx", scatter_dimension=0, tiled=True)
    sent = half_products(rows_in, rows_out, parts, None)
    got = swap(sent, "ctx", 1)
    kept = half_products(rows_in, rows_out, parts, got).transpose(1, 0, 2)
    groups = [list(range(core, count, 2)) for core in range(2)]
    return lax.psum_scatter(kept, "ctx", scatter_dimension=0, tiled=True, axis_index_groups=groups)


def down_back_kernel(count, *refs):
    rows_refs, (w_ref, y_ref, x_buf) = refs[:count], refs[count:]
    join_rows(x_buf, rows_refs)
    y_ref[...] = nn(x_buf[...], w_ref[0])


def down_back(blocks, weights):
    width = blocks[0].shape[1]
    rows = blocks[0].shape[0] * len(blocks)
    hidden = weights.shape[2]
    tile = FFN_TILE
    return pl.pallas_call(
        lambda *refs: down_back_kernel(len(blocks), *refs),
        grid=(hidden // tile,),
        out_shape=pltpu.HBM((rows, hidden), F32),
        in_specs=[pl.BlockSpec(block.shape, lambda j: (0, 0)) for block in blocks]
        + [pl.BlockSpec((1, width, tile), lambda j: (2, 0, j))],
        out_specs=pl.BlockSpec((rows, tile), lambda j: (0, j)),
        scratch_shapes=[pltpu.VMEM((rows, width), BF)],
        compiler_params=pltpu.CompilerParams(vmem_limit_bytes=24 << 20),
        cost_estimate=pl.CostEstimate(
            flops=2 * rows * width * hidden,
            bytes_accessed=2 * width * hidden,
            transcendentals=0,
        ),
        name="down_back",
    )(*blocks, weights)


def down_kernel(a_ref, b_ref, w_ref, *y_refs):
    rows = a_ref.shape[1] * 2 // len(y_refs)
    totals = [nt(ref[0], w_ref[0]) for ref in (a_ref, b_ref)]
    half = len(y_refs) // 2
    for i, y_ref in enumerate(y_refs):
        start = i % half * rows
        y_ref[...] = totals[i // half][start : start + rows].astype(y_ref.dtype)


def down_forward(parts, weights, count):
    _, rows, hidden = parts[0].shape
    width = weights.shape[1]
    tile = FFN_TILE
    height = 2 * rows // count
    left = pl.BlockSpec((1, rows, hidden), lambda j: (2, 0, 0))
    return pl.pallas_call(
        down_kernel,
        grid=(width // tile,),
        out_shape=tuple(
            jax.ShapeDtypeStruct((height, width), BF if i else F32) for i in range(count)
        ),
        in_specs=[left, left, pl.BlockSpec((1, tile, hidden), lambda j: (2, j, 0))],
        out_specs=tuple(pl.BlockSpec((height, tile), lambda j: (0, j)) for _ in range(count)),
        compiler_params=pltpu.CompilerParams(vmem_limit_bytes=24 << 20),
        cost_estimate=pl.CostEstimate(
            flops=4 * rows * width * hidden,
            bytes_accessed=2 * width * hidden,
            transcendentals=0,
        ),
        name="down_forward",
    )(*parts, weights)


def share_kernel(count, sizes, ids_ref, *refs):
    products = len(sizes)
    lefts = [refs[i * count : (i + 1) * count] for i in range(products)]
    rest = refs[products * count :]
    rights = []
    for size in sizes:
        rights.append(rest[:size])
        rest = rest[size:]
    bufs = rest[len(rest) - products :]
    terms, (kept_ref, sent_ref) = rest[: -products - 2], rest[-products - 2 : -products]
    half = kept_ref.shape[1]
    own = ids_ref[0] % 2 == 0

    @pl.when(pl.program_id(0) == 0)
    def _():
        for parts, buf in zip(rights, bufs):
            rows = buf.shape[0] // count
            for away in range(count):
                if len(parts) > 1:
                    block = parts[away][...]
                else:
                    start = (ids_ref[1] ^ away) * rows
                    block = parts[0][pl.ds(pl.multiple_of(start, 16), rows), :]
                buf[away * rows : (away + 1) * rows] = block

    def emit(part, column):
        at = slice(column, column + part.shape[1])
        kept_ref[0, :, at] = jnp.where(own, part[:half], part[half:])
        sent_ref[0, :, at] = jnp.where(own, part[half:], part[:half])

    column = 0
    for left, buf in zip(lefts, bufs):
        joined = jnp.concatenate([ref[...] for ref in left], axis=0)
        emit(tn(joined, buf[...]).astype(BF), column)
        column += buf.shape[1]
    for term in terms:
        tall = jnp.broadcast_to(term[...], (128, term.shape[1]))
        emit(jnp.transpose(tall).astype(BF), column)
        column += 128


def share_products(lefts, rights, terms):
    ctx_count = lax.axis_size("ctx")
    pairs = ctx_count // 2
    count = len(lefts[0])
    rows, width = lefts[0][0].shape
    height = width // ctx_count
    groups = [right if isinstance(right, list) else [right] for right in rights]
    widths = [group[0].shape[1] for group in groups]
    columns = sum(widths) + 128 * len(terms)

    def place(j, ids_ref):
        return (0, (ids_ref[0] // 2) ^ j)

    def whole(array):
        return pl.BlockSpec(array.shape, lambda j, ids_ref: (0, 0))

    shape = jax.ShapeDtypeStruct((pairs, height, columns), BF)
    out = pl.BlockSpec((1, height, columns), lambda j, ids_ref: (j, 0, 0))
    flat_lefts = [block for left in lefts for block in left]
    flat_rights = [block for group in groups for block in group]
    return pl.pallas_call(
        lambda *refs: share_kernel(count, [len(group) for group in groups], *refs),
        grid_spec=pltpu.PrefetchScalarGridSpec(
            num_scalar_prefetch=1,
            grid=(pairs,),
            in_specs=[pl.BlockSpec((rows, 2 * height), place) for _ in flat_lefts]
            + [whole(block) for block in flat_rights]
            + [pl.BlockSpec((1, 2 * height), place) for _ in terms],
            out_specs=(out, out),
            scratch_shapes=[pltpu.VMEM((count * rows, size), BF) for size in widths],
        ),
        out_shape=(shape, shape),
        compiler_params=pltpu.CompilerParams(vmem_limit_bytes=32 << 20),
        cost_estimate=pl.CostEstimate(
            flops=2 * count * rows * width * columns,
            bytes_accessed=2 * (count * rows + columns) * width,
            transcendentals=0,
        ),
        name="share_terms" if terms else "share_products",
    )(jnp.stack(ids()), *flat_lefts, *flat_rights, *[term[None] for term in terms])


def in_fsdp_order(value):
    if not isinstance(value, list):
        return value
    plane = lax.axis_index("fsdp")
    stacked = jnp.stack(value)
    parts = [
        lax.dynamic_index_in_dim(stacked, plane ^ away, 0, keepdims=False)
        for away in range(len(value))
    ]
    return jnp.concatenate(parts, axis=0)


def share_start(lefts, rights, terms):
    pairs = lax.axis_size("ctx") // 2
    if (lefts[0][0].shape[1] // pairs) % 128:
        values = [tn(in_fsdp_order(a), in_fsdp_order(b)) for a, b in zip(lefts, rights)]
        values += [jnp.broadcast_to(term[:, None], (term.shape[0], 128)) for term in terms]
        return [ctx_rows_sum(jnp.concatenate(values, axis=1))]
    kept, sent = share_products(lefts, rights, terms)
    got = swap(sent, "ctx", 1)
    parts = [kept[0], got[0]]
    for pair in range(1, pairs):
        part = (kept[pair].astype(F32) + got[pair].astype(F32)).astype(BF)
        parts.append(swap(part, "ctx", 2 * pair))
    return parts


def share_finish(parts):
    total = parts[0].astype(F32)
    for part in parts[1:]:
        total = total + part.astype(F32)
    return total


def own_rows_of(values, height):
    index = lax.axis_index("ctx") * lax.axis_size("fsdp") + lax.axis_index("fsdp")
    return lax.dynamic_slice_in_dim(values, index * height, height, 0)


def feature_parts(values):
    count, plane = lax.axis_size("fsdp"), lax.axis_index("fsdp")
    values = by_feature(values)
    rows, width = values.shape
    width //= count
    return [
        lax.dynamic_slice(values, (0, (plane ^ away) * width), (rows, width))
        for away in range(count)
    ]


def feature_rows(parts):
    return [swap(part, "fsdp", away) if away else part for away, part in enumerate(parts)]


def own_features(terms):
    ctx_count, fsdp_count = lax.axis_size("ctx"), lax.axis_size("fsdp")
    total = jnp.stack(terms)
    away = 1
    while away < fsdp_count:
        total = total + swap(total, "fsdp", away)
        away *= 2
    blocks = total.reshape(len(terms), ctx_count, fsdp_count, -1)
    own = lax.dynamic_index_in_dim(blocks, lax.axis_index("fsdp"), 2, keepdims=False)
    own = own.reshape(len(terms), -1)
    return [own[i] for i in range(len(terms))]


def layer(
    hidden_in,
    out_grad,
    positions,
    block_order,
    attn_gain,
    ffn_gain,
    qkv_weight,
    out_weight,
    ffn_weight,
):
    ctx_count, fsdp_count = lax.axis_size("ctx"), lax.axis_size("fsdp")
    me, _ = ids()
    rows = hidden_in.shape[1]
    queries_width, kv_width = H * HD, KV * HD
    ffn_parts = in_hbm(ffn_weight.transpose(1, 0, 2))

    frequency = jnp.power(ROPE_BASE, -(jnp.arange(HD // 2, dtype=F32) * 2.0 / HD))
    angles = positions[0].astype(F32)[:, None] * frequency[None, :]
    cosine = jnp.tile(jnp.cos(angles), (1, 4))
    sine = jnp.tile(jnp.concatenate([-jnp.sin(angles), jnp.sin(angles)], axis=1), (1, 2))
    own_anchor = anchors_of(block_order, me, rows)[None]
    key_anchor = jnp.concatenate(
        [anchors_of(block_order, me ^ offset, rows) for offset in key_offsets()]
    )
    key_anchor = jnp.broadcast_to(key_anchor[:, None], (rows * ctx_count, 128))

    inputs = hidden_in[0].astype(F32)
    grad_in = out_grad[0]
    scale_one = norm_scale(inputs)
    normed_one = (inputs * scale_one * attn_gain).astype(BF)

    one_parts = feature_parts(normed_one)
    fast = ctx_count == 8 and (qkv_weight.shape[1] // ctx_count) % 128 == 0
    if fast:
        early = (cosine, sine, own_anchor, key_anchor, one_parts)
        qkv_pieces, marks = gather_pieces(qkv_weight, early)
        out_blocks = gather_blocks(out_weight, *marks)
        queries, pair, qkv_full = pieces_forward(
            normed_one, qkv_weight, qkv_pieces, cosine, sine
        )
    else:
        marks = (normed_one, normed_one)
        out_blocks = gather_blocks(out_weight, *marks)
        qkv_full = whole_of(qkv_weight, gather_blocks(qkv_weight, normed_one, normed_one))
        projected = nn(normed_one, qkv_full)
        turned = rotate(
            projected[:, : queries_width + kv_width].reshape(rows, H + KV, HD), positions[0]
        ).reshape(rows, queries_width + kv_width)
        queries = (turned[:, :queries_width] * (1.0 / math.sqrt(HD))).astype(BF)
        pair = jnp.concatenate(
            [turned[:, queries_width:], projected[:, queries_width + kv_width :]], axis=1
        ).astype(BF)
    own_one = feature_rows(after(one_parts, pair))
    keys_values = gather_keys(pair)
    rows_out = send_rows(after(grad_in, pair))
    attn_rows, attended, logs = attend(queries, keys_values, key_anchor, own_anchor)
    rows_out = relay_rows(after(rows_out, attn_rows))
    residual, normed_two = out_forward(
        attn_rows, out_weight, out_blocks, hidden_in[0], ffn_gain
    )
    scale_two = norm_scale(residual)
    rows_in = pass_rows(normed_two)
    rows_out = after(rows_out, normed_two)
    act_grad = down_back(rows_out, ffn_parts)

    all_attn = pass_rows(after(attn_rows, rows_in[2]))
    middle = []
    half = fsdp_count // 2
    passing = 3 if fsdp_count == 4 else 0
    for index in range(2):
        blocks = rows_in[index * half : (index + 1) * half]
        kinds = [F32 if index * half + i in (0, passing) else BF for i in range(half)]
        middle.append(ffn_middle(blocks, in_hbm(act_grad), index, ffn_parts, kinds))
    parts, partial = [in_hbm(m[0]) for m in middle], [block for m in middle for block in m[1]]
    sum_grad = share_finish(sum_rows(partial, True))
    ffn_weight_grad = ffn_gradient(rows_in, rows_out, parts)
    ffn_weight_grad = ffn_weight_grad.astype(F32)
    out_partial = list(down_forward(parts, ffn_parts, fsdp_count))

    unit_two = residual * scale_two
    ffn_gain_term = jnp.sum(sum_grad * unit_two, axis=0)
    scaled_two = ffn_gain * sum_grad
    residual_grad = grad_in.astype(F32) + scale_two * (
        scaled_two - unit_two * jnp.mean(scaled_two * unit_two, axis=-1, keepdims=True)
    )
    residual_bf = residual_grad.astype(BF)
    (ffn_term,) = own_features([ffn_gain_term])
    attn_grad = out_back(residual_bf, out_weight, out_blocks)
    query_part, kept, sent = attend_back(
        queries, attn_grad, attended, keys_values, key_anchor, own_anchor, logs, cosine, sine
    )
    query_planes = pass_rows(query_part)
    pair_copies, near = sum_pairs(kept, sent, cosine, sine)
    own_residual = feature_rows(feature_parts(after(residual_bf, near)))
    all_pair = lax.all_to_all(pair_copies, "fsdp", split_axis=0, concat_axis=0, tiled=True)
    input_grad = one_back(
        query_part, pair_copies, qkv_full, hidden_in[0], attn_gain, residual_grad
    )
    out_sum = sum_rows([after(part, input_grad) for part in out_partial], False)
    first_sums = share_start(
        [own_residual, own_one], [after(all_attn, input_grad), after(query_planes, input_grad)], []
    )
    last_sums = share_start([own_one], [all_pair], [ffn_term])
    last_sums = share_finish(last_sums)
    first_sums = share_finish(after(first_sums, last_sums))
    output = (residual + share_finish(after(out_sum, last_sums))).astype(BF)

    pairs_width = 2 * kv_width
    out_weight_grad = first_sums[:, :queries_width]
    qkv_grad = jnp.concatenate(
        [first_sums[:, queries_width:], last_sums[:, :pairs_width]], axis=1
    )
    features = own_rows_of(attn_gain, qkv_grad.shape[0])
    gain_grad = jnp.sum(own_rows_of(qkv_full, qkv_grad.shape[0]).astype(F32) * qkv_grad, axis=1)
    return (
        output[None],
        input_grad[None],
        qkv_grad,
        out_weight_grad,
        ffn_weight_grad,
        gain_grad / features,
        last_sums[:, pairs_width],
    )


def solution(mesh):
    step = sharded(mesh)
    return step


def sharded(mesh):
    return jax.shard_map(
        layer,
        mesh=mesh,
        in_specs=(
            P("fsdp", "ctx", None),
            P("fsdp", "ctx", None),
            P("fsdp", "ctx"),
            P(),
            P(),
            P(),
            P("fsdp", None),
            P("fsdp", None),
            P(None, None, "fsdp"),
        ),
        out_specs=(
            P("fsdp", "ctx", None),
            P("fsdp", "ctx", None),
            P(("ctx", "fsdp"), None),
            P(("ctx", "fsdp"), None),
            P("ctx", None, "fsdp"),
            P(("ctx", "fsdp")),
            P(("ctx", "fsdp")),
        ),
        check_vma=False,
    )
```

```python
import math

import jax
import jax.numpy as jnp
from jax import lax
from jax.experimental import pallas as pl
from jax.experimental.pallas import tpu as pltpu
from jax.sharding import PartitionSpec as P


H = 32
KV = 8
HD = 64

NORM_EPS = 1e-05
ROPE_BASE = 500000.0
FFN_TILE = 512
KEY_CHUNK = 256


BF = jnp.bfloat16
F32 = jnp.float32


def mm(a, b, dims):
    return lax.dot_general(a, b, (dims, ((), ())), preferred_element_type=F32)


def nn(a, b):
    return mm(a, b, ((1,), (0,)))


def nt(a, b):
    return mm(a, b, ((1,), (1,)))


def tn(a, b):
    return mm(a, b, ((0,), (0,)))


def swap(value, axis, offset):
    count = lax.axis_size(axis)
    return lax.ppermute(value, axis, [(i, i ^ offset) for i in range(count)])


def rotate(values, token_places):
    head_dim = values.shape[-1]
    half_dim = head_dim // 2
    frequency = jnp.power(ROPE_BASE, -(jnp.arange(half_dim, dtype=F32) * 2.0 / head_dim))
    angles = token_places.astype(F32)[:, None] * frequency[None, :]
    cosine = jnp.concatenate([jnp.cos(angles), jnp.cos(angles)], axis=-1)[:, None, :]
    sine_part = jnp.concatenate([jnp.sin(angles), jnp.sin(angles)], axis=-1)[:, None, :]
    turned = jnp.concatenate([-values[..., half_dim:], values[..., :half_dim]], axis=-1)
    return values * cosine + turned * sine_part


def norm_scale(values):
    return lax.rsqrt(jnp.mean(values * values, axis=-1, keepdims=True) + NORM_EPS)


def lookup(entries, row_ids):
    matches = row_ids[:, None] == jnp.arange(entries.shape[0], dtype=jnp.int32)[None, :]
    return jnp.sum(jnp.where(matches, entries[None, :], 0), axis=1)


def anchors_of(block_order, owner, row_count):
    block_len = row_count // 2
    row_ids = owner * row_count + jnp.arange(row_count, dtype=jnp.int32)
    return lookup(block_order, row_ids // block_len) * block_len + row_ids % block_len


def after(value, *earlier):
    return lax.optimization_barrier((value, earlier))[0]


def ids():
    return lax.axis_index("ctx"), lax.axis_index("fsdp")


def gather_pieces(weight, early):
    rows, columns = weight.shape
    share = columns // lax.axis_size("ctx")
    half = rows // 2
    mine = lax.dynamic_slice(weight, (0, lax.axis_index("ctx") * share), (rows, share))
    planes = {}
    planes[3] = swap(mine, "fsdp", 3)
    planes[1] = swap(mine, "fsdp", 1)
    planes[2] = swap(after(planes[3], early), "fsdp", 1)
    pieces = []
    for away in (1, 3, 2):
        first = planes[away]
        along_x, along_y = swap(first, "ctx", 2), swap(first, "ctx", 4)
        top, low = swap(along_y[:half], "ctx", 2), swap(along_x[half:], "ctx", 4)
        parts = [(0, 0, first), (2, 0, along_x), (4, 0, along_y), (6, 0, top), (6, half, low)]
        for offset, start, part in parts:
            pieces.append((away, offset, start, part))
            pieces.append((away, offset + 1, start, swap(part, "ctx", 1)))
    return pieces, (planes[2], (pieces[-4][3], pieces[-2][3]))


def pieces_kernel(places, rows_in, share, ids_ref, x_ref, own_ref, *refs):
    count = len(places)
    piece_refs, refs = refs[:count], refs[count:]
    cos_ref, sin_ref, q_ref, pair_ref, full_ref, y_ref, buf, in_sems, out_sems = refs
    me, plane = ids_ref[0], ids_ref[1]

    def block(away):
        return pl.ds(pl.multiple_of((plane ^ away) * rows_in, 128), rows_in)

    own_copy = pltpu.make_async_copy(own_ref, buf.at[block(0)], in_sems.at[count])
    own_copy.start()
    copies = []
    for i, (away, offset, start, height) in enumerate(places):
        at = pl.ds(pl.multiple_of((plane ^ away) * rows_in + start, 128), height)
        columns = pl.ds(pl.multiple_of((me ^ offset) * share, 128), share)
        copies.append(pltpu.make_async_copy(piece_refs[i], buf.at[at, columns], in_sems.at[i]))
        copies[-1].start()
    outs = []
    order = [0] + list(dict.fromkeys(away for away, _, _, _ in places))
    for away in order:
        if away:
            for copy, place in zip(copies, places):
                if place[0] == away:
                    copy.wait()
        else:
            own_copy.wait()
        outs.append(
            pltpu.make_async_copy(buf.at[block(away)], full_ref.at[block(away)], out_sems.at[away])
        )
        outs[-1].start()
        part = nn(x_ref[:, block(away)], buf[block(away)])
        y_ref[...] = part if away == 0 else y_ref[...] + part
    cosine, sine = cos_ref[...], sin_ref[...]
    queries, keys = H * HD, KV * HD
    for start in range(0, queries + keys, 128):
        tile = turn(y_ref[:, start : start + 128], cosine, sine)
        if start < queries:
            q_ref[:, start : start + 128] = (tile * (1.0 / math.sqrt(HD))).astype(BF)
        else:
            pair_ref[:, start - queries : start - queries + 128] = tile.astype(BF)
    pair_ref[:, keys:] = y_ref[:, queries + keys :].astype(BF)
    for copy in outs:
        copy.wait()


def pieces_forward(x, own, pieces, cosine, sine):
    me, plane = ids()
    rows_in, columns = own.shape
    rows, width = x.shape
    share = columns // lax.axis_size("ctx")
    places = tuple((away, offset, start, part.shape[0]) for away, offset, start, part in pieces)
    arrays = [part for _, _, _, part in pieces]
    hbm, vmem = pl.BlockSpec(memory_space=pltpu.HBM), pl.BlockSpec(memory_space=pltpu.VMEM)
    return pl.pallas_call(
        lambda *refs: pieces_kernel(places, rows_in, share, *refs),
        out_shape=(
            jax.ShapeDtypeStruct((rows, H * HD), BF),
            jax.ShapeDtypeStruct((rows, 2 * KV * HD), BF),
            pltpu.HBM((width, columns), BF),
        ),
        in_specs=[pl.BlockSpec(memory_space=pltpu.SMEM), vmem, hbm]
        + [pl.BlockSpec(memory_space=pl.ANY)] * len(arrays)
        + [vmem, vmem],
        out_specs=(vmem, vmem, hbm),
        scratch_shapes=[
            pltpu.VMEM((rows, columns), F32),
            pltpu.VMEM((width, columns), BF),
            pltpu.SemaphoreType.DMA((len(arrays) + 1,)),
            pltpu.SemaphoreType.DMA((width // rows_in,)),
        ],
        compiler_params=pltpu.CompilerParams(vmem_limit_bytes=32 << 20),
        cost_estimate=pl.CostEstimate(
            flops=2 * rows * width * columns, bytes_accessed=4 * width * columns, transcendentals=0
        ),
        name="pieces_forward",
    )(jnp.stack([me, plane]), x, in_hbm(own), *arrays, cosine, sine)


def gather_blocks(weight, before_fsdp, before_ctx):
    rows, columns = weight.shape
    me, plane = ids()
    share = columns // lax.axis_size("ctx")
    mine = lax.dynamic_slice(weight, (0, me * share), (rows, share))
    planes = lax.all_gather(after(mine, before_fsdp), "fsdp")
    others = jnp.stack(
        [
            lax.dynamic_index_in_dim(planes, plane ^ away, 0, keepdims=False)
            for away in range(1, planes.shape[0])
        ]
    )
    return lax.all_gather(after(others, before_ctx), "ctx")


def whole_of(own, blocks):
    ctx_count, others, rows, share = blocks.shape
    plane = lax.axis_index("fsdp")
    columns = ctx_count * share
    full = jnp.zeros(((others + 1) * rows, columns), own.dtype)
    full = lax.dynamic_update_slice(full, own, (plane * rows, 0))
    for away in range(1, others + 1):
        part = blocks[:, away - 1].transpose(1, 0, 2).reshape(rows, columns)
        full = lax.dynamic_update_slice(full, part, ((plane ^ away) * rows, 0))
    return full


def in_hbm(value):
    return pltpu.with_memory_space_constraint(value, pltpu.HBM)


def out_kernel(back, ids_ref, x_ref, own_ref, blocks_ref, *refs):
    hidden_ref, gain_ref = (None, None) if back else refs[:2]
    outs = refs if back else refs[2:]
    own_buf, buf, sems = outs[-3:]
    ctx_count, others, rows, share = buf.shape
    plane = ids_ref[1]

    def block_copy(c):
        return pltpu.make_async_copy(blocks_ref.at[c], buf.at[c], sems.at[c])

    own_copy = pltpu.make_async_copy(own_ref, own_buf, sems.at[ctx_count])
    own_copy.start()
    for c in range(ctx_count):
        block_copy(c).start()

    def features(away):
        return pl.ds(pl.multiple_of((plane ^ away) * rows, 128), rows)

    def columns(c):
        return pl.ds(pl.multiple_of(c * share, 128), share)

    own_copy.wait()
    if back:
        y_ref = outs[0]

        @pl.loop(0, ctx_count)
        def _(c):
            block_copy(c).wait()
            total = nn(x_ref[:, features(0)], own_buf[:, columns(c)])
            for away in range(1, others + 1):
                total += nn(x_ref[:, features(away)], buf[c, away - 1])
            y_ref[:, columns(c)] = total.astype(BF)

        return
    residual_ref, normed_ref = outs[:2]
    residual_ref[...] = hidden_ref[...].astype(F32)

    @pl.loop(0, ctx_count)
    def _(c):
        block_copy(c).wait()
        x = x_ref[:, columns(c)]
        residual_ref[:, features(0)] += nt(x, own_buf[:, columns(c)])
        for away in range(1, others + 1):
            residual_ref[:, features(away)] += nt(x, buf[c, away - 1])

    residual = residual_ref[...]
    normed_ref[...] = (residual * norm_scale(residual) * gain_ref[...]).astype(BF)


def out_call(back, x, own, blocks, extra, out_shape):
    vmem, hbm = pl.BlockSpec(memory_space=pltpu.VMEM), pl.BlockSpec(memory_space=pltpu.HBM)
    return pl.pallas_call(
        lambda *refs: out_kernel(back, *refs),
        out_shape=out_shape,
        in_specs=[pl.BlockSpec(memory_space=pltpu.SMEM), vmem, hbm, hbm] + [vmem] * len(extra),
        out_specs=jax.tree.map(lambda _: vmem, out_shape),
        scratch_shapes=[
            pltpu.VMEM(own.shape, own.dtype),
            pltpu.VMEM(blocks.shape, blocks.dtype),
            pltpu.SemaphoreType.DMA((blocks.shape[0] + 1,)),
        ],
        compiler_params=pltpu.CompilerParams(vmem_limit_bytes=24 << 20),
        cost_estimate=pl.CostEstimate(
            flops=2 * x.shape[0] * own.size * (blocks.shape[1] + 1),
            bytes_accessed=2 * own.size * (blocks.shape[1] + 1),
            transcendentals=0,
        ),
        name="out_back" if back else "out_forward",
    )(jnp.stack(ids()), x, in_hbm(own), in_hbm(blocks), *extra)


def out_forward(attn_rows, own, blocks, hidden, gain):
    if blocks.shape[3] % 128:
        residual = hidden.astype(F32) + nt(attn_rows, whole_of(own, blocks))
        return residual, (residual * norm_scale(residual) * gain).astype(BF)
    out_shape = (
        jax.ShapeDtypeStruct(hidden.shape, F32),
        jax.ShapeDtypeStruct(hidden.shape, BF),
    )
    return out_call(False, attn_rows, own, blocks, [hidden, gain[None]], out_shape)


def out_back(x, own, blocks):
    if blocks.shape[3] % 128:
        return nn(x, whole_of(own, blocks)).astype(BF)
    out_shape = jax.ShapeDtypeStruct((x.shape[0], own.shape[1]), BF)
    return out_call(True, x, own, blocks, [], out_shape)


def one_back_kernel(
    query_ref, pair_ref, w_ref, hidden_ref, gain_ref, residual_ref, y_ref
):
    step = pl.program_id(0)
    rows = w_ref.shape[0]
    split = query_ref.shape[1]
    y_ref[:, pl.ds(pl.multiple_of(step * rows, 128), rows)] = nt(
        query_ref[...], w_ref[:, :split]
    ) + nt(pair_ref[...], w_ref[:, split:])

    @pl.when(step == pl.num_programs(0) - 1)
    def _():
        grad = y_ref[...]
        inputs = hidden_ref[...].astype(F32)
        scale = norm_scale(inputs)
        unit = inputs * scale
        scaled = gain_ref[...] * grad
        y_ref[...] = residual_ref[...] + scale * (
            scaled - unit * jnp.mean(scaled * unit, axis=-1, keepdims=True)
        )


def one_back(query_part, pair_part, weight, hidden, gain, residual_grad):
    rows, width = hidden.shape
    columns = weight.shape[1]
    tile = FFN_TILE

    def whole(array):
        return pl.BlockSpec(array.shape, lambda j: (0, 0))

    gain = gain[None]
    return pl.pallas_call(
        one_back_kernel,
        grid=(width // tile,),
        out_shape=jax.ShapeDtypeStruct((rows, width), F32),
        in_specs=[
            whole(query_part),
            pl.BlockSpec((rows, pair_part.shape[1]), lambda j: (0, 0)),
            pl.BlockSpec((tile, columns), lambda j: (j, 0)),
            whole(hidden),
            whole(gain),
            whole(residual_grad),
        ],
        out_specs=pl.BlockSpec((rows, width), lambda j: (0, 0)),
        compiler_params=pltpu.CompilerParams(vmem_limit_bytes=24 << 20),
        cost_estimate=pl.CostEstimate(
            flops=2 * rows * width * columns,
            bytes_accessed=2 * width * columns,
            transcendentals=0,
        ),
        name="one_back",
    )(query_part, pair_part, in_hbm(weight), hidden, gain, residual_grad)


def send_rows(values):
    if lax.axis_size("fsdp") != 4:
        return fetch_rows(values)
    third = swap(values, "fsdp", 3)
    return [values, swap(values, "fsdp", 1), third]


def relay_rows(planes):
    if lax.axis_size("fsdp") != 4:
        return planes
    values, first, third = planes
    return [values, first, swap(third, "fsdp", 1), third]


def pass_rows(values):
    return relay_rows(send_rows(values))


def fetch_rows(values):
    count = lax.axis_size("fsdp")
    return [values] + [swap(values, "fsdp", away) for away in range(1, count)]


def sum_rows(parts, forward):
    count = len(parts)
    if count == 4 and forward:
        passed = swap(parts[2], "fsdp", 1).astype(F32)
        one = swap(parts[1], "fsdp", 1)
        third = swap((parts[3].astype(F32) + passed).astype(BF), "fsdp", 3)
        return [parts[0], one, third]
    return parts[:1] + [swap(parts[i], "fsdp", i) for i in range(1, count)]


def by_feature(values):
    rows, width = values.shape
    ctx_count, fsdp_count = lax.axis_size("ctx"), lax.axis_size("fsdp")
    blocks = values.reshape(rows, ctx_count, fsdp_count, width // (ctx_count * fsdp_count))
    return blocks.transpose(0, 2, 1, 3).reshape(rows, width)


def sum_over_ctx(part_for):
    pairs = lax.axis_size("ctx") // 2
    sent = jnp.stack([part_for(2 * pair + 1).astype(BF) for pair in range(pairs)])
    got = swap(sent, "ctx", 1)
    sums = [part_for(2 * pair).astype(F32) + got[pair].astype(F32) for pair in range(pairs)]
    total = sums[0]
    for pair in range(1, pairs):
        total = total + swap(sums[pair].astype(BF), "ctx", 2 * pair).astype(F32)
    return total


def ctx_rows_sum(values):
    height = values.shape[0] // lax.axis_size("ctx")
    me = lax.axis_index("ctx")

    def part(offset):
        return lax.dynamic_slice(
            values, ((me ^ offset) * height, 0), (height, values.shape[1])
        )

    return sum_over_ctx(part)


def key_offsets():
    count = lax.axis_size("ctx")
    return list(range(0, count, 2)) + list(range(1, count, 2))


def gather_keys(piece):
    same = [piece] + [swap(piece, "ctx", far) for far in range(2, lax.axis_size("ctx"), 2)]
    mine = jnp.concatenate(same, axis=0)
    return mine, swap(mine, "ctx", 1)


def sum_pairs(kept, sent, cosine, sine):
    _, count, width = kept.shape
    pairs = lax.axis_size("ctx") // 2
    got = swap(sent, "ctx", 1)
    sums = (kept.astype(F32) + got.astype(F32)).reshape(2, pairs, count // pairs, width)
    far = [swap(sums[:, pair].astype(BF), "ctx", 2 * pair) for pair in range(1, pairs)]
    return pair_turn(sums[:, 0], far, cosine, sine), got


def half_mask(shape):
    return lax.broadcasted_iota(jnp.int32, shape, len(shape) - 1) % 128 < HD


def turn(values, cosine, sine):
    lanes = lax.broadcasted_iota(jnp.int32, values.shape, 1) % HD
    turned = jnp.where(
        lanes < HD // 2, pltpu.roll(values, 128 - HD // 2, 1), pltpu.roll(values, HD // 2, 1)
    )
    return values * cosine + turned * sine


def doubled(tile, odd):
    wide = tile.astype(F32)
    other = pltpu.roll(wide, HD, 1)
    return jnp.where(half_mask(tile.shape) == (odd == 0), wide, other).astype(BF)


def split_heads(tile_pair):
    zero = jnp.zeros((), tile_pair.dtype)
    parts = []
    for j in range(2):
        tile = tile_pair[:, j * 128 : (j + 1) * 128]
        mask = half_mask(tile.shape)
        parts += [jnp.where(mask, tile, zero), jnp.where(mask, zero, tile)]
    return jnp.concatenate(parts, axis=0)


def merge_heads(stacked):
    rows = stacked.shape[0] // 4
    tiles = []
    for j in range(2):
        even = stacked[2 * j * rows : (2 * j + 1) * rows]
        odd = stacked[(2 * j + 1) * rows : (2 * j + 2) * rows]
        tiles.append(jnp.where(half_mask(even.shape), even, odd))
    return jnp.concatenate(tiles, axis=1)


def key_chunks(refs, chunk):
    first = 0
    for k_ref, v_ref in refs:
        for start in range(0, k_ref.shape[0], chunk):
            at = slice(start, start + chunk)
            yield first + start, k_ref.at[at, :], v_ref.at[at, :]
        first += k_ref.shape[0]


def masked_scores(keys, queries, key_ref, own_ref, start):
    allowed = key_ref[start : start + keys.shape[0], :1] <= own_ref[...]
    bias = jnp.where(allowed, 0.0, -1e30).astype(F32)
    return nt(keys, queries) + jnp.concatenate([bias] * 4, axis=1)


def attend_kernel(
    chunk, q_ref, ka_ref, va_ref, kb_ref, vb_ref, key_ref, own_ref, rows_ref, attended_ref, log_ref
):
    odd = pl.program_id(0) % 2
    rows = q_ref.shape[0]
    queries = split_heads(q_ref[...])
    parts = list(key_chunks(((ka_ref, va_ref), (kb_ref, vb_ref)), chunk))
    scores = [
        masked_scores(doubled(k_ref[...], odd), queries, key_ref, own_ref, start)
        for start, k_ref, _ in parts
    ]
    top = jnp.max(scores[0], axis=0, keepdims=True)
    for score in scores[1:]:
        top = jnp.maximum(top, jnp.max(score, axis=0, keepdims=True))
    total = jnp.zeros_like(top)
    summed = jnp.zeros((4 * rows, 128), F32)
    for score, (_, _, v_ref) in zip(scores, parts):
        weights = jnp.exp(score - top)
        total += jnp.sum(weights, axis=0, keepdims=True)
        summed += tn(weights.astype(BF), doubled(v_ref[...], odd))
    log_ref[0] = top + jnp.log(total)
    attended = merge_heads(summed / jnp.transpose(jnp.broadcast_to(total, (128, 4 * rows))))
    attended_ref[...] = attended
    rows_ref[...] = attended.astype(BF)


def key_specs(parts):
    tiles = parts[0].shape[1] // 256
    specs, arrays = [], []
    for part in parts:
        specs.append(pl.BlockSpec((part.shape[0], 128), lambda g: (0, g // 2)))
        specs.append(pl.BlockSpec((part.shape[0], 128), lambda g: (0, tiles + g // 2)))
        arrays += [part, part]
    return specs, arrays


def attend(queries, keys_values, key_anchor, own_anchor):
    rows, width = queries.shape
    count = key_anchor.shape[0]
    specs, arrays = key_specs(keys_values)
    wide = pl.BlockSpec((rows, 256), lambda g: (0, g))
    return pl.pallas_call(
        lambda *refs: attend_kernel(KEY_CHUNK, *refs),
        grid=(KV,),
        out_shape=(
            jax.ShapeDtypeStruct((rows, width), BF),
            jax.ShapeDtypeStruct((rows, width), F32),
            jax.ShapeDtypeStruct((KV, 1, 4 * rows), F32),
        ),
        in_specs=[wide]
        + specs
        + [
            pl.BlockSpec((count, 128), lambda g: (0, 0)),
            pl.BlockSpec((1, rows), lambda g: (0, 0)),
        ],
        out_specs=(wide, wide, pl.BlockSpec((1, 1, 4 * rows), lambda g: (g, 0, 0))),
        compiler_params=pltpu.CompilerParams(vmem_limit_bytes=48 << 20),
        cost_estimate=pl.CostEstimate(
            flops=4 * rows * width * count,
            bytes_accessed=4 * count * KV * HD,
            transcendentals=rows * H * count,
        ),
        name="attend",
    )(queries, *arrays, key_anchor, own_anchor)


def attend_back_kernel(
    chunk, q_ref, grad_ref, attended_ref, ka_ref, va_ref, kb_ref, vb_ref, key_ref, own_ref, log_ref,
    cos_ref, sin_ref, dq_ref, kept_ref, sent_ref,
):
    odd = pl.program_id(0) % 2
    rows = q_ref.shape[0]
    half = ka_ref.shape[0]
    queries, grads = split_heads(q_ref[...]), split_heads(grad_ref[...])
    product = grads.astype(F32) * split_heads(attended_ref[...])
    delta = jnp.sum(jnp.transpose(product), axis=0, keepdims=True)
    log_total = log_ref[0]
    total = jnp.zeros((4 * rows, 128), F32)
    keep = half_mask((chunk, 128)) == (odd == 0)
    for start, k_ref, v_ref in key_chunks(((ka_ref, va_ref), (kb_ref, vb_ref)), chunk):
        keys, values = doubled(k_ref[...], odd), doubled(v_ref[...], odd)
        scores = masked_scores(keys, queries, key_ref, own_ref, start)
        probs = jnp.exp(scores - log_total)
        value_grad = nn(probs.astype(BF), grads)
        score_grad = (probs * (nt(values, grads) - delta)).astype(BF)
        key_grad = nn(score_grad, queries)
        total += tn(score_grad, keys)
        out_ref = kept_ref if start < half else sent_ref
        at = slice(start % half, start % half + chunk)
        for part, value in enumerate((key_grad, value_grad)):
            value = (value + pltpu.roll(value, HD, 1)).astype(BF)
            out_ref[part, at, :] = jnp.where(keep, value, out_ref[part, at, :])
    merged = merge_heads(total) * (1.0 / math.sqrt(HD))
    cosine, sine = cos_ref[...], sin_ref[...]
    for j in range(2):
        tile = slice(j * 128, (j + 1) * 128)
        dq_ref[:, tile] = turn(merged[:, tile], cosine, -sine).astype(BF)


def attend_back(queries, grads, attended, keys_values, key_anchor, own_anchor, logs, cosine, sine):
    rows, width = queries.shape
    count = key_anchor.shape[0]
    specs, arrays = key_specs(keys_values)
    wide = pl.BlockSpec((rows, 256), lambda g: (0, g))
    small = pl.BlockSpec((rows, 128), lambda g: (0, 0))
    pair = pl.BlockSpec((2, count // 2, 128), lambda g: (0, 0, g // 2))
    return pl.pallas_call(
        lambda *refs: attend_back_kernel(KEY_CHUNK, *refs),
        grid=(KV,),
        out_shape=(
            jax.ShapeDtypeStruct((rows, width), BF),
            jax.ShapeDtypeStruct((2, count // 2, KV * HD), BF),
            jax.ShapeDtypeStruct((2, count // 2, KV * HD), BF),
        ),
        in_specs=[wide, wide, wide]
        + specs
        + [
            pl.BlockSpec((count, 128), lambda g: (0, 0)),
            pl.BlockSpec((1, rows), lambda g: (0, 0)),
            pl.BlockSpec((1, 1, 4 * rows), lambda g: (g, 0, 0)),
            small,
            small,
        ],
        out_specs=(wide, pair, pair),
        compiler_params=pltpu.CompilerParams(vmem_limit_bytes=48 << 20),
        cost_estimate=pl.CostEstimate(
            flops=10 * rows * width * count,
            bytes_accessed=8 * count * KV * HD,
            transcendentals=rows * H * count,
        ),
        name="attend_back",
    )(queries, grads, attended, *arrays, key_anchor, own_anchor, logs, cosine, sine)


def pair_turn_kernel(copies, own_ref, *refs):
    got, (cos_ref, sin_ref, y_ref) = refs[:-3], refs[-3:]
    total = own_ref[...]
    for ref in got:
        total = total + ref[...].astype(F32)
    cosine, sine = cos_ref[...], sin_ref[...]
    _, rows, width = total.shape
    tiles = [
        turn(total[0, :, start : start + 128], cosine, -sine).astype(BF)
        for start in range(0, width, 128)
    ]
    values = total[1].astype(BF)
    for copy in range(copies):
        at = slice(copy * rows, (copy + 1) * rows)
        for i, tile in enumerate(tiles):
            y_ref[at, i * 128 : (i + 1) * 128] = tile
        y_ref[at, width:] = values


def pair_turn(own, got, cosine, sine):
    _, rows, width = own.shape
    copies = lax.axis_size("fsdp")
    return pl.pallas_call(
        lambda *refs: pair_turn_kernel(copies, *refs),
        out_shape=jax.ShapeDtypeStruct((copies * rows, 2 * width), BF),
        name="pair_turn",
    )(own, *got, cosine, sine)


def join_rows(x_buf, refs):
    @pl.when((pl.program_id(0) == 0))
    def _():
        rows = refs[0].shape[0]
        for i, ref in enumerate(refs):
            x_buf[i * rows : (i + 1) * rows] = ref[...]


def ffn_kernel(count, earlier, *refs):
    rows_refs, (act_ref, w_ref), refs = refs[:count], refs[count : count + 2], refs[count + 2 :]
    out_ref, refs = refs[earlier], refs[earlier + 1 :]
    sum_refs, (x_buf, sum_buf) = refs[:count], refs[count:]
    join_rows(x_buf, rows_refs)
    step = pl.program_id(0)
    gate_w, up_w = w_ref[0], w_ref[1]
    x = x_buf[...]
    gate, up = nn(x, gate_w), nn(x, up_w)
    act_grad = act_ref[...]
    sig = jax.nn.sigmoid(gate)
    silu = gate * sig
    gate_grad = (act_grad * up * sig * (1.0 + gate * (1.0 - sig))).astype(BF)
    up_grad = (act_grad * silu).astype(BF)
    out_ref[0], out_ref[1], out_ref[2] = gate_grad, up_grad, (silu * up).astype(BF)
    part = nt(gate_grad, gate_w) + nt(up_grad, up_w)

    @pl.when(step == 0)
    def _():
        sum_buf[...] = part

    @pl.when(step > 0)
    def _():
        sum_buf[...] += part

    @pl.when(step == pl.num_programs(0) - 1)
    def _():
        rows = sum_refs[0].shape[0]
        for i, ref in enumerate(sum_refs):
            ref[...] = sum_buf[i * rows : (i + 1) * rows].astype(ref.dtype)


def ffn_middle(blocks, act_grad, half, weights, kinds, earlier):
    width = blocks[0].shape[1]
    rows = blocks[0].shape[0] * len(blocks)
    hidden = weights.shape[2]
    tile = FFN_TILE
    whole = [pl.BlockSpec(block.shape, lambda j: (0, 0)) for block in blocks]
    out = pl.pallas_call(
        lambda *refs: ffn_kernel(len(blocks), len(earlier), *refs),
        grid=(hidden // tile,),
        out_shape=(
            pltpu.HBM((3, 2 * rows, hidden), BF),
            *[jax.ShapeDtypeStruct(block.shape, kind) for block, kind in zip(blocks, kinds)],
        ),
        in_specs=whole
        + [
            pl.BlockSpec((rows, tile), lambda j: (half, j)),
            pl.BlockSpec((2, width, tile), lambda j: (0, 0, j)),
        ]
        + [pl.BlockSpec(memory_space=pltpu.HBM)] * len(earlier),
        out_specs=(pl.BlockSpec((3, rows, tile), lambda j: (0, half, j)), *whole),
        input_output_aliases={len(blocks) + 2: 0} if earlier else {},
        scratch_shapes=[pltpu.VMEM((rows, width), BF), pltpu.VMEM((rows, width), F32)],
        compiler_params=pltpu.CompilerParams(vmem_limit_bytes=40 << 20),
        cost_estimate=pl.CostEstimate(
            flops=8 * rows * width * hidden,
            bytes_accessed=4 * width * hidden,
            transcendentals=rows * hidden,
        ),
        name="ffn_middle",
    )(*blocks, act_grad, weights, *earlier)
    return out[0], list(out[1:])


def products_kernel(count, added, ids_ref, *refs):
    in_refs, grad_refs = refs[: 2 * count], refs[2 * count : 4 * count]
    right, rest = refs[4 * count], refs[4 * count + 1 :]
    out_ref, left = rest[-2:]

    def join(blocks):
        rows, height = blocks[0].shape
        for j in range(2):
            for i in range(count):
                at = (slice(i * rows, (i + 1) * rows), slice(j * height, (j + 1) * height))
                left[at] = blocks[j * count + i][...]

    @pl.when(pl.program_id(0) < 2)
    def _():
        join(in_refs)

    @pl.when(pl.program_id(0) == 2)
    def _():
        join(grad_refs)

    part = tn(left[...], right[0])
    if added:
        part = part + rest[0][0].astype(F32)
    out_ref[0] = part.astype(BF)


def half_products(rows_in, rows_out, parts, got):
    count = len(rows_in)
    rows, width = rows_in[0].shape
    hidden = parts.shape[2]
    ctx_count = lax.axis_size("ctx")
    height = width // ctx_count
    last = ctx_count // 4 - 1

    def column(i, j, ids_ref):
        own = ids_ref[0] % 2
        return 2 * (2 * i + j) + (own if got is not None else 1 - own)

    def left(j):
        return pl.BlockSpec(
            (rows, height),
            lambda k, i, ids_ref: (0, column(jnp.where(k < 2, i, last), j, ids_ref)),
        )

    def grad(j):
        return pl.BlockSpec(
            (rows, height),
            lambda k, i, ids_ref: (0, column(jnp.where(k == 2, i, 0), j, ids_ref)),
        )

    right = pl.BlockSpec((1, rows * count, hidden), lambda k, i, ids_ref: (k, 0, 0))
    out = pl.BlockSpec((1, 2 * height, hidden), lambda k, i, ids_ref: (k, i, 0))
    extra = [] if got is None else [got]
    return pl.pallas_call(
        lambda *refs: products_kernel(count, got is not None, *refs),
        grid_spec=pltpu.PrefetchScalarGridSpec(
            num_scalar_prefetch=1,
            grid=(3, ctx_count // 4),
            in_specs=[left(0)] * count
            + [left(1)] * count
            + [grad(0)] * count
            + [grad(1)] * count
            + [right]
            + [out] * len(extra),
            out_specs=out,
            scratch_shapes=[pltpu.VMEM((count * rows, 2 * height), BF)],
        ),
        out_shape=pltpu.HBM((3, width // 2, hidden), BF),
        compiler_params=pltpu.CompilerParams(vmem_limit_bytes=32 << 20),
        cost_estimate=pl.CostEstimate(
            flops=3 * count * rows * width * hidden,
            bytes_accessed=3 * width * hidden,
            transcendentals=0,
        ),
        name="kept_products" if extra else "sent_products",
    )(jnp.stack(ids()), *rows_in, *rows_in, *rows_out, *rows_out, parts, *extra)


def ffn_gradient(rows_in, rows_out, parts):
    count = lax.axis_size("ctx")
    if count % 4 or (rows_in[0].shape[1] // count) % 128:
        left, grad = (jnp.concatenate(rows, axis=0) for rows in (rows_in, rows_out))
        products = [tn(left, parts[0]), tn(left, parts[1]), tn(grad, parts[2])]
        products = jnp.stack(products, axis=1).astype(BF)
        return lax.psum_scatter(products, "ctx", scatter_dimension=0, tiled=True)
    sent = half_products(rows_in, rows_out, parts, None)
    got = swap(sent, "ctx", 1)
    kept = half_products(rows_in, rows_out, parts, got).transpose(1, 0, 2)
    groups = [list(range(core, count, 2)) for core in range(2)]
    return lax.psum_scatter(kept, "ctx", scatter_dimension=0, tiled=True, axis_index_groups=groups)


def down_back_kernel(count, *refs):
    rows_refs, (w_ref, y_ref, x_buf) = refs[:count], refs[count:]
    join_rows(x_buf, rows_refs)
    y_ref[...] = nn(x_buf[...], w_ref[0])


def down_back(blocks, weights):
    width = blocks[0].shape[1]
    rows = blocks[0].shape[0] * len(blocks)
    hidden = weights.shape[2]
    tile = FFN_TILE
    return pl.pallas_call(
        lambda *refs: down_back_kernel(len(blocks), *refs),
        grid=(hidden // tile,),
        out_shape=pltpu.HBM((rows, hidden), F32),
        in_specs=[pl.BlockSpec(block.shape, lambda j: (0, 0)) for block in blocks]
        + [pl.BlockSpec((1, width, tile), lambda j: (2, 0, j))],
        out_specs=pl.BlockSpec((rows, tile), lambda j: (0, j)),
        scratch_shapes=[pltpu.VMEM((rows, width), BF)],
        compiler_params=pltpu.CompilerParams(vmem_limit_bytes=24 << 20),
        cost_estimate=pl.CostEstimate(
            flops=2 * rows * width * hidden,
            bytes_accessed=2 * width * hidden,
            transcendentals=0,
        ),
        name="down_back",
    )(*blocks, weights)


def down_kernel(x_ref, w_ref, *y_refs):
    rows = x_ref.shape[1] // len(y_refs)
    total = nt(x_ref[0], w_ref[0])
    for i, y_ref in enumerate(y_refs):
        y_ref[...] = total[i * rows : (i + 1) * rows].astype(y_ref.dtype)


def down_forward(parts, weights, count):
    _, rows, hidden = parts.shape
    width = weights.shape[1]
    tile = FFN_TILE
    height = rows // count
    return pl.pallas_call(
        down_kernel,
        grid=(width // tile,),
        out_shape=tuple(
            jax.ShapeDtypeStruct((height, width), BF if i else F32) for i in range(count)
        ),
        in_specs=[
            pl.BlockSpec((1, rows, hidden), lambda j: (2, 0, 0)),
            pl.BlockSpec((1, tile, hidden), lambda j: (2, j, 0)),
        ],
        out_specs=tuple(pl.BlockSpec((height, tile), lambda j: (0, j)) for _ in range(count)),
        compiler_params=pltpu.CompilerParams(vmem_limit_bytes=24 << 20),
        cost_estimate=pl.CostEstimate(
            flops=2 * rows * width * hidden,
            bytes_accessed=2 * width * hidden,
            transcendentals=0,
        ),
        name="down_forward",
    )(parts, weights)


def share_kernel(count, sizes, ids_ref, *refs):
    products = len(sizes)
    lefts = [refs[i * count : (i + 1) * count] for i in range(products)]
    rest = refs[products * count :]
    rights = []
    for size in sizes:
        rights.append(rest[:size])
        rest = rest[size:]
    bufs = rest[len(rest) - products :]
    terms, (kept_ref, sent_ref) = rest[: -products - 2], rest[-products - 2 : -products]
    half = kept_ref.shape[1]
    own = ids_ref[0] % 2 == 0

    @pl.when(pl.program_id(0) == 0)
    def _():
        for parts, buf in zip(rights, bufs):
            rows = buf.shape[0] // count
            for away in range(count):
                if len(parts) > 1:
                    block = parts[away][...]
                else:
                    start = (ids_ref[1] ^ away) * rows
                    block = parts[0][pl.ds(pl.multiple_of(start, 16), rows), :]
                buf[away * rows : (away + 1) * rows] = block

    def emit(part, column):
        at = slice(column, column + part.shape[1])
        kept_ref[0, :, at] = jnp.where(own, part[:half], part[half:])
        sent_ref[0, :, at] = jnp.where(own, part[half:], part[:half])

    column = 0
    for left, buf in zip(lefts, bufs):
        joined = jnp.concatenate([ref[...] for ref in left], axis=0)
        emit(tn(joined, buf[...]).astype(BF), column)
        column += buf.shape[1]
    for term in terms:
        tall = jnp.broadcast_to(term[...], (128, term.shape[1]))
        emit(jnp.transpose(tall).astype(BF), column)
        column += 128


def share_products(lefts, rights, terms):
    ctx_count = lax.axis_size("ctx")
    pairs = ctx_count // 2
    count = len(lefts[0])
    rows, width = lefts[0][0].shape
    height = width // ctx_count
    groups = [right if isinstance(right, list) else [right] for right in rights]
    widths = [group[0].shape[1] for group in groups]
    columns = sum(widths) + 128 * len(terms)

    def place(j, ids_ref):
        return (0, (ids_ref[0] // 2) ^ j)

    def whole(array):
        return pl.BlockSpec(array.shape, lambda j, ids_ref: (0, 0))

    shape = jax.ShapeDtypeStruct((pairs, height, columns), BF)
    out = pl.BlockSpec((1, height, columns), lambda j, ids_ref: (j, 0, 0))
    flat_lefts = [block for left in lefts for block in left]
    flat_rights = [block for group in groups for block in group]
    return pl.pallas_call(
        lambda *refs: share_kernel(count, [len(group) for group in groups], *refs),
        grid_spec=pltpu.PrefetchScalarGridSpec(
            num_scalar_prefetch=1,
            grid=(pairs,),
            in_specs=[pl.BlockSpec((rows, 2 * height), place) for _ in flat_lefts]
            + [whole(block) for block in flat_rights]
            + [pl.BlockSpec((1, 2 * height), place) for _ in terms],
            out_specs=(out, out),
            scratch_shapes=[pltpu.VMEM((count * rows, size), BF) for size in widths],
        ),
        out_shape=(shape, shape),
        compiler_params=pltpu.CompilerParams(vmem_limit_bytes=32 << 20),
        cost_estimate=pl.CostEstimate(
            flops=2 * count * rows * width * columns,
            bytes_accessed=2 * (count * rows + columns) * width,
            transcendentals=0,
        ),
        name="share_terms" if terms else "share_products",
    )(jnp.stack(ids()), *flat_lefts, *flat_rights, *[term[None] for term in terms])


def in_fsdp_order(value):
    if not isinstance(value, list):
        return value
    plane = lax.axis_index("fsdp")
    stacked = jnp.stack(value)
    parts = [
        lax.dynamic_index_in_dim(stacked, plane ^ away, 0, keepdims=False)
        for away in range(len(value))
    ]
    return jnp.concatenate(parts, axis=0)


def share_start(lefts, rights, terms):
    pairs = lax.axis_size("ctx") // 2
    if (lefts[0][0].shape[1] // pairs) % 128:
        values = [tn(in_fsdp_order(a), in_fsdp_order(b)) for a, b in zip(lefts, rights)]
        values += [jnp.broadcast_to(term[:, None], (term.shape[0], 128)) for term in terms]
        return [ctx_rows_sum(jnp.concatenate(values, axis=1))]
    kept, sent = share_products(lefts, rights, terms)
    got = swap(sent, "ctx", 1)
    parts = [kept[0], got[0]]
    for pair in range(1, pairs):
        part = (kept[pair].astype(F32) + got[pair].astype(F32)).astype(BF)
        parts.append(swap(part, "ctx", 2 * pair))
    return parts


def share_finish(parts):
    total = parts[0].astype(F32)
    for part in parts[1:]:
        total = total + part.astype(F32)
    return total


def own_rows_of(values, height):
    index = lax.axis_index("ctx") * lax.axis_size("fsdp") + lax.axis_index("fsdp")
    return lax.dynamic_slice_in_dim(values, index * height, height, 0)


def feature_parts(values):
    count, plane = lax.axis_size("fsdp"), lax.axis_index("fsdp")
    values = by_feature(values)
    rows, width = values.shape
    width //= count
    return [
        lax.dynamic_slice(values, (0, (plane ^ away) * width), (rows, width))
        for away in range(count)
    ]


def feature_rows(parts):
    return [swap(part, "fsdp", away) if away else part for away, part in enumerate(parts)]


def own_features(terms):
    ctx_count, fsdp_count = lax.axis_size("ctx"), lax.axis_size("fsdp")
    total = jnp.stack(terms)
    away = 1
    while away < fsdp_count:
        total = total + swap(total, "fsdp", away)
        away *= 2
    blocks = total.reshape(len(terms), ctx_count, fsdp_count, -1)
    own = lax.dynamic_index_in_dim(blocks, lax.axis_index("fsdp"), 2, keepdims=False)
    own = own.reshape(len(terms), -1)
    return [own[i] for i in range(len(terms))]


def layer(
    hidden_in,
    out_grad,
    positions,
    block_order,
    attn_gain,
    ffn_gain,
    qkv_weight,
    out_weight,
    ffn_weight,
):
    ctx_count, fsdp_count = lax.axis_size("ctx"), lax.axis_size("fsdp")
    me, _ = ids()
    rows = hidden_in.shape[1]
    queries_width, kv_width = H * HD, KV * HD
    ffn_parts = in_hbm(ffn_weight.transpose(1, 0, 2))

    frequency = jnp.power(ROPE_BASE, -(jnp.arange(HD // 2, dtype=F32) * 2.0 / HD))
    angles = positions[0].astype(F32)[:, None] * frequency[None, :]
    cosine = jnp.tile(jnp.cos(angles), (1, 4))
    sine = jnp.tile(jnp.concatenate([-jnp.sin(angles), jnp.sin(angles)], axis=1), (1, 2))
    own_anchor = anchors_of(block_order, me, rows)[None]
    key_anchor = jnp.concatenate(
        [anchors_of(block_order, me ^ offset, rows) for offset in key_offsets()]
    )
    key_anchor = jnp.broadcast_to(key_anchor[:, None], (rows * ctx_count, 128))

    inputs = hidden_in[0].astype(F32)
    grad_in = out_grad[0]
    scale_one = norm_scale(inputs)
    normed_one = (inputs * scale_one * attn_gain).astype(BF)

    one_parts = feature_parts(normed_one)
    fast = ctx_count == 8 and (qkv_weight.shape[1] // ctx_count) % 128 == 0
    if fast:
        early = (cosine, sine, own_anchor, key_anchor, one_parts)
        qkv_pieces, marks = gather_pieces(qkv_weight, early)
        out_blocks = gather_blocks(out_weight, *marks)
        queries, pair, qkv_full = pieces_forward(
            normed_one, qkv_weight, qkv_pieces, cosine, sine
        )
    else:
        marks = (normed_one, normed_one)
        out_blocks = gather_blocks(out_weight, *marks)
        qkv_full = whole_of(qkv_weight, gather_blocks(qkv_weight, normed_one, normed_one))
        projected = nn(normed_one, qkv_full)
        turned = rotate(
            projected[:, : queries_width + kv_width].reshape(rows, H + KV, HD), positions[0]
        ).reshape(rows, queries_width + kv_width)
        queries = (turned[:, :queries_width] * (1.0 / math.sqrt(HD))).astype(BF)
        pair = jnp.concatenate(
            [turned[:, queries_width:], projected[:, queries_width + kv_width :]], axis=1
        ).astype(BF)
    own_one = feature_rows(after(one_parts, pair))
    keys_values = gather_keys(pair)
    rows_out = send_rows(after(grad_in, pair))
    attn_rows, attended, logs = attend(queries, keys_values, key_anchor, own_anchor)
    rows_out = relay_rows(after(rows_out, attn_rows))
    residual, normed_two = out_forward(
        attn_rows, out_weight, out_blocks, hidden_in[0], ffn_gain
    )
    scale_two = norm_scale(residual)
    rows_in = pass_rows(normed_two)
    rows_out = after(rows_out, normed_two)
    act_grad = down_back(rows_out, ffn_parts)

    all_attn = pass_rows(after(attn_rows, rows_in[2]))
    parts, partial = [], []
    half = fsdp_count // 2
    passing = 3 if fsdp_count == 4 else 0
    for index in range(2):
        blocks = rows_in[index * half : (index + 1) * half]
        kinds = [F32 if index * half + i in (0, passing) else BF for i in range(half)]
        out, terms = ffn_middle(blocks, in_hbm(act_grad), index, ffn_parts, kinds, parts)
        parts, partial = [out], partial + terms
    parts = parts[0]
    sum_grad = share_finish(sum_rows(partial, True))
    ffn_weight_grad = ffn_gradient(rows_in, rows_out, parts)
    ffn_weight_grad = ffn_weight_grad.astype(F32)
    out_partial = list(down_forward(parts, ffn_parts, fsdp_count))

    unit_two = residual * scale_two
    ffn_gain_term = jnp.sum(sum_grad * unit_two, axis=0)
    scaled_two = ffn_gain * sum_grad
    residual_grad = grad_in.astype(F32) + scale_two * (
        scaled_two - unit_two * jnp.mean(scaled_two * unit_two, axis=-1, keepdims=True)
    )
    residual_bf = residual_grad.astype(BF)
    out_sum = sum_rows([after(part, residual_bf) for part in out_partial], False)
    (ffn_term,) = own_features([ffn_gain_term])
    attn_grad = out_back(residual_bf, out_weight, out_blocks)
    query_part, kept, sent = attend_back(
        queries, attn_grad, attended, keys_values, key_anchor, own_anchor, logs, cosine, sine
    )
    query_planes = pass_rows(query_part)
    pair_copies, near = sum_pairs(kept, sent, cosine, sine)
    own_residual = feature_rows(feature_parts(after(residual_bf, near)))
    all_pair = lax.all_to_all(pair_copies, "fsdp", split_axis=0, concat_axis=0, tiled=True)
    input_grad = one_back(
        query_part, pair_copies, qkv_full, hidden_in[0], attn_gain, residual_grad
    )
    out_sums = share_start([own_residual], [after(all_attn, input_grad)], [])
    output = (residual + share_finish(after(out_sum, input_grad))).astype(BF)
    qkv_sums = share_start([own_one, own_one], [after(query_planes, output), all_pair], [ffn_term])
    qkv_sums = share_finish(qkv_sums)
    out_weight_grad = share_finish(after(out_sums, qkv_sums))
    qkv_grad = qkv_sums[:, : qkv_weight.shape[1]]
    features = own_rows_of(attn_gain, qkv_grad.shape[0])
    gain_grad = jnp.sum(own_rows_of(qkv_full, qkv_grad.shape[0]).astype(F32) * qkv_grad, axis=1)
    return (
        output[None],
        input_grad[None],
        qkv_grad,
        out_weight_grad,
        ffn_weight_grad,
        gain_grad / features,
        qkv_sums[:, qkv_weight.shape[1]],
    )


def solution(mesh):
    step = sharded(mesh)
    return step


def sharded(mesh):
    return jax.shard_map(
        layer,
        mesh=mesh,
        in_specs=(
            P("fsdp", "ctx", None),
            P("fsdp", "ctx", None),
            P("fsdp", "ctx"),
            P(),
            P(),
            P(),
            P("fsdp", None),
            P("fsdp", None),
            P(None, None, "fsdp"),
        ),
        out_specs=(
            P("fsdp", "ctx", None),
            P("fsdp", "ctx", None),
            P(("ctx", "fsdp"), None),
            P(("ctx", "fsdp"), None),
            P("ctx", None, "fsdp"),
            P(("ctx", "fsdp")),
            P(("ctx", "fsdp")),
        ),
        check_vma=False,
    )
```

```python
import math

import jax
import jax.numpy as jnp
from jax import lax
from jax.experimental import pallas as pl
from jax.experimental.pallas import tpu as pltpu
from jax.sharding import PartitionSpec as P


H = 32
KV = 8
HD = 64

NORM_EPS = 1e-05
ROPE_BASE = 500000.0
FFN_TILE = 512
KEY_CHUNK = 256


BF = jnp.bfloat16
F32 = jnp.float32


def mm(a, b, dims):
    return lax.dot_general(a, b, (dims, ((), ())), preferred_element_type=F32)


def nn(a, b):
    return mm(a, b, ((1,), (0,)))


def nt(a, b):
    return mm(a, b, ((1,), (1,)))


def tn(a, b):
    return mm(a, b, ((0,), (0,)))


def swap(value, axis, offset):
    count = lax.axis_size(axis)
    return lax.ppermute(value, axis, [(i, i ^ offset) for i in range(count)])


def rotate(values, token_places):
    head_dim = values.shape[-1]
    half_dim = head_dim // 2
    frequency = jnp.power(ROPE_BASE, -(jnp.arange(half_dim, dtype=F32) * 2.0 / head_dim))
    angles = token_places.astype(F32)[:, None] * frequency[None, :]
    cosine = jnp.concatenate([jnp.cos(angles), jnp.cos(angles)], axis=-1)[:, None, :]
    sine_part = jnp.concatenate([jnp.sin(angles), jnp.sin(angles)], axis=-1)[:, None, :]
    turned = jnp.concatenate([-values[..., half_dim:], values[..., :half_dim]], axis=-1)
    return values * cosine + turned * sine_part


def norm_scale(values):
    return lax.rsqrt(jnp.mean(values * values, axis=-1, keepdims=True) + NORM_EPS)


def lookup(entries, row_ids):
    matches = row_ids[:, None] == jnp.arange(entries.shape[0], dtype=jnp.int32)[None, :]
    return jnp.sum(jnp.where(matches, entries[None, :], 0), axis=1)


def anchors_of(block_order, owner, row_count):
    block_len = row_count // 2
    row_ids = owner * row_count + jnp.arange(row_count, dtype=jnp.int32)
    return lookup(block_order, row_ids // block_len) * block_len + row_ids % block_len


def after(value, *earlier):
    return lax.optimization_barrier((value, earlier))[0]


def ids():
    return lax.axis_index("ctx"), lax.axis_index("fsdp")


def gather_pieces(weight, early):
    rows, columns = weight.shape
    share = columns // lax.axis_size("ctx")
    half = rows // 2
    mine = lax.dynamic_slice(weight, (0, lax.axis_index("ctx") * share), (rows, share))
    planes = {}
    planes[3] = swap(mine, "fsdp", 3)
    planes[1] = swap(mine, "fsdp", 1)
    planes[2] = swap(after(planes[3], early), "fsdp", 1)
    pieces = []
    for away in (1, 3, 2):
        first = planes[away]
        along_x, along_y = swap(first, "ctx", 2), swap(first, "ctx", 4)
        top, low = swap(along_y[:half], "ctx", 2), swap(along_x[half:], "ctx", 4)
        parts = [(0, 0, first), (2, 0, along_x), (4, 0, along_y), (6, 0, top), (6, half, low)]
        for offset, start, part in parts:
            pieces.append((away, offset, start, part))
            pieces.append((away, offset + 1, start, swap(part, "ctx", 1)))
    return pieces, (planes[2], (pieces[-4][3], pieces[-2][3]))


def pieces_kernel(places, rows_in, share, ids_ref, x_ref, own_ref, *refs):
    count = len(places)
    piece_refs, refs = refs[:count], refs[count:]
    cos_ref, sin_ref, q_ref, pair_ref, full_ref, y_ref, buf, in_sems, out_sems = refs
    me, plane = ids_ref[0], ids_ref[1]

    def block(away):
        return pl.ds(pl.multiple_of((plane ^ away) * rows_in, 128), rows_in)

    own_copy = pltpu.make_async_copy(own_ref, buf.at[block(0)], in_sems.at[count])
    own_copy.start()
    copies = []
    for i, (away, offset, start, height) in enumerate(places):
        at = pl.ds(pl.multiple_of((plane ^ away) * rows_in + start, 128), height)
        columns = pl.ds(pl.multiple_of((me ^ offset) * share, 128), share)
        copies.append(pltpu.make_async_copy(piece_refs[i], buf.at[at, columns], in_sems.at[i]))
        copies[-1].start()
    outs = []
    order = [0] + list(dict.fromkeys(away for away, _, _, _ in places))
    for away in order:
        if away:
            for copy, place in zip(copies, places):
                if place[0] == away:
                    copy.wait()
        else:
            own_copy.wait()
        outs.append(
            pltpu.make_async_copy(buf.at[block(away)], full_ref.at[block(away)], out_sems.at[away])
        )
        outs[-1].start()
        part = nn(x_ref[:, block(away)], buf[block(away)])
        y_ref[...] = part if away == 0 else y_ref[...] + part
    cosine, sine = cos_ref[...], sin_ref[...]
    queries, keys = H * HD, KV * HD
    for start in range(0, queries + keys, 128):
        tile = turn(y_ref[:, start : start + 128], cosine, sine)
        if start < queries:
            q_ref[:, start : start + 128] = (tile * (1.0 / math.sqrt(HD))).astype(BF)
        else:
            pair_ref[:, start - queries : start - queries + 128] = tile.astype(BF)
    pair_ref[:, keys:] = y_ref[:, queries + keys :].astype(BF)
    for copy in outs:
        copy.wait()


def pieces_forward(x, own, pieces, cosine, sine):
    me, plane = ids()
    rows_in, columns = own.shape
    rows, width = x.shape
    share = columns // lax.axis_size("ctx")
    places = tuple((away, offset, start, part.shape[0]) for away, offset, start, part in pieces)
    arrays = [part for _, _, _, part in pieces]
    hbm, vmem = pl.BlockSpec(memory_space=pltpu.HBM), pl.BlockSpec(memory_space=pltpu.VMEM)
    return pl.pallas_call(
        lambda *refs: pieces_kernel(places, rows_in, share, *refs),
        out_shape=(
            jax.ShapeDtypeStruct((rows, H * HD), BF),
            jax.ShapeDtypeStruct((rows, 2 * KV * HD), BF),
            pltpu.HBM((width, columns), BF),
        ),
        in_specs=[pl.BlockSpec(memory_space=pltpu.SMEM), vmem, hbm]
        + [hbm] * len(arrays)
        + [vmem, vmem],
        out_specs=(vmem, vmem, hbm),
        scratch_shapes=[
            pltpu.VMEM((rows, columns), F32),
            pltpu.VMEM((width, columns), BF),
            pltpu.SemaphoreType.DMA((len(arrays) + 1,)),
            pltpu.SemaphoreType.DMA((width // rows_in,)),
        ],
        compiler_params=pltpu.CompilerParams(vmem_limit_bytes=32 << 20),
        cost_estimate=pl.CostEstimate(
            flops=2 * rows * width * columns, bytes_accessed=4 * width * columns, transcendentals=0
        ),
        name="pieces_forward",
    )(jnp.stack([me, plane]), x, in_hbm(own), *[in_hbm(part) for part in arrays], cosine, sine)


def gather_blocks(weight, before_fsdp, before_ctx):
    rows, columns = weight.shape
    me, plane = ids()
    share = columns // lax.axis_size("ctx")
    mine = lax.dynamic_slice(weight, (0, me * share), (rows, share))
    planes = lax.all_gather(after(mine, before_fsdp), "fsdp")
    others = jnp.stack(
        [
            lax.dynamic_index_in_dim(planes, plane ^ away, 0, keepdims=False)
            for away in range(1, planes.shape[0])
        ]
    )
    return lax.all_gather(after(others, before_ctx), "ctx")


def whole_of(own, blocks):
    ctx_count, others, rows, share = blocks.shape
    plane = lax.axis_index("fsdp")
    columns = ctx_count * share
    full = jnp.zeros(((others + 1) * rows, columns), own.dtype)
    full = lax.dynamic_update_slice(full, own, (plane * rows, 0))
    for away in range(1, others + 1):
        part = blocks[:, away - 1].transpose(1, 0, 2).reshape(rows, columns)
        full = lax.dynamic_update_slice(full, part, ((plane ^ away) * rows, 0))
    return full


def in_hbm(value):
    return pltpu.with_memory_space_constraint(value, pltpu.HBM)


def out_kernel(back, ids_ref, x_ref, own_ref, blocks_ref, *refs):
    hidden_ref, gain_ref = (None, None) if back else refs[:2]
    outs = refs if back else refs[2:]
    own_buf, buf, sems = outs[-3:]
    ctx_count, others, rows, share = buf.shape
    plane = ids_ref[1]

    def block_copy(c):
        return pltpu.make_async_copy(blocks_ref.at[c], buf.at[c], sems.at[c])

    own_copy = pltpu.make_async_copy(own_ref, own_buf, sems.at[ctx_count])
    own_copy.start()
    for c in range(ctx_count):
        block_copy(c).start()

    def features(away):
        return pl.ds(pl.multiple_of((plane ^ away) * rows, 128), rows)

    def columns(c):
        return pl.ds(pl.multiple_of(c * share, 128), share)

    own_copy.wait()
    if back:
        y_ref = outs[0]

        @pl.loop(0, ctx_count)
        def _(c):
            block_copy(c).wait()
            total = nn(x_ref[:, features(0)], own_buf[:, columns(c)])
            for away in range(1, others + 1):
                total += nn(x_ref[:, features(away)], buf[c, away - 1])
            y_ref[:, columns(c)] = total.astype(BF)

        return
    residual_ref, normed_ref = outs[:2]
    residual_ref[...] = hidden_ref[...].astype(F32)

    @pl.loop(0, ctx_count)
    def _(c):
        block_copy(c).wait()
        x = x_ref[:, columns(c)]
        residual_ref[:, features(0)] += nt(x, own_buf[:, columns(c)])
        for away in range(1, others + 1):
            residual_ref[:, features(away)] += nt(x, buf[c, away - 1])

    residual = residual_ref[...]
    normed_ref[...] = (residual * norm_scale(residual) * gain_ref[...]).astype(BF)


def out_call(back, x, own, blocks, extra, out_shape):
    vmem, hbm = pl.BlockSpec(memory_space=pltpu.VMEM), pl.BlockSpec(memory_space=pltpu.HBM)
    return pl.pallas_call(
        lambda *refs: out_kernel(back, *refs),
        out_shape=out_shape,
        in_specs=[pl.BlockSpec(memory_space=pltpu.SMEM), vmem, hbm, hbm] + [vmem] * len(extra),
        out_specs=jax.tree.map(lambda _: vmem, out_shape),
        scratch_shapes=[
            pltpu.VMEM(own.shape, own.dtype),
            pltpu.VMEM(blocks.shape, blocks.dtype),
            pltpu.SemaphoreType.DMA((blocks.shape[0] + 1,)),
        ],
        compiler_params=pltpu.CompilerParams(vmem_limit_bytes=24 << 20),
        cost_estimate=pl.CostEstimate(
            flops=2 * x.shape[0] * own.size * (blocks.shape[1] + 1),
            bytes_accessed=2 * own.size * (blocks.shape[1] + 1),
            transcendentals=0,
        ),
        name="out_back" if back else "out_forward",
    )(jnp.stack(ids()), x, in_hbm(own), in_hbm(blocks), *extra)


def out_forward(attn_rows, own, blocks, hidden, gain):
    if blocks.shape[3] % 128:
        residual = hidden.astype(F32) + nt(attn_rows, whole_of(own, blocks))
        return residual, (residual * norm_scale(residual) * gain).astype(BF)
    out_shape = (
        jax.ShapeDtypeStruct(hidden.shape, F32),
        jax.ShapeDtypeStruct(hidden.shape, BF),
    )
    return out_call(False, attn_rows, own, blocks, [hidden, gain[None]], out_shape)


def out_back(x, own, blocks):
    if blocks.shape[3] % 128:
        return nn(x, whole_of(own, blocks)).astype(BF)
    out_shape = jax.ShapeDtypeStruct((x.shape[0], own.shape[1]), BF)
    return out_call(True, x, own, blocks, [], out_shape)


def one_back_kernel(
    query_ref, pair_ref, w_ref, hidden_ref, gain_ref, residual_ref, y_ref
):
    step = pl.program_id(0)
    rows = w_ref.shape[0]
    split = query_ref.shape[1]
    y_ref[:, pl.ds(pl.multiple_of(step * rows, 128), rows)] = nt(
        query_ref[...], w_ref[:, :split]
    ) + nt(pair_ref[...], w_ref[:, split:])

    @pl.when(step == pl.num_programs(0) - 1)
    def _():
        grad = y_ref[...]
        inputs = hidden_ref[...].astype(F32)
        scale = norm_scale(inputs)
        unit = inputs * scale
        scaled = gain_ref[...] * grad
        y_ref[...] = residual_ref[...] + scale * (
            scaled - unit * jnp.mean(scaled * unit, axis=-1, keepdims=True)
        )


def one_back(query_part, pair_part, weight, hidden, gain, residual_grad):
    rows, width = hidden.shape
    columns = weight.shape[1]
    tile = FFN_TILE

    def whole(array):
        return pl.BlockSpec(array.shape, lambda j: (0, 0))

    gain = gain[None]
    return pl.pallas_call(
        one_back_kernel,
        grid=(width // tile,),
        out_shape=jax.ShapeDtypeStruct((rows, width), F32),
        in_specs=[
            whole(query_part),
            pl.BlockSpec((rows, pair_part.shape[1]), lambda j: (0, 0)),
            pl.BlockSpec((tile, columns), lambda j: (j, 0)),
            whole(hidden),
            whole(gain),
            whole(residual_grad),
        ],
        out_specs=pl.BlockSpec((rows, width), lambda j: (0, 0)),
        compiler_params=pltpu.CompilerParams(vmem_limit_bytes=24 << 20),
        cost_estimate=pl.CostEstimate(
            flops=2 * rows * width * columns,
            bytes_accessed=2 * width * columns,
            transcendentals=0,
        ),
        name="one_back",
    )(query_part, pair_part, in_hbm(weight), hidden, gain, residual_grad)


def send_rows(values):
    if lax.axis_size("fsdp") != 4:
        return fetch_rows(values)
    third = swap(values, "fsdp", 3)
    return [values, swap(values, "fsdp", 1), third]


def relay_rows(planes):
    if lax.axis_size("fsdp") != 4:
        return planes
    values, first, third = planes
    return [values, first, swap(third, "fsdp", 1), third]


def pass_rows(values):
    return relay_rows(send_rows(values))


def fetch_rows(values):
    count = lax.axis_size("fsdp")
    return [values] + [swap(values, "fsdp", away) for away in range(1, count)]


def sum_rows(parts, forward):
    count = len(parts)
    if count == 4 and forward:
        passed = swap(parts[2], "fsdp", 1).astype(F32)
        one = swap(parts[1], "fsdp", 1)
        third = swap((parts[3].astype(F32) + passed).astype(BF), "fsdp", 3)
        return [parts[0], one, third]
    return parts[:1] + [swap(parts[i], "fsdp", i) for i in range(1, count)]


def by_feature(values):
    rows, width = values.shape
    ctx_count, fsdp_count = lax.axis_size("ctx"), lax.axis_size("fsdp")
    blocks = values.reshape(rows, ctx_count, fsdp_count, width // (ctx_count * fsdp_count))
    return blocks.transpose(0, 2, 1, 3).reshape(rows, width)


def sum_over_ctx(part_for):
    pairs = lax.axis_size("ctx") // 2
    sent = jnp.stack([part_for(2 * pair + 1).astype(BF) for pair in range(pairs)])
    got = swap(sent, "ctx", 1)
    sums = [part_for(2 * pair).astype(F32) + got[pair].astype(F32) for pair in range(pairs)]
    total = sums[0]
    for pair in range(1, pairs):
        total = total + swap(sums[pair].astype(BF), "ctx", 2 * pair).astype(F32)
    return total


def ctx_rows_sum(values):
    height = values.shape[0] // lax.axis_size("ctx")
    me = lax.axis_index("ctx")

    def part(offset):
        return lax.dynamic_slice(
            values, ((me ^ offset) * height, 0), (height, values.shape[1])
        )

    return sum_over_ctx(part)


def key_offsets():
    count = lax.axis_size("ctx")
    return list(range(0, count, 2)) + list(range(1, count, 2))


def gather_keys(piece):
    same = [piece] + [swap(piece, "ctx", far) for far in range(2, lax.axis_size("ctx"), 2)]
    mine = jnp.concatenate(same, axis=0)
    return mine, swap(mine, "ctx", 1)


def sum_pairs(kept, sent, cosine, sine):
    _, count, width = kept.shape
    pairs = lax.axis_size("ctx") // 2
    got = swap(sent, "ctx", 1)
    sums = (kept.astype(F32) + got.astype(F32)).reshape(2, pairs, count // pairs, width)
    far = [swap(sums[:, pair].astype(BF), "ctx", 2 * pair) for pair in range(1, pairs)]
    return pair_turn(sums[:, 0], far, cosine, sine), got


def half_mask(shape):
    return lax.broadcasted_iota(jnp.int32, shape, len(shape) - 1) % 128 < HD


def turn(values, cosine, sine):
    lanes = lax.broadcasted_iota(jnp.int32, values.shape, 1) % HD
    turned = jnp.where(
        lanes < HD // 2, pltpu.roll(values, 128 - HD // 2, 1), pltpu.roll(values, HD // 2, 1)
    )
    return values * cosine + turned * sine


def doubled(tile, odd):
    wide = tile.astype(F32)
    other = pltpu.roll(wide, HD, 1)
    return jnp.where(half_mask(tile.shape) == (odd == 0), wide, other).astype(BF)


def split_heads(tile_pair):
    zero = jnp.zeros((), tile_pair.dtype)
    parts = []
    for j in range(2):
        tile = tile_pair[:, j * 128 : (j + 1) * 128]
        mask = half_mask(tile.shape)
        parts += [jnp.where(mask, tile, zero), jnp.where(mask, zero, tile)]
    return jnp.concatenate(parts, axis=0)


def merge_heads(stacked):
    rows = stacked.shape[0] // 4
    tiles = []
    for j in range(2):
        even = stacked[2 * j * rows : (2 * j + 1) * rows]
        odd = stacked[(2 * j + 1) * rows : (2 * j + 2) * rows]
        tiles.append(jnp.where(half_mask(even.shape), even, odd))
    return jnp.concatenate(tiles, axis=1)


def key_chunks(refs, chunk):
    first = 0
    for k_ref, v_ref in refs:
        for start in range(0, k_ref.shape[0], chunk):
            at = slice(start, start + chunk)
            yield first + start, k_ref.at[at, :], v_ref.at[at, :]
        first += k_ref.shape[0]


def masked_scores(keys, queries, key_ref, own_ref, start):
    allowed = key_ref[start : start + keys.shape[0], :1] <= own_ref[...]
    bias = jnp.where(allowed, 0.0, -1e30).astype(F32)
    return nt(keys, queries) + jnp.concatenate([bias] * 4, axis=1)


def attend_kernel(
    chunk, q_ref, ka_ref, va_ref, kb_ref, vb_ref, key_ref, own_ref, rows_ref, attended_ref, log_ref
):
    odd = pl.program_id(0) % 2
    rows = q_ref.shape[0]
    queries = split_heads(q_ref[...])
    parts = list(key_chunks(((ka_ref, va_ref), (kb_ref, vb_ref)), chunk))
    scores = [
        masked_scores(doubled(k_ref[...], odd), queries, key_ref, own_ref, start)
        for start, k_ref, _ in parts
    ]
    top = jnp.max(scores[0], axis=0, keepdims=True)
    for score in scores[1:]:
        top = jnp.maximum(top, jnp.max(score, axis=0, keepdims=True))
    total = jnp.zeros_like(top)
    summed = jnp.zeros((4 * rows, 128), F32)
    for score, (_, _, v_ref) in zip(scores, parts):
        weights = jnp.exp(score - top)
        total += jnp.sum(weights, axis=0, keepdims=True)
        summed += tn(weights.astype(BF), doubled(v_ref[...], odd))
    log_ref[0] = top + jnp.log(total)
    attended = merge_heads(summed / jnp.transpose(jnp.broadcast_to(total, (128, 4 * rows))))
    attended_ref[...] = attended
    rows_ref[...] = attended.astype(BF)


def key_specs(parts):
    tiles = parts[0].shape[1] // 256
    specs, arrays = [], []
    for part in parts:
        specs.append(pl.BlockSpec((part.shape[0], 128), lambda g: (0, g // 2)))
        specs.append(pl.BlockSpec((part.shape[0], 128), lambda g: (0, tiles + g // 2)))
        arrays += [part, part]
    return specs, arrays


def attend(queries, keys_values, key_anchor, own_anchor):
    rows, width = queries.shape
    count = key_anchor.shape[0]
    specs, arrays = key_specs(keys_values)
    wide = pl.BlockSpec((rows, 256), lambda g: (0, g))
    return pl.pallas_call(
        lambda *refs: attend_kernel(KEY_CHUNK, *refs),
        grid=(KV,),
        out_shape=(
            jax.ShapeDtypeStruct((rows, width), BF),
            jax.ShapeDtypeStruct((rows, width), F32),
            jax.ShapeDtypeStruct((KV, 1, 4 * rows), F32),
        ),
        in_specs=[wide]
        + specs
        + [
            pl.BlockSpec((count, 128), lambda g: (0, 0)),
            pl.BlockSpec((1, rows), lambda g: (0, 0)),
        ],
        out_specs=(wide, wide, pl.BlockSpec((1, 1, 4 * rows), lambda g: (g, 0, 0))),
        compiler_params=pltpu.CompilerParams(vmem_limit_bytes=48 << 20),
        cost_estimate=pl.CostEstimate(
            flops=4 * rows * width * count,
            bytes_accessed=4 * count * KV * HD,
            transcendentals=rows * H * count,
        ),
        name="attend",
    )(queries, *arrays, key_anchor, own_anchor)


def attend_back_kernel(
    chunk, q_ref, grad_ref, attended_ref, ka_ref, va_ref, kb_ref, vb_ref, key_ref, own_ref, log_ref,
    cos_ref, sin_ref, dq_ref, kept_ref, sent_ref,
):
    odd = pl.program_id(0) % 2
    rows = q_ref.shape[0]
    half = ka_ref.shape[0]
    queries, grads = split_heads(q_ref[...]), split_heads(grad_ref[...])
    product = grads.astype(F32) * split_heads(attended_ref[...])
    delta = jnp.sum(jnp.transpose(product), axis=0, keepdims=True)
    log_total = log_ref[0]
    total = jnp.zeros((4 * rows, 128), F32)
    keep = half_mask((chunk, 128)) == (odd == 0)
    for start, k_ref, v_ref in key_chunks(((ka_ref, va_ref), (kb_ref, vb_ref)), chunk):
        keys, values = doubled(k_ref[...], odd), doubled(v_ref[...], odd)
        scores = masked_scores(keys, queries, key_ref, own_ref, start)
        probs = jnp.exp(scores - log_total)
        value_grad = nn(probs.astype(BF), grads)
        score_grad = (probs * (nt(values, grads) - delta)).astype(BF)
        key_grad = nn(score_grad, queries)
        total += tn(score_grad, keys)
        out_ref = kept_ref if start < half else sent_ref
        at = slice(start % half, start % half + chunk)
        for part, value in enumerate((key_grad, value_grad)):
            value = (value + pltpu.roll(value, HD, 1)).astype(BF)
            out_ref[part, at, :] = jnp.where(keep, value, out_ref[part, at, :])
    merged = merge_heads(total) * (1.0 / math.sqrt(HD))
    cosine, sine = cos_ref[...], sin_ref[...]
    for j in range(2):
        tile = slice(j * 128, (j + 1) * 128)
        dq_ref[:, tile] = turn(merged[:, tile], cosine, -sine).astype(BF)


def attend_back(queries, grads, attended, keys_values, key_anchor, own_anchor, logs, cosine, sine):
    rows, width = queries.shape
    count = key_anchor.shape[0]
    specs, arrays = key_specs(keys_values)
    wide = pl.BlockSpec((rows, 256), lambda g: (0, g))
    small = pl.BlockSpec((rows, 128), lambda g: (0, 0))
    pair = pl.BlockSpec((2, count // 2, 128), lambda g: (0, 0, g // 2))
    return pl.pallas_call(
        lambda *refs: attend_back_kernel(KEY_CHUNK, *refs),
        grid=(KV,),
        out_shape=(
            jax.ShapeDtypeStruct((rows, width), BF),
            jax.ShapeDtypeStruct((2, count // 2, KV * HD), BF),
            jax.ShapeDtypeStruct((2, count // 2, KV * HD), BF),
        ),
        in_specs=[wide, wide, wide]
        + specs
        + [
            pl.BlockSpec((count, 128), lambda g: (0, 0)),
            pl.BlockSpec((1, rows), lambda g: (0, 0)),
            pl.BlockSpec((1, 1, 4 * rows), lambda g: (g, 0, 0)),
            small,
            small,
        ],
        out_specs=(wide, pair, pair),
        compiler_params=pltpu.CompilerParams(vmem_limit_bytes=48 << 20),
        cost_estimate=pl.CostEstimate(
            flops=10 * rows * width * count,
            bytes_accessed=8 * count * KV * HD,
            transcendentals=rows * H * count,
        ),
        name="attend_back",
    )(queries, grads, attended, *arrays, key_anchor, own_anchor, logs, cosine, sine)


def pair_turn_kernel(copies, own_ref, *refs):
    got, (cos_ref, sin_ref, y_ref) = refs[:-3], refs[-3:]
    total = own_ref[...]
    for ref in got:
        total = total + ref[...].astype(F32)
    cosine, sine = cos_ref[...], sin_ref[...]
    _, rows, width = total.shape
    tiles = [
        turn(total[0, :, start : start + 128], cosine, -sine).astype(BF)
        for start in range(0, width, 128)
    ]
    values = total[1].astype(BF)
    for copy in range(copies):
        at = slice(copy * rows, (copy + 1) * rows)
        for i, tile in enumerate(tiles):
            y_ref[at, i * 128 : (i + 1) * 128] = tile
        y_ref[at, width:] = values


def pair_turn(own, got, cosine, sine):
    _, rows, width = own.shape
    copies = lax.axis_size("fsdp")
    return pl.pallas_call(
        lambda *refs: pair_turn_kernel(copies, *refs),
        out_shape=jax.ShapeDtypeStruct((copies * rows, 2 * width), BF),
        name="pair_turn",
    )(own, *got, cosine, sine)


def join_rows(x_buf, refs):
    @pl.when((pl.program_id(0) == 0))
    def _():
        rows = refs[0].shape[0]
        for i, ref in enumerate(refs):
            x_buf[i * rows : (i + 1) * rows] = ref[...]


def ffn_kernel(count, earlier, *refs):
    rows_refs, (act_ref, w_ref), refs = refs[:count], refs[count : count + 2], refs[count + 2 :]
    out_ref, refs = refs[earlier], refs[earlier + 1 :]
    sum_refs, (x_buf, sum_buf) = refs[:count], refs[count:]
    join_rows(x_buf, rows_refs)
    step = pl.program_id(0)
    gate_w, up_w = w_ref[0], w_ref[1]
    x = x_buf[...]
    gate, up = nn(x, gate_w), nn(x, up_w)
    act_grad = act_ref[...]
    sig = jax.nn.sigmoid(gate)
    silu = gate * sig
    gate_grad = (act_grad * up * sig * (1.0 + gate * (1.0 - sig))).astype(BF)
    up_grad = (act_grad * silu).astype(BF)
    out_ref[0], out_ref[1], out_ref[2] = gate_grad, up_grad, (silu * up).astype(BF)
    part = nt(gate_grad, gate_w) + nt(up_grad, up_w)

    @pl.when(step == 0)
    def _():
        sum_buf[...] = part

    @pl.when(step > 0)
    def _():
        sum_buf[...] += part

    @pl.when(step == pl.num_programs(0) - 1)
    def _():
        rows = sum_refs[0].shape[0]
        for i, ref in enumerate(sum_refs):
            ref[...] = sum_buf[i * rows : (i + 1) * rows].astype(ref.dtype)


def ffn_middle(blocks, act_grad, half, weights, kinds, earlier):
    width = blocks[0].shape[1]
    rows = blocks[0].shape[0] * len(blocks)
    hidden = weights.shape[2]
    tile = FFN_TILE
    whole = [pl.BlockSpec(block.shape, lambda j: (0, 0)) for block in blocks]
    out = pl.pallas_call(
        lambda *refs: ffn_kernel(len(blocks), len(earlier), *refs),
        grid=(hidden // tile,),
        out_shape=(
            pltpu.HBM((3, 2 * rows, hidden), BF),
            *[jax.ShapeDtypeStruct(block.shape, kind) for block, kind in zip(blocks, kinds)],
        ),
        in_specs=whole
        + [
            pl.BlockSpec((rows, tile), lambda j: (half, j)),
            pl.BlockSpec((2, width, tile), lambda j: (0, 0, j)),
        ]
        + [pl.BlockSpec(memory_space=pltpu.HBM)] * len(earlier),
        out_specs=(pl.BlockSpec((3, rows, tile), lambda j: (0, half, j)), *whole),
        input_output_aliases={len(blocks) + 2: 0} if earlier else {},
        scratch_shapes=[pltpu.VMEM((rows, width), BF), pltpu.VMEM((rows, width), F32)],
        compiler_params=pltpu.CompilerParams(vmem_limit_bytes=40 << 20),
        cost_estimate=pl.CostEstimate(
            flops=8 * rows * width * hidden,
            bytes_accessed=4 * width * hidden,
            transcendentals=rows * hidden,
        ),
        name="ffn_middle",
    )(*blocks, act_grad, weights, *earlier)
    return out[0], list(out[1:])


def products_kernel(count, added, ids_ref, *refs):
    blocks, right, rest = refs[: 2 * count], refs[2 * count], refs[2 * count + 1 :]
    out_ref, left = rest[-2:]
    rows, height = blocks[0].shape
    for j in range(2):
        for i in range(count):
            at = (slice(i * rows, (i + 1) * rows), slice(j * height, (j + 1) * height))
            left[at] = blocks[j * count + i][...]
    part = tn(left[...], right[0])
    if added:
        part = part + rest[0][0].astype(F32)
    out_ref[0] = part.astype(BF)


def half_products(rows_of, parts, first, size, got, earlier):
    count = len(rows_of)
    rows, width = rows_of[0].shape
    matrices, _, hidden = parts.shape
    ctx_count = lax.axis_size("ctx")
    height = width // ctx_count
    kept = got is not None

    def left(j):
        def place(k, i, ids_ref):
            own = ids_ref[0] % 2
            return (0, 2 * (2 * i + j) + (own if kept else 1 - own))

        return pl.BlockSpec((rows, height), place)

    def out(start):
        return pl.BlockSpec((1, 2 * height, hidden), lambda k, i, ids_ref: (start + k, i, 0))

    right = pl.BlockSpec((1, rows * count, hidden), lambda k, i, ids_ref: (first + k, 0, 0))
    extra = ([got] if kept else []) + earlier
    operands = 2 * count + 1 + len(extra)
    return pl.pallas_call(
        lambda *refs: products_kernel(count, kept, *refs),
        grid_spec=pltpu.PrefetchScalarGridSpec(
            num_scalar_prefetch=1,
            grid=(size, ctx_count // 4),
            in_specs=[left(0)] * count
            + [left(1)] * count
            + [right]
            + [out(0)] * kept
            + [pl.BlockSpec(memory_space=pltpu.HBM)] * len(earlier),
            out_specs=out(first if kept else 0),
            scratch_shapes=[pltpu.VMEM((count * rows, 2 * height), BF)],
        ),
        out_shape=pltpu.HBM((matrices if kept else size, width // 2, hidden), BF),
        input_output_aliases={operands: 0} if earlier else {},
        compiler_params=pltpu.CompilerParams(vmem_limit_bytes=24 << 20),
        cost_estimate=pl.CostEstimate(
            flops=size * count * rows * width * hidden,
            bytes_accessed=size * width * hidden,
            transcendentals=0,
        ),
    )(jnp.stack(ids()), *rows_of, *rows_of, in_hbm(parts), *extra)


def ffn_gradient(rows_in, rows_out, parts):
    count = lax.axis_size("ctx")
    if count % 4 or (rows_in[0].shape[1] // count) % 128:
        left, grad = (jnp.concatenate(rows, axis=0) for rows in (rows_in, rows_out))
        products = [tn(left, parts[0]), tn(left, parts[1]), tn(grad, parts[2])]
        products = jnp.stack(products, axis=1).astype(BF)
        return lax.psum_scatter(products, "ctx", scatter_dimension=0, tiled=True)
    calls = ((rows_out, 2, 1), (rows_in, 0, 2))
    got = []
    for rows_of, first, size in calls:
        sent = half_products(rows_of, parts, first, size, None, [])
        got.append(swap(sent, "ctx", 1))
    kept = []
    for (rows_of, first, size), part in zip(calls, got):
        kept = [half_products(rows_of, parts, first, size, part, kept)]
    groups = [list(range(core, count, 2)) for core in range(2)]
    return lax.psum_scatter(
        kept[0].transpose(1, 0, 2),
        "ctx",
        scatter_dimension=0,
        tiled=True,
        axis_index_groups=groups,
    )


def down_back_kernel(count, *refs):
    rows_refs, (w_ref, y_ref, x_buf) = refs[:count], refs[count:]
    join_rows(x_buf, rows_refs)
    y_ref[...] = nn(x_buf[...], w_ref[0])


def down_back(blocks, weights):
    width = blocks[0].shape[1]
    rows = blocks[0].shape[0] * len(blocks)
    hidden = weights.shape[2]
    tile = FFN_TILE
    return pl.pallas_call(
        lambda *refs: down_back_kernel(len(blocks), *refs),
        grid=(hidden // tile,),
        out_shape=pltpu.HBM((rows, hidden), F32),
        in_specs=[pl.BlockSpec(block.shape, lambda j: (0, 0)) for block in blocks]
        + [pl.BlockSpec((1, width, tile), lambda j: (2, 0, j))],
        out_specs=pl.BlockSpec((rows, tile), lambda j: (0, j)),
        scratch_shapes=[pltpu.VMEM((rows, width), BF)],
        compiler_params=pltpu.CompilerParams(vmem_limit_bytes=24 << 20),
        cost_estimate=pl.CostEstimate(
            flops=2 * rows * width * hidden,
            bytes_accessed=2 * width * hidden,
            transcendentals=0,
        ),
        name="down_back",
    )(*blocks, weights)


def down_kernel(x_ref, w_ref, *y_refs):
    rows = x_ref.shape[1] // len(y_refs)
    total = nt(x_ref[0], w_ref[0])
    for i, y_ref in enumerate(y_refs):
        y_ref[...] = total[i * rows : (i + 1) * rows].astype(y_ref.dtype)


def down_forward(parts, weights, count):
    _, rows, hidden = parts.shape
    width = weights.shape[1]
    tile = FFN_TILE
    height = rows // count
    return pl.pallas_call(
        down_kernel,
        grid=(width // tile,),
        out_shape=tuple(
            jax.ShapeDtypeStruct((height, width), BF if i else F32) for i in range(count)
        ),
        in_specs=[
            pl.BlockSpec((1, rows, hidden), lambda j: (2, 0, 0)),
            pl.BlockSpec((1, tile, hidden), lambda j: (2, j, 0)),
        ],
        out_specs=tuple(pl.BlockSpec((height, tile), lambda j: (0, j)) for _ in range(count)),
        compiler_params=pltpu.CompilerParams(vmem_limit_bytes=24 << 20),
        cost_estimate=pl.CostEstimate(
            flops=2 * rows * width * hidden,
            bytes_accessed=2 * width * hidden,
            transcendentals=0,
        ),
        name="down_forward",
    )(in_hbm(parts), weights)


def share_kernel(count, sizes, ids_ref, *refs):
    products = len(sizes)
    lefts = [refs[i * count : (i + 1) * count] for i in range(products)]
    rest = refs[products * count :]
    rights = []
    for size in sizes:
        rights.append(rest[:size])
        rest = rest[size:]
    bufs = rest[len(rest) - products :]
    terms, (kept_ref, sent_ref) = rest[: -products - 2], rest[-products - 2 : -products]
    half = kept_ref.shape[1]
    own = ids_ref[0] % 2 == 0

    @pl.when(pl.program_id(0) == 0)
    def _():
        for parts, buf in zip(rights, bufs):
            rows = buf.shape[0] // count
            for away in range(count):
                if len(parts) > 1:
                    block = parts[away][...]
                else:
                    start = (ids_ref[1] ^ away) * rows
                    block = parts[0][pl.ds(pl.multiple_of(start, 16), rows), :]
                buf[away * rows : (away + 1) * rows] = block

    def emit(part, column):
        at = slice(column, column + part.shape[1])
        kept_ref[0, :, at] = jnp.where(own, part[:half], part[half:])
        sent_ref[0, :, at] = jnp.where(own, part[half:], part[:half])

    column = 0
    for left, buf in zip(lefts, bufs):
        joined = jnp.concatenate([ref[...] for ref in left], axis=0)
        emit(tn(joined, buf[...]).astype(BF), column)
        column += buf.shape[1]
    for term in terms:
        tall = jnp.broadcast_to(term[...], (128, term.shape[1]))
        emit(jnp.transpose(tall).astype(BF), column)
        column += 128


def share_products(lefts, rights, terms):
    ctx_count = lax.axis_size("ctx")
    pairs = ctx_count // 2
    count = len(lefts[0])
    rows, width = lefts[0][0].shape
    height = width // ctx_count
    groups = [right if isinstance(right, list) else [right] for right in rights]
    widths = [group[0].shape[1] for group in groups]
    columns = sum(widths) + 128 * len(terms)

    def place(j, ids_ref):
        return (0, (ids_ref[0] // 2) ^ j)

    def whole(array):
        return pl.BlockSpec(array.shape, lambda j, ids_ref: (0, 0))

    shape = jax.ShapeDtypeStruct((pairs, height, columns), BF)
    out = pl.BlockSpec((1, height, columns), lambda j, ids_ref: (j, 0, 0))
    flat_lefts = [block for left in lefts for block in left]
    flat_rights = [block for group in groups for block in group]
    return pl.pallas_call(
        lambda *refs: share_kernel(count, [len(group) for group in groups], *refs),
        grid_spec=pltpu.PrefetchScalarGridSpec(
            num_scalar_prefetch=1,
            grid=(pairs,),
            in_specs=[pl.BlockSpec((rows, 2 * height), place) for _ in flat_lefts]
            + [whole(block) for block in flat_rights]
            + [pl.BlockSpec((1, 2 * height), place) for _ in terms],
            out_specs=(out, out),
            scratch_shapes=[pltpu.VMEM((count * rows, size), BF) for size in widths],
        ),
        out_shape=(shape, shape),
        compiler_params=pltpu.CompilerParams(vmem_limit_bytes=32 << 20),
        cost_estimate=pl.CostEstimate(
            flops=2 * count * rows * width * columns,
            bytes_accessed=2 * (count * rows + columns) * width,
            transcendentals=0,
        ),
        name="share_terms" if terms else "share_products",
    )(jnp.stack(ids()), *flat_lefts, *flat_rights, *[term[None] for term in terms])


def in_fsdp_order(value):
    if not isinstance(value, list):
        return value
    plane = lax.axis_index("fsdp")
    stacked = jnp.stack(value)
    parts = [
        lax.dynamic_index_in_dim(stacked, plane ^ away, 0, keepdims=False)
        for away in range(len(value))
    ]
    return jnp.concatenate(parts, axis=0)


def share_start(lefts, rights, terms):
    pairs = lax.axis_size("ctx") // 2
    if (lefts[0][0].shape[1] // pairs) % 128:
        values = [tn(in_fsdp_order(a), in_fsdp_order(b)) for a, b in zip(lefts, rights)]
        values += [jnp.broadcast_to(term[:, None], (term.shape[0], 128)) for term in terms]
        return [ctx_rows_sum(jnp.concatenate(values, axis=1))]
    kept, sent = share_products(lefts, rights, terms)
    got = swap(sent, "ctx", 1)
    parts = [kept[0], got[0]]
    for pair in range(1, pairs):
        part = (kept[pair].astype(F32) + got[pair].astype(F32)).astype(BF)
        parts.append(swap(part, "ctx", 2 * pair))
    return parts


def share_finish(parts):
    total = parts[0].astype(F32)
    for part in parts[1:]:
        total = total + part.astype(F32)
    return total


def own_rows_of(values, height):
    index = lax.axis_index("ctx") * lax.axis_size("fsdp") + lax.axis_index("fsdp")
    return lax.dynamic_slice_in_dim(values, index * height, height, 0)


def feature_parts(values):
    count, plane = lax.axis_size("fsdp"), lax.axis_index("fsdp")
    values = by_feature(values)
    rows, width = values.shape
    width //= count
    return [
        lax.dynamic_slice(values, (0, (plane ^ away) * width), (rows, width))
        for away in range(count)
    ]


def feature_rows(parts):
    return [swap(part, "fsdp", away) if away else part for away, part in enumerate(parts)]


def own_features(terms):
    ctx_count, fsdp_count = lax.axis_size("ctx"), lax.axis_size("fsdp")
    total = jnp.stack(terms)
    away = 1
    while away < fsdp_count:
        total = total + swap(total, "fsdp", away)
        away *= 2
    blocks = total.reshape(len(terms), ctx_count, fsdp_count, -1)
    own = lax.dynamic_index_in_dim(blocks, lax.axis_index("fsdp"), 2, keepdims=False)
    own = own.reshape(len(terms), -1)
    return [own[i] for i in range(len(terms))]


def layer(
    hidden_in,
    out_grad,
    positions,
    block_order,
    attn_gain,
    ffn_gain,
    qkv_weight,
    out_weight,
    ffn_weight,
):
    ctx_count, fsdp_count = lax.axis_size("ctx"), lax.axis_size("fsdp")
    me, _ = ids()
    rows = hidden_in.shape[1]
    queries_width, kv_width = H * HD, KV * HD
    ffn_parts = in_hbm(ffn_weight.transpose(1, 0, 2))

    frequency = jnp.power(ROPE_BASE, -(jnp.arange(HD // 2, dtype=F32) * 2.0 / HD))
    angles = positions[0].astype(F32)[:, None] * frequency[None, :]
    cosine = jnp.tile(jnp.cos(angles), (1, 4))
    sine = jnp.tile(jnp.concatenate([-jnp.sin(angles), jnp.sin(angles)], axis=1), (1, 2))
    own_anchor = anchors_of(block_order, me, rows)[None]
    key_anchor = jnp.concatenate(
        [anchors_of(block_order, me ^ offset, rows) for offset in key_offsets()]
    )
    key_anchor = jnp.broadcast_to(key_anchor[:, None], (rows * ctx_count, 128))

    inputs = hidden_in[0].astype(F32)
    grad_in = out_grad[0]
    scale_one = norm_scale(inputs)
    normed_one = (inputs * scale_one * attn_gain).astype(BF)

    one_parts = feature_parts(normed_one)
    fast = ctx_count == 8 and (qkv_weight.shape[1] // ctx_count) % 128 == 0
    if fast:
        early = (cosine, sine, own_anchor, key_anchor, one_parts)
        qkv_pieces, marks = gather_pieces(qkv_weight, early)
        out_blocks = gather_blocks(out_weight, *marks)
        queries, pair, qkv_full = pieces_forward(
            normed_one, qkv_weight, qkv_pieces, cosine, sine
        )
    else:
        marks = (normed_one, normed_one)
        out_blocks = gather_blocks(out_weight, *marks)
        qkv_full = whole_of(qkv_weight, gather_blocks(qkv_weight, normed_one, normed_one))
        projected = nn(normed_one, qkv_full)
        turned = rotate(
            projected[:, : queries_width + kv_width].reshape(rows, H + KV, HD), positions[0]
        ).reshape(rows, queries_width + kv_width)
        queries = (turned[:, :queries_width] * (1.0 / math.sqrt(HD))).astype(BF)
        pair = jnp.concatenate(
            [turned[:, queries_width:], projected[:, queries_width + kv_width :]], axis=1
        ).astype(BF)
    own_one = feature_rows(after(one_parts, pair))
    keys_values = gather_keys(pair)
    rows_out = send_rows(after(grad_in, pair))
    attn_rows, attended, logs = attend(queries, keys_values, key_anchor, own_anchor)
    rows_out = relay_rows(after(rows_out, attn_rows))
    residual, normed_two = out_forward(
        attn_rows, out_weight, out_blocks, hidden_in[0], ffn_gain
    )
    scale_two = norm_scale(residual)
    rows_in = pass_rows(normed_two)
    rows_out = after(rows_out, normed_two)
    act_grad = down_back(rows_out, ffn_parts)

    all_attn = pass_rows(after(attn_rows, rows_in[2]))
    parts, partial = [], []
    half = fsdp_count // 2
    passing = 3 if fsdp_count == 4 else 0
    for index in range(2):
        blocks = rows_in[index * half : (index + 1) * half]
        kinds = [F32 if index * half + i in (0, passing) else BF for i in range(half)]
        out, terms = ffn_middle(blocks, in_hbm(act_grad), index, ffn_parts, kinds, parts)
        parts, partial = [out], partial + terms
    parts = parts[0]
    sum_grad = share_finish(sum_rows(partial, True))
    ffn_weight_grad = ffn_gradient(rows_in, rows_out, parts)
    ffn_weight_grad = ffn_weight_grad.astype(F32)
    out_partial = list(down_forward(parts, ffn_parts, fsdp_count))

    unit_two = residual * scale_two
    ffn_gain_term = jnp.sum(sum_grad * unit_two, axis=0)
    scaled_two = ffn_gain * sum_grad
    residual_grad = grad_in.astype(F32) + scale_two * (
        scaled_two - unit_two * jnp.mean(scaled_two * unit_two, axis=-1, keepdims=True)
    )
    residual_bf = residual_grad.astype(BF)
    out_sum = sum_rows([after(part, residual_bf) for part in out_partial], False)
    (ffn_term,) = own_features([ffn_gain_term])
    attn_grad = out_back(residual_bf, out_weight, out_blocks)
    query_part, kept, sent = attend_back(
        queries, attn_grad, attended, keys_values, key_anchor, own_anchor, logs, cosine, sine
    )
    query_planes = pass_rows(query_part)
    pair_copies, near = sum_pairs(kept, sent, cosine, sine)
    own_residual = feature_rows(feature_parts(after(residual_bf, near)))
    all_pair = lax.all_to_all(pair_copies, "fsdp", split_axis=0, concat_axis=0, tiled=True)
    input_grad = one_back(
        query_part, pair_copies, qkv_full, hidden_in[0], attn_gain, residual_grad
    )
    out_sums = share_start([own_residual], [after(all_attn, input_grad)], [])
    output = (residual + share_finish(after(out_sum, input_grad))).astype(BF)
    qkv_sums = share_start([own_one, own_one], [after(query_planes, output), all_pair], [ffn_term])
    qkv_sums = share_finish(qkv_sums)
    out_weight_grad = share_finish(after(out_sums, qkv_sums))
    qkv_grad = qkv_sums[:, : qkv_weight.shape[1]]
    features = own_rows_of(attn_gain, qkv_grad.shape[0])
    gain_grad = jnp.sum(own_rows_of(qkv_full, qkv_grad.shape[0]).astype(F32) * qkv_grad, axis=1)
    return (
        output[None],
        input_grad[None],
        qkv_grad,
        out_weight_grad,
        ffn_weight_grad,
        gain_grad / features,
        qkv_sums[:, qkv_weight.shape[1]],
    )


def solution(mesh):
    step = sharded(mesh)
    return step


def sharded(mesh):
    return jax.shard_map(
        layer,
        mesh=mesh,
        in_specs=(
            P("fsdp", "ctx", None),
            P("fsdp", "ctx", None),
            P("fsdp", "ctx"),
            P(),
            P(),
            P(),
            P("fsdp", None),
            P("fsdp", None),
            P(None, None, "fsdp"),
        ),
        out_specs=(
            P("fsdp", "ctx", None),
            P("fsdp", "ctx", None),
            P(("ctx", "fsdp"), None),
            P(("ctx", "fsdp"), None),
            P("ctx", None, "fsdp"),
            P(("ctx", "fsdp")),
            P(("ctx", "fsdp")),
        ),
        check_vma=False,
    )
```

```python
import math

import jax
import jax.numpy as jnp
from jax import lax
from jax.experimental import pallas as pl
from jax.experimental.pallas import tpu as pltpu
from jax.sharding import PartitionSpec as P


H = 32
KV = 8
HD = 64

NORM_EPS = 1e-05
ROPE_BASE = 500000.0
FFN_TILE = 512
KEY_CHUNK = 256


BF = jnp.bfloat16
F32 = jnp.float32


def mm(a, b, dims):
    return lax.dot_general(a, b, (dims, ((), ())), preferred_element_type=F32)


def nn(a, b):
    return mm(a, b, ((1,), (0,)))


def nt(a, b):
    return mm(a, b, ((1,), (1,)))


def tn(a, b):
    return mm(a, b, ((0,), (0,)))


def swap(value, axis, offset):
    count = lax.axis_size(axis)
    return lax.ppermute(value, axis, [(i, i ^ offset) for i in range(count)])


def rotate(values, token_places):
    head_dim = values.shape[-1]
    half_dim = head_dim // 2
    frequency = jnp.power(ROPE_BASE, -(jnp.arange(half_dim, dtype=F32) * 2.0 / head_dim))
    angles = token_places.astype(F32)[:, None] * frequency[None, :]
    cosine = jnp.concatenate([jnp.cos(angles), jnp.cos(angles)], axis=-1)[:, None, :]
    sine_part = jnp.concatenate([jnp.sin(angles), jnp.sin(angles)], axis=-1)[:, None, :]
    turned = jnp.concatenate([-values[..., half_dim:], values[..., :half_dim]], axis=-1)
    return values * cosine + turned * sine_part


def norm_scale(values):
    return lax.rsqrt(jnp.mean(values * values, axis=-1, keepdims=True) + NORM_EPS)


def lookup(entries, row_ids):
    matches = row_ids[:, None] == jnp.arange(entries.shape[0], dtype=jnp.int32)[None, :]
    return jnp.sum(jnp.where(matches, entries[None, :], 0), axis=1)


def anchors_of(block_order, owner, row_count):
    block_len = row_count // 2
    row_ids = owner * row_count + jnp.arange(row_count, dtype=jnp.int32)
    return lookup(block_order, row_ids // block_len) * block_len + row_ids % block_len


def after(value, *earlier):
    return lax.optimization_barrier((value, earlier))[0]


def ids():
    return lax.axis_index("ctx"), lax.axis_index("fsdp")


def gather_pieces(weight, early):
    rows, columns = weight.shape
    share = columns // lax.axis_size("ctx")
    half = rows // 2
    mine = lax.dynamic_slice(weight, (0, lax.axis_index("ctx") * share), (rows, share))
    planes = {}
    planes[3] = swap(mine, "fsdp", 3)
    planes[1] = swap(mine, "fsdp", 1)
    planes[2] = swap(after(planes[3], early), "fsdp", 1)
    pieces = []
    for away in (1, 3, 2):
        first = planes[away]
        along_x, along_y = swap(first, "ctx", 2), swap(first, "ctx", 4)
        if away == 1:
            corners = [(6, 0, swap(along_y, "ctx", 2))]
        elif away == 3:
            corners = [(6, 0, swap(along_x, "ctx", 4))]
        else:
            top, low = swap(along_y[:half], "ctx", 2), swap(along_x[half:], "ctx", 4)
            corners = [(6, 0, jnp.concatenate([top, low], axis=0))]
        parts = [(0, 0, first), (2, 0, along_x), (4, 0, along_y)] + corners
        for offset, start, part in parts:
            pieces.append((away, offset, start, part))
            pieces.append((away, offset + 1, start, swap(part, "ctx", 1)))
    return pieces, (planes[2], pieces[-2][3])


def pieces_kernel(places, rows_in, share, ids_ref, x_ref, own_ref, *refs):
    count = len(places)
    piece_refs, refs = refs[:count], refs[count:]
    cos_ref, sin_ref, q_ref, pair_ref, full_ref, y_ref, buf, in_sems, out_sems = refs
    me, plane = ids_ref[0], ids_ref[1]

    def block(away):
        return pl.ds(pl.multiple_of((plane ^ away) * rows_in, 128), rows_in)

    own_copy = pltpu.make_async_copy(own_ref, buf.at[block(0)], in_sems.at[count])
    own_copy.start()
    copies = []
    for i, (away, offset, start, height) in enumerate(places):
        at = pl.ds(pl.multiple_of((plane ^ away) * rows_in + start, 128), height)
        columns = pl.ds(pl.multiple_of((me ^ offset) * share, 128), share)
        copies.append(pltpu.make_async_copy(piece_refs[i], buf.at[at, columns], in_sems.at[i]))
        copies[-1].start()
    outs = []
    order = [0] + list(dict.fromkeys(away for away, _, _, _ in places))
    for away in order:
        if away:
            for copy, place in zip(copies, places):
                if place[0] == away:
                    copy.wait()
        else:
            own_copy.wait()
        outs.append(
            pltpu.make_async_copy(buf.at[block(away)], full_ref.at[block(away)], out_sems.at[away])
        )
        outs[-1].start()
        part = nn(x_ref[:, block(away)], buf[block(away)])
        y_ref[...] = part if away == 0 else y_ref[...] + part
    cosine, sine = cos_ref[...], sin_ref[...]
    queries, keys = H * HD, KV * HD
    for start in range(0, queries + keys, 128):
        tile = turn(y_ref[:, start : start + 128], cosine, sine)
        if start < queries:
            q_ref[:, start : start + 128] = (tile * (1.0 / math.sqrt(HD))).astype(BF)
        else:
            pair_ref[:, start - queries : start - queries + 128] = tile.astype(BF)
    pair_ref[:, keys:] = y_ref[:, queries + keys :].astype(BF)
    for copy in outs:
        copy.wait()


def pieces_forward(x, own, pieces, cosine, sine):
    me, plane = ids()
    rows_in, columns = own.shape
    rows, width = x.shape
    share = columns // lax.axis_size("ctx")
    places = tuple((away, offset, start, part.shape[0]) for away, offset, start, part in pieces)
    arrays = [part for _, _, _, part in pieces]
    hbm, vmem = pl.BlockSpec(memory_space=pltpu.HBM), pl.BlockSpec(memory_space=pltpu.VMEM)
    return pl.pallas_call(
        lambda *refs: pieces_kernel(places, rows_in, share, *refs),
        out_shape=(
            jax.ShapeDtypeStruct((rows, H * HD), BF),
            jax.ShapeDtypeStruct((rows, 2 * KV * HD), BF),
            pltpu.HBM((width, columns), BF),
        ),
        in_specs=[pl.BlockSpec(memory_space=pltpu.SMEM), vmem, hbm]
        + [hbm] * len(arrays)
        + [vmem, vmem],
        out_specs=(vmem, vmem, hbm),
        scratch_shapes=[
            pltpu.VMEM((rows, columns), F32),
            pltpu.VMEM((width, columns), BF),
            pltpu.SemaphoreType.DMA((len(arrays) + 1,)),
            pltpu.SemaphoreType.DMA((width // rows_in,)),
        ],
        compiler_params=pltpu.CompilerParams(vmem_limit_bytes=32 << 20),
        cost_estimate=pl.CostEstimate(
            flops=2 * rows * width * columns, bytes_accessed=4 * width * columns, transcendentals=0
        ),
        name="pieces_forward",
    )(jnp.stack([me, plane]), x, in_hbm(own), *[in_hbm(part) for part in arrays], cosine, sine)


def gather_blocks(weight, before_fsdp, before_ctx):
    rows, columns = weight.shape
    me, plane = ids()
    share = columns // lax.axis_size("ctx")
    mine = lax.dynamic_slice(weight, (0, me * share), (rows, share))
    planes = lax.all_gather(after(mine, before_fsdp), "fsdp")
    others = jnp.stack(
        [
            lax.dynamic_index_in_dim(planes, plane ^ away, 0, keepdims=False)
            for away in range(1, planes.shape[0])
        ]
    )
    return lax.all_gather(after(others, before_ctx), "ctx")


def whole_of(own, blocks):
    ctx_count, others, rows, share = blocks.shape
    plane = lax.axis_index("fsdp")
    columns = ctx_count * share
    full = jnp.zeros(((others + 1) * rows, columns), own.dtype)
    full = lax.dynamic_update_slice(full, own, (plane * rows, 0))
    for away in range(1, others + 1):
        part = blocks[:, away - 1].transpose(1, 0, 2).reshape(rows, columns)
        full = lax.dynamic_update_slice(full, part, ((plane ^ away) * rows, 0))
    return full


def in_hbm(value):
    return pltpu.with_memory_space_constraint(value, pltpu.HBM)


def out_kernel(back, ids_ref, x_ref, own_ref, blocks_ref, *refs):
    hidden_ref, gain_ref = (None, None) if back else refs[:2]
    outs = refs if back else refs[2:]
    own_buf, buf, sems = outs[-3:]
    ctx_count, others, rows, share = buf.shape
    plane = ids_ref[1]

    def block_copy(c):
        return pltpu.make_async_copy(blocks_ref.at[c], buf.at[c], sems.at[c])

    own_copy = pltpu.make_async_copy(own_ref, own_buf, sems.at[ctx_count])
    own_copy.start()
    for c in range(ctx_count):
        block_copy(c).start()

    def features(away):
        return pl.ds(pl.multiple_of((plane ^ away) * rows, 128), rows)

    def columns(c):
        return pl.ds(pl.multiple_of(c * share, 128), share)

    own_copy.wait()
    if back:
        y_ref = outs[0]

        @pl.loop(0, ctx_count)
        def _(c):
            block_copy(c).wait()
            total = nn(x_ref[:, features(0)], own_buf[:, columns(c)])
            for away in range(1, others + 1):
                total += nn(x_ref[:, features(away)], buf[c, away - 1])
            y_ref[:, columns(c)] = total.astype(BF)

        return
    residual_ref, normed_ref = outs[:2]
    residual_ref[...] = hidden_ref[...].astype(F32)

    @pl.loop(0, ctx_count)
    def _(c):
        block_copy(c).wait()
        x = x_ref[:, columns(c)]
        residual_ref[:, features(0)] += nt(x, own_buf[:, columns(c)])
        for away in range(1, others + 1):
            residual_ref[:, features(away)] += nt(x, buf[c, away - 1])

    residual = residual_ref[...]
    normed_ref[...] = (residual * norm_scale(residual) * gain_ref[...]).astype(BF)


def out_call(back, x, own, blocks, extra, out_shape):
    vmem, hbm = pl.BlockSpec(memory_space=pltpu.VMEM), pl.BlockSpec(memory_space=pltpu.HBM)
    return pl.pallas_call(
        lambda *refs: out_kernel(back, *refs),
        out_shape=out_shape,
        in_specs=[pl.BlockSpec(memory_space=pltpu.SMEM), vmem, hbm, hbm] + [vmem] * len(extra),
        out_specs=jax.tree.map(lambda _: vmem, out_shape),
        scratch_shapes=[
            pltpu.VMEM(own.shape, own.dtype),
            pltpu.VMEM(blocks.shape, blocks.dtype),
            pltpu.SemaphoreType.DMA((blocks.shape[0] + 1,)),
        ],
        compiler_params=pltpu.CompilerParams(vmem_limit_bytes=24 << 20),
        cost_estimate=pl.CostEstimate(
            flops=2 * x.shape[0] * own.size * (blocks.shape[1] + 1),
            bytes_accessed=2 * own.size * (blocks.shape[1] + 1),
            transcendentals=0,
        ),
        name="out_back" if back else "out_forward",
    )(jnp.stack(ids()), x, in_hbm(own), in_hbm(blocks), *extra)


def out_forward(attn_rows, own, blocks, hidden, gain):
    if blocks.shape[3] % 128:
        residual = hidden.astype(F32) + nt(attn_rows, whole_of(own, blocks))
        return residual, (residual * norm_scale(residual) * gain).astype(BF)
    out_shape = (
        jax.ShapeDtypeStruct(hidden.shape, F32),
        jax.ShapeDtypeStruct(hidden.shape, BF),
    )
    return out_call(False, attn_rows, own, blocks, [hidden, gain[None]], out_shape)


def out_back(x, own, blocks):
    if blocks.shape[3] % 128:
        return nn(x, whole_of(own, blocks)).astype(BF)
    out_shape = jax.ShapeDtypeStruct((x.shape[0], own.shape[1]), BF)
    return out_call(True, x, own, blocks, [], out_shape)


def one_back_kernel(
    query_ref, pair_ref, w_ref, hidden_ref, gain_ref, residual_ref, y_ref
):
    step = pl.program_id(0)
    rows = w_ref.shape[0]
    split = query_ref.shape[1]
    y_ref[:, pl.ds(pl.multiple_of(step * rows, 128), rows)] = nt(
        query_ref[...], w_ref[:, :split]
    ) + nt(pair_ref[...], w_ref[:, split:])

    @pl.when(step == pl.num_programs(0) - 1)
    def _():
        grad = y_ref[...]
        inputs = hidden_ref[...].astype(F32)
        scale = norm_scale(inputs)
        unit = inputs * scale
        scaled = gain_ref[...] * grad
        y_ref[...] = residual_ref[...] + scale * (
            scaled - unit * jnp.mean(scaled * unit, axis=-1, keepdims=True)
        )


def one_back(query_part, pair_part, weight, hidden, gain, residual_grad):
    rows, width = hidden.shape
    columns = weight.shape[1]
    tile = FFN_TILE

    def whole(array):
        return pl.BlockSpec(array.shape, lambda j: (0, 0))

    gain = gain[None]
    return pl.pallas_call(
        one_back_kernel,
        grid=(width // tile,),
        out_shape=jax.ShapeDtypeStruct((rows, width), F32),
        in_specs=[
            whole(query_part),
            pl.BlockSpec((rows, pair_part.shape[1]), lambda j: (0, 0)),
            pl.BlockSpec((tile, columns), lambda j: (j, 0)),
            whole(hidden),
            whole(gain),
            whole(residual_grad),
        ],
        out_specs=pl.BlockSpec((rows, width), lambda j: (0, 0)),
        compiler_params=pltpu.CompilerParams(vmem_limit_bytes=24 << 20),
        cost_estimate=pl.CostEstimate(
            flops=2 * rows * width * columns,
            bytes_accessed=2 * width * columns,
            transcendentals=0,
        ),
        name="one_back",
    )(query_part, pair_part, in_hbm(weight), hidden, gain, residual_grad)


def send_rows(values):
    if lax.axis_size("fsdp") != 4:
        return fetch_rows(values)
    third = swap(values, "fsdp", 3)
    return [values, swap(values, "fsdp", 1), third]


def relay_rows(planes):
    if lax.axis_size("fsdp") != 4:
        return planes
    values, first, third = planes
    return [values, first, swap(third, "fsdp", 1), third]


def pass_rows(values):
    return relay_rows(send_rows(values))


def fetch_rows(values):
    count = lax.axis_size("fsdp")
    return [values] + [swap(values, "fsdp", away) for away in range(1, count)]


def sum_rows(parts, forward):
    count = len(parts)
    if count == 4 and forward:
        passed = swap(parts[2], "fsdp", 1).astype(F32)
        one = swap(parts[1], "fsdp", 1)
        third = swap((parts[3].astype(F32) + passed).astype(BF), "fsdp", 3)
        return [parts[0], one, third]
    return parts[:1] + [swap(parts[i], "fsdp", i) for i in range(1, count)]


def by_feature(values):
    rows, width = values.shape
    ctx_count, fsdp_count = lax.axis_size("ctx"), lax.axis_size("fsdp")
    blocks = values.reshape(rows, ctx_count, fsdp_count, width // (ctx_count * fsdp_count))
    return blocks.transpose(0, 2, 1, 3).reshape(rows, width)


def sum_over_ctx(part_for):
    pairs = lax.axis_size("ctx") // 2
    sent = jnp.stack([part_for(2 * pair + 1).astype(BF) for pair in range(pairs)])
    got = swap(sent, "ctx", 1)
    sums = [part_for(2 * pair).astype(F32) + got[pair].astype(F32) for pair in range(pairs)]
    total = sums[0]
    for pair in range(1, pairs):
        total = total + swap(sums[pair].astype(BF), "ctx", 2 * pair).astype(F32)
    return total


def ctx_rows_sum(values):
    height = values.shape[0] // lax.axis_size("ctx")
    me = lax.axis_index("ctx")

    def part(offset):
        return lax.dynamic_slice(
            values, ((me ^ offset) * height, 0), (height, values.shape[1])
        )

    return sum_over_ctx(part)


def key_offsets():
    count = lax.axis_size("ctx")
    return list(range(0, count, 2)) + list(range(1, count, 2))


def gather_keys(piece):
    same = [piece] + [swap(piece, "ctx", far) for far in range(2, lax.axis_size("ctx"), 2)]
    mine = jnp.concatenate(same, axis=0)
    return mine, swap(mine, "ctx", 1)


def sum_pairs(kept, sent, cosine, sine):
    _, count, width = kept.shape
    pairs = lax.axis_size("ctx") // 2
    got = swap(sent, "ctx", 1)
    sums = (kept.astype(F32) + got.astype(F32)).reshape(2, pairs, count // pairs, width)
    far = [swap(sums[:, pair].astype(BF), "ctx", 2 * pair) for pair in range(1, pairs)]
    return pair_turn(sums[:, 0], far, cosine, sine), got


def half_mask(shape):
    return lax.broadcasted_iota(jnp.int32, shape, len(shape) - 1) % 128 < HD


def turn(values, cosine, sine):
    lanes = lax.broadcasted_iota(jnp.int32, values.shape, 1) % HD
    turned = jnp.where(
        lanes < HD // 2, pltpu.roll(values, 128 - HD // 2, 1), pltpu.roll(values, HD // 2, 1)
    )
    return values * cosine + turned * sine


def doubled(tile, odd):
    wide = tile.astype(F32)
    other = pltpu.roll(wide, HD, 1)
    return jnp.where(half_mask(tile.shape) == (odd == 0), wide, other).astype(BF)


def split_heads(tile_pair):
    zero = jnp.zeros((), tile_pair.dtype)
    parts = []
    for j in range(2):
        tile = tile_pair[:, j * 128 : (j + 1) * 128]
        mask = half_mask(tile.shape)
        parts += [jnp.where(mask, tile, zero), jnp.where(mask, zero, tile)]
    return jnp.concatenate(parts, axis=0)


def merge_heads(stacked):
    rows = stacked.shape[0] // 4
    tiles = []
    for j in range(2):
        even = stacked[2 * j * rows : (2 * j + 1) * rows]
        odd = stacked[(2 * j + 1) * rows : (2 * j + 2) * rows]
        tiles.append(jnp.where(half_mask(even.shape), even, odd))
    return jnp.concatenate(tiles, axis=1)


def key_chunks(refs, chunk):
    first = 0
    for k_ref, v_ref in refs:
        for start in range(0, k_ref.shape[0], chunk):
            at = slice(start, start + chunk)
            yield first + start, k_ref.at[at, :], v_ref.at[at, :]
        first += k_ref.shape[0]


def masked_scores(keys, queries, key_ref, own_ref, start):
    allowed = key_ref[start : start + keys.shape[0], :1] <= own_ref[...]
    bias = jnp.where(allowed, 0.0, -1e30).astype(F32)
    return nt(keys, queries) + jnp.concatenate([bias] * 4, axis=1)


def attend_kernel(
    chunk, q_ref, ka_ref, va_ref, kb_ref, vb_ref, key_ref, own_ref, rows_ref, attended_ref, log_ref
):
    odd = pl.program_id(0) % 2
    rows = q_ref.shape[0]
    queries = split_heads(q_ref[...])
    parts = list(key_chunks(((ka_ref, va_ref), (kb_ref, vb_ref)), chunk))
    scores = [
        masked_scores(doubled(k_ref[...], odd), queries, key_ref, own_ref, start)
        for start, k_ref, _ in parts
    ]
    top = jnp.max(scores[0], axis=0, keepdims=True)
    for score in scores[1:]:
        top = jnp.maximum(top, jnp.max(score, axis=0, keepdims=True))
    total = jnp.zeros_like(top)
    summed = jnp.zeros((4 * rows, 128), F32)
    for score, (_, _, v_ref) in zip(scores, parts):
        weights = jnp.exp(score - top)
        total += jnp.sum(weights, axis=0, keepdims=True)
        summed += tn(weights.astype(BF), doubled(v_ref[...], odd))
    log_ref[0] = top + jnp.log(total)
    attended = merge_heads(summed / jnp.transpose(jnp.broadcast_to(total, (128, 4 * rows))))
    attended_ref[...] = attended
    rows_ref[...] = attended.astype(BF)


def key_specs(parts):
    tiles = parts[0].shape[1] // 256
    specs, arrays = [], []
    for part in parts:
        specs.append(pl.BlockSpec((part.shape[0], 128), lambda g: (0, g // 2)))
        specs.append(pl.BlockSpec((part.shape[0], 128), lambda g: (0, tiles + g // 2)))
        arrays += [part, part]
    return specs, arrays


def attend(queries, keys_values, key_anchor, own_anchor):
    rows, width = queries.shape
    count = key_anchor.shape[0]
    specs, arrays = key_specs(keys_values)
    wide = pl.BlockSpec((rows, 256), lambda g: (0, g))
    return pl.pallas_call(
        lambda *refs: attend_kernel(KEY_CHUNK, *refs),
        grid=(KV,),
        out_shape=(
            jax.ShapeDtypeStruct((rows, width), BF),
            jax.ShapeDtypeStruct((rows, width), F32),
            jax.ShapeDtypeStruct((KV, 1, 4 * rows), F32),
        ),
        in_specs=[wide]
        + specs
        + [
            pl.BlockSpec((count, 128), lambda g: (0, 0)),
            pl.BlockSpec((1, rows), lambda g: (0, 0)),
        ],
        out_specs=(wide, wide, pl.BlockSpec((1, 1, 4 * rows), lambda g: (g, 0, 0))),
        compiler_params=pltpu.CompilerParams(vmem_limit_bytes=48 << 20),
        cost_estimate=pl.CostEstimate(
            flops=4 * rows * width * count,
            bytes_accessed=4 * count * KV * HD,
            transcendentals=rows * H * count,
        ),
        name="attend",
    )(queries, *arrays, key_anchor, own_anchor)


def attend_back_kernel(
    chunk, q_ref, grad_ref, attended_ref, ka_ref, va_ref, kb_ref, vb_ref, key_ref, own_ref, log_ref,
    cos_ref, sin_ref, dq_ref, kept_ref, sent_ref,
):
    odd = pl.program_id(0) % 2
    rows = q_ref.shape[0]
    half = ka_ref.shape[0]
    queries, grads = split_heads(q_ref[...]), split_heads(grad_ref[...])
    product = grads.astype(F32) * split_heads(attended_ref[...])
    delta = jnp.sum(jnp.transpose(product), axis=0, keepdims=True)
    log_total = log_ref[0]
    total = jnp.zeros((4 * rows, 128), F32)
    keep = half_mask((chunk, 128)) == (odd == 0)
    for start, k_ref, v_ref in key_chunks(((ka_ref, va_ref), (kb_ref, vb_ref)), chunk):
        keys, values = doubled(k_ref[...], odd), doubled(v_ref[...], odd)
        scores = masked_scores(keys, queries, key_ref, own_ref, start)
        probs = jnp.exp(scores - log_total)
        value_grad = nn(probs.astype(BF), grads)
        score_grad = (probs * (nt(values, grads) - delta)).astype(BF)
        key_grad = nn(score_grad, queries)
        total += tn(score_grad, keys)
        out_ref = kept_ref if start < half else sent_ref
        at = slice(start % half, start % half + chunk)
        for part, value in enumerate((key_grad, value_grad)):
            value = (value + pltpu.roll(value, HD, 1)).astype(BF)
            out_ref[part, at, :] = jnp.where(keep, value, out_ref[part, at, :])
    merged = merge_heads(total) * (1.0 / math.sqrt(HD))
    cosine, sine = cos_ref[...], sin_ref[...]
    for j in range(2):
        tile = slice(j * 128, (j + 1) * 128)
        dq_ref[:, tile] = turn(merged[:, tile], cosine, -sine).astype(BF)


def attend_back(queries, grads, attended, keys_values, key_anchor, own_anchor, logs, cosine, sine):
    rows, width = queries.shape
    count = key_anchor.shape[0]
    specs, arrays = key_specs(keys_values)
    wide = pl.BlockSpec((rows, 256), lambda g: (0, g))
    small = pl.BlockSpec((rows, 128), lambda g: (0, 0))
    pair = pl.BlockSpec((2, count // 2, 128), lambda g: (0, 0, g // 2))
    return pl.pallas_call(
        lambda *refs: attend_back_kernel(KEY_CHUNK, *refs),
        grid=(KV,),
        out_shape=(
            jax.ShapeDtypeStruct((rows, width), BF),
            jax.ShapeDtypeStruct((2, count // 2, KV * HD), BF),
            jax.ShapeDtypeStruct((2, count // 2, KV * HD), BF),
        ),
        in_specs=[wide, wide, wide]
        + specs
        + [
            pl.BlockSpec((count, 128), lambda g: (0, 0)),
            pl.BlockSpec((1, rows), lambda g: (0, 0)),
            pl.BlockSpec((1, 1, 4 * rows), lambda g: (g, 0, 0)),
            small,
            small,
        ],
        out_specs=(wide, pair, pair),
        compiler_params=pltpu.CompilerParams(vmem_limit_bytes=48 << 20),
        cost_estimate=pl.CostEstimate(
            flops=10 * rows * width * count,
            bytes_accessed=8 * count * KV * HD,
            transcendentals=rows * H * count,
        ),
        name="attend_back",
    )(queries, grads, attended, *arrays, key_anchor, own_anchor, logs, cosine, sine)


def pair_turn_kernel(copies, own_ref, *refs):
    got, (cos_ref, sin_ref, y_ref) = refs[:-3], refs[-3:]
    total = own_ref[...]
    for ref in got:
        total = total + ref[...].astype(F32)
    cosine, sine = cos_ref[...], sin_ref[...]
    _, rows, width = total.shape
    tiles = [
        turn(total[0, :, start : start + 128], cosine, -sine).astype(BF)
        for start in range(0, width, 128)
    ]
    values = total[1].astype(BF)
    for copy in range(copies):
        at = slice(copy * rows, (copy + 1) * rows)
        for i, tile in enumerate(tiles):
            y_ref[at, i * 128 : (i + 1) * 128] = tile
        y_ref[at, width:] = values


def pair_turn(own, got, cosine, sine):
    _, rows, width = own.shape
    copies = lax.axis_size("fsdp")
    return pl.pallas_call(
        lambda *refs: pair_turn_kernel(copies, *refs),
        out_shape=jax.ShapeDtypeStruct((copies * rows, 2 * width), BF),
        name="pair_turn",
    )(own, *got, cosine, sine)


def join_rows(x_buf, refs):
    @pl.when((pl.program_id(0) == 0))
    def _():
        rows = refs[0].shape[0]
        for i, ref in enumerate(refs):
            x_buf[i * rows : (i + 1) * rows] = ref[...]


def ffn_kernel(count, earlier, *refs):
    rows_refs, (act_ref, w_ref), refs = refs[:count], refs[count : count + 2], refs[count + 2 :]
    out_ref, refs = refs[earlier], refs[earlier + 1 :]
    sum_refs, (x_buf, sum_buf) = refs[:count], refs[count:]
    join_rows(x_buf, rows_refs)
    step = pl.program_id(0)
    gate_w, up_w = w_ref[0], w_ref[1]
    x = x_buf[...]
    gate, up = nn(x, gate_w), nn(x, up_w)
    act_grad = act_ref[...]
    sig = jax.nn.sigmoid(gate)
    silu = gate * sig
    gate_grad = (act_grad * up * sig * (1.0 + gate * (1.0 - sig))).astype(BF)
    up_grad = (act_grad * silu).astype(BF)
    out_ref[0], out_ref[1], out_ref[2] = gate_grad, up_grad, (silu * up).astype(BF)
    part = nt(gate_grad, gate_w) + nt(up_grad, up_w)

    @pl.when(step == 0)
    def _():
        sum_buf[...] = part

    @pl.when(step > 0)
    def _():
        sum_buf[...] += part

    @pl.when(step == pl.num_programs(0) - 1)
    def _():
        rows = sum_refs[0].shape[0]
        for i, ref in enumerate(sum_refs):
            ref[...] = sum_buf[i * rows : (i + 1) * rows].astype(ref.dtype)


def ffn_middle(blocks, act_grad, half, weights, kinds, earlier):
    width = blocks[0].shape[1]
    rows = blocks[0].shape[0] * len(blocks)
    hidden = weights.shape[2]
    tile = FFN_TILE
    whole = [pl.BlockSpec(block.shape, lambda j: (0, 0)) for block in blocks]
    out = pl.pallas_call(
        lambda *refs: ffn_kernel(len(blocks), len(earlier), *refs),
        grid=(hidden // tile,),
        out_shape=(
            pltpu.HBM((3, 2 * rows, hidden), BF),
            *[jax.ShapeDtypeStruct(block.shape, kind) for block, kind in zip(blocks, kinds)],
        ),
        in_specs=whole
        + [
            pl.BlockSpec((rows, tile), lambda j: (half, j)),
            pl.BlockSpec((2, width, tile), lambda j: (0, 0, j)),
        ]
        + [pl.BlockSpec(memory_space=pltpu.HBM)] * len(earlier),
        out_specs=(pl.BlockSpec((3, rows, tile), lambda j: (0, half, j)), *whole),
        input_output_aliases={len(blocks) + 2: 0} if earlier else {},
        scratch_shapes=[pltpu.VMEM((rows, width), BF), pltpu.VMEM((rows, width), F32)],
        compiler_params=pltpu.CompilerParams(vmem_limit_bytes=40 << 20),
        cost_estimate=pl.CostEstimate(
            flops=8 * rows * width * hidden,
            bytes_accessed=4 * width * hidden,
            transcendentals=rows * hidden,
        ),
        name="ffn_middle",
    )(*blocks, act_grad, weights, *earlier)
    return out[0], list(out[1:])


def products_kernel(count, added, ids_ref, *refs):
    blocks, right, rest = refs[: 2 * count], refs[2 * count], refs[2 * count + 1 :]
    out_ref, left = rest[-2:]
    rows, height = blocks[0].shape
    for j in range(2):
        for i in range(count):
            at = (slice(i * rows, (i + 1) * rows), slice(j * height, (j + 1) * height))
            left[at] = blocks[j * count + i][...]
    part = tn(left[...], right[0])
    if added:
        part = part + rest[0][0].astype(F32)
    out_ref[0] = part.astype(BF)


def half_products(rows_of, parts, first, size, got, earlier):
    count = len(rows_of)
    rows, width = rows_of[0].shape
    matrices, _, hidden = parts.shape
    ctx_count = lax.axis_size("ctx")
    height = width // ctx_count
    kept = got is not None

    def left(j):
        def place(k, i, ids_ref):
            own = ids_ref[0] % 2
            return (0, 2 * (2 * i + j) + (own if kept else 1 - own))

        return pl.BlockSpec((rows, height), place)

    def out(start):
        return pl.BlockSpec((1, 2 * height, hidden), lambda k, i, ids_ref: (start + k, i, 0))

    right = pl.BlockSpec((1, rows * count, hidden), lambda k, i, ids_ref: (first + k, 0, 0))
    extra = ([got] if kept else []) + earlier
    operands = 2 * count + 1 + len(extra)
    return pl.pallas_call(
        lambda *refs: products_kernel(count, kept, *refs),
        grid_spec=pltpu.PrefetchScalarGridSpec(
            num_scalar_prefetch=1,
            grid=(size, ctx_count // 4),
            in_specs=[left(0)] * count
            + [left(1)] * count
            + [right]
            + [out(0)] * kept
            + [pl.BlockSpec(memory_space=pltpu.HBM)] * len(earlier),
            out_specs=out(first if kept else 0),
            scratch_shapes=[pltpu.VMEM((count * rows, 2 * height), BF)],
        ),
        out_shape=pltpu.HBM((matrices if kept else size, width // 2, hidden), BF),
        input_output_aliases={operands: 0} if earlier else {},
        compiler_params=pltpu.CompilerParams(vmem_limit_bytes=24 << 20),
        cost_estimate=pl.CostEstimate(
            flops=size * count * rows * width * hidden,
            bytes_accessed=size * width * hidden,
            transcendentals=0,
        ),
    )(jnp.stack(ids()), *rows_of, *rows_of, in_hbm(parts), *extra)


def ffn_gradient(rows_in, rows_out, parts):
    count = lax.axis_size("ctx")
    if count % 4 or (rows_in[0].shape[1] // count) % 128:
        left, grad = (jnp.concatenate(rows, axis=0) for rows in (rows_in, rows_out))
        products = [tn(left, parts[0]), tn(left, parts[1]), tn(grad, parts[2])]
        products = jnp.stack(products, axis=1).astype(BF)
        return lax.psum_scatter(products, "ctx", scatter_dimension=0, tiled=True), parts
    calls = ((rows_out, 2, 1), (rows_in, 0, 1), (rows_in, 1, 1))
    got = []
    for rows_of, first, size in calls:
        sent = half_products(rows_of, parts, first, size, None, [])
        got.append(swap(sent, "ctx", 1))
    kept = []
    for (rows_of, first, size), part in zip(calls, got):
        kept = [half_products(rows_of, parts, first, size, part, kept)]
    groups = [list(range(core, count, 2)) for core in range(2)]
    kept = kept[0].transpose(1, 0, 2)
    rows = lax.psum_scatter(kept, "ctx", scatter_dimension=0, tiled=True, axis_index_groups=groups)
    return rows, after(parts, kept)


def widen_kernel(x_ref, y_ref):
    y_ref[...] = x_ref[...].astype(F32)


def widened(values):
    values = values.transpose(1, 0, 2)
    matrices, rows, hidden = values.shape
    block = pl.BlockSpec((1, rows // 2, hidden), lambda k, i: (k, i, 0))
    return pl.pallas_call(
        widen_kernel,
        grid=(matrices, 2),
        out_shape=jax.ShapeDtypeStruct(values.shape, F32),
        in_specs=[block],
        out_specs=block,
        compiler_params=pltpu.CompilerParams(vmem_limit_bytes=16 << 20),
        name="widened",
    )(values).transpose(1, 0, 2)


def down_back_kernel(count, *refs):
    rows_refs, (w_ref, y_ref, x_buf) = refs[:count], refs[count:]
    join_rows(x_buf, rows_refs)
    y_ref[...] = nn(x_buf[...], w_ref[0])


def down_back(blocks, weights):
    width = blocks[0].shape[1]
    rows = blocks[0].shape[0] * len(blocks)
    hidden = weights.shape[2]
    tile = FFN_TILE
    return pl.pallas_call(
        lambda *refs: down_back_kernel(len(blocks), *refs),
        grid=(hidden // tile,),
        out_shape=pltpu.HBM((rows, hidden), F32),
        in_specs=[pl.BlockSpec(block.shape, lambda j: (0, 0)) for block in blocks]
        + [pl.BlockSpec((1, width, tile), lambda j: (2, 0, j))],
        out_specs=pl.BlockSpec((rows, tile), lambda j: (0, j)),
        scratch_shapes=[pltpu.VMEM((rows, width), BF)],
        compiler_params=pltpu.CompilerParams(vmem_limit_bytes=24 << 20),
        cost_estimate=pl.CostEstimate(
            flops=2 * rows * width * hidden,
            bytes_accessed=2 * width * hidden,
            transcendentals=0,
        ),
        name="down_back",
    )(*blocks, weights)


def down_kernel(x_ref, w_ref, *y_refs):
    rows = x_ref.shape[1] // len(y_refs)
    total = nt(x_ref[0], w_ref[0])
    for i, y_ref in enumerate(y_refs):
        y_ref[...] = total[i * rows : (i + 1) * rows].astype(y_ref.dtype)


def down_forward(parts, weights, count):
    _, rows, hidden = parts.shape
    width = weights.shape[1]
    tile = FFN_TILE
    height = rows // count
    return pl.pallas_call(
        down_kernel,
        grid=(width // tile,),
        out_shape=tuple(
            jax.ShapeDtypeStruct((height, width), BF if i else F32) for i in range(count)
        ),
        in_specs=[
            pl.BlockSpec((1, rows, hidden), lambda j: (2, 0, 0)),
            pl.BlockSpec((1, tile, hidden), lambda j: (2, j, 0)),
        ],
        out_specs=tuple(pl.BlockSpec((height, tile), lambda j: (0, j)) for _ in range(count)),
        compiler_params=pltpu.CompilerParams(vmem_limit_bytes=24 << 20),
        cost_estimate=pl.CostEstimate(
            flops=2 * rows * width * hidden,
            bytes_accessed=2 * width * hidden,
            transcendentals=0,
        ),
        name="down_forward",
    )(in_hbm(parts), weights)


def share_kernel(count, sizes, ids_ref, *refs):
    products = len(sizes)
    lefts = [refs[i * count : (i + 1) * count] for i in range(products)]
    rest = refs[products * count :]
    rights = []
    for size in sizes:
        rights.append(rest[:size])
        rest = rest[size:]
    bufs = rest[len(rest) - products :]
    terms, (kept_ref, sent_ref) = rest[: -products - 2], rest[-products - 2 : -products]
    half = kept_ref.shape[1]
    own = ids_ref[0] % 2 == 0

    @pl.when(pl.program_id(0) == 0)
    def _():
        for parts, buf in zip(rights, bufs):
            rows = buf.shape[0] // count
            for away in range(count):
                if len(parts) > 1:
                    block = parts[away][...]
                else:
                    start = (ids_ref[1] ^ away) * rows
                    block = parts[0][pl.ds(pl.multiple_of(start, 16), rows), :]
                buf[away * rows : (away + 1) * rows] = block

    def emit(part, column):
        at = slice(column, column + part.shape[1])
        kept_ref[0, :, at] = jnp.where(own, part[:half], part[half:])
        sent_ref[0, :, at] = jnp.where(own, part[half:], part[:half])

    column = 0
    for left, buf in zip(lefts, bufs):
        joined = jnp.concatenate([ref[...] for ref in left], axis=0)
        emit(tn(joined, buf[...]).astype(BF), column)
        column += buf.shape[1]
    for term in terms:
        tall = jnp.broadcast_to(term[...], (128, term.shape[1]))
        emit(jnp.transpose(tall).astype(BF), column)
        column += 128


def share_products(lefts, rights, terms):
    ctx_count = lax.axis_size("ctx")
    pairs = ctx_count // 2
    count = len(lefts[0])
    rows, width = lefts[0][0].shape
    height = width // ctx_count
    groups = [right if isinstance(right, list) else [right] for right in rights]
    widths = [group[0].shape[1] for group in groups]
    columns = sum(widths) + 128 * len(terms)

    def place(j, ids_ref):
        return (0, (ids_ref[0] // 2) ^ j)

    def whole(array):
        return pl.BlockSpec(array.shape, lambda j, ids_ref: (0, 0))

    shape = jax.ShapeDtypeStruct((pairs, height, columns), BF)
    out = pl.BlockSpec((1, height, columns), lambda j, ids_ref: (j, 0, 0))
    flat_lefts = [block for left in lefts for block in left]
    flat_rights = [block for group in groups for block in group]
    return pl.pallas_call(
        lambda *refs: share_kernel(count, [len(group) for group in groups], *refs),
        grid_spec=pltpu.PrefetchScalarGridSpec(
            num_scalar_prefetch=1,
            grid=(pairs,),
            in_specs=[pl.BlockSpec((rows, 2 * height), place) for _ in flat_lefts]
            + [whole(block) for block in flat_rights]
            + [pl.BlockSpec((1, 2 * height), place) for _ in terms],
            out_specs=(out, out),
            scratch_shapes=[pltpu.VMEM((count * rows, size), BF) for size in widths],
        ),
        out_shape=(shape, shape),
        compiler_params=pltpu.CompilerParams(vmem_limit_bytes=32 << 20),
        cost_estimate=pl.CostEstimate(
            flops=2 * count * rows * width * columns,
            bytes_accessed=2 * (count * rows + columns) * width,
            transcendentals=0,
        ),
        name="share_terms" if terms else "share_products",
    )(jnp.stack(ids()), *flat_lefts, *flat_rights, *[term[None] for term in terms])


def in_fsdp_order(value):
    if not isinstance(value, list):
        return value
    plane = lax.axis_index("fsdp")
    stacked = jnp.stack(value)
    parts = [
        lax.dynamic_index_in_dim(stacked, plane ^ away, 0, keepdims=False)
        for away in range(len(value))
    ]
    return jnp.concatenate(parts, axis=0)


def share_start(lefts, rights, terms):
    pairs = lax.axis_size("ctx") // 2
    if (lefts[0][0].shape[1] // pairs) % 128:
        values = [tn(in_fsdp_order(a), in_fsdp_order(b)) for a, b in zip(lefts, rights)]
        values += [jnp.broadcast_to(term[:, None], (term.shape[0], 128)) for term in terms]
        return [ctx_rows_sum(jnp.concatenate(values, axis=1))]
    kept, sent = share_products(lefts, rights, terms)
    got = swap(sent, "ctx", 1)
    parts = [kept[0], got[0]]
    for pair in range(1, pairs):
        part = (kept[pair].astype(F32) + got[pair].astype(F32)).astype(BF)
        parts.append(swap(part, "ctx", 2 * pair))
    return parts


def share_finish(parts):
    total = parts[0].astype(F32)
    for part in parts[1:]:
        total = total + part.astype(F32)
    return total


def own_rows_of(values, height):
    index = lax.axis_index("ctx") * lax.axis_size("fsdp") + lax.axis_index("fsdp")
    return lax.dynamic_slice_in_dim(values, index * height, height, 0)


def feature_parts(values):
    count, plane = lax.axis_size("fsdp"), lax.axis_index("fsdp")
    values = by_feature(values)
    rows, width = values.shape
    width //= count
    return [
        lax.dynamic_slice(values, (0, (plane ^ away) * width), (rows, width))
        for away in range(count)
    ]


def feature_rows(parts):
    return [swap(part, "fsdp", away) if away else part for away, part in enumerate(parts)]


def own_features(terms):
    ctx_count, fsdp_count = lax.axis_size("ctx"), lax.axis_size("fsdp")
    total = jnp.stack(terms)
    away = 1
    while away < fsdp_count:
        total = total + swap(total, "fsdp", away)
        away *= 2
    blocks = total.reshape(len(terms), ctx_count, fsdp_count, -1)
    own = lax.dynamic_index_in_dim(blocks, lax.axis_index("fsdp"), 2, keepdims=False)
    own = own.reshape(len(terms), -1)
    return [own[i] for i in range(len(terms))]


def layer(
    hidden_in,
    out_grad,
    positions,
    block_order,
    attn_gain,
    ffn_gain,
    qkv_weight,
    out_weight,
    ffn_weight,
):
    ctx_count, fsdp_count = lax.axis_size("ctx"), lax.axis_size("fsdp")
    me, _ = ids()
    rows = hidden_in.shape[1]
    queries_width, kv_width = H * HD, KV * HD
    ffn_parts = in_hbm(ffn_weight.transpose(1, 0, 2))

    frequency = jnp.power(ROPE_BASE, -(jnp.arange(HD // 2, dtype=F32) * 2.0 / HD))
    angles = positions[0].astype(F32)[:, None] * frequency[None, :]
    cosine = jnp.tile(jnp.cos(angles), (1, 4))
    sine = jnp.tile(jnp.concatenate([-jnp.sin(angles), jnp.sin(angles)], axis=1), (1, 2))
    own_anchor = anchors_of(block_order, me, rows)[None]
    key_anchor = jnp.concatenate(
        [anchors_of(block_order, me ^ offset, rows) for offset in key_offsets()]
    )
    key_anchor = jnp.broadcast_to(key_anchor[:, None], (rows * ctx_count, 128))

    inputs = hidden_in[0].astype(F32)
    grad_in = out_grad[0]
    scale_one = norm_scale(inputs)
    normed_one = (inputs * scale_one * attn_gain).astype(BF)

    one_parts = feature_parts(normed_one)
    fast = ctx_count == 8 and (qkv_weight.shape[1] // ctx_count) % 128 == 0
    if fast:
        early = (cosine, sine, own_anchor, key_anchor, one_parts)
        qkv_pieces, marks = gather_pieces(qkv_weight, early)
        out_blocks = gather_blocks(out_weight, *marks)
        queries, pair, qkv_full = pieces_forward(
            normed_one, qkv_weight, qkv_pieces, cosine, sine
        )
    else:
        marks = (normed_one, normed_one)
        out_blocks = gather_blocks(out_weight, *marks)
        qkv_full = whole_of(qkv_weight, gather_blocks(qkv_weight, normed_one, normed_one))
        projected = nn(normed_one, qkv_full)
        turned = rotate(
            projected[:, : queries_width + kv_width].reshape(rows, H + KV, HD), positions[0]
        ).reshape(rows, queries_width + kv_width)
        queries = (turned[:, :queries_width] * (1.0 / math.sqrt(HD))).astype(BF)
        pair = jnp.concatenate(
            [turned[:, queries_width:], projected[:, queries_width + kv_width :]], axis=1
        ).astype(BF)
    own_one = feature_rows(after(one_parts, pair))
    keys_values = gather_keys(pair)
    rows_out = send_rows(after(grad_in, pair))
    attn_rows, attended, logs = attend(queries, keys_values, key_anchor, own_anchor)
    rows_out = relay_rows(after(rows_out, attn_rows))
    residual, normed_two = out_forward(
        attn_rows, out_weight, out_blocks, hidden_in[0], ffn_gain
    )
    scale_two = norm_scale(residual)
    rows_in = pass_rows(normed_two)
    rows_out = after(rows_out, normed_two)
    act_grad = down_back(rows_out, ffn_parts)

    all_attn = pass_rows(after(attn_rows, rows_in[2]))
    parts, partial = [], []
    half = fsdp_count // 2
    passing = 3 if fsdp_count == 4 else 0
    for index in range(2):
        blocks = rows_in[index * half : (index + 1) * half]
        kinds = [F32 if index * half + i in (0, passing) else BF for i in range(half)]
        out, terms = ffn_middle(blocks, in_hbm(act_grad), index, ffn_parts, kinds, parts)
        parts, partial = [out], partial + terms
    parts = parts[0]
    sum_grad = share_finish(sum_rows(partial, True))
    ffn_weight_grad, parts = ffn_gradient(rows_in, rows_out, parts)
    ffn_weight_grad = widened(ffn_weight_grad)
    out_partial = list(down_forward(parts, ffn_parts, fsdp_count))

    unit_two = residual * scale_two
    ffn_gain_term = jnp.sum(sum_grad * unit_two, axis=0)
    scaled_two = ffn_gain * sum_grad
    residual_grad = grad_in.astype(F32) + scale_two * (
        scaled_two - unit_two * jnp.mean(scaled_two * unit_two, axis=-1, keepdims=True)
    )
    residual_bf = residual_grad.astype(BF)
    out_sum = sum_rows([after(part, residual_bf) for part in out_partial], False)
    (ffn_term,) = own_features([ffn_gain_term])
    attn_grad = out_back(residual_bf, out_weight, out_blocks)
    query_part, kept, sent = attend_back(
        queries, attn_grad, attended, keys_values, key_anchor, own_anchor, logs, cosine, sine
    )
    query_planes = pass_rows(query_part)
    pair_copies, near = sum_pairs(kept, sent, cosine, sine)
    own_residual = feature_rows(feature_parts(after(residual_bf, near)))
    all_pair = lax.all_to_all(pair_copies, "fsdp", split_axis=0, concat_axis=0, tiled=True)
    input_grad = one_back(
        query_part, pair_copies, qkv_full, hidden_in[0], attn_gain, residual_grad
    )
    out_sums = share_start([own_residual], [after(all_attn, input_grad)], [])
    output = (residual + share_finish(after(out_sum, input_grad))).astype(BF)
    qkv_sums = share_start([own_one, own_one], [after(query_planes, output), all_pair], [ffn_term])
    qkv_sums = share_finish(qkv_sums)
    out_weight_grad = share_finish(after(out_sums, qkv_sums))
    qkv_grad = qkv_sums[:, : qkv_weight.shape[1]]
    features = own_rows_of(attn_gain, qkv_grad.shape[0])
    gain_grad = jnp.sum(own_rows_of(qkv_full, qkv_grad.shape[0]).astype(F32) * qkv_grad, axis=1)
    return (
        output[None],
        input_grad[None],
        qkv_grad,
        out_weight_grad,
        ffn_weight_grad,
        gain_grad / features,
        qkv_sums[:, qkv_weight.shape[1]],
    )


def solution(mesh):
    step = sharded(mesh)
    return step


def sharded(mesh):
    return jax.shard_map(
        layer,
        mesh=mesh,
        in_specs=(
            P("fsdp", "ctx", None),
            P("fsdp", "ctx", None),
            P("fsdp", "ctx"),
            P(),
            P(),
            P(),
            P("fsdp", None),
            P("fsdp", None),
            P(None, None, "fsdp"),
        ),
        out_specs=(
            P("fsdp", "ctx", None),
            P("fsdp", "ctx", None),
            P(("ctx", "fsdp"), None),
            P(("ctx", "fsdp"), None),
            P("ctx", None, "fsdp"),
            P(("ctx", "fsdp")),
            P(("ctx", "fsdp")),
        ),
        check_vma=False,
    )
```

```python
import math

import jax
import jax.numpy as jnp
from jax import lax
from jax.experimental import pallas as pl
from jax.experimental.pallas import tpu as pltpu
from jax.sharding import PartitionSpec as P


H = 32
KV = 8
HD = 64

NORM_EPS = 1e-05
ROPE_BASE = 500000.0
FFN_TILE = 512
KEY_CHUNK = 256


BF = jnp.bfloat16
F32 = jnp.float32


def mm(a, b, dims):
    return lax.dot_general(a, b, (dims, ((), ())), preferred_element_type=F32)


def nn(a, b):
    return mm(a, b, ((1,), (0,)))


def nt(a, b):
    return mm(a, b, ((1,), (1,)))


def tn(a, b):
    return mm(a, b, ((0,), (0,)))


def swap(value, axis, offset):
    count = lax.axis_size(axis)
    return lax.ppermute(value, axis, [(i, i ^ offset) for i in range(count)])


def rotate(values, token_places):
    head_dim = values.shape[-1]
    half_dim = head_dim // 2
    frequency = jnp.power(ROPE_BASE, -(jnp.arange(half_dim, dtype=F32) * 2.0 / head_dim))
    angles = token_places.astype(F32)[:, None] * frequency[None, :]
    cosine = jnp.concatenate([jnp.cos(angles), jnp.cos(angles)], axis=-1)[:, None, :]
    sine_part = jnp.concatenate([jnp.sin(angles), jnp.sin(angles)], axis=-1)[:, None, :]
    turned = jnp.concatenate([-values[..., half_dim:], values[..., :half_dim]], axis=-1)
    return values * cosine + turned * sine_part


def norm_scale(values):
    return lax.rsqrt(jnp.mean(values * values, axis=-1, keepdims=True) + NORM_EPS)


def lookup(entries, row_ids):
    matches = row_ids[:, None] == jnp.arange(entries.shape[0], dtype=jnp.int32)[None, :]
    return jnp.sum(jnp.where(matches, entries[None, :], 0), axis=1)


def anchors_of(block_order, owner, row_count):
    block_len = row_count // 2
    row_ids = owner * row_count + jnp.arange(row_count, dtype=jnp.int32)
    return lookup(block_order, row_ids // block_len) * block_len + row_ids % block_len


def after(value, *earlier):
    return lax.optimization_barrier((value, earlier))[0]


def ids():
    return lax.axis_index("ctx"), lax.axis_index("fsdp")


def gather_pieces(weight, early):
    rows, columns = weight.shape
    share = columns // lax.axis_size("ctx")
    half = rows // 2
    mine = lax.dynamic_slice(weight, (0, lax.axis_index("ctx") * share), (rows, share))
    planes = {}
    planes[3] = swap(mine, "fsdp", 3)
    planes[1] = swap(mine, "fsdp", 1)
    planes[2] = swap(after(planes[3], early), "fsdp", 1)
    pieces = []
    for away in (1, 3, 2):
        first = planes[away]
        along_x, along_y = swap(first, "ctx", 2), swap(first, "ctx", 4)
        if away == 1:
            corners = [(6, 0, swap(along_y, "ctx", 2))]
        elif away == 3:
            corners = [(6, 0, swap(along_x, "ctx", 4))]
        else:
            top, low = swap(along_y[:half], "ctx", 2), swap(along_x[half:], "ctx", 4)
            corners = [(6, 0, jnp.concatenate([top, low], axis=0))]
        parts = [(0, 0, first), (2, 0, along_x), (4, 0, along_y)] + corners
        for offset, start, part in parts:
            pieces.append((away, offset, start, part))
            pieces.append((away, offset + 1, start, swap(part, "ctx", 1)))
    return pieces, (planes[2], pieces[-2][3])


def pieces_kernel(places, rows_in, share, ids_ref, x_ref, own_ref, *refs):
    count = len(places)
    piece_refs, refs = refs[:count], refs[count:]
    cos_ref, sin_ref, q_ref, pair_ref, full_ref, y_ref, buf, in_sems, out_sems = refs
    me, plane = ids_ref[0], ids_ref[1]

    def block(away):
        return pl.ds(pl.multiple_of((plane ^ away) * rows_in, 128), rows_in)

    own_copy = pltpu.make_async_copy(own_ref, buf.at[block(0)], in_sems.at[count])
    own_copy.start()
    copies = []
    for i, (away, offset, start, height) in enumerate(places):
        at = pl.ds(pl.multiple_of((plane ^ away) * rows_in + start, 128), height)
        columns = pl.ds(pl.multiple_of((me ^ offset) * share, 128), share)
        copies.append(pltpu.make_async_copy(piece_refs[i], buf.at[at, columns], in_sems.at[i]))
        copies[-1].start()
    outs = []
    order = [0] + list(dict.fromkeys(away for away, _, _, _ in places))
    for away in order:
        if away:
            for copy, place in zip(copies, places):
                if place[0] == away:
                    copy.wait()
        else:
            own_copy.wait()
        outs.append(
            pltpu.make_async_copy(buf.at[block(away)], full_ref.at[block(away)], out_sems.at[away])
        )
        outs[-1].start()
        part = nn(x_ref[:, block(away)], buf[block(away)])
        y_ref[...] = part if away == 0 else y_ref[...] + part
    cosine, sine = cos_ref[...], sin_ref[...]
    queries, keys = H * HD, KV * HD
    for start in range(0, queries + keys, 128):
        tile = turn(y_ref[:, start : start + 128], cosine, sine)
        if start < queries:
            q_ref[:, start : start + 128] = (tile * (1.0 / math.sqrt(HD))).astype(BF)
        else:
            pair_ref[:, start - queries : start - queries + 128] = tile.astype(BF)
    pair_ref[:, keys:] = y_ref[:, queries + keys :].astype(BF)
    for copy in outs:
        copy.wait()


def pieces_forward(x, own, pieces, cosine, sine):
    me, plane = ids()
    rows_in, columns = own.shape
    rows, width = x.shape
    share = columns // lax.axis_size("ctx")
    places = tuple((away, offset, start, part.shape[0]) for away, offset, start, part in pieces)
    arrays = [part for _, _, _, part in pieces]
    hbm, vmem = pl.BlockSpec(memory_space=pltpu.HBM), pl.BlockSpec(memory_space=pltpu.VMEM)
    return pl.pallas_call(
        lambda *refs: pieces_kernel(places, rows_in, share, *refs),
        out_shape=(
            jax.ShapeDtypeStruct((rows, H * HD), BF),
            jax.ShapeDtypeStruct((rows, 2 * KV * HD), BF),
            pltpu.HBM((width, columns), BF),
        ),
        in_specs=[pl.BlockSpec(memory_space=pltpu.SMEM), vmem, hbm]
        + [hbm] * len(arrays)
        + [vmem, vmem],
        out_specs=(vmem, vmem, hbm),
        scratch_shapes=[
            pltpu.VMEM((rows, columns), F32),
            pltpu.VMEM((width, columns), BF),
            pltpu.SemaphoreType.DMA((len(arrays) + 1,)),
            pltpu.SemaphoreType.DMA((width // rows_in,)),
        ],
        compiler_params=pltpu.CompilerParams(vmem_limit_bytes=32 << 20),
        cost_estimate=pl.CostEstimate(
            flops=2 * rows * width * columns, bytes_accessed=4 * width * columns, transcendentals=0
        ),
        name="pieces_forward",
    )(jnp.stack([me, plane]), x, in_hbm(own), *[in_hbm(part) for part in arrays], cosine, sine)


def gather_blocks(weight, before_fsdp, before_ctx):
    rows, columns = weight.shape
    me, plane = ids()
    share = columns // lax.axis_size("ctx")
    mine = lax.dynamic_slice(weight, (0, me * share), (rows, share))
    planes = lax.all_gather(after(mine, before_fsdp), "fsdp")
    others = jnp.stack(
        [
            lax.dynamic_index_in_dim(planes, plane ^ away, 0, keepdims=False)
            for away in range(1, planes.shape[0])
        ]
    )
    return lax.all_gather(after(others, before_ctx), "ctx")


def whole_of(own, blocks):
    ctx_count, others, rows, share = blocks.shape
    plane = lax.axis_index("fsdp")
    columns = ctx_count * share
    full = jnp.zeros(((others + 1) * rows, columns), own.dtype)
    full = lax.dynamic_update_slice(full, own, (plane * rows, 0))
    for away in range(1, others + 1):
        part = blocks[:, away - 1].transpose(1, 0, 2).reshape(rows, columns)
        full = lax.dynamic_update_slice(full, part, ((plane ^ away) * rows, 0))
    return full


def in_hbm(value):
    return pltpu.with_memory_space_constraint(value, pltpu.HBM)


def out_kernel(back, ids_ref, x_ref, own_ref, blocks_ref, *refs):
    hidden_ref, gain_ref = (None, None) if back else refs[:2]
    outs = refs if back else refs[2:]
    own_buf, buf, sems = outs[-3:]
    ctx_count, others, rows, share = buf.shape
    plane = ids_ref[1]

    def block_copy(c):
        return pltpu.make_async_copy(blocks_ref.at[c], buf.at[c], sems.at[c])

    own_copy = pltpu.make_async_copy(own_ref, own_buf, sems.at[ctx_count])
    own_copy.start()
    for c in range(ctx_count):
        block_copy(c).start()

    def features(away):
        return pl.ds(pl.multiple_of((plane ^ away) * rows, 128), rows)

    def columns(c):
        return pl.ds(pl.multiple_of(c * share, 128), share)

    own_copy.wait()
    if back:
        y_ref = outs[0]

        @pl.loop(0, ctx_count)
        def _(c):
            block_copy(c).wait()
            total = nn(x_ref[:, features(0)], own_buf[:, columns(c)])
            for away in range(1, others + 1):
                total += nn(x_ref[:, features(away)], buf[c, away - 1])
            y_ref[:, columns(c)] = total.astype(BF)

        return
    residual_ref, normed_ref = outs[:2]
    residual_ref[...] = hidden_ref[...].astype(F32)

    @pl.loop(0, ctx_count)
    def _(c):
        block_copy(c).wait()
        x = x_ref[:, columns(c)]
        residual_ref[:, features(0)] += nt(x, own_buf[:, columns(c)])
        for away in range(1, others + 1):
            residual_ref[:, features(away)] += nt(x, buf[c, away - 1])

    residual = residual_ref[...]
    normed_ref[...] = (residual * norm_scale(residual) * gain_ref[...]).astype(BF)


def out_call(back, x, own, blocks, extra, out_shape):
    vmem, hbm = pl.BlockSpec(memory_space=pltpu.VMEM), pl.BlockSpec(memory_space=pltpu.HBM)
    return pl.pallas_call(
        lambda *refs: out_kernel(back, *refs),
        out_shape=out_shape,
        in_specs=[pl.BlockSpec(memory_space=pltpu.SMEM), vmem, hbm, hbm] + [vmem] * len(extra),
        out_specs=jax.tree.map(lambda _: vmem, out_shape),
        scratch_shapes=[
            pltpu.VMEM(own.shape, own.dtype),
            pltpu.VMEM(blocks.shape, blocks.dtype),
            pltpu.SemaphoreType.DMA((blocks.shape[0] + 1,)),
        ],
        compiler_params=pltpu.CompilerParams(vmem_limit_bytes=24 << 20),
        cost_estimate=pl.CostEstimate(
            flops=2 * x.shape[0] * own.size * (blocks.shape[1] + 1),
            bytes_accessed=2 * own.size * (blocks.shape[1] + 1),
            transcendentals=0,
        ),
        name="out_back" if back else "out_forward",
    )(jnp.stack(ids()), x, in_hbm(own), in_hbm(blocks), *extra)


def out_forward(attn_rows, own, blocks, hidden, gain):
    if blocks.shape[3] % 128:
        residual = hidden.astype(F32) + nt(attn_rows, whole_of(own, blocks))
        return residual, (residual * norm_scale(residual) * gain).astype(BF)
    out_shape = (
        jax.ShapeDtypeStruct(hidden.shape, F32),
        jax.ShapeDtypeStruct(hidden.shape, BF),
    )
    return out_call(False, attn_rows, own, blocks, [hidden, gain[None]], out_shape)


def out_back(x, own, blocks):
    if blocks.shape[3] % 128:
        return nn(x, whole_of(own, blocks)).astype(BF)
    out_shape = jax.ShapeDtypeStruct((x.shape[0], own.shape[1]), BF)
    return out_call(True, x, own, blocks, [], out_shape)


def one_back_kernel(
    query_ref, pair_ref, w_ref, hidden_ref, gain_ref, residual_ref, y_ref
):
    step = pl.program_id(0)
    rows = w_ref.shape[0]
    split = query_ref.shape[1]
    y_ref[:, pl.ds(pl.multiple_of(step * rows, 128), rows)] = nt(
        query_ref[...], w_ref[:, :split]
    ) + nt(pair_ref[...], w_ref[:, split:])

    @pl.when(step == pl.num_programs(0) - 1)
    def _():
        grad = y_ref[...]
        inputs = hidden_ref[...].astype(F32)
        scale = norm_scale(inputs)
        unit = inputs * scale
        scaled = gain_ref[...] * grad
        y_ref[...] = residual_ref[...] + scale * (
            scaled - unit * jnp.mean(scaled * unit, axis=-1, keepdims=True)
        )


def one_back(query_part, pair_part, weight, hidden, gain, residual_grad):
    rows, width = hidden.shape
    columns = weight.shape[1]
    tile = FFN_TILE

    def whole(array):
        return pl.BlockSpec(array.shape, lambda j: (0, 0))

    gain = gain[None]
    return pl.pallas_call(
        one_back_kernel,
        grid=(width // tile,),
        out_shape=jax.ShapeDtypeStruct((rows, width), F32),
        in_specs=[
            whole(query_part),
            pl.BlockSpec((rows, pair_part.shape[1]), lambda j: (0, 0)),
            pl.BlockSpec((tile, columns), lambda j: (j, 0)),
            whole(hidden),
            whole(gain),
            whole(residual_grad),
        ],
        out_specs=pl.BlockSpec((rows, width), lambda j: (0, 0)),
        compiler_params=pltpu.CompilerParams(vmem_limit_bytes=24 << 20),
        cost_estimate=pl.CostEstimate(
            flops=2 * rows * width * columns,
            bytes_accessed=2 * width * columns,
            transcendentals=0,
        ),
        name="one_back",
    )(query_part, pair_part, in_hbm(weight), hidden, gain, residual_grad)


def send_rows(values):
    if lax.axis_size("fsdp") != 4:
        return fetch_rows(values)
    third = swap(values, "fsdp", 3)
    return [values, swap(values, "fsdp", 1), third]


def relay_rows(planes):
    if lax.axis_size("fsdp") != 4:
        return planes
    values, first, third = planes
    return [values, first, swap(third, "fsdp", 1), third]


def pass_rows(values):
    return relay_rows(send_rows(values))


def fetch_rows(values):
    count = lax.axis_size("fsdp")
    return [values] + [swap(values, "fsdp", away) for away in range(1, count)]


def sum_rows(parts, forward):
    count = len(parts)
    if count == 4 and forward:
        passed = swap(parts[2], "fsdp", 1).astype(F32)
        one = swap(parts[1], "fsdp", 1)
        third = swap((parts[3].astype(F32) + passed).astype(BF), "fsdp", 3)
        return [parts[0], one, third]
    return parts[:1] + [swap(parts[i], "fsdp", i) for i in range(1, count)]


def by_feature(values):
    rows, width = values.shape
    ctx_count, fsdp_count = lax.axis_size("ctx"), lax.axis_size("fsdp")
    blocks = values.reshape(rows, ctx_count, fsdp_count, width // (ctx_count * fsdp_count))
    return blocks.transpose(0, 2, 1, 3).reshape(rows, width)


def sum_over_ctx(part_for):
    pairs = lax.axis_size("ctx") // 2
    sent = jnp.stack([part_for(2 * pair + 1).astype(BF) for pair in range(pairs)])
    got = swap(sent, "ctx", 1)
    sums = [part_for(2 * pair).astype(F32) + got[pair].astype(F32) for pair in range(pairs)]
    total = sums[0]
    for pair in range(1, pairs):
        total = total + swap(sums[pair].astype(BF), "ctx", 2 * pair).astype(F32)
    return total


def ctx_rows_sum(values):
    height = values.shape[0] // lax.axis_size("ctx")
    me = lax.axis_index("ctx")

    def part(offset):
        return lax.dynamic_slice(
            values, ((me ^ offset) * height, 0), (height, values.shape[1])
        )

    return sum_over_ctx(part)


def key_offsets():
    count = lax.axis_size("ctx")
    return list(range(0, count, 2)) + list(range(1, count, 2))


def gather_keys(piece):
    same = [piece] + [swap(piece, "ctx", far) for far in range(2, lax.axis_size("ctx"), 2)]
    mine = jnp.concatenate(same, axis=0)
    return mine, swap(mine, "ctx", 1)


def sum_pairs(kept, sent, cosine, sine):
    _, count, width = kept.shape
    pairs = lax.axis_size("ctx") // 2
    got = swap(sent, "ctx", 1)
    sums = (kept.astype(F32) + got.astype(F32)).reshape(2, pairs, count // pairs, width)
    far = [swap(sums[:, pair].astype(BF), "ctx", 2 * pair) for pair in range(1, pairs)]
    return pair_turn(sums[:, 0], far, cosine, sine), got


def half_mask(shape):
    return lax.broadcasted_iota(jnp.int32, shape, len(shape) - 1) % 128 < HD


def turn(values, cosine, sine):
    lanes = lax.broadcasted_iota(jnp.int32, values.shape, 1) % HD
    turned = jnp.where(
        lanes < HD // 2, pltpu.roll(values, 128 - HD // 2, 1), pltpu.roll(values, HD // 2, 1)
    )
    return values * cosine + turned * sine


def doubled(tile, odd):
    wide = tile.astype(F32)
    other = pltpu.roll(wide, HD, 1)
    return jnp.where(half_mask(tile.shape) == (odd == 0), wide, other).astype(BF)


def split_heads(tile_pair):
    zero = jnp.zeros((), tile_pair.dtype)
    parts = []
    for j in range(2):
        tile = tile_pair[:, j * 128 : (j + 1) * 128]
        mask = half_mask(tile.shape)
        parts += [jnp.where(mask, tile, zero), jnp.where(mask, zero, tile)]
    return jnp.concatenate(parts, axis=0)


def merge_heads(stacked):
    rows = stacked.shape[0] // 4
    tiles = []
    for j in range(2):
        even = stacked[2 * j * rows : (2 * j + 1) * rows]
        odd = stacked[(2 * j + 1) * rows : (2 * j + 2) * rows]
        tiles.append(jnp.where(half_mask(even.shape), even, odd))
    return jnp.concatenate(tiles, axis=1)


def key_chunks(refs, chunk):
    first = 0
    for k_ref, v_ref in refs:
        for start in range(0, k_ref.shape[0], chunk):
            at = slice(start, start + chunk)
            yield first + start, k_ref.at[at, :], v_ref.at[at, :]
        first += k_ref.shape[0]


def masked_scores(keys, queries, key_ref, own_ref, start):
    allowed = key_ref[start : start + keys.shape[0], :1] <= own_ref[...]
    bias = jnp.where(allowed, 0.0, -1e30).astype(F32)
    return nt(keys, queries) + jnp.concatenate([bias] * 4, axis=1)


def attend_kernel(
    chunk, q_ref, ka_ref, va_ref, kb_ref, vb_ref, key_ref, own_ref, rows_ref, attended_ref, log_ref
):
    odd = pl.program_id(0) % 2
    rows = q_ref.shape[0]
    queries = split_heads(q_ref[...])
    parts = list(key_chunks(((ka_ref, va_ref), (kb_ref, vb_ref)), chunk))
    scores = [
        masked_scores(doubled(k_ref[...], odd), queries, key_ref, own_ref, start)
        for start, k_ref, _ in parts
    ]
    top = jnp.max(scores[0], axis=0, keepdims=True)
    for score in scores[1:]:
        top = jnp.maximum(top, jnp.max(score, axis=0, keepdims=True))
    total = jnp.zeros_like(top)
    summed = jnp.zeros((4 * rows, 128), F32)
    for score, (_, _, v_ref) in zip(scores, parts):
        weights = jnp.exp(score - top)
        total += jnp.sum(weights, axis=0, keepdims=True)
        summed += tn(weights.astype(BF), doubled(v_ref[...], odd))
    log_ref[0] = top + jnp.log(total)
    attended = merge_heads(summed / jnp.transpose(jnp.broadcast_to(total, (128, 4 * rows))))
    attended_ref[...] = attended
    rows_ref[...] = attended.astype(BF)


def key_specs(parts):
    tiles = parts[0].shape[1] // 256
    specs, arrays = [], []
    for part in parts:
        specs.append(pl.BlockSpec((part.shape[0], 128), lambda g: (0, g // 2)))
        specs.append(pl.BlockSpec((part.shape[0], 128), lambda g: (0, tiles + g // 2)))
        arrays += [part, part]
    return specs, arrays


def attend(queries, keys_values, key_anchor, own_anchor):
    rows, width = queries.shape
    count = key_anchor.shape[0]
    specs, arrays = key_specs(keys_values)
    wide = pl.BlockSpec((rows, 256), lambda g: (0, g))
    return pl.pallas_call(
        lambda *refs: attend_kernel(KEY_CHUNK, *refs),
        grid=(KV,),
        out_shape=(
            jax.ShapeDtypeStruct((rows, width), BF),
            jax.ShapeDtypeStruct((rows, width), F32),
            jax.ShapeDtypeStruct((KV, 1, 4 * rows), F32),
        ),
        in_specs=[wide]
        + specs
        + [
            pl.BlockSpec((count, 128), lambda g: (0, 0)),
            pl.BlockSpec((1, rows), lambda g: (0, 0)),
        ],
        out_specs=(wide, wide, pl.BlockSpec((1, 1, 4 * rows), lambda g: (g, 0, 0))),
        compiler_params=pltpu.CompilerParams(vmem_limit_bytes=48 << 20),
        cost_estimate=pl.CostEstimate(
            flops=4 * rows * width * count,
            bytes_accessed=4 * count * KV * HD,
            transcendentals=rows * H * count,
        ),
        name="attend",
    )(queries, *arrays, key_anchor, own_anchor)


def attend_back_kernel(
    chunk, q_ref, grad_ref, attended_ref, ka_ref, va_ref, kb_ref, vb_ref, key_ref, own_ref, log_ref,
    cos_ref, sin_ref, dq_ref, kept_ref, sent_ref,
):
    odd = pl.program_id(0) % 2
    rows = q_ref.shape[0]
    half = ka_ref.shape[0]
    queries, grads = split_heads(q_ref[...]), split_heads(grad_ref[...])
    product = grads.astype(F32) * split_heads(attended_ref[...])
    delta = jnp.sum(jnp.transpose(product), axis=0, keepdims=True)
    log_total = log_ref[0]
    total = jnp.zeros((4 * rows, 128), F32)
    keep = half_mask((chunk, 128)) == (odd == 0)
    for start, k_ref, v_ref in key_chunks(((ka_ref, va_ref), (kb_ref, vb_ref)), chunk):
        keys, values = doubled(k_ref[...], odd), doubled(v_ref[...], odd)
        scores = masked_scores(keys, queries, key_ref, own_ref, start)
        probs = jnp.exp(scores - log_total)
        value_grad = nn(probs.astype(BF), grads)
        score_grad = (probs * (nt(values, grads) - delta)).astype(BF)
        key_grad = nn(score_grad, queries)
        total += tn(score_grad, keys)
        out_ref = kept_ref if start < half else sent_ref
        at = slice(start % half, start % half + chunk)
        for part, value in enumerate((key_grad, value_grad)):
            value = (value + pltpu.roll(value, HD, 1)).astype(BF)
            out_ref[part, at, :] = jnp.where(keep, value, out_ref[part, at, :])
    merged = merge_heads(total) * (1.0 / math.sqrt(HD))
    cosine, sine = cos_ref[...], sin_ref[...]
    for j in range(2):
        tile = slice(j * 128, (j + 1) * 128)
        dq_ref[:, tile] = turn(merged[:, tile], cosine, -sine).astype(BF)


def attend_back(queries, grads, attended, keys_values, key_anchor, own_anchor, logs, cosine, sine):
    rows, width = queries.shape
    count = key_anchor.shape[0]
    specs, arrays = key_specs(keys_values)
    wide = pl.BlockSpec((rows, 256), lambda g: (0, g))
    small = pl.BlockSpec((rows, 128), lambda g: (0, 0))
    pair = pl.BlockSpec((2, count // 2, 128), lambda g: (0, 0, g // 2))
    return pl.pallas_call(
        lambda *refs: attend_back_kernel(KEY_CHUNK, *refs),
        grid=(KV,),
        out_shape=(
            jax.ShapeDtypeStruct((rows, width), BF),
            jax.ShapeDtypeStruct((2, count // 2, KV * HD), BF),
            jax.ShapeDtypeStruct((2, count // 2, KV * HD), BF),
        ),
        in_specs=[wide, wide, wide]
        + specs
        + [
            pl.BlockSpec((count, 128), lambda g: (0, 0)),
            pl.BlockSpec((1, rows), lambda g: (0, 0)),
            pl.BlockSpec((1, 1, 4 * rows), lambda g: (g, 0, 0)),
            small,
            small,
        ],
        out_specs=(wide, pair, pair),
        compiler_params=pltpu.CompilerParams(vmem_limit_bytes=48 << 20),
        cost_estimate=pl.CostEstimate(
            flops=10 * rows * width * count,
            bytes_accessed=8 * count * KV * HD,
            transcendentals=rows * H * count,
        ),
        name="attend_back",
    )(queries, grads, attended, *arrays, key_anchor, own_anchor, logs, cosine, sine)


def pair_turn_kernel(copies, own_ref, *refs):
    got, (cos_ref, sin_ref, y_ref) = refs[:-3], refs[-3:]
    total = own_ref[...]
    for ref in got:
        total = total + ref[...].astype(F32)
    cosine, sine = cos_ref[...], sin_ref[...]
    _, rows, width = total.shape
    tiles = [
        turn(total[0, :, start : start + 128], cosine, -sine).astype(BF)
        for start in range(0, width, 128)
    ]
    values = total[1].astype(BF)
    for copy in range(copies):
        at = slice(copy * rows, (copy + 1) * rows)
        for i, tile in enumerate(tiles):
            y_ref[at, i * 128 : (i + 1) * 128] = tile
        y_ref[at, width:] = values


def pair_turn(own, got, cosine, sine):
    _, rows, width = own.shape
    copies = lax.axis_size("fsdp")
    return pl.pallas_call(
        lambda *refs: pair_turn_kernel(copies, *refs),
        out_shape=jax.ShapeDtypeStruct((copies * rows, 2 * width), BF),
        name="pair_turn",
    )(own, *got, cosine, sine)


def join_rows(x_buf, refs):
    @pl.when((pl.program_id(0) == 0))
    def _():
        rows = refs[0].shape[0]
        for i, ref in enumerate(refs):
            x_buf[i * rows : (i + 1) * rows] = ref[...]


def ffn_kernel(count, earlier, *refs):
    rows_refs, (act_ref, w_ref), refs = refs[:count], refs[count : count + 2], refs[count + 2 :]
    out_ref, refs = refs[earlier], refs[earlier + 1 :]
    sum_refs, (x_buf, sum_buf) = refs[:count], refs[count:]
    join_rows(x_buf, rows_refs)
    step = pl.program_id(0)
    gate_w, up_w = w_ref[0], w_ref[1]
    x = x_buf[...]
    gate, up = nn(x, gate_w), nn(x, up_w)
    act_grad = act_ref[...]
    sig = jax.nn.sigmoid(gate)
    silu = gate * sig
    gate_grad = (act_grad * up * sig * (1.0 + gate * (1.0 - sig))).astype(BF)
    up_grad = (act_grad * silu).astype(BF)
    out_ref[0], out_ref[1], out_ref[2] = gate_grad, up_grad, (silu * up).astype(BF)
    part = nt(gate_grad, gate_w) + nt(up_grad, up_w)

    @pl.when(step == 0)
    def _():
        sum_buf[...] = part

    @pl.when(step > 0)
    def _():
        sum_buf[...] += part

    @pl.when(step == pl.num_programs(0) - 1)
    def _():
        rows = sum_refs[0].shape[0]
        for i, ref in enumerate(sum_refs):
            ref[...] = sum_buf[i * rows : (i + 1) * rows].astype(ref.dtype)


def ffn_middle(blocks, act_grad, half, weights, kinds, earlier):
    width = blocks[0].shape[1]
    rows = blocks[0].shape[0] * len(blocks)
    hidden = weights.shape[2]
    tile = FFN_TILE
    whole = [pl.BlockSpec(block.shape, lambda j: (0, 0)) for block in blocks]
    out = pl.pallas_call(
        lambda *refs: ffn_kernel(len(blocks), len(earlier), *refs),
        grid=(hidden // tile,),
        out_shape=(
            pltpu.HBM((3, 2 * rows, hidden), BF),
            *[jax.ShapeDtypeStruct(block.shape, kind) for block, kind in zip(blocks, kinds)],
        ),
        in_specs=whole
        + [
            pl.BlockSpec((rows, tile), lambda j: (half, j)),
            pl.BlockSpec((2, width, tile), lambda j: (0, 0, j)),
        ]
        + [pl.BlockSpec(memory_space=pltpu.HBM)] * len(earlier),
        out_specs=(pl.BlockSpec((3, rows, tile), lambda j: (0, half, j)), *whole),
        input_output_aliases={len(blocks) + 2: 0} if earlier else {},
        scratch_shapes=[pltpu.VMEM((rows, width), BF), pltpu.VMEM((rows, width), F32)],
        compiler_params=pltpu.CompilerParams(vmem_limit_bytes=40 << 20),
        cost_estimate=pl.CostEstimate(
            flops=8 * rows * width * hidden,
            bytes_accessed=4 * width * hidden,
            transcendentals=rows * hidden,
        ),
        name="ffn_middle",
    )(*blocks, act_grad, weights, *earlier)
    return out[0], list(out[1:])


def products_kernel(count, added, ids_ref, *refs):
    blocks, right, rest = refs[: 2 * count], refs[2 * count], refs[2 * count + 1 :]
    out_ref, left = rest[-2:]
    rows, height = blocks[0].shape
    for j in range(2):
        for i in range(count):
            at = (slice(i * rows, (i + 1) * rows), slice(j * height, (j + 1) * height))
            left[at] = blocks[j * count + i][...]
    part = tn(left[...], right[0])
    if added:
        part = part + rest[0][0].astype(F32)
    out_ref[0] = part.astype(BF)


def half_products(rows_of, parts, first, size, got, earlier):
    count = len(rows_of)
    rows, width = rows_of[0].shape
    matrices, _, hidden = parts.shape
    ctx_count = lax.axis_size("ctx")
    height = width // ctx_count
    kept = got is not None

    def left(j):
        def place(k, i, ids_ref):
            own = ids_ref[0] % 2
            return (0, 2 * (2 * i + j) + (own if kept else 1 - own))

        return pl.BlockSpec((rows, height), place)

    def out(start):
        return pl.BlockSpec((1, 2 * height, hidden), lambda k, i, ids_ref: (start + k, i, 0))

    right = pl.BlockSpec((1, rows * count, hidden), lambda k, i, ids_ref: (first + k, 0, 0))
    extra = ([got] if kept else []) + earlier
    operands = 2 * count + 1 + len(extra)
    return pl.pallas_call(
        lambda *refs: products_kernel(count, kept, *refs),
        grid_spec=pltpu.PrefetchScalarGridSpec(
            num_scalar_prefetch=1,
            grid=(size, ctx_count // 4),
            in_specs=[left(0)] * count
            + [left(1)] * count
            + [right]
            + [out(0)] * kept
            + [pl.BlockSpec(memory_space=pltpu.HBM)] * len(earlier),
            out_specs=out(first if kept else 0),
            scratch_shapes=[pltpu.VMEM((count * rows, 2 * height), BF)],
        ),
        out_shape=pltpu.HBM((matrices if kept else size, width // 2, hidden), BF),
        input_output_aliases={operands: 0} if earlier else {},
        compiler_params=pltpu.CompilerParams(vmem_limit_bytes=24 << 20),
        cost_estimate=pl.CostEstimate(
            flops=size * count * rows * width * hidden,
            bytes_accessed=size * width * hidden,
            transcendentals=0,
        ),
    )(jnp.stack(ids()), *rows_of, *rows_of, in_hbm(parts), *extra)


def ffn_gradient(rows_in, rows_out, parts):
    count = lax.axis_size("ctx")
    if count % 4 or (rows_in[0].shape[1] // count) % 128:
        left, grad = (jnp.concatenate(rows, axis=0) for rows in (rows_in, rows_out))
        products = [tn(left, parts[0]), tn(left, parts[1]), tn(grad, parts[2])]
        products = jnp.stack(products, axis=1).astype(BF)
        return lax.psum_scatter(products, "ctx", scatter_dimension=0, tiled=True), parts
    calls = ((rows_out, 2, 1), (rows_in, 0, 2))
    got = []
    for rows_of, first, size in calls:
        sent = half_products(rows_of, parts, first, size, None, [])
        got.append(swap(sent, "ctx", 1))
    kept = []
    for (rows_of, first, size), part in zip(calls, got):
        kept = [half_products(rows_of, parts, first, size, part, kept)]
    groups = [list(range(core, count, 2)) for core in range(2)]
    kept = kept[0].transpose(1, 0, 2)
    rows = lax.psum_scatter(kept, "ctx", scatter_dimension=0, tiled=True, axis_index_groups=groups)
    return rows, after(parts, kept)


def widen_kernel(x_ref, y_ref):
    y_ref[...] = x_ref[...].astype(F32)


def widened(values):
    values = values.transpose(1, 0, 2)
    matrices, rows, hidden = values.shape
    block = pl.BlockSpec((1, rows // 2, hidden), lambda k, i: (k, i, 0))
    return pl.pallas_call(
        widen_kernel,
        grid=(matrices, 2),
        out_shape=jax.ShapeDtypeStruct(values.shape, F32),
        in_specs=[block],
        out_specs=block,
        compiler_params=pltpu.CompilerParams(vmem_limit_bytes=16 << 20),
        name="widened",
    )(values).transpose(1, 0, 2)


def down_back_kernel(count, *refs):
    rows_refs, (w_ref, y_ref, x_buf) = refs[:count], refs[count:]
    join_rows(x_buf, rows_refs)
    y_ref[...] = nn(x_buf[...], w_ref[0])


def down_back(blocks, weights):
    width = blocks[0].shape[1]
    rows = blocks[0].shape[0] * len(blocks)
    hidden = weights.shape[2]
    tile = FFN_TILE
    return pl.pallas_call(
        lambda *refs: down_back_kernel(len(blocks), *refs),
        grid=(hidden // tile,),
        out_shape=pltpu.HBM((rows, hidden), F32),
        in_specs=[pl.BlockSpec(block.shape, lambda j: (0, 0)) for block in blocks]
        + [pl.BlockSpec((1, width, tile), lambda j: (2, 0, j))],
        out_specs=pl.BlockSpec((rows, tile), lambda j: (0, j)),
        scratch_shapes=[pltpu.VMEM((rows, width), BF)],
        compiler_params=pltpu.CompilerParams(vmem_limit_bytes=24 << 20),
        cost_estimate=pl.CostEstimate(
            flops=2 * rows * width * hidden,
            bytes_accessed=2 * width * hidden,
            transcendentals=0,
        ),
        name="down_back",
    )(*blocks, weights)


def down_kernel(x_ref, w_ref, *y_refs):
    rows = x_ref.shape[1] // len(y_refs)
    total = nt(x_ref[0], w_ref[0])
    for i, y_ref in enumerate(y_refs):
        y_ref[...] = total[i * rows : (i + 1) * rows].astype(y_ref.dtype)


def down_forward(parts, weights, count):
    _, rows, hidden = parts.shape
    width = weights.shape[1]
    tile = FFN_TILE
    height = rows // count
    return pl.pallas_call(
        down_kernel,
        grid=(width // tile,),
        out_shape=tuple(
            jax.ShapeDtypeStruct((height, width), BF if i else F32) for i in range(count)
        ),
        in_specs=[
            pl.BlockSpec((1, rows, hidden), lambda j: (2, 0, 0)),
            pl.BlockSpec((1, tile, hidden), lambda j: (2, j, 0)),
        ],
        out_specs=tuple(pl.BlockSpec((height, tile), lambda j: (0, j)) for _ in range(count)),
        compiler_params=pltpu.CompilerParams(vmem_limit_bytes=24 << 20),
        cost_estimate=pl.CostEstimate(
            flops=2 * rows * width * hidden,
            bytes_accessed=2 * width * hidden,
            transcendentals=0,
        ),
        name="down_forward",
    )(in_hbm(parts), weights)


def share_kernel(count, sizes, ids_ref, *refs):
    products = len(sizes)
    lefts = [refs[i * count : (i + 1) * count] for i in range(products)]
    rest = refs[products * count :]
    rights = []
    for size in sizes:
        rights.append(rest[:size])
        rest = rest[size:]
    bufs = rest[len(rest) - products :]
    terms, (kept_ref, sent_ref) = rest[: -products - 2], rest[-products - 2 : -products]
    half = kept_ref.shape[1]
    own = ids_ref[0] % 2 == 0

    @pl.when(pl.program_id(0) == 0)
    def _():
        for parts, buf in zip(rights, bufs):
            rows = buf.shape[0] // count
            for away in range(count):
                if len(parts) > 1:
                    block = parts[away][...]
                else:
                    start = (ids_ref[1] ^ away) * rows
                    block = parts[0][pl.ds(pl.multiple_of(start, 16), rows), :]
                buf[away * rows : (away + 1) * rows] = block

    def emit(part, column):
        at = slice(column, column + part.shape[1])
        kept_ref[0, :, at] = jnp.where(own, part[:half], part[half:])
        sent_ref[0, :, at] = jnp.where(own, part[half:], part[:half])

    column = 0
    for left, buf in zip(lefts, bufs):
        joined = jnp.concatenate([ref[...] for ref in left], axis=0)
        emit(tn(joined, buf[...]).astype(BF), column)
        column += buf.shape[1]
    for term in terms:
        tall = jnp.broadcast_to(term[...], (128, term.shape[1]))
        emit(jnp.transpose(tall).astype(BF), column)
        column += 128


def share_products(lefts, rights, terms):
    ctx_count = lax.axis_size("ctx")
    pairs = ctx_count // 2
    count = len(lefts[0])
    rows, width = lefts[0][0].shape
    height = width // ctx_count
    groups = [right if isinstance(right, list) else [right] for right in rights]
    widths = [group[0].shape[1] for group in groups]
    columns = sum(widths) + 128 * len(terms)

    def place(j, ids_ref):
        return (0, (ids_ref[0] // 2) ^ j)

    def whole(array):
        return pl.BlockSpec(array.shape, lambda j, ids_ref: (0, 0))

    shape = jax.ShapeDtypeStruct((pairs, height, columns), BF)
    out = pl.BlockSpec((1, height, columns), lambda j, ids_ref: (j, 0, 0))
    flat_lefts = [block for left in lefts for block in left]
    flat_rights = [block for group in groups for block in group]
    return pl.pallas_call(
        lambda *refs: share_kernel(count, [len(group) for group in groups], *refs),
        grid_spec=pltpu.PrefetchScalarGridSpec(
            num_scalar_prefetch=1,
            grid=(pairs,),
            in_specs=[pl.BlockSpec((rows, 2 * height), place) for _ in flat_lefts]
            + [whole(block) for block in flat_rights]
            + [pl.BlockSpec((1, 2 * height), place) for _ in terms],
            out_specs=(out, out),
            scratch_shapes=[pltpu.VMEM((count * rows, size), BF) for size in widths],
        ),
        out_shape=(shape, shape),
        compiler_params=pltpu.CompilerParams(vmem_limit_bytes=32 << 20),
        cost_estimate=pl.CostEstimate(
            flops=2 * count * rows * width * columns,
            bytes_accessed=2 * (count * rows + columns) * width,
            transcendentals=0,
        ),
        name="share_terms" if terms else "share_products",
    )(jnp.stack(ids()), *flat_lefts, *flat_rights, *[term[None] for term in terms])


def in_fsdp_order(value):
    if not isinstance(value, list):
        return value
    plane = lax.axis_index("fsdp")
    stacked = jnp.stack(value)
    parts = [
        lax.dynamic_index_in_dim(stacked, plane ^ away, 0, keepdims=False)
        for away in range(len(value))
    ]
    return jnp.concatenate(parts, axis=0)


def share_start(lefts, rights, terms):
    pairs = lax.axis_size("ctx") // 2
    if (lefts[0][0].shape[1] // pairs) % 128:
        values = [tn(in_fsdp_order(a), in_fsdp_order(b)) for a, b in zip(lefts, rights)]
        values += [jnp.broadcast_to(term[:, None], (term.shape[0], 128)) for term in terms]
        return [ctx_rows_sum(jnp.concatenate(values, axis=1))]
    kept, sent = share_products(lefts, rights, terms)
    got = swap(sent, "ctx", 1)
    parts = [kept[0], got[0]]
    for pair in range(1, pairs):
        part = (kept[pair].astype(F32) + got[pair].astype(F32)).astype(BF)
        parts.append(swap(part, "ctx", 2 * pair))
    return parts


def share_finish(parts):
    total = parts[0].astype(F32)
    for part in parts[1:]:
        total = total + part.astype(F32)
    return total


def own_rows_of(values, height):
    index = lax.axis_index("ctx") * lax.axis_size("fsdp") + lax.axis_index("fsdp")
    return lax.dynamic_slice_in_dim(values, index * height, height, 0)


def feature_parts(values):
    count, plane = lax.axis_size("fsdp"), lax.axis_index("fsdp")
    values = by_feature(values)
    rows, width = values.shape
    width //= count
    return [
        lax.dynamic_slice(values, (0, (plane ^ away) * width), (rows, width))
        for away in range(count)
    ]


def feature_rows(parts):
    return [swap(part, "fsdp", away) if away else part for away, part in enumerate(parts)]


def own_features(terms):
    ctx_count, fsdp_count = lax.axis_size("ctx"), lax.axis_size("fsdp")
    total = jnp.stack(terms)
    away = 1
    while away < fsdp_count:
        total = total + swap(total, "fsdp", away)
        away *= 2
    blocks = total.reshape(len(terms), ctx_count, fsdp_count, -1)
    own = lax.dynamic_index_in_dim(blocks, lax.axis_index("fsdp"), 2, keepdims=False)
    own = own.reshape(len(terms), -1)
    return [own[i] for i in range(len(terms))]


def layer(
    hidden_in,
    out_grad,
    positions,
    block_order,
    attn_gain,
    ffn_gain,
    qkv_weight,
    out_weight,
    ffn_weight,
):
    ctx_count, fsdp_count = lax.axis_size("ctx"), lax.axis_size("fsdp")
    me, _ = ids()
    rows = hidden_in.shape[1]
    queries_width, kv_width = H * HD, KV * HD
    ffn_parts = in_hbm(ffn_weight.transpose(1, 0, 2))

    frequency = jnp.power(ROPE_BASE, -(jnp.arange(HD // 2, dtype=F32) * 2.0 / HD))
    angles = positions[0].astype(F32)[:, None] * frequency[None, :]
    cosine = jnp.tile(jnp.cos(angles), (1, 4))
    sine = jnp.tile(jnp.concatenate([-jnp.sin(angles), jnp.sin(angles)], axis=1), (1, 2))
    own_anchor = anchors_of(block_order, me, rows)[None]
    key_anchor = jnp.concatenate(
        [anchors_of(block_order, me ^ offset, rows) for offset in key_offsets()]
    )
    key_anchor = jnp.broadcast_to(key_anchor[:, None], (rows * ctx_count, 128))

    inputs = hidden_in[0].astype(F32)
    grad_in = out_grad[0]
    scale_one = norm_scale(inputs)
    normed_one = (inputs * scale_one * attn_gain).astype(BF)

    one_parts = feature_parts(normed_one)
    fast = ctx_count == 8 and (qkv_weight.shape[1] // ctx_count) % 128 == 0
    if fast:
        early = (cosine, sine, own_anchor, key_anchor, one_parts)
        qkv_pieces, marks = gather_pieces(qkv_weight, early)
        out_blocks = gather_blocks(out_weight, *marks)
        queries, pair, qkv_full = pieces_forward(
            normed_one, qkv_weight, qkv_pieces, cosine, sine
        )
    else:
        marks = (normed_one, normed_one)
        out_blocks = gather_blocks(out_weight, *marks)
        qkv_full = whole_of(qkv_weight, gather_blocks(qkv_weight, normed_one, normed_one))
        projected = nn(normed_one, qkv_full)
        turned = rotate(
            projected[:, : queries_width + kv_width].reshape(rows, H + KV, HD), positions[0]
        ).reshape(rows, queries_width + kv_width)
        queries = (turned[:, :queries_width] * (1.0 / math.sqrt(HD))).astype(BF)
        pair = jnp.concatenate(
            [turned[:, queries_width:], projected[:, queries_width + kv_width :]], axis=1
        ).astype(BF)
    own_one = feature_rows(after(one_parts, pair))
    keys_values = gather_keys(pair)
    rows_out = send_rows(after(grad_in, pair))
    attn_rows, attended, logs = attend(queries, keys_values, key_anchor, own_anchor)
    rows_out = relay_rows(after(rows_out, attn_rows))
    residual, normed_two = out_forward(
        attn_rows, out_weight, out_blocks, hidden_in[0], ffn_gain
    )
    scale_two = norm_scale(residual)
    rows_in = pass_rows(normed_two)
    rows_out = after(rows_out, normed_two)
    act_grad = down_back(rows_out, ffn_parts)

    all_attn = pass_rows(after(attn_rows, rows_in[2]))
    parts, partial = [], []
    half = fsdp_count // 2
    passing = 3 if fsdp_count == 4 else 0
    for index in range(2):
        blocks = rows_in[index * half : (index + 1) * half]
        kinds = [F32 if index * half + i in (0, passing) else BF for i in range(half)]
        out, terms = ffn_middle(blocks, in_hbm(act_grad), index, ffn_parts, kinds, parts)
        parts, partial = [out], partial + terms
    parts = parts[0]
    sum_grad = share_finish(sum_rows(partial, True))
    ffn_weight_grad, parts = ffn_gradient(rows_in, rows_out, parts)
    ffn_weight_grad = widened(ffn_weight_grad)
    out_partial = list(down_forward(parts, ffn_parts, fsdp_count))

    unit_two = residual * scale_two
    ffn_gain_term = jnp.sum(sum_grad * unit_two, axis=0)
    scaled_two = ffn_gain * sum_grad
    residual_grad = grad_in.astype(F32) + scale_two * (
        scaled_two - unit_two * jnp.mean(scaled_two * unit_two, axis=-1, keepdims=True)
    )
    residual_bf = residual_grad.astype(BF)
    out_sum = sum_rows([after(part, residual_bf) for part in out_partial], True)
    (ffn_term,) = own_features([ffn_gain_term])
    attn_grad = out_back(residual_bf, out_weight, out_blocks)
    query_part, kept, sent = attend_back(
        queries, attn_grad, attended, keys_values, key_anchor, own_anchor, logs, cosine, sine
    )
    query_planes = pass_rows(query_part)
    pair_copies, near = sum_pairs(kept, sent, cosine, sine)
    own_residual = feature_rows(feature_parts(after(residual_bf, near)))
    all_pair = lax.all_to_all(pair_copies, "fsdp", split_axis=0, concat_axis=0, tiled=True)
    input_grad = one_back(
        query_part, pair_copies, qkv_full, hidden_in[0], attn_gain, residual_grad
    )
    out_sums = share_start([own_residual], [after(all_attn, input_grad)], [])
    output = (residual + share_finish(after(out_sum, input_grad))).astype(BF)
    qkv_sums = share_start([own_one, own_one], [after(query_planes, output), all_pair], [ffn_term])
    qkv_sums = share_finish(qkv_sums)
    out_weight_grad = share_finish(out_sums)
    qkv_grad = qkv_sums[:, : qkv_weight.shape[1]]
    features = own_rows_of(attn_gain, qkv_grad.shape[0])
    gain_grad = jnp.sum(own_rows_of(qkv_full, qkv_grad.shape[0]).astype(F32) * qkv_grad, axis=1)
    return (
        output[None],
        input_grad[None],
        qkv_grad,
        out_weight_grad,
        ffn_weight_grad,
        gain_grad / features,
        qkv_sums[:, qkv_weight.shape[1]],
    )


def solution(mesh):
    step = sharded(mesh)
    return step


def sharded(mesh):
    return jax.shard_map(
        layer,
        mesh=mesh,
        in_specs=(
            P("fsdp", "ctx", None),
            P("fsdp", "ctx", None),
            P("fsdp", "ctx"),
            P(),
            P(),
            P(),
            P("fsdp", None),
            P("fsdp", None),
            P(None, None, "fsdp"),
        ),
        out_specs=(
            P("fsdp", "ctx", None),
            P("fsdp", "ctx", None),
            P(("ctx", "fsdp"), None),
            P(("ctx", "fsdp"), None),
            P("ctx", None, "fsdp"),
            P(("ctx", "fsdp")),
            P(("ctx", "fsdp")),
        ),
        check_vma=False,
    )
```

```python
import math

import jax
import jax.numpy as jnp
from jax import lax
from jax.experimental import pallas as pl
from jax.experimental.pallas import tpu as pltpu
from jax.sharding import PartitionSpec as P


H = 32
KV = 8
HD = 64

NORM_EPS = 1e-05
ROPE_BASE = 500000.0
FFN_TILE = 512
KEY_CHUNK = 256


BF = jnp.bfloat16
F32 = jnp.float32


def mm(a, b, dims):
    return lax.dot_general(a, b, (dims, ((), ())), preferred_element_type=F32)


def nn(a, b):
    return mm(a, b, ((1,), (0,)))


def nt(a, b):
    return mm(a, b, ((1,), (1,)))


def tn(a, b):
    return mm(a, b, ((0,), (0,)))


def swap(value, axis, offset):
    count = lax.axis_size(axis)
    return lax.ppermute(value, axis, [(i, i ^ offset) for i in range(count)])


def rotate(values, token_places):
    head_dim = values.shape[-1]
    half_dim = head_dim // 2
    frequency = jnp.power(ROPE_BASE, -(jnp.arange(half_dim, dtype=F32) * 2.0 / head_dim))
    angles = token_places.astype(F32)[:, None] * frequency[None, :]
    cosine = jnp.concatenate([jnp.cos(angles), jnp.cos(angles)], axis=-1)[:, None, :]
    sine_part = jnp.concatenate([jnp.sin(angles), jnp.sin(angles)], axis=-1)[:, None, :]
    turned = jnp.concatenate([-values[..., half_dim:], values[..., :half_dim]], axis=-1)
    return values * cosine + turned * sine_part


def norm_scale(values):
    return lax.rsqrt(jnp.mean(values * values, axis=-1, keepdims=True) + NORM_EPS)


def lookup(entries, row_ids):
    matches = row_ids[:, None] == jnp.arange(entries.shape[0], dtype=jnp.int32)[None, :]
    return jnp.sum(jnp.where(matches, entries[None, :], 0), axis=1)


def anchors_of(block_order, owner, row_count):
    block_len = row_count // 2
    row_ids = owner * row_count + jnp.arange(row_count, dtype=jnp.int32)
    return lookup(block_order, row_ids // block_len) * block_len + row_ids % block_len


def after(value, *earlier):
    return lax.optimization_barrier((value, earlier))[0]


def ids():
    return lax.axis_index("ctx"), lax.axis_index("fsdp")


def gather_pieces(weight, early):
    rows, columns = weight.shape
    share = columns // lax.axis_size("ctx")
    half = rows // 2
    mine = lax.dynamic_slice(weight, (0, lax.axis_index("ctx") * share), (rows, share))
    planes = {}
    planes[3] = swap(mine, "fsdp", 3)
    planes[1] = swap(mine, "fsdp", 1)
    planes[2] = swap(after(planes[3], early), "fsdp", 1)
    pieces = []
    for away in (1, 3, 2):
        first = planes[away]
        along_x, along_y = swap(first, "ctx", 2), swap(first, "ctx", 4)
        if away == 1:
            corners = [(6, 0, swap(along_y, "ctx", 2))]
        elif away == 3:
            corners = [(6, 0, swap(along_x, "ctx", 4))]
        else:
            top, low = swap(along_y[:half], "ctx", 2), swap(along_x[half:], "ctx", 4)
            corners = [(6, 0, jnp.concatenate([top, low], axis=0))]
        parts = [(0, 0, first), (2, 0, along_x), (4, 0, along_y)] + corners
        for offset, start, part in parts:
            pieces.append((away, offset, start, part))
            pieces.append((away, offset + 1, start, swap(part, "ctx", 1)))
    return pieces, (planes[2], pieces[-2][3])


def pieces_kernel(places, rows_in, share, ids_ref, x_ref, own_ref, *refs):
    count = len(places)
    piece_refs, refs = refs[:count], refs[count:]
    cos_ref, sin_ref, q_ref, pair_ref, full_ref, y_ref, buf, in_sems, out_sems = refs
    me, plane = ids_ref[0], ids_ref[1]

    def block(away):
        return pl.ds(pl.multiple_of((plane ^ away) * rows_in, 128), rows_in)

    own_copy = pltpu.make_async_copy(own_ref, buf.at[block(0)], in_sems.at[count])
    own_copy.start()
    copies = []
    for i, (away, offset, start, height) in enumerate(places):
        at = pl.ds(pl.multiple_of((plane ^ away) * rows_in + start, 128), height)
        columns = pl.ds(pl.multiple_of((me ^ offset) * share, 128), share)
        copies.append(pltpu.make_async_copy(piece_refs[i], buf.at[at, columns], in_sems.at[i]))
        copies[-1].start()
    outs = []
    order = [0] + list(dict.fromkeys(away for away, _, _, _ in places))
    for away in order:
        if away:
            for copy, place in zip(copies, places):
                if place[0] == away:
                    copy.wait()
        else:
            own_copy.wait()
        outs.append(
            pltpu.make_async_copy(buf.at[block(away)], full_ref.at[block(away)], out_sems.at[away])
        )
        outs[-1].start()
        part = nn(x_ref[:, block(away)], buf[block(away)])
        y_ref[...] = part if away == 0 else y_ref[...] + part
    cosine, sine = cos_ref[...], sin_ref[...]
    queries, keys = H * HD, KV * HD
    for start in range(0, queries + keys, 128):
        tile = turn(y_ref[:, start : start + 128], cosine, sine)
        if start < queries:
            q_ref[:, start : start + 128] = (tile * (1.0 / math.sqrt(HD))).astype(BF)
        else:
            pair_ref[:, start - queries : start - queries + 128] = tile.astype(BF)
    pair_ref[:, keys:] = y_ref[:, queries + keys :].astype(BF)
    for copy in outs:
        copy.wait()


def pieces_forward(x, own, pieces, cosine, sine):
    me, plane = ids()
    rows_in, columns = own.shape
    rows, width = x.shape
    share = columns // lax.axis_size("ctx")
    places = tuple((away, offset, start, part.shape[0]) for away, offset, start, part in pieces)
    arrays = [part for _, _, _, part in pieces]
    hbm, vmem = pl.BlockSpec(memory_space=pltpu.HBM), pl.BlockSpec(memory_space=pltpu.VMEM)
    return pl.pallas_call(
        lambda *refs: pieces_kernel(places, rows_in, share, *refs),
        out_shape=(
            jax.ShapeDtypeStruct((rows, H * HD), BF),
            jax.ShapeDtypeStruct((rows, 2 * KV * HD), BF),
            pltpu.HBM((width, columns), BF),
        ),
        in_specs=[pl.BlockSpec(memory_space=pltpu.SMEM), vmem, hbm]
        + [hbm] * len(arrays)
        + [vmem, vmem],
        out_specs=(vmem, vmem, hbm),
        scratch_shapes=[
            pltpu.VMEM((rows, columns), F32),
            pltpu.VMEM((width, columns), BF),
            pltpu.SemaphoreType.DMA((len(arrays) + 1,)),
            pltpu.SemaphoreType.DMA((width // rows_in,)),
        ],
        compiler_params=pltpu.CompilerParams(vmem_limit_bytes=32 << 20),
        cost_estimate=pl.CostEstimate(
            flops=2 * rows * width * columns, bytes_accessed=4 * width * columns, transcendentals=0
        ),
        name="pieces_forward",
    )(jnp.stack([me, plane]), x, in_hbm(own), *[in_hbm(part) for part in arrays], cosine, sine)


def gather_blocks(weight, before_fsdp, before_ctx):
    rows, columns = weight.shape
    me, plane = ids()
    share = columns // lax.axis_size("ctx")
    mine = lax.dynamic_slice(weight, (0, me * share), (rows, share))
    planes = lax.all_gather(after(mine, before_fsdp), "fsdp")
    others = jnp.stack(
        [
            lax.dynamic_index_in_dim(planes, plane ^ away, 0, keepdims=False)
            for away in range(1, planes.shape[0])
        ]
    )
    return lax.all_gather(after(others, before_ctx), "ctx")


def whole_of(own, blocks):
    ctx_count, others, rows, share = blocks.shape
    plane = lax.axis_index("fsdp")
    columns = ctx_count * share
    full = jnp.zeros(((others + 1) * rows, columns), own.dtype)
    full = lax.dynamic_update_slice(full, own, (plane * rows, 0))
    for away in range(1, others + 1):
        part = blocks[:, away - 1].transpose(1, 0, 2).reshape(rows, columns)
        full = lax.dynamic_update_slice(full, part, ((plane ^ away) * rows, 0))
    return full


def in_hbm(value):
    return pltpu.with_memory_space_constraint(value, pltpu.HBM)


def out_kernel(back, ids_ref, x_ref, own_ref, blocks_ref, *refs):
    hidden_ref, gain_ref = (None, None) if back else refs[:2]
    outs = refs if back else refs[2:]
    own_buf, buf, sems = outs[-3:]
    ctx_count, others, rows, share = buf.shape
    plane = ids_ref[1]

    def block_copy(c):
        return pltpu.make_async_copy(blocks_ref.at[c], buf.at[c], sems.at[c])

    own_copy = pltpu.make_async_copy(own_ref, own_buf, sems.at[ctx_count])
    own_copy.start()
    for c in range(ctx_count):
        block_copy(c).start()

    def features(away):
        return pl.ds(pl.multiple_of((plane ^ away) * rows, 128), rows)

    def columns(c):
        return pl.ds(pl.multiple_of(c * share, 128), share)

    own_copy.wait()
    if back:
        y_ref = outs[0]

        @pl.loop(0, ctx_count)
        def _(c):
            block_copy(c).wait()
            total = nn(x_ref[:, features(0)], own_buf[:, columns(c)])
            for away in range(1, others + 1):
                total += nn(x_ref[:, features(away)], buf[c, away - 1])
            y_ref[:, columns(c)] = total.astype(BF)

        return
    residual_ref, normed_ref = outs[:2]
    residual_ref[...] = hidden_ref[...].astype(F32)

    @pl.loop(0, ctx_count)
    def _(c):
        block_copy(c).wait()
        x = x_ref[:, columns(c)]
        residual_ref[:, features(0)] += nt(x, own_buf[:, columns(c)])
        for away in range(1, others + 1):
            residual_ref[:, features(away)] += nt(x, buf[c, away - 1])

    residual = residual_ref[...]
    normed_ref[...] = (residual * norm_scale(residual) * gain_ref[...]).astype(BF)


def out_call(back, x, own, blocks, extra, out_shape):
    vmem, hbm = pl.BlockSpec(memory_space=pltpu.VMEM), pl.BlockSpec(memory_space=pltpu.HBM)
    return pl.pallas_call(
        lambda *refs: out_kernel(back, *refs),
        out_shape=out_shape,
        in_specs=[pl.BlockSpec(memory_space=pltpu.SMEM), vmem, hbm, hbm] + [vmem] * len(extra),
        out_specs=jax.tree.map(lambda _: vmem, out_shape),
        scratch_shapes=[
            pltpu.VMEM(own.shape, own.dtype),
            pltpu.VMEM(blocks.shape, blocks.dtype),
            pltpu.SemaphoreType.DMA((blocks.shape[0] + 1,)),
        ],
        compiler_params=pltpu.CompilerParams(vmem_limit_bytes=24 << 20),
        cost_estimate=pl.CostEstimate(
            flops=2 * x.shape[0] * own.size * (blocks.shape[1] + 1),
            bytes_accessed=2 * own.size * (blocks.shape[1] + 1),
            transcendentals=0,
        ),
        name="out_back" if back else "out_forward",
    )(jnp.stack(ids()), x, in_hbm(own), in_hbm(blocks), *extra)


def out_forward(attn_rows, own, blocks, hidden, gain):
    if blocks.shape[3] % 128:
        residual = hidden.astype(F32) + nt(attn_rows, whole_of(own, blocks))
        return residual, (residual * norm_scale(residual) * gain).astype(BF)
    out_shape = (
        jax.ShapeDtypeStruct(hidden.shape, F32),
        jax.ShapeDtypeStruct(hidden.shape, BF),
    )
    return out_call(False, attn_rows, own, blocks, [hidden, gain[None]], out_shape)


def out_back(x, own, blocks):
    if blocks.shape[3] % 128:
        return nn(x, whole_of(own, blocks)).astype(BF)
    out_shape = jax.ShapeDtypeStruct((x.shape[0], own.shape[1]), BF)
    return out_call(True, x, own, blocks, [], out_shape)


def one_back_kernel(
    query_ref, pair_ref, w_ref, hidden_ref, gain_ref, residual_ref, y_ref
):
    step = pl.program_id(0)
    rows = w_ref.shape[0]
    split = query_ref.shape[1]
    y_ref[:, pl.ds(pl.multiple_of(step * rows, 128), rows)] = nt(
        query_ref[...], w_ref[:, :split]
    ) + nt(pair_ref[...], w_ref[:, split:])

    @pl.when(step == pl.num_programs(0) - 1)
    def _():
        grad = y_ref[...]
        inputs = hidden_ref[...].astype(F32)
        scale = norm_scale(inputs)
        unit = inputs * scale
        scaled = gain_ref[...] * grad
        y_ref[...] = residual_ref[...] + scale * (
            scaled - unit * jnp.mean(scaled * unit, axis=-1, keepdims=True)
        )


def one_back(query_part, pair_part, weight, hidden, gain, residual_grad):
    rows, width = hidden.shape
    columns = weight.shape[1]
    tile = FFN_TILE

    def whole(array):
        return pl.BlockSpec(array.shape, lambda j: (0, 0))

    gain = gain[None]
    return pl.pallas_call(
        one_back_kernel,
        grid=(width // tile,),
        out_shape=jax.ShapeDtypeStruct((rows, width), F32),
        in_specs=[
            whole(query_part),
            pl.BlockSpec((rows, pair_part.shape[1]), lambda j: (0, 0)),
            pl.BlockSpec((tile, columns), lambda j: (j, 0)),
            whole(hidden),
            whole(gain),
            whole(residual_grad),
        ],
        out_specs=pl.BlockSpec((rows, width), lambda j: (0, 0)),
        compiler_params=pltpu.CompilerParams(vmem_limit_bytes=24 << 20),
        cost_estimate=pl.CostEstimate(
            flops=2 * rows * width * columns,
            bytes_accessed=2 * width * columns,
            transcendentals=0,
        ),
        name="one_back",
    )(query_part, pair_part, in_hbm(weight), hidden, gain, residual_grad)


def send_rows(values):
    if lax.axis_size("fsdp") != 4:
        return fetch_rows(values)
    third = swap(values, "fsdp", 3)
    return [values, swap(values, "fsdp", 1), third]


def relay_rows(planes):
    if lax.axis_size("fsdp") != 4:
        return planes
    values, first, third = planes
    return [values, first, swap(third, "fsdp", 1), third]


def pass_rows(values):
    return relay_rows(send_rows(values))


def fetch_rows(values):
    count = lax.axis_size("fsdp")
    return [values] + [swap(values, "fsdp", away) for away in range(1, count)]


def sum_rows(parts, forward):
    count = len(parts)
    if count == 4 and forward:
        passed = swap(parts[2], "fsdp", 1).astype(F32)
        one = swap(parts[1], "fsdp", 1)
        third = swap((parts[3].astype(F32) + passed).astype(BF), "fsdp", 3)
        return [parts[0], one, third]
    return parts[:1] + [swap(parts[i], "fsdp", i) for i in range(1, count)]


def by_feature(values):
    rows, width = values.shape
    ctx_count, fsdp_count = lax.axis_size("ctx"), lax.axis_size("fsdp")
    blocks = values.reshape(rows, ctx_count, fsdp_count, width // (ctx_count * fsdp_count))
    return blocks.transpose(0, 2, 1, 3).reshape(rows, width)


def sum_over_ctx(part_for):
    pairs = lax.axis_size("ctx") // 2
    sent = jnp.stack([part_for(2 * pair + 1).astype(BF) for pair in range(pairs)])
    got = swap(sent, "ctx", 1)
    sums = [part_for(2 * pair).astype(F32) + got[pair].astype(F32) for pair in range(pairs)]
    total = sums[0]
    for pair in range(1, pairs):
        total = total + swap(sums[pair].astype(BF), "ctx", 2 * pair).astype(F32)
    return total


def ctx_rows_sum(values):
    height = values.shape[0] // lax.axis_size("ctx")
    me = lax.axis_index("ctx")

    def part(offset):
        return lax.dynamic_slice(
            values, ((me ^ offset) * height, 0), (height, values.shape[1])
        )

    return sum_over_ctx(part)


def key_offsets():
    count = lax.axis_size("ctx")
    return list(range(0, count, 2)) + list(range(1, count, 2))


def gather_keys(piece):
    same = [piece] + [swap(piece, "ctx", far) for far in range(2, lax.axis_size("ctx"), 2)]
    mine = jnp.concatenate(same, axis=0)
    return mine, swap(mine, "ctx", 1)


def sum_pairs(kept, sent, cosine, sine):
    _, count, width = kept.shape
    pairs = lax.axis_size("ctx") // 2
    got = swap(sent, "ctx", 1)
    sums = (kept.astype(F32) + got.astype(F32)).reshape(2, pairs, count // pairs, width)
    far = [swap(sums[:, pair].astype(BF), "ctx", 2 * pair) for pair in range(1, pairs)]
    return pair_turn(sums[:, 0], far, cosine, sine), got


def half_mask(shape):
    return lax.broadcasted_iota(jnp.int32, shape, len(shape) - 1) % 128 < HD


def turn(values, cosine, sine):
    lanes = lax.broadcasted_iota(jnp.int32, values.shape, 1) % HD
    turned = jnp.where(
        lanes < HD // 2, pltpu.roll(values, 128 - HD // 2, 1), pltpu.roll(values, HD // 2, 1)
    )
    return values * cosine + turned * sine


def doubled(tile, odd):
    wide = tile.astype(F32)
    other = pltpu.roll(wide, HD, 1)
    return jnp.where(half_mask(tile.shape) == (odd == 0), wide, other).astype(BF)


def split_heads(tile_pair):
    zero = jnp.zeros((), tile_pair.dtype)
    parts = []
    for j in range(2):
        tile = tile_pair[:, j * 128 : (j + 1) * 128]
        mask = half_mask(tile.shape)
        parts += [jnp.where(mask, tile, zero), jnp.where(mask, zero, tile)]
    return jnp.concatenate(parts, axis=0)


def merge_heads(stacked):
    rows = stacked.shape[0] // 4
    tiles = []
    for j in range(2):
        even = stacked[2 * j * rows : (2 * j + 1) * rows]
        odd = stacked[(2 * j + 1) * rows : (2 * j + 2) * rows]
        tiles.append(jnp.where(half_mask(even.shape), even, odd))
    return jnp.concatenate(tiles, axis=1)


def key_chunks(refs, chunk):
    first = 0
    for k_ref, v_ref in refs:
        for start in range(0, k_ref.shape[0], chunk):
            at = slice(start, start + chunk)
            yield first + start, k_ref.at[at, :], v_ref.at[at, :]
        first += k_ref.shape[0]


def masked_scores(keys, queries, key_ref, own_ref, start):
    allowed = key_ref[start : start + keys.shape[0], :1] <= own_ref[...]
    bias = jnp.where(allowed, 0.0, -1e30).astype(F32)
    return nt(keys, queries) + jnp.concatenate([bias] * 4, axis=1)


def attend_kernel(
    chunk, q_ref, ka_ref, va_ref, kb_ref, vb_ref, key_ref, own_ref, rows_ref, attended_ref, log_ref
):
    odd = pl.program_id(0) % 2
    rows = q_ref.shape[0]
    queries = split_heads(q_ref[...])
    parts = list(key_chunks(((ka_ref, va_ref), (kb_ref, vb_ref)), chunk))
    scores = [
        masked_scores(doubled(k_ref[...], odd), queries, key_ref, own_ref, start)
        for start, k_ref, _ in parts
    ]
    top = jnp.max(scores[0], axis=0, keepdims=True)
    for score in scores[1:]:
        top = jnp.maximum(top, jnp.max(score, axis=0, keepdims=True))
    total = jnp.zeros_like(top)
    summed = jnp.zeros((4 * rows, 128), F32)
    for score, (_, _, v_ref) in zip(scores, parts):
        weights = jnp.exp(score - top)
        total += jnp.sum(weights, axis=0, keepdims=True)
        summed += tn(weights.astype(BF), doubled(v_ref[...], odd))
    log_ref[0] = top + jnp.log(total)
    attended = merge_heads(summed / jnp.transpose(jnp.broadcast_to(total, (128, 4 * rows))))
    attended_ref[...] = attended
    rows_ref[...] = attended.astype(BF)


def key_specs(parts):
    tiles = parts[0].shape[1] // 256
    specs, arrays = [], []
    for part in parts:
        specs.append(pl.BlockSpec((part.shape[0], 128), lambda g: (0, g // 2)))
        specs.append(pl.BlockSpec((part.shape[0], 128), lambda g: (0, tiles + g // 2)))
        arrays += [part, part]
    return specs, arrays


def attend(queries, keys_values, key_anchor, own_anchor):
    rows, width = queries.shape
    count = key_anchor.shape[0]
    specs, arrays = key_specs(keys_values)
    wide = pl.BlockSpec((rows, 256), lambda g: (0, g))
    return pl.pallas_call(
        lambda *refs: attend_kernel(KEY_CHUNK, *refs),
        grid=(KV,),
        out_shape=(
            jax.ShapeDtypeStruct((rows, width), BF),
            jax.ShapeDtypeStruct((rows, width), F32),
            jax.ShapeDtypeStruct((KV, 1, 4 * rows), F32),
        ),
        in_specs=[wide]
        + specs
        + [
            pl.BlockSpec((count, 128), lambda g: (0, 0)),
            pl.BlockSpec((1, rows), lambda g: (0, 0)),
        ],
        out_specs=(wide, wide, pl.BlockSpec((1, 1, 4 * rows), lambda g: (g, 0, 0))),
        compiler_params=pltpu.CompilerParams(vmem_limit_bytes=48 << 20),
        cost_estimate=pl.CostEstimate(
            flops=4 * rows * width * count,
            bytes_accessed=4 * count * KV * HD,
            transcendentals=rows * H * count,
        ),
        name="attend",
    )(queries, *arrays, key_anchor, own_anchor)


def attend_back_kernel(
    chunk, q_ref, grad_ref, attended_ref, ka_ref, va_ref, kb_ref, vb_ref, key_ref, own_ref, log_ref,
    cos_ref, sin_ref, dq_ref, kept_ref, sent_ref,
):
    odd = pl.program_id(0) % 2
    rows = q_ref.shape[0]
    half = ka_ref.shape[0]
    queries, grads = split_heads(q_ref[...]), split_heads(grad_ref[...])
    product = grads.astype(F32) * split_heads(attended_ref[...])
    delta = jnp.sum(jnp.transpose(product), axis=0, keepdims=True)
    log_total = log_ref[0]
    total = jnp.zeros((4 * rows, 128), F32)
    keep = half_mask((chunk, 128)) == (odd == 0)
    for start, k_ref, v_ref in key_chunks(((ka_ref, va_ref), (kb_ref, vb_ref)), chunk):
        keys, values = doubled(k_ref[...], odd), doubled(v_ref[...], odd)
        scores = masked_scores(keys, queries, key_ref, own_ref, start)
        probs = jnp.exp(scores - log_total)
        value_grad = nn(probs.astype(BF), grads)
        score_grad = (probs * (nt(values, grads) - delta)).astype(BF)
        key_grad = nn(score_grad, queries)
        total += tn(score_grad, keys)
        out_ref = kept_ref if start < half else sent_ref
        at = slice(start % half, start % half + chunk)
        for part, value in enumerate((key_grad, value_grad)):
            value = (value + pltpu.roll(value, HD, 1)).astype(BF)
            out_ref[part, at, :] = jnp.where(keep, value, out_ref[part, at, :])
    merged = merge_heads(total) * (1.0 / math.sqrt(HD))
    cosine, sine = cos_ref[...], sin_ref[...]
    for j in range(2):
        tile = slice(j * 128, (j + 1) * 128)
        dq_ref[:, tile] = turn(merged[:, tile], cosine, -sine).astype(BF)


def attend_back(queries, grads, attended, keys_values, key_anchor, own_anchor, logs, cosine, sine):
    rows, width = queries.shape
    count = key_anchor.shape[0]
    specs, arrays = key_specs(keys_values)
    wide = pl.BlockSpec((rows, 256), lambda g: (0, g))
    small = pl.BlockSpec((rows, 128), lambda g: (0, 0))
    pair = pl.BlockSpec((2, count // 2, 128), lambda g: (0, 0, g // 2))
    return pl.pallas_call(
        lambda *refs: attend_back_kernel(KEY_CHUNK, *refs),
        grid=(KV,),
        out_shape=(
            jax.ShapeDtypeStruct((rows, width), BF),
            jax.ShapeDtypeStruct((2, count // 2, KV * HD), BF),
            jax.ShapeDtypeStruct((2, count // 2, KV * HD), BF),
        ),
        in_specs=[wide, wide, wide]
        + specs
        + [
            pl.BlockSpec((count, 128), lambda g: (0, 0)),
            pl.BlockSpec((1, rows), lambda g: (0, 0)),
            pl.BlockSpec((1, 1, 4 * rows), lambda g: (g, 0, 0)),
            small,
            small,
        ],
        out_specs=(wide, pair, pair),
        compiler_params=pltpu.CompilerParams(vmem_limit_bytes=48 << 20),
        cost_estimate=pl.CostEstimate(
            flops=10 * rows * width * count,
            bytes_accessed=8 * count * KV * HD,
            transcendentals=rows * H * count,
        ),
        name="attend_back",
    )(queries, grads, attended, *arrays, key_anchor, own_anchor, logs, cosine, sine)


def pair_turn_kernel(copies, own_ref, *refs):
    got, (cos_ref, sin_ref, y_ref) = refs[:-3], refs[-3:]
    total = own_ref[...]
    for ref in got:
        total = total + ref[...].astype(F32)
    cosine, sine = cos_ref[...], sin_ref[...]
    _, rows, width = total.shape
    tiles = [
        turn(total[0, :, start : start + 128], cosine, -sine).astype(BF)
        for start in range(0, width, 128)
    ]
    values = total[1].astype(BF)
    for copy in range(copies):
        at = slice(copy * rows, (copy + 1) * rows)
        for i, tile in enumerate(tiles):
            y_ref[at, i * 128 : (i + 1) * 128] = tile
        y_ref[at, width:] = values


def pair_turn(own, got, cosine, sine):
    _, rows, width = own.shape
    copies = lax.axis_size("fsdp")
    return pl.pallas_call(
        lambda *refs: pair_turn_kernel(copies, *refs),
        out_shape=jax.ShapeDtypeStruct((copies * rows, 2 * width), BF),
        name="pair_turn",
    )(own, *got, cosine, sine)


def join_rows(x_buf, refs):
    @pl.when((pl.program_id(0) == 0))
    def _():
        rows = refs[0].shape[0]
        for i, ref in enumerate(refs):
            x_buf[i * rows : (i + 1) * rows] = ref[...]


def ffn_kernel(count, earlier, *refs):
    rows_refs, (act_ref, w_ref), refs = refs[:count], refs[count : count + 2], refs[count + 2 :]
    out_ref, refs = refs[earlier], refs[earlier + 1 :]
    sum_refs, (x_buf, sum_buf) = refs[:count], refs[count:]
    join_rows(x_buf, rows_refs)
    step = pl.program_id(0)
    gate_w, up_w = w_ref[0], w_ref[1]
    x = x_buf[...]
    gate, up = nn(x, gate_w), nn(x, up_w)
    act_grad = act_ref[...]
    sig = jax.nn.sigmoid(gate)
    silu = gate * sig
    gate_grad = (act_grad * up * sig * (1.0 + gate * (1.0 - sig))).astype(BF)
    up_grad = (act_grad * silu).astype(BF)
    out_ref[0], out_ref[1], out_ref[2] = gate_grad, up_grad, (silu * up).astype(BF)
    part = nt(gate_grad, gate_w) + nt(up_grad, up_w)

    @pl.when(step == 0)
    def _():
        sum_buf[...] = part

    @pl.when(step > 0)
    def _():
        sum_buf[...] += part

    @pl.when(step == pl.num_programs(0) - 1)
    def _():
        rows = sum_refs[0].shape[0]
        for i, ref in enumerate(sum_refs):
            ref[...] = sum_buf[i * rows : (i + 1) * rows].astype(ref.dtype)


def ffn_middle(blocks, act_grad, half, weights, kinds, earlier):
    width = blocks[0].shape[1]
    rows = blocks[0].shape[0] * len(blocks)
    hidden = weights.shape[2]
    tile = FFN_TILE
    whole = [pl.BlockSpec(block.shape, lambda j: (0, 0)) for block in blocks]
    out = pl.pallas_call(
        lambda *refs: ffn_kernel(len(blocks), len(earlier), *refs),
        grid=(hidden // tile,),
        out_shape=(
            pltpu.HBM((3, 2 * rows, hidden), BF),
            *[jax.ShapeDtypeStruct(block.shape, kind) for block, kind in zip(blocks, kinds)],
        ),
        in_specs=whole
        + [
            pl.BlockSpec((rows, tile), lambda j: (half, j)),
            pl.BlockSpec((2, width, tile), lambda j: (0, 0, j)),
        ]
        + [pl.BlockSpec(memory_space=pltpu.HBM)] * len(earlier),
        out_specs=(pl.BlockSpec((3, rows, tile), lambda j: (0, half, j)), *whole),
        input_output_aliases={len(blocks) + 2: 0} if earlier else {},
        scratch_shapes=[pltpu.VMEM((rows, width), BF), pltpu.VMEM((rows, width), F32)],
        compiler_params=pltpu.CompilerParams(vmem_limit_bytes=40 << 20),
        cost_estimate=pl.CostEstimate(
            flops=8 * rows * width * hidden,
            bytes_accessed=4 * width * hidden,
            transcendentals=rows * hidden,
        ),
        name="ffn_middle",
    )(*blocks, act_grad, weights, *earlier)
    return out[0], list(out[1:])


def products_kernel(count, added, ids_ref, *refs):
    blocks, right, rest = refs[: 2 * count], refs[2 * count], refs[2 * count + 1 :]
    out_ref, left = rest[-2:]
    rows, height = blocks[0].shape
    for j in range(2):
        for i in range(count):
            at = (slice(i * rows, (i + 1) * rows), slice(j * height, (j + 1) * height))
            left[at] = blocks[j * count + i][...]
    part = tn(left[...], right[0])
    if added:
        part = part + rest[0][0].astype(F32)
    out_ref[0] = part.astype(BF)


def half_products(rows_of, parts, first, size, got, earlier):
    count = len(rows_of)
    rows, width = rows_of[0].shape
    matrices, _, hidden = parts.shape
    ctx_count = lax.axis_size("ctx")
    height = width // ctx_count
    kept = got is not None

    def left(j):
        def place(k, i, ids_ref):
            own = ids_ref[0] % 2
            return (0, 2 * (2 * i + j) + (own if kept else 1 - own))

        return pl.BlockSpec((rows, height), place)

    def out(start):
        return pl.BlockSpec((1, 2 * height, hidden), lambda k, i, ids_ref: (start + k, i, 0))

    right = pl.BlockSpec((1, rows * count, hidden), lambda k, i, ids_ref: (first + k, 0, 0))
    extra = ([got] if kept else []) + earlier
    operands = 2 * count + 1 + len(extra)
    return pl.pallas_call(
        lambda *refs: products_kernel(count, kept, *refs),
        grid_spec=pltpu.PrefetchScalarGridSpec(
            num_scalar_prefetch=1,
            grid=(size, ctx_count // 4),
            in_specs=[left(0)] * count
            + [left(1)] * count
            + [right]
            + [out(0)] * kept
            + [pl.BlockSpec(memory_space=pltpu.HBM)] * len(earlier),
            out_specs=out(first if kept else 0),
            scratch_shapes=[pltpu.VMEM((count * rows, 2 * height), BF)],
        ),
        out_shape=pltpu.HBM((matrices if kept else size, width // 2, hidden), BF),
        input_output_aliases={operands: 0} if earlier else {},
        compiler_params=pltpu.CompilerParams(vmem_limit_bytes=24 << 20),
        cost_estimate=pl.CostEstimate(
            flops=size * count * rows * width * hidden,
            bytes_accessed=size * width * hidden,
            transcendentals=0,
        ),
    )(jnp.stack(ids()), *rows_of, *rows_of, in_hbm(parts), *extra)


def ffn_gradient(rows_in, rows_out, parts):
    count = lax.axis_size("ctx")
    if count % 4 or (rows_in[0].shape[1] // count) % 128:
        left, grad = (jnp.concatenate(rows, axis=0) for rows in (rows_in, rows_out))
        products = [tn(left, parts[0]), tn(left, parts[1]), tn(grad, parts[2])]
        products = jnp.stack(products, axis=1).astype(BF)
        return lax.psum_scatter(products, "ctx", scatter_dimension=0, tiled=True), parts
    calls = ((rows_out, 2, 1), (rows_in, 0, 2))
    got = []
    for rows_of, first, size in calls:
        sent = half_products(rows_of, parts, first, size, None, [])
        got.append(swap(sent, "ctx", 1))
    kept = []
    for (rows_of, first, size), part in zip(calls, got):
        kept = [half_products(rows_of, parts, first, size, part, kept)]
    groups = [list(range(core, count, 2)) for core in range(2)]
    kept = kept[0].transpose(1, 0, 2)
    rows = lax.psum_scatter(kept, "ctx", scatter_dimension=0, tiled=True, axis_index_groups=groups)
    return rows, after(parts, kept)


def widen_kernel(x_ref, y_ref):
    y_ref[...] = x_ref[...].astype(F32)


def widened(values):
    values = values.transpose(1, 0, 2)
    matrices, rows, hidden = values.shape
    block = pl.BlockSpec((1, rows // 2, hidden), lambda k, i: (k, i, 0))
    return pl.pallas_call(
        widen_kernel,
        grid=(matrices, 2),
        out_shape=jax.ShapeDtypeStruct(values.shape, F32),
        in_specs=[block],
        out_specs=block,
        compiler_params=pltpu.CompilerParams(vmem_limit_bytes=16 << 20),
        name="widened",
    )(values).transpose(1, 0, 2)


def down_back_kernel(count, *refs):
    rows_refs, (w_ref, y_ref, x_buf) = refs[:count], refs[count:]
    join_rows(x_buf, rows_refs)
    y_ref[...] = nn(x_buf[...], w_ref[0])


def down_back(blocks, weights):
    width = blocks[0].shape[1]
    rows = blocks[0].shape[0] * len(blocks)
    hidden = weights.shape[2]
    tile = FFN_TILE
    return pl.pallas_call(
        lambda *refs: down_back_kernel(len(blocks), *refs),
        grid=(hidden // tile,),
        out_shape=pltpu.HBM((rows, hidden), F32),
        in_specs=[pl.BlockSpec(block.shape, lambda j: (0, 0)) for block in blocks]
        + [pl.BlockSpec((1, width, tile), lambda j: (2, 0, j))],
        out_specs=pl.BlockSpec((rows, tile), lambda j: (0, j)),
        scratch_shapes=[pltpu.VMEM((rows, width), BF)],
        compiler_params=pltpu.CompilerParams(vmem_limit_bytes=24 << 20),
        cost_estimate=pl.CostEstimate(
            flops=2 * rows * width * hidden,
            bytes_accessed=2 * width * hidden,
            transcendentals=0,
        ),
        name="down_back",
    )(*blocks, weights)


def down_kernel(x_ref, w_ref, *y_refs):
    rows = x_ref.shape[1] // len(y_refs)
    total = nt(x_ref[0], w_ref[0])
    for i, y_ref in enumerate(y_refs):
        y_ref[...] = total[i * rows : (i + 1) * rows].astype(y_ref.dtype)


def down_forward(parts, weights, count):
    _, rows, hidden = parts.shape
    width = weights.shape[1]
    tile = FFN_TILE
    height = rows // count
    return pl.pallas_call(
        down_kernel,
        grid=(width // tile,),
        out_shape=tuple(
            jax.ShapeDtypeStruct((height, width), BF if i else F32) for i in range(count)
        ),
        in_specs=[
            pl.BlockSpec((1, rows, hidden), lambda j: (2, 0, 0)),
            pl.BlockSpec((1, tile, hidden), lambda j: (2, j, 0)),
        ],
        out_specs=tuple(pl.BlockSpec((height, tile), lambda j: (0, j)) for _ in range(count)),
        compiler_params=pltpu.CompilerParams(vmem_limit_bytes=24 << 20),
        cost_estimate=pl.CostEstimate(
            flops=2 * rows * width * hidden,
            bytes_accessed=2 * width * hidden,
            transcendentals=0,
        ),
        name="down_forward",
    )(in_hbm(parts), weights)


def share_kernel(count, sizes, ids_ref, *refs):
    products = len(sizes)
    lefts = [refs[i * count : (i + 1) * count] for i in range(products)]
    rest = refs[products * count :]
    rights = []
    for size in sizes:
        rights.append(rest[:size])
        rest = rest[size:]
    bufs = rest[len(rest) - products :]
    terms, (kept_ref, sent_ref) = rest[: -products - 2], rest[-products - 2 : -products]
    half = kept_ref.shape[1]
    own = ids_ref[0] % 2 == 0

    @pl.when(pl.program_id(0) == 0)
    def _():
        for parts, buf in zip(rights, bufs):
            rows = buf.shape[0] // count
            for away in range(count):
                if len(parts) > 1:
                    block = parts[away][...]
                else:
                    start = (ids_ref[1] ^ away) * rows
                    block = parts[0][pl.ds(pl.multiple_of(start, 16), rows), :]
                buf[away * rows : (away + 1) * rows] = block

    def emit(part, column):
        at = slice(column, column + part.shape[1])
        kept_ref[0, :, at] = jnp.where(own, part[:half], part[half:])
        sent_ref[0, :, at] = jnp.where(own, part[half:], part[:half])

    column = 0
    for left, buf in zip(lefts, bufs):
        joined = jnp.concatenate([ref[...] for ref in left], axis=0)
        emit(tn(joined, buf[...]).astype(BF), column)
        column += buf.shape[1]
    for term in terms:
        tall = jnp.broadcast_to(term[...], (128, term.shape[1]))
        emit(jnp.transpose(tall).astype(BF), column)
        column += 128


def share_products(lefts, rights, terms):
    ctx_count = lax.axis_size("ctx")
    pairs = ctx_count // 2
    count = len(lefts[0])
    rows, width = lefts[0][0].shape
    height = width // ctx_count
    groups = [right if isinstance(right, list) else [right] for right in rights]
    widths = [group[0].shape[1] for group in groups]
    columns = sum(widths) + 128 * len(terms)

    def place(j, ids_ref):
        return (0, (ids_ref[0] // 2) ^ j)

    def whole(array):
        return pl.BlockSpec(array.shape, lambda j, ids_ref: (0, 0))

    shape = jax.ShapeDtypeStruct((pairs, height, columns), BF)
    out = pl.BlockSpec((1, height, columns), lambda j, ids_ref: (j, 0, 0))
    flat_lefts = [block for left in lefts for block in left]
    flat_rights = [block for group in groups for block in group]
    return pl.pallas_call(
        lambda *refs: share_kernel(count, [len(group) for group in groups], *refs),
        grid_spec=pltpu.PrefetchScalarGridSpec(
            num_scalar_prefetch=1,
            grid=(pairs,),
            in_specs=[pl.BlockSpec((rows, 2 * height), place) for _ in flat_lefts]
            + [whole(block) for block in flat_rights]
            + [pl.BlockSpec((1, 2 * height), place) for _ in terms],
            out_specs=(out, out),
            scratch_shapes=[pltpu.VMEM((count * rows, size), BF) for size in widths],
        ),
        out_shape=(shape, shape),
        compiler_params=pltpu.CompilerParams(vmem_limit_bytes=32 << 20),
        cost_estimate=pl.CostEstimate(
            flops=2 * count * rows * width * columns,
            bytes_accessed=2 * (count * rows + columns) * width,
            transcendentals=0,
        ),
        name="share_terms" if terms else "share_products",
    )(jnp.stack(ids()), *flat_lefts, *flat_rights, *[term[None] for term in terms])


def in_fsdp_order(value):
    if not isinstance(value, list):
        return value
    plane = lax.axis_index("fsdp")
    stacked = jnp.stack(value)
    parts = [
        lax.dynamic_index_in_dim(stacked, plane ^ away, 0, keepdims=False)
        for away in range(len(value))
    ]
    return jnp.concatenate(parts, axis=0)


def share_start(lefts, rights, terms):
    pairs = lax.axis_size("ctx") // 2
    if (lefts[0][0].shape[1] // pairs) % 128:
        values = [tn(in_fsdp_order(a), in_fsdp_order(b)) for a, b in zip(lefts, rights)]
        values += [jnp.broadcast_to(term[:, None], (term.shape[0], 128)) for term in terms]
        return [ctx_rows_sum(jnp.concatenate(values, axis=1))]
    kept, sent = share_products(lefts, rights, terms)
    got = swap(sent, "ctx", 1)
    parts = [kept[0], got[0]]
    for pair in range(1, pairs):
        part = (kept[pair].astype(F32) + got[pair].astype(F32)).astype(BF)
        parts.append(swap(part, "ctx", 2 * pair))
    return parts


def share_finish(parts):
    total = parts[0].astype(F32)
    for part in parts[1:]:
        total = total + part.astype(F32)
    return total


def own_rows_of(values, height):
    index = lax.axis_index("ctx") * lax.axis_size("fsdp") + lax.axis_index("fsdp")
    return lax.dynamic_slice_in_dim(values, index * height, height, 0)


def feature_parts(values):
    count, plane = lax.axis_size("fsdp"), lax.axis_index("fsdp")
    values = by_feature(values)
    rows, width = values.shape
    width //= count
    return [
        lax.dynamic_slice(values, (0, (plane ^ away) * width), (rows, width))
        for away in range(count)
    ]


def feature_rows(parts):
    return [swap(part, "fsdp", away) if away else part for away, part in enumerate(parts)]


def own_features(terms):
    ctx_count, fsdp_count = lax.axis_size("ctx"), lax.axis_size("fsdp")
    total = jnp.stack(terms)
    away = 1
    while away < fsdp_count:
        total = total + swap(total, "fsdp", away)
        away *= 2
    blocks = total.reshape(len(terms), ctx_count, fsdp_count, -1)
    own = lax.dynamic_index_in_dim(blocks, lax.axis_index("fsdp"), 2, keepdims=False)
    own = own.reshape(len(terms), -1)
    return [own[i] for i in range(len(terms))]


def layer(
    hidden_in,
    out_grad,
    positions,
    block_order,
    attn_gain,
    ffn_gain,
    qkv_weight,
    out_weight,
    ffn_weight,
):
    ctx_count, fsdp_count = lax.axis_size("ctx"), lax.axis_size("fsdp")
    me, _ = ids()
    rows = hidden_in.shape[1]
    queries_width, kv_width = H * HD, KV * HD
    ffn_parts = in_hbm(ffn_weight.transpose(1, 0, 2))

    frequency = jnp.power(ROPE_BASE, -(jnp.arange(HD // 2, dtype=F32) * 2.0 / HD))
    angles = positions[0].astype(F32)[:, None] * frequency[None, :]
    cosine = jnp.tile(jnp.cos(angles), (1, 4))
    sine = jnp.tile(jnp.concatenate([-jnp.sin(angles), jnp.sin(angles)], axis=1), (1, 2))
    own_anchor = anchors_of(block_order, me, rows)[None]
    key_anchor = jnp.concatenate(
        [anchors_of(block_order, me ^ offset, rows) for offset in key_offsets()]
    )
    key_anchor = jnp.broadcast_to(key_anchor[:, None], (rows * ctx_count, 128))

    inputs = hidden_in[0].astype(F32)
    grad_in = out_grad[0]
    scale_one = norm_scale(inputs)
    normed_one = (inputs * scale_one * attn_gain).astype(BF)

    one_parts = feature_parts(normed_one)
    fast = ctx_count == 8 and (qkv_weight.shape[1] // ctx_count) % 128 == 0
    if fast:
        early = (cosine, sine, own_anchor, key_anchor, one_parts)
        qkv_pieces, marks = gather_pieces(qkv_weight, early)
        out_blocks = gather_blocks(out_weight, *marks)
        queries, pair, qkv_full = pieces_forward(
            normed_one, qkv_weight, qkv_pieces, cosine, sine
        )
    else:
        marks = (normed_one, normed_one)
        out_blocks = gather_blocks(out_weight, *marks)
        qkv_full = whole_of(qkv_weight, gather_blocks(qkv_weight, normed_one, normed_one))
        projected = nn(normed_one, qkv_full)
        turned = rotate(
            projected[:, : queries_width + kv_width].reshape(rows, H + KV, HD), positions[0]
        ).reshape(rows, queries_width + kv_width)
        queries = (turned[:, :queries_width] * (1.0 / math.sqrt(HD))).astype(BF)
        pair = jnp.concatenate(
            [turned[:, queries_width:], projected[:, queries_width + kv_width :]], axis=1
        ).astype(BF)
    own_one = feature_rows(after(one_parts, pair))
    keys_values = gather_keys(pair)
    rows_out = send_rows(after(grad_in, pair))
    attn_rows, attended, logs = attend(queries, keys_values, key_anchor, own_anchor)
    rows_out = relay_rows(after(rows_out, attn_rows))
    residual, normed_two = out_forward(
        attn_rows, out_weight, out_blocks, hidden_in[0], ffn_gain
    )
    scale_two = norm_scale(residual)
    rows_in = pass_rows(normed_two)
    rows_out = after(rows_out, normed_two)
    act_grad = down_back(rows_out, ffn_parts)

    all_attn = pass_rows(after(attn_rows, rows_in[2]))
    parts, partial = [], []
    half = fsdp_count // 2
    passing = 3 if fsdp_count == 4 else 0
    for index in range(2):
        blocks = rows_in[index * half : (index + 1) * half]
        kinds = [F32 if index * half + i in (0, passing) else BF for i in range(half)]
        out, terms = ffn_middle(blocks, in_hbm(act_grad), index, ffn_parts, kinds, parts)
        parts, partial = [out], partial + terms
    parts = parts[0]
    sum_grad = share_finish(sum_rows(partial, True))
    ffn_weight_grad, parts = ffn_gradient(rows_in, rows_out, parts)
    ffn_weight_grad = widened(ffn_weight_grad)
    out_partial = list(down_forward(parts, ffn_parts, fsdp_count))

    unit_two = residual * scale_two
    ffn_gain_term = jnp.sum(sum_grad * unit_two, axis=0)
    scaled_two = ffn_gain * sum_grad
    residual_grad = grad_in.astype(F32) + scale_two * (
        scaled_two - unit_two * jnp.mean(scaled_two * unit_two, axis=-1, keepdims=True)
    )
    residual_bf = residual_grad.astype(BF)
    (ffn_term,) = own_features([ffn_gain_term])
    attn_grad = out_back(residual_bf, out_weight, out_blocks)
    query_part, kept, sent = attend_back(
        queries, attn_grad, attended, keys_values, key_anchor, own_anchor, logs, cosine, sine
    )
    query_planes = pass_rows(query_part)
    pair_copies, near = sum_pairs(kept, sent, cosine, sine)
    own_residual = feature_rows(feature_parts(after(residual_bf, near)))
    all_pair = lax.all_to_all(pair_copies, "fsdp", split_axis=0, concat_axis=0, tiled=True)
    input_grad = one_back(
        query_part, pair_copies, qkv_full, hidden_in[0], attn_gain, residual_grad
    )
    out_sums = share_start([own_residual], [after(all_attn, input_grad)], [])
    out_sum = sum_rows([after(part, input_grad) for part in out_partial], False)
    qkv_sums = share_start(
        [own_one, own_one], [after(query_planes, input_grad), all_pair], [ffn_term]
    )
    qkv_sums = share_finish(qkv_sums)
    output = (residual + share_finish(after(out_sum, qkv_sums))).astype(BF)
    out_weight_grad = share_finish(out_sums)
    qkv_grad = qkv_sums[:, : qkv_weight.shape[1]]
    features = own_rows_of(attn_gain, qkv_grad.shape[0])
    gain_grad = jnp.sum(own_rows_of(qkv_full, qkv_grad.shape[0]).astype(F32) * qkv_grad, axis=1)
    return (
        output[None],
        input_grad[None],
        qkv_grad,
        out_weight_grad,
        ffn_weight_grad,
        gain_grad / features,
        qkv_sums[:, qkv_weight.shape[1]],
    )


def solution(mesh):
    step = sharded(mesh)
    return step


def sharded(mesh):
    return jax.shard_map(
        layer,
        mesh=mesh,
        in_specs=(
            P("fsdp", "ctx", None),
            P("fsdp", "ctx", None),
            P("fsdp", "ctx"),
            P(),
            P(),
            P(),
            P("fsdp", None),
            P("fsdp", None),
            P(None, None, "fsdp"),
        ),
        out_specs=(
            P("fsdp", "ctx", None),
            P("fsdp", "ctx", None),
            P(("ctx", "fsdp"), None),
            P(("ctx", "fsdp"), None),
            P("ctx", None, "fsdp"),
            P(("ctx", "fsdp")),
            P(("ctx", "fsdp")),
        ),
        check_vma=False,
    )
```

```python
import math

import jax
import jax.numpy as jnp
from jax import lax
from jax.experimental import pallas as pl
from jax.experimental.pallas import tpu as pltpu
from jax.sharding import PartitionSpec as P


H = 32
KV = 8
HD = 64

NORM_EPS = 1e-05
ROPE_BASE = 500000.0
FFN_TILE = 512
KEY_CHUNK = 256


BF = jnp.bfloat16
F32 = jnp.float32


def mm(a, b, dims):
    return lax.dot_general(a, b, (dims, ((), ())), preferred_element_type=F32)


def nn(a, b):
    return mm(a, b, ((1,), (0,)))


def nt(a, b):
    return mm(a, b, ((1,), (1,)))


def tn(a, b):
    return mm(a, b, ((0,), (0,)))


def swap(value, axis, offset):
    count = lax.axis_size(axis)
    return lax.ppermute(value, axis, [(i, i ^ offset) for i in range(count)])


def rotate(values, token_places):
    head_dim = values.shape[-1]
    half_dim = head_dim // 2
    frequency = jnp.power(ROPE_BASE, -(jnp.arange(half_dim, dtype=F32) * 2.0 / head_dim))
    angles = token_places.astype(F32)[:, None] * frequency[None, :]
    cosine = jnp.concatenate([jnp.cos(angles), jnp.cos(angles)], axis=-1)[:, None, :]
    sine_part = jnp.concatenate([jnp.sin(angles), jnp.sin(angles)], axis=-1)[:, None, :]
    turned = jnp.concatenate([-values[..., half_dim:], values[..., :half_dim]], axis=-1)
    return values * cosine + turned * sine_part


def norm_scale(values):
    return lax.rsqrt(jnp.mean(values * values, axis=-1, keepdims=True) + NORM_EPS)


def lookup(entries, row_ids):
    matches = row_ids[:, None] == jnp.arange(entries.shape[0], dtype=jnp.int32)[None, :]
    return jnp.sum(jnp.where(matches, entries[None, :], 0), axis=1)


def anchors_of(block_order, owner, row_count):
    block_len = row_count // 2
    row_ids = owner * row_count + jnp.arange(row_count, dtype=jnp.int32)
    return lookup(block_order, row_ids // block_len) * block_len + row_ids % block_len


def after(value, *earlier):
    return lax.optimization_barrier((value, earlier))[0]


def ids():
    return lax.axis_index("ctx"), lax.axis_index("fsdp")


def gather_pieces(weight, early):
    rows, columns = weight.shape
    share = columns // lax.axis_size("ctx")
    half = rows // 2
    mine = lax.dynamic_slice(weight, (0, lax.axis_index("ctx") * share), (rows, share))
    planes = {}
    planes[3] = swap(mine, "fsdp", 3)
    planes[1] = swap(mine, "fsdp", 1)
    planes[2] = swap(after(planes[3], early), "fsdp", 1)
    pieces = []
    for away in (1, 3, 2):
        first = planes[away]
        along_x, along_y = swap(first, "ctx", 2), swap(first, "ctx", 4)
        if away == 1:
            corners = [(6, 0, swap(along_y, "ctx", 2))]
        elif away == 3:
            corners = [(6, 0, swap(along_x, "ctx", 4))]
        else:
            top, low = swap(along_y[:half], "ctx", 2), swap(along_x[half:], "ctx", 4)
            corners = [(6, 0, jnp.concatenate([top, low], axis=0))]
        parts = [(0, 0, first), (2, 0, along_x), (4, 0, along_y)] + corners
        for offset, start, part in parts:
            pieces.append((away, offset, start, part))
            pieces.append((away, offset + 1, start, swap(part, "ctx", 1)))
    return pieces, (planes[2], pieces[-2][3])


def pieces_kernel(places, rows_in, share, ids_ref, x_ref, own_ref, *refs):
    count = len(places)
    piece_refs, refs = refs[:count], refs[count:]
    cos_ref, sin_ref, q_ref, pair_ref, full_ref, y_ref, buf, in_sems, out_sems = refs
    me, plane = ids_ref[0], ids_ref[1]

    def block(away):
        return pl.ds(pl.multiple_of((plane ^ away) * rows_in, 128), rows_in)

    own_copy = pltpu.make_async_copy(own_ref, buf.at[block(0)], in_sems.at[count])
    own_copy.start()
    copies = []
    for i, (away, offset, start, height) in enumerate(places):
        at = pl.ds(pl.multiple_of((plane ^ away) * rows_in + start, 128), height)
        columns = pl.ds(pl.multiple_of((me ^ offset) * share, 128), share)
        copies.append(pltpu.make_async_copy(piece_refs[i], buf.at[at, columns], in_sems.at[i]))
        copies[-1].start()
    outs = []
    order = [0] + list(dict.fromkeys(away for away, _, _, _ in places))
    for away in order:
        if away:
            for copy, place in zip(copies, places):
                if place[0] == away:
                    copy.wait()
        else:
            own_copy.wait()
        outs.append(
            pltpu.make_async_copy(buf.at[block(away)], full_ref.at[block(away)], out_sems.at[away])
        )
        outs[-1].start()
        part = nn(x_ref[:, block(away)], buf[block(away)])
        y_ref[...] = part if away == 0 else y_ref[...] + part
    cosine, sine = cos_ref[...], sin_ref[...]
    queries, keys = H * HD, KV * HD
    for start in range(0, queries + keys, 128):
        tile = turn(y_ref[:, start : start + 128], cosine, sine)
        if start < queries:
            q_ref[:, start : start + 128] = (tile * (1.0 / math.sqrt(HD))).astype(BF)
        else:
            pair_ref[:, start - queries : start - queries + 128] = tile.astype(BF)
    pair_ref[:, keys:] = y_ref[:, queries + keys :].astype(BF)
    for copy in outs:
        copy.wait()


def pieces_forward(x, own, pieces, cosine, sine):
    me, plane = ids()
    rows_in, columns = own.shape
    rows, width = x.shape
    share = columns // lax.axis_size("ctx")
    places = tuple((away, offset, start, part.shape[0]) for away, offset, start, part in pieces)
    arrays = [part for _, _, _, part in pieces]
    hbm, vmem = pl.BlockSpec(memory_space=pltpu.HBM), pl.BlockSpec(memory_space=pltpu.VMEM)
    return pl.pallas_call(
        lambda *refs: pieces_kernel(places, rows_in, share, *refs),
        out_shape=(
            jax.ShapeDtypeStruct((rows, H * HD), BF),
            jax.ShapeDtypeStruct((rows, 2 * KV * HD), BF),
            pltpu.HBM((width, columns), BF),
        ),
        in_specs=[pl.BlockSpec(memory_space=pltpu.SMEM), vmem, hbm]
        + [hbm] * len(arrays)
        + [vmem, vmem],
        out_specs=(vmem, vmem, hbm),
        scratch_shapes=[
            pltpu.VMEM((rows, columns), F32),
            pltpu.VMEM((width, columns), BF),
            pltpu.SemaphoreType.DMA((len(arrays) + 1,)),
            pltpu.SemaphoreType.DMA((width // rows_in,)),
        ],
        compiler_params=pltpu.CompilerParams(vmem_limit_bytes=32 << 20),
        cost_estimate=pl.CostEstimate(
            flops=2 * rows * width * columns, bytes_accessed=4 * width * columns, transcendentals=0
        ),
        name="pieces_forward",
    )(jnp.stack([me, plane]), x, in_hbm(own), *[in_hbm(part) for part in arrays], cosine, sine)


def gather_blocks(weight, before_fsdp, before_ctx):
    rows, columns = weight.shape
    me, plane = ids()
    share = columns // lax.axis_size("ctx")
    mine = lax.dynamic_slice(weight, (0, me * share), (rows, share))
    planes = lax.all_gather(after(mine, before_fsdp), "fsdp")
    others = jnp.stack(
        [
            lax.dynamic_index_in_dim(planes, plane ^ away, 0, keepdims=False)
            for away in range(1, planes.shape[0])
        ]
    )
    return lax.all_gather(after(others, before_ctx), "ctx")


def whole_of(own, blocks):
    ctx_count, others, rows, share = blocks.shape
    plane = lax.axis_index("fsdp")
    columns = ctx_count * share
    full = jnp.zeros(((others + 1) * rows, columns), own.dtype)
    full = lax.dynamic_update_slice(full, own, (plane * rows, 0))
    for away in range(1, others + 1):
        part = blocks[:, away - 1].transpose(1, 0, 2).reshape(rows, columns)
        full = lax.dynamic_update_slice(full, part, ((plane ^ away) * rows, 0))
    return full


def in_hbm(value):
    return pltpu.with_memory_space_constraint(value, pltpu.HBM)


def out_kernel(back, ids_ref, x_ref, own_ref, blocks_ref, *refs):
    hidden_ref, gain_ref = (None, None) if back else refs[:2]
    outs = refs if back else refs[2:]
    own_buf, buf, sems = outs[-3:]
    ctx_count, others, rows, share = buf.shape
    plane = ids_ref[1]

    def block_copy(c):
        return pltpu.make_async_copy(blocks_ref.at[c], buf.at[c], sems.at[c])

    own_copy = pltpu.make_async_copy(own_ref, own_buf, sems.at[ctx_count])
    own_copy.start()
    for c in range(ctx_count):
        block_copy(c).start()

    def features(away):
        return pl.ds(pl.multiple_of((plane ^ away) * rows, 128), rows)

    def columns(c):
        return pl.ds(pl.multiple_of(c * share, 128), share)

    own_copy.wait()
    if back:
        y_ref = outs[0]

        @pl.loop(0, ctx_count)
        def _(c):
            block_copy(c).wait()
            total = nn(x_ref[:, features(0)], own_buf[:, columns(c)])
            for away in range(1, others + 1):
                total += nn(x_ref[:, features(away)], buf[c, away - 1])
            y_ref[:, columns(c)] = total.astype(BF)

        return
    residual_ref, normed_ref = outs[:2]
    residual_ref[...] = hidden_ref[...].astype(F32)

    @pl.loop(0, ctx_count)
    def _(c):
        block_copy(c).wait()
        x = x_ref[:, columns(c)]
        residual_ref[:, features(0)] += nt(x, own_buf[:, columns(c)])
        for away in range(1, others + 1):
            residual_ref[:, features(away)] += nt(x, buf[c, away - 1])

    residual = residual_ref[...]
    normed_ref[...] = (residual * norm_scale(residual) * gain_ref[...]).astype(BF)


def out_call(back, x, own, blocks, extra, out_shape):
    vmem, hbm = pl.BlockSpec(memory_space=pltpu.VMEM), pl.BlockSpec(memory_space=pltpu.HBM)
    return pl.pallas_call(
        lambda *refs: out_kernel(back, *refs),
        out_shape=out_shape,
        in_specs=[pl.BlockSpec(memory_space=pltpu.SMEM), vmem, hbm, hbm] + [vmem] * len(extra),
        out_specs=jax.tree.map(lambda _: vmem, out_shape),
        scratch_shapes=[
            pltpu.VMEM(own.shape, own.dtype),
            pltpu.VMEM(blocks.shape, blocks.dtype),
            pltpu.SemaphoreType.DMA((blocks.shape[0] + 1,)),
        ],
        compiler_params=pltpu.CompilerParams(vmem_limit_bytes=24 << 20),
        cost_estimate=pl.CostEstimate(
            flops=2 * x.shape[0] * own.size * (blocks.shape[1] + 1),
            bytes_accessed=2 * own.size * (blocks.shape[1] + 1),
            transcendentals=0,
        ),
        name="out_back" if back else "out_forward",
    )(jnp.stack(ids()), x, in_hbm(own), in_hbm(blocks), *extra)


def out_forward(attn_rows, own, blocks, hidden, gain):
    if blocks.shape[3] % 128:
        residual = hidden.astype(F32) + nt(attn_rows, whole_of(own, blocks))
        return residual, (residual * norm_scale(residual) * gain).astype(BF)
    out_shape = (
        jax.ShapeDtypeStruct(hidden.shape, F32),
        jax.ShapeDtypeStruct(hidden.shape, BF),
    )
    return out_call(False, attn_rows, own, blocks, [hidden, gain[None]], out_shape)


def out_back(x, own, blocks):
    if blocks.shape[3] % 128:
        return nn(x, whole_of(own, blocks)).astype(BF)
    out_shape = jax.ShapeDtypeStruct((x.shape[0], own.shape[1]), BF)
    return out_call(True, x, own, blocks, [], out_shape)


def one_back_kernel(
    query_ref, pair_ref, w_ref, hidden_ref, gain_ref, residual_ref, y_ref
):
    step = pl.program_id(0)
    rows = w_ref.shape[0]
    split = query_ref.shape[1]
    y_ref[:, pl.ds(pl.multiple_of(step * rows, 128), rows)] = nt(
        query_ref[...], w_ref[:, :split]
    ) + nt(pair_ref[...], w_ref[:, split:])

    @pl.when(step == pl.num_programs(0) - 1)
    def _():
        grad = y_ref[...]
        inputs = hidden_ref[...].astype(F32)
        scale = norm_scale(inputs)
        unit = inputs * scale
        scaled = gain_ref[...] * grad
        y_ref[...] = residual_ref[...] + scale * (
            scaled - unit * jnp.mean(scaled * unit, axis=-1, keepdims=True)
        )


def one_back(query_part, pair_part, weight, hidden, gain, residual_grad):
    rows, width = hidden.shape
    columns = weight.shape[1]
    tile = FFN_TILE

    def whole(array):
        return pl.BlockSpec(array.shape, lambda j: (0, 0))

    gain = gain[None]
    return pl.pallas_call(
        one_back_kernel,
        grid=(width // tile,),
        out_shape=jax.ShapeDtypeStruct((rows, width), F32),
        in_specs=[
            whole(query_part),
            pl.BlockSpec((rows, pair_part.shape[1]), lambda j: (0, 0)),
            pl.BlockSpec((tile, columns), lambda j: (j, 0)),
            whole(hidden),
            whole(gain),
            whole(residual_grad),
        ],
        out_specs=pl.BlockSpec((rows, width), lambda j: (0, 0)),
        compiler_params=pltpu.CompilerParams(vmem_limit_bytes=24 << 20),
        cost_estimate=pl.CostEstimate(
            flops=2 * rows * width * columns,
            bytes_accessed=2 * width * columns,
            transcendentals=0,
        ),
        name="one_back",
    )(query_part, pair_part, in_hbm(weight), hidden, gain, residual_grad)


def send_rows(values):
    if lax.axis_size("fsdp") != 4:
        return fetch_rows(values)
    third = swap(values, "fsdp", 3)
    return [values, swap(values, "fsdp", 1), third]


def relay_rows(planes):
    if lax.axis_size("fsdp") != 4:
        return planes
    values, first, third = planes
    return [values, first, swap(third, "fsdp", 1), third]


def pass_rows(values):
    return relay_rows(send_rows(values))


def fetch_rows(values):
    count = lax.axis_size("fsdp")
    return [values] + [swap(values, "fsdp", away) for away in range(1, count)]


def sum_rows(parts, forward):
    count = len(parts)
    if count == 4 and forward:
        passed = swap(parts[2], "fsdp", 1).astype(F32)
        one = swap(parts[1], "fsdp", 1)
        third = swap((parts[3].astype(F32) + passed).astype(BF), "fsdp", 3)
        return [parts[0], one, third]
    return parts[:1] + [swap(parts[i], "fsdp", i) for i in range(1, count)]


def by_feature(values):
    rows, width = values.shape
    ctx_count, fsdp_count = lax.axis_size("ctx"), lax.axis_size("fsdp")
    blocks = values.reshape(rows, ctx_count, fsdp_count, width // (ctx_count * fsdp_count))
    return blocks.transpose(0, 2, 1, 3).reshape(rows, width)


def sum_over_ctx(part_for):
    pairs = lax.axis_size("ctx") // 2
    sent = jnp.stack([part_for(2 * pair + 1).astype(BF) for pair in range(pairs)])
    got = swap(sent, "ctx", 1)
    sums = [part_for(2 * pair).astype(F32) + got[pair].astype(F32) for pair in range(pairs)]
    total = sums[0]
    for pair in range(1, pairs):
        total = total + swap(sums[pair].astype(BF), "ctx", 2 * pair).astype(F32)
    return total


def ctx_rows_sum(values):
    height = values.shape[0] // lax.axis_size("ctx")
    me = lax.axis_index("ctx")

    def part(offset):
        return lax.dynamic_slice(
            values, ((me ^ offset) * height, 0), (height, values.shape[1])
        )

    return sum_over_ctx(part)


def key_offsets():
    count = lax.axis_size("ctx")
    return list(range(0, count, 2)) + list(range(1, count, 2))


def gather_keys(piece):
    same = [piece] + [swap(piece, "ctx", far) for far in range(2, lax.axis_size("ctx"), 2)]
    mine = jnp.concatenate(same, axis=0)
    return mine, swap(mine, "ctx", 1)


def sum_pairs(kept, sent, cosine, sine):
    _, count, width = kept.shape
    pairs = lax.axis_size("ctx") // 2
    got = swap(sent, "ctx", 1)
    sums = (kept.astype(F32) + got.astype(F32)).reshape(2, pairs, count // pairs, width)
    far = [swap(sums[:, pair].astype(BF), "ctx", 2 * pair) for pair in range(1, pairs)]
    return pair_turn(sums[:, 0], far, cosine, sine), got


def half_mask(shape):
    return lax.broadcasted_iota(jnp.int32, shape, len(shape) - 1) % 128 < HD


def turn(values, cosine, sine):
    lanes = lax.broadcasted_iota(jnp.int32, values.shape, 1) % HD
    turned = jnp.where(
        lanes < HD // 2, pltpu.roll(values, 128 - HD // 2, 1), pltpu.roll(values, HD // 2, 1)
    )
    return values * cosine + turned * sine


def doubled(tile, odd):
    wide = tile.astype(F32)
    other = pltpu.roll(wide, HD, 1)
    return jnp.where(half_mask(tile.shape) == (odd == 0), wide, other).astype(BF)


def split_heads(tile_pair):
    zero = jnp.zeros((), tile_pair.dtype)
    parts = []
    for j in range(2):
        tile = tile_pair[:, j * 128 : (j + 1) * 128]
        mask = half_mask(tile.shape)
        parts += [jnp.where(mask, tile, zero), jnp.where(mask, zero, tile)]
    return jnp.concatenate(parts, axis=0)


def merge_heads(stacked):
    rows = stacked.shape[0] // 4
    tiles = []
    for j in range(2):
        even = stacked[2 * j * rows : (2 * j + 1) * rows]
        odd = stacked[(2 * j + 1) * rows : (2 * j + 2) * rows]
        tiles.append(jnp.where(half_mask(even.shape), even, odd))
    return jnp.concatenate(tiles, axis=1)


def key_chunks(refs, chunk):
    first = 0
    for k_ref, v_ref in refs:
        for start in range(0, k_ref.shape[0], chunk):
            at = slice(start, start + chunk)
            yield first + start, k_ref.at[at, :], v_ref.at[at, :]
        first += k_ref.shape[0]


def masked_scores(keys, queries, key_ref, own_ref, start):
    allowed = key_ref[start : start + keys.shape[0], :1] <= own_ref[...]
    bias = jnp.where(allowed, 0.0, -1e30).astype(F32)
    return nt(keys, queries) + jnp.concatenate([bias] * 4, axis=1)


def attend_kernel(
    chunk, q_ref, ka_ref, va_ref, kb_ref, vb_ref, key_ref, own_ref, rows_ref, attended_ref, log_ref
):
    odd = pl.program_id(0) % 2
    rows = q_ref.shape[0]
    queries = split_heads(q_ref[...])
    parts = list(key_chunks(((ka_ref, va_ref), (kb_ref, vb_ref)), chunk))
    scores = [
        masked_scores(doubled(k_ref[...], odd), queries, key_ref, own_ref, start)
        for start, k_ref, _ in parts
    ]
    top = jnp.max(scores[0], axis=0, keepdims=True)
    for score in scores[1:]:
        top = jnp.maximum(top, jnp.max(score, axis=0, keepdims=True))
    total = jnp.zeros_like(top)
    summed = jnp.zeros((4 * rows, 128), F32)
    for score, (_, _, v_ref) in zip(scores, parts):
        weights = jnp.exp(score - top)
        total += jnp.sum(weights, axis=0, keepdims=True)
        summed += tn(weights.astype(BF), doubled(v_ref[...], odd))
    log_ref[0] = top + jnp.log(total)
    attended = merge_heads(summed / jnp.transpose(jnp.broadcast_to(total, (128, 4 * rows))))
    attended_ref[...] = attended
    rows_ref[...] = attended.astype(BF)


def key_specs(parts):
    tiles = parts[0].shape[1] // 256
    specs, arrays = [], []
    for part in parts:
        specs.append(pl.BlockSpec((part.shape[0], 128), lambda g: (0, g // 2)))
        specs.append(pl.BlockSpec((part.shape[0], 128), lambda g: (0, tiles + g // 2)))
        arrays += [part, part]
    return specs, arrays


def attend(queries, keys_values, key_anchor, own_anchor):
    rows, width = queries.shape
    count = key_anchor.shape[0]
    specs, arrays = key_specs(keys_values)
    wide = pl.BlockSpec((rows, 256), lambda g: (0, g))
    return pl.pallas_call(
        lambda *refs: attend_kernel(KEY_CHUNK, *refs),
        grid=(KV,),
        out_shape=(
            jax.ShapeDtypeStruct((rows, width), BF),
            jax.ShapeDtypeStruct((rows, width), F32),
            jax.ShapeDtypeStruct((KV, 1, 4 * rows), F32),
        ),
        in_specs=[wide]
        + specs
        + [
            pl.BlockSpec((count, 128), lambda g: (0, 0)),
            pl.BlockSpec((1, rows), lambda g: (0, 0)),
        ],
        out_specs=(wide, wide, pl.BlockSpec((1, 1, 4 * rows), lambda g: (g, 0, 0))),
        compiler_params=pltpu.CompilerParams(vmem_limit_bytes=48 << 20),
        cost_estimate=pl.CostEstimate(
            flops=4 * rows * width * count,
            bytes_accessed=4 * count * KV * HD,
            transcendentals=rows * H * count,
        ),
        name="attend",
    )(queries, *arrays, key_anchor, own_anchor)


def attend_back_kernel(
    chunk, q_ref, grad_ref, attended_ref, ka_ref, va_ref, kb_ref, vb_ref, key_ref, own_ref, log_ref,
    cos_ref, sin_ref, dq_ref, kept_ref, sent_ref,
):
    odd = pl.program_id(0) % 2
    rows = q_ref.shape[0]
    half = ka_ref.shape[0]
    queries, grads = split_heads(q_ref[...]), split_heads(grad_ref[...])
    product = grads.astype(F32) * split_heads(attended_ref[...])
    delta = jnp.sum(jnp.transpose(product), axis=0, keepdims=True)
    log_total = log_ref[0]
    total = jnp.zeros((4 * rows, 128), F32)
    keep = half_mask((chunk, 128)) == (odd == 0)
    for start, k_ref, v_ref in key_chunks(((ka_ref, va_ref), (kb_ref, vb_ref)), chunk):
        keys, values = doubled(k_ref[...], odd), doubled(v_ref[...], odd)
        scores = masked_scores(keys, queries, key_ref, own_ref, start)
        probs = jnp.exp(scores - log_total)
        value_grad = nn(probs.astype(BF), grads)
        score_grad = (probs * (nt(values, grads) - delta)).astype(BF)
        key_grad = nn(score_grad, queries)
        total += tn(score_grad, keys)
        out_ref = kept_ref if start < half else sent_ref
        at = slice(start % half, start % half + chunk)
        for part, value in enumerate((key_grad, value_grad)):
            value = (value + pltpu.roll(value, HD, 1)).astype(BF)
            out_ref[part, at, :] = jnp.where(keep, value, out_ref[part, at, :])
    merged = merge_heads(total) * (1.0 / math.sqrt(HD))
    cosine, sine = cos_ref[...], sin_ref[...]
    for j in range(2):
        tile = slice(j * 128, (j + 1) * 128)
        dq_ref[:, tile] = turn(merged[:, tile], cosine, -sine).astype(BF)


def attend_back(queries, grads, attended, keys_values, key_anchor, own_anchor, logs, cosine, sine):
    rows, width = queries.shape
    count = key_anchor.shape[0]
    specs, arrays = key_specs(keys_values)
    wide = pl.BlockSpec((rows, 256), lambda g: (0, g))
    small = pl.BlockSpec((rows, 128), lambda g: (0, 0))
    pair = pl.BlockSpec((2, count // 2, 128), lambda g: (0, 0, g // 2))
    return pl.pallas_call(
        lambda *refs: attend_back_kernel(KEY_CHUNK, *refs),
        grid=(KV,),
        out_shape=(
            jax.ShapeDtypeStruct((rows, width), BF),
            jax.ShapeDtypeStruct((2, count // 2, KV * HD), BF),
            jax.ShapeDtypeStruct((2, count // 2, KV * HD), BF),
        ),
        in_specs=[wide, wide, wide]
        + specs
        + [
            pl.BlockSpec((count, 128), lambda g: (0, 0)),
            pl.BlockSpec((1, rows), lambda g: (0, 0)),
            pl.BlockSpec((1, 1, 4 * rows), lambda g: (g, 0, 0)),
            small,
            small,
        ],
        out_specs=(wide, pair, pair),
        compiler_params=pltpu.CompilerParams(vmem_limit_bytes=48 << 20),
        cost_estimate=pl.CostEstimate(
            flops=10 * rows * width * count,
            bytes_accessed=8 * count * KV * HD,
            transcendentals=rows * H * count,
        ),
        name="attend_back",
    )(queries, grads, attended, *arrays, key_anchor, own_anchor, logs, cosine, sine)


def pair_turn_kernel(copies, own_ref, *refs):
    got, (cos_ref, sin_ref, y_ref) = refs[:-3], refs[-3:]
    total = own_ref[...]
    for ref in got:
        total = total + ref[...].astype(F32)
    cosine, sine = cos_ref[...], sin_ref[...]
    _, rows, width = total.shape
    tiles = [
        turn(total[0, :, start : start + 128], cosine, -sine).astype(BF)
        for start in range(0, width, 128)
    ]
    values = total[1].astype(BF)
    for copy in range(copies):
        at = slice(copy * rows, (copy + 1) * rows)
        for i, tile in enumerate(tiles):
            y_ref[at, i * 128 : (i + 1) * 128] = tile
        y_ref[at, width:] = values


def pair_turn(own, got, cosine, sine):
    _, rows, width = own.shape
    copies = lax.axis_size("fsdp")
    return pl.pallas_call(
        lambda *refs: pair_turn_kernel(copies, *refs),
        out_shape=jax.ShapeDtypeStruct((copies * rows, 2 * width), BF),
        name="pair_turn",
    )(own, *got, cosine, sine)


def join_rows(x_buf, refs):
    @pl.when((pl.program_id(0) == 0))
    def _():
        rows = refs[0].shape[0]
        for i, ref in enumerate(refs):
            x_buf[i * rows : (i + 1) * rows] = ref[...]


def ffn_kernel(count, earlier, *refs):
    rows_refs, (act_ref, w_ref), refs = refs[:count], refs[count : count + 2], refs[count + 2 :]
    out_ref, refs = refs[earlier], refs[earlier + 1 :]
    sum_refs, (x_buf, sum_buf) = refs[:count], refs[count:]
    join_rows(x_buf, rows_refs)
    step = pl.program_id(0)
    gate_w, up_w = w_ref[0], w_ref[1]
    x = x_buf[...]
    gate, up = nn(x, gate_w), nn(x, up_w)
    act_grad = act_ref[...]
    sig = jax.nn.sigmoid(gate)
    silu = gate * sig
    gate_grad = (act_grad * up * sig * (1.0 + gate * (1.0 - sig))).astype(BF)
    up_grad = (act_grad * silu).astype(BF)
    out_ref[0], out_ref[1], out_ref[2] = gate_grad, up_grad, (silu * up).astype(BF)
    part = nt(gate_grad, gate_w) + nt(up_grad, up_w)

    @pl.when(step == 0)
    def _():
        sum_buf[...] = part

    @pl.when(step > 0)
    def _():
        sum_buf[...] += part

    @pl.when(step == pl.num_programs(0) - 1)
    def _():
        rows = sum_refs[0].shape[0]
        for i, ref in enumerate(sum_refs):
            ref[...] = sum_buf[i * rows : (i + 1) * rows].astype(ref.dtype)


def ffn_middle(blocks, act_grad, half, weights, kinds, earlier):
    width = blocks[0].shape[1]
    rows = blocks[0].shape[0] * len(blocks)
    hidden = weights.shape[2]
    tile = FFN_TILE
    whole = [pl.BlockSpec(block.shape, lambda j: (0, 0)) for block in blocks]
    out = pl.pallas_call(
        lambda *refs: ffn_kernel(len(blocks), len(earlier), *refs),
        grid=(hidden // tile,),
        out_shape=(
            pltpu.HBM((3, 2 * rows, hidden), BF),
            *[jax.ShapeDtypeStruct(block.shape, kind) for block, kind in zip(blocks, kinds)],
        ),
        in_specs=whole
        + [
            pl.BlockSpec((rows, tile), lambda j: (half, j)),
            pl.BlockSpec((2, width, tile), lambda j: (0, 0, j)),
        ]
        + [pl.BlockSpec(memory_space=pltpu.HBM)] * len(earlier),
        out_specs=(pl.BlockSpec((3, rows, tile), lambda j: (0, half, j)), *whole),
        input_output_aliases={len(blocks) + 2: 0} if earlier else {},
        scratch_shapes=[pltpu.VMEM((rows, width), BF), pltpu.VMEM((rows, width), F32)],
        compiler_params=pltpu.CompilerParams(vmem_limit_bytes=40 << 20),
        cost_estimate=pl.CostEstimate(
            flops=8 * rows * width * hidden,
            bytes_accessed=4 * width * hidden,
            transcendentals=rows * hidden,
        ),
        name="ffn_middle",
    )(*blocks, act_grad, weights, *earlier)
    return out[0], list(out[1:])


def products_kernel(count, added, ids_ref, *refs):
    blocks, right, rest = refs[: 2 * count], refs[2 * count], refs[2 * count + 1 :]
    out_ref, left = rest[-2:]
    rows, height = blocks[0].shape
    for j in range(2):
        for i in range(count):
            at = (slice(i * rows, (i + 1) * rows), slice(j * height, (j + 1) * height))
            left[at] = blocks[j * count + i][...]
    part = tn(left[...], right[0])
    if added:
        part = part + rest[0][0].astype(F32)
    out_ref[0] = part.astype(BF)


def half_products(rows_of, parts, first, size, got, earlier):
    count = len(rows_of)
    rows, width = rows_of[0].shape
    matrices, _, hidden = parts.shape
    ctx_count = lax.axis_size("ctx")
    height = width // ctx_count
    kept = got is not None

    def left(j):
        def place(k, i, ids_ref):
            own = ids_ref[0] % 2
            return (0, 2 * (2 * i + j) + (own if kept else 1 - own))

        return pl.BlockSpec((rows, height), place)

    def out(start):
        return pl.BlockSpec((1, 2 * height, hidden), lambda k, i, ids_ref: (start + k, i, 0))

    right = pl.BlockSpec((1, rows * count, hidden), lambda k, i, ids_ref: (first + k, 0, 0))
    extra = ([got] if kept else []) + earlier
    operands = 2 * count + 1 + len(extra)
    return pl.pallas_call(
        lambda *refs: products_kernel(count, kept, *refs),
        grid_spec=pltpu.PrefetchScalarGridSpec(
            num_scalar_prefetch=1,
            grid=(size, ctx_count // 4),
            in_specs=[left(0)] * count
            + [left(1)] * count
            + [right]
            + [out(0)] * kept
            + [pl.BlockSpec(memory_space=pltpu.HBM)] * len(earlier),
            out_specs=out(first if kept else 0),
            scratch_shapes=[pltpu.VMEM((count * rows, 2 * height), BF)],
        ),
        out_shape=pltpu.HBM((matrices if kept else size, width // 2, hidden), BF),
        input_output_aliases={operands: 0} if earlier else {},
        compiler_params=pltpu.CompilerParams(vmem_limit_bytes=24 << 20),
        cost_estimate=pl.CostEstimate(
            flops=size * count * rows * width * hidden,
            bytes_accessed=size * width * hidden,
            transcendentals=0,
        ),
    )(jnp.stack(ids()), *rows_of, *rows_of, in_hbm(parts), *extra)


def ffn_gradient(rows_in, rows_out, parts):
    count = lax.axis_size("ctx")
    if count % 4 or (rows_in[0].shape[1] // count) % 128:
        left, grad = (jnp.concatenate(rows, axis=0) for rows in (rows_in, rows_out))
        products = [tn(left, parts[0]), tn(left, parts[1]), tn(grad, parts[2])]
        products = jnp.stack(products, axis=1).astype(BF)
        return lax.psum_scatter(products, "ctx", scatter_dimension=0, tiled=True), parts
    calls = ((rows_out, 2, 1), (rows_in, 0, 2))
    got = []
    for rows_of, first, size in calls:
        sent = half_products(rows_of, parts, first, size, None, [])
        got.append(swap(sent, "ctx", 1))
    kept = []
    for (rows_of, first, size), part in zip(calls, got):
        kept = [half_products(rows_of, parts, first, size, part, kept)]
    groups = [list(range(core, count, 2)) for core in range(2)]
    kept = kept[0].transpose(1, 0, 2)
    rows = lax.psum_scatter(kept, "ctx", scatter_dimension=0, tiled=True, axis_index_groups=groups)
    return rows, after(parts, kept)


def widen_kernel(x_ref, y_ref):
    y_ref[...] = x_ref[...].astype(F32)


def widened(values):
    values = values.transpose(1, 0, 2)
    matrices, rows, hidden = values.shape
    block = pl.BlockSpec((1, rows // 2, hidden), lambda k, i: (k, i, 0))
    return pl.pallas_call(
        widen_kernel,
        grid=(matrices, 2),
        out_shape=jax.ShapeDtypeStruct(values.shape, F32),
        in_specs=[block],
        out_specs=block,
        compiler_params=pltpu.CompilerParams(vmem_limit_bytes=16 << 20),
        name="widened",
    )(values).transpose(1, 0, 2)


def down_back_kernel(count, *refs):
    rows_refs, (w_ref, y_ref, x_buf) = refs[:count], refs[count:]
    join_rows(x_buf, rows_refs)
    y_ref[...] = nn(x_buf[...], w_ref[0])


def down_back(blocks, weights):
    width = blocks[0].shape[1]
    rows = blocks[0].shape[0] * len(blocks)
    hidden = weights.shape[2]
    tile = FFN_TILE
    return pl.pallas_call(
        lambda *refs: down_back_kernel(len(blocks), *refs),
        grid=(hidden // tile,),
        out_shape=pltpu.HBM((rows, hidden), F32),
        in_specs=[pl.BlockSpec(block.shape, lambda j: (0, 0)) for block in blocks]
        + [pl.BlockSpec((1, width, tile), lambda j: (2, 0, j))],
        out_specs=pl.BlockSpec((rows, tile), lambda j: (0, j)),
        scratch_shapes=[pltpu.VMEM((rows, width), BF)],
        compiler_params=pltpu.CompilerParams(vmem_limit_bytes=24 << 20),
        cost_estimate=pl.CostEstimate(
            flops=2 * rows * width * hidden,
            bytes_accessed=2 * width * hidden,
            transcendentals=0,
        ),
        name="down_back",
    )(*blocks, weights)


def down_kernel(x_ref, w_ref, *y_refs):
    rows = x_ref.shape[1] // len(y_refs)
    total = nt(x_ref[0], w_ref[0])
    for i, y_ref in enumerate(y_refs):
        y_ref[...] = total[i * rows : (i + 1) * rows].astype(y_ref.dtype)


def down_forward(parts, weights, count):
    _, rows, hidden = parts.shape
    width = weights.shape[1]
    tile = FFN_TILE
    height = rows // count
    return pl.pallas_call(
        down_kernel,
        grid=(width // tile,),
        out_shape=tuple(
            jax.ShapeDtypeStruct((height, width), BF if i else F32) for i in range(count)
        ),
        in_specs=[
            pl.BlockSpec((1, rows, hidden), lambda j: (2, 0, 0)),
            pl.BlockSpec((1, tile, hidden), lambda j: (2, j, 0)),
        ],
        out_specs=tuple(pl.BlockSpec((height, tile), lambda j: (0, j)) for _ in range(count)),
        compiler_params=pltpu.CompilerParams(vmem_limit_bytes=24 << 20),
        cost_estimate=pl.CostEstimate(
            flops=2 * rows * width * hidden,
            bytes_accessed=2 * width * hidden,
            transcendentals=0,
        ),
        name="down_forward",
    )(in_hbm(parts), weights)


def share_kernel(count, sizes, ids_ref, *refs):
    products = len(sizes)
    lefts = [refs[i * count : (i + 1) * count] for i in range(products)]
    rest = refs[products * count :]
    rights = []
    for size in sizes:
        rights.append(rest[:size])
        rest = rest[size:]
    bufs = rest[len(rest) - products :]
    terms, (kept_ref, sent_ref) = rest[: -products - 2], rest[-products - 2 : -products]
    half = kept_ref.shape[1]
    own = ids_ref[0] % 2 == 0

    @pl.when(pl.program_id(0) == 0)
    def _():
        for parts, buf in zip(rights, bufs):
            rows = buf.shape[0] // count
            for away in range(count):
                if len(parts) > 1:
                    block = parts[away][...]
                else:
                    start = (ids_ref[1] ^ away) * rows
                    block = parts[0][pl.ds(pl.multiple_of(start, 16), rows), :]
                buf[away * rows : (away + 1) * rows] = block

    def emit(part, column):
        at = slice(column, column + part.shape[1])
        kept_ref[0, :, at] = jnp.where(own, part[:half], part[half:])
        sent_ref[0, :, at] = jnp.where(own, part[half:], part[:half])

    column = 0
    for left, buf in zip(lefts, bufs):
        joined = jnp.concatenate([ref[...] for ref in left], axis=0)
        emit(tn(joined, buf[...]).astype(BF), column)
        column += buf.shape[1]
    for term in terms:
        tall = jnp.broadcast_to(term[...], (128, term.shape[1]))
        emit(jnp.transpose(tall).astype(BF), column)
        column += 128


def share_products(lefts, rights, terms):
    ctx_count = lax.axis_size("ctx")
    pairs = ctx_count // 2
    count = len(lefts[0])
    rows, width = lefts[0][0].shape
    height = width // ctx_count
    groups = [right if isinstance(right, list) else [right] for right in rights]
    widths = [group[0].shape[1] for group in groups]
    columns = sum(widths) + 128 * len(terms)

    def place(j, ids_ref):
        return (0, (ids_ref[0] // 2) ^ j)

    def whole(array):
        return pl.BlockSpec(array.shape, lambda j, ids_ref: (0, 0))

    shape = jax.ShapeDtypeStruct((pairs, height, columns), BF)
    out = pl.BlockSpec((1, height, columns), lambda j, ids_ref: (j, 0, 0))
    flat_lefts = [block for left in lefts for block in left]
    flat_rights = [block for group in groups for block in group]
    return pl.pallas_call(
        lambda *refs: share_kernel(count, [len(group) for group in groups], *refs),
        grid_spec=pltpu.PrefetchScalarGridSpec(
            num_scalar_prefetch=1,
            grid=(pairs,),
            in_specs=[pl.BlockSpec((rows, 2 * height), place) for _ in flat_lefts]
            + [whole(block) for block in flat_rights]
            + [pl.BlockSpec((1, 2 * height), place) for _ in terms],
            out_specs=(out, out),
            scratch_shapes=[pltpu.VMEM((count * rows, size), BF) for size in widths],
        ),
        out_shape=(shape, shape),
        compiler_params=pltpu.CompilerParams(vmem_limit_bytes=32 << 20),
        cost_estimate=pl.CostEstimate(
            flops=2 * count * rows * width * columns,
            bytes_accessed=2 * (count * rows + columns) * width,
            transcendentals=0,
        ),
        name="share_terms" if terms else "share_products",
    )(jnp.stack(ids()), *flat_lefts, *flat_rights, *[term[None] for term in terms])


def in_fsdp_order(value):
    if not isinstance(value, list):
        return value
    plane = lax.axis_index("fsdp")
    stacked = jnp.stack(value)
    parts = [
        lax.dynamic_index_in_dim(stacked, plane ^ away, 0, keepdims=False)
        for away in range(len(value))
    ]
    return jnp.concatenate(parts, axis=0)


def share_start(lefts, rights, terms):
    pairs = lax.axis_size("ctx") // 2
    if (lefts[0][0].shape[1] // pairs) % 128:
        values = [tn(in_fsdp_order(a), in_fsdp_order(b)) for a, b in zip(lefts, rights)]
        values += [jnp.broadcast_to(term[:, None], (term.shape[0], 128)) for term in terms]
        return [ctx_rows_sum(jnp.concatenate(values, axis=1))]
    kept, sent = share_products(lefts, rights, terms)
    got = swap(sent, "ctx", 1)
    parts = [kept[0], got[0]]
    for pair in range(1, pairs):
        part = (kept[pair].astype(F32) + got[pair].astype(F32)).astype(BF)
        parts.append(swap(part, "ctx", 2 * pair))
    return parts


def finish_kernel(w_ref, gain_ref, *refs):
    parts, (grad_ref, gain_grad_ref, term_ref) = refs[:-3], refs[-3:]
    columns = grad_ref.shape[1]
    total = parts[0][...].astype(F32)
    for part in parts[1:]:
        total = total + part[...].astype(F32)
    grad = total[:, :columns]
    grad_ref[...] = grad
    row_sum = jnp.sum(w_ref[...].astype(F32) * grad, axis=1, keepdims=True)
    gain_grad_ref[...] = row_sum / gain_ref[...]
    term_ref[...] = total[:, columns:]


def finish_last(parts, weight_rows, gain_rows):
    rows, columns = weight_rows.shape
    wide = jax.ShapeDtypeStruct((rows, 128), F32)
    gains = jnp.broadcast_to(gain_rows[:, None], (rows, 128))
    return pl.pallas_call(
        finish_kernel,
        out_shape=(jax.ShapeDtypeStruct((rows, columns), F32), wide, wide),
        compiler_params=pltpu.CompilerParams(vmem_limit_bytes=16 << 20),
        name="finish_last",
    )(weight_rows, gains, *parts)


def share_finish(parts):
    total = parts[0].astype(F32)
    for part in parts[1:]:
        total = total + part.astype(F32)
    return total


def own_rows_of(values, height):
    index = lax.axis_index("ctx") * lax.axis_size("fsdp") + lax.axis_index("fsdp")
    return lax.dynamic_slice_in_dim(values, index * height, height, 0)


def feature_parts(values):
    count, plane = lax.axis_size("fsdp"), lax.axis_index("fsdp")
    values = by_feature(values)
    rows, width = values.shape
    width //= count
    return [
        lax.dynamic_slice(values, (0, (plane ^ away) * width), (rows, width))
        for away in range(count)
    ]


def feature_rows(parts):
    return [swap(part, "fsdp", away) if away else part for away, part in enumerate(parts)]


def own_features(terms):
    ctx_count, fsdp_count = lax.axis_size("ctx"), lax.axis_size("fsdp")
    total = jnp.stack(terms)
    away = 1
    while away < fsdp_count:
        total = total + swap(total, "fsdp", away)
        away *= 2
    blocks = total.reshape(len(terms), ctx_count, fsdp_count, -1)
    own = lax.dynamic_index_in_dim(blocks, lax.axis_index("fsdp"), 2, keepdims=False)
    own = own.reshape(len(terms), -1)
    return [own[i] for i in range(len(terms))]


def layer(
    hidden_in,
    out_grad,
    positions,
    block_order,
    attn_gain,
    ffn_gain,
    qkv_weight,
    out_weight,
    ffn_weight,
):
    ctx_count, fsdp_count = lax.axis_size("ctx"), lax.axis_size("fsdp")
    me, _ = ids()
    rows = hidden_in.shape[1]
    queries_width, kv_width = H * HD, KV * HD
    ffn_parts = in_hbm(ffn_weight.transpose(1, 0, 2))

    frequency = jnp.power(ROPE_BASE, -(jnp.arange(HD // 2, dtype=F32) * 2.0 / HD))
    angles = positions[0].astype(F32)[:, None] * frequency[None, :]
    cosine = jnp.tile(jnp.cos(angles), (1, 4))
    sine = jnp.tile(jnp.concatenate([-jnp.sin(angles), jnp.sin(angles)], axis=1), (1, 2))
    own_anchor = anchors_of(block_order, me, rows)[None]
    key_anchor = jnp.concatenate(
        [anchors_of(block_order, me ^ offset, rows) for offset in key_offsets()]
    )
    key_anchor = jnp.broadcast_to(key_anchor[:, None], (rows * ctx_count, 128))

    inputs = hidden_in[0].astype(F32)
    grad_in = out_grad[0]
    scale_one = norm_scale(inputs)
    normed_one = (inputs * scale_one * attn_gain).astype(BF)

    one_parts = feature_parts(normed_one)
    fast = ctx_count == 8 and (qkv_weight.shape[1] // ctx_count) % 128 == 0
    if fast:
        early = (cosine, sine, own_anchor, key_anchor, one_parts)
        qkv_pieces, marks = gather_pieces(qkv_weight, early)
        out_blocks = gather_blocks(out_weight, *marks)
        queries, pair, qkv_full = pieces_forward(
            normed_one, qkv_weight, qkv_pieces, cosine, sine
        )
    else:
        marks = (normed_one, normed_one)
        out_blocks = gather_blocks(out_weight, *marks)
        qkv_full = whole_of(qkv_weight, gather_blocks(qkv_weight, normed_one, normed_one))
        projected = nn(normed_one, qkv_full)
        turned = rotate(
            projected[:, : queries_width + kv_width].reshape(rows, H + KV, HD), positions[0]
        ).reshape(rows, queries_width + kv_width)
        queries = (turned[:, :queries_width] * (1.0 / math.sqrt(HD))).astype(BF)
        pair = jnp.concatenate(
            [turned[:, queries_width:], projected[:, queries_width + kv_width :]], axis=1
        ).astype(BF)
    own_one = feature_rows(after(one_parts, pair))
    keys_values = gather_keys(pair)
    rows_out = send_rows(after(grad_in, pair))
    attn_rows, attended, logs = attend(queries, keys_values, key_anchor, own_anchor)
    rows_out = relay_rows(after(rows_out, attn_rows))
    residual, normed_two = out_forward(
        attn_rows, out_weight, out_blocks, hidden_in[0], ffn_gain
    )
    scale_two = norm_scale(residual)
    rows_in = pass_rows(normed_two)
    rows_out = after(rows_out, normed_two)
    act_grad = down_back(rows_out, ffn_parts)

    all_attn = pass_rows(after(attn_rows, rows_in[2]))
    parts, partial = [], []
    half = fsdp_count // 2
    passing = 3 if fsdp_count == 4 else 0
    for index in range(2):
        blocks = rows_in[index * half : (index + 1) * half]
        kinds = [F32 if index * half + i in (0, passing) else BF for i in range(half)]
        out, terms = ffn_middle(blocks, in_hbm(act_grad), index, ffn_parts, kinds, parts)
        parts, partial = [out], partial + terms
    parts = parts[0]
    sum_grad = share_finish(sum_rows(partial, True))
    ffn_weight_grad, parts = ffn_gradient(rows_in, rows_out, parts)
    ffn_weight_grad = widened(ffn_weight_grad)
    out_partial = list(down_forward(parts, ffn_parts, fsdp_count))

    unit_two = residual * scale_two
    ffn_gain_term = jnp.sum(sum_grad * unit_two, axis=0)
    scaled_two = ffn_gain * sum_grad
    residual_grad = grad_in.astype(F32) + scale_two * (
        scaled_two - unit_two * jnp.mean(scaled_two * unit_two, axis=-1, keepdims=True)
    )
    residual_bf = residual_grad.astype(BF)
    (ffn_term,) = own_features([ffn_gain_term])
    attn_grad = out_back(residual_bf, out_weight, out_blocks)
    query_part, kept, sent = attend_back(
        queries, attn_grad, attended, keys_values, key_anchor, own_anchor, logs, cosine, sine
    )
    query_planes = pass_rows(query_part)
    pair_copies, near = sum_pairs(kept, sent, cosine, sine)
    own_residual = feature_rows(feature_parts(after(residual_bf, near)))
    all_pair = lax.all_to_all(pair_copies, "fsdp", split_axis=0, concat_axis=0, tiled=True)
    input_grad = one_back(
        query_part, pair_copies, qkv_full, hidden_in[0], attn_gain, residual_grad
    )
    out_sums = share_start([own_residual], [after(all_attn, input_grad)], [])
    out_sum = sum_rows([after(part, input_grad) for part in out_partial], False)
    qkv_sums = share_start(
        [own_one, own_one], [after(query_planes, (input_grad, ffn_term)), all_pair], [ffn_term]
    )
    own_rows = qkv_weight.shape[0] // ctx_count
    qkv_grad, gain_grad, term_grad = finish_last(
        qkv_sums, own_rows_of(qkv_full, own_rows), own_rows_of(attn_gain, own_rows)
    )
    output = (residual + share_finish(after(out_sum, qkv_sums[2:3]))).astype(BF)
    out_weight_grad = share_finish(out_sums)
    return (
        output[None],
        input_grad[None],
        qkv_grad,
        out_weight_grad,
        ffn_weight_grad,
        gain_grad[:, 0],
        term_grad[:, 0],
    )


def solution(mesh):
    step = sharded(mesh)
    return step


def sharded(mesh):
    return jax.shard_map(
        layer,
        mesh=mesh,
        in_specs=(
            P("fsdp", "ctx", None),
            P("fsdp", "ctx", None),
            P("fsdp", "ctx"),
            P(),
            P(),
            P(),
            P("fsdp", None),
            P("fsdp", None),
            P(None, None, "fsdp"),
        ),
        out_specs=(
            P("fsdp", "ctx", None),
            P("fsdp", "ctx", None),
            P(("ctx", "fsdp"), None),
            P(("ctx", "fsdp"), None),
            P("ctx", None, "fsdp"),
            P(("ctx", "fsdp")),
            P(("ctx", "fsdp")),
        ),
        check_vma=False,
    )
```

```python
import math

import jax
import jax.numpy as jnp
from jax import lax
from jax.experimental import pallas as pl
from jax.experimental.pallas import tpu as pltpu
from jax.sharding import PartitionSpec as P


H = 32
KV = 8
HD = 64

NORM_EPS = 1e-05
ROPE_BASE = 500000.0
FFN_TILE = 512
KEY_CHUNK = 256


BF = jnp.bfloat16
CTX, FSDP = "ctx", "fsdp"
F32 = jnp.float32


def mm(a, b, dims):
    return lax.dot_general(a, b, (dims, ((), ())), preferred_element_type=F32)


def nn(a, b):
    return mm(a, b, ((1,), (0,)))


def nt(a, b):
    return mm(a, b, ((1,), (1,)))


def tn(a, b):
    return mm(a, b, ((0,), (0,)))


def swap(value, axis, offset):
    count = lax.axis_size(axis)
    return lax.ppermute(value, axis, [(i, i ^ offset) for i in range(count)])


def rotate(values, token_places):
    head_dim = values.shape[-1]
    half_dim = head_dim // 2
    frequency = jnp.power(ROPE_BASE, -(jnp.arange(half_dim, dtype=F32) * 2.0 / head_dim))
    angles = token_places.astype(F32)[:, None] * frequency[None, :]
    cosine = jnp.concatenate([jnp.cos(angles), jnp.cos(angles)], axis=-1)[:, None, :]
    sine_part = jnp.concatenate([jnp.sin(angles), jnp.sin(angles)], axis=-1)[:, None, :]
    turned = jnp.concatenate([-values[..., half_dim:], values[..., :half_dim]], axis=-1)
    return values * cosine + turned * sine_part


def norm_scale(values):
    return lax.rsqrt(jnp.mean(values * values, axis=-1, keepdims=True) + NORM_EPS)


def lookup(entries, row_ids):
    matches = row_ids[:, None] == jnp.arange(entries.shape[0], dtype=jnp.int32)[None, :]
    return jnp.sum(jnp.where(matches, entries[None, :], 0), axis=1)


def anchors_of(block_order, owner, row_count):
    block_len = row_count // 2
    row_ids = owner * row_count + jnp.arange(row_count, dtype=jnp.int32)
    return lookup(block_order, row_ids // block_len) * block_len + row_ids % block_len


def after(value, *earlier):
    return lax.optimization_barrier((value, earlier))[0]


def ids():
    return lax.axis_index(CTX), lax.axis_index(FSDP)


def gather_pieces(weight, early):
    rows, columns = weight.shape
    share = columns // lax.axis_size(CTX)
    half = rows // 2
    mine = lax.dynamic_slice(weight, (0, lax.axis_index(CTX) * share), (rows, share))
    planes = {}
    planes[3] = swap(mine, FSDP, 3)
    planes[1] = swap(mine, FSDP, 1)
    planes[2] = swap(after(planes[3], early), FSDP, 1)
    pieces = []
    for away in (1, 3, 2):
        first = planes[away]
        along_x, along_y = swap(first, CTX, 2), swap(first, CTX, 4)
        if away == 1:
            corners = [(6, 0, swap(along_y, CTX, 2))]
        elif away == 3:
            corners = [(6, 0, swap(along_x, CTX, 4))]
        else:
            top, low = swap(along_y[:half], CTX, 2), swap(along_x[half:], CTX, 4)
            corners = [(6, 0, jnp.concatenate([top, low], axis=0))]
        parts = [(0, 0, first), (2, 0, along_x), (4, 0, along_y)] + corners
        for offset, start, part in parts:
            pieces.append((away, offset, start, part))
            pieces.append((away, offset + 1, start, swap(part, CTX, 1)))
    return pieces, (planes[2], pieces[-2][3])


def pieces_kernel(places, rows_in, share, ids_ref, x_ref, own_ref, *refs):
    count = len(places)
    piece_refs, refs = refs[:count], refs[count:]
    cos_ref, sin_ref, q_ref, pair_ref, full_ref, y_ref, buf, in_sems, out_sems = refs
    me, plane = ids_ref[0], ids_ref[1]

    def block(away):
        return pl.ds(pl.multiple_of((plane ^ away) * rows_in, 128), rows_in)

    own_copy = pltpu.make_async_copy(own_ref, buf.at[block(0)], in_sems.at[count])
    own_copy.start()
    copies = []
    for i, (away, offset, start, height) in enumerate(places):
        at = pl.ds(pl.multiple_of((plane ^ away) * rows_in + start, 128), height)
        columns = pl.ds(pl.multiple_of((me ^ offset) * share, 128), share)
        copies.append(pltpu.make_async_copy(piece_refs[i], buf.at[at, columns], in_sems.at[i]))
        copies[-1].start()
    outs = []
    order = [0] + list(dict.fromkeys(away for away, _, _, _ in places))
    for away in order:
        if away:
            for copy, place in zip(copies, places):
                if place[0] == away:
                    copy.wait()
        else:
            own_copy.wait()
        outs.append(
            pltpu.make_async_copy(buf.at[block(away)], full_ref.at[block(away)], out_sems.at[away])
        )
        outs[-1].start()
        part = nn(x_ref[:, block(away)], buf[block(away)])
        y_ref[...] = part if away == 0 else y_ref[...] + part
    cosine, sine = cos_ref[...], sin_ref[...]
    queries, keys = H * HD, KV * HD
    for start in range(0, queries + keys, 128):
        tile = turn(y_ref[:, start : start + 128], cosine, sine)
        if start < queries:
            q_ref[:, start : start + 128] = (tile * (1.0 / math.sqrt(HD))).astype(BF)
        else:
            pair_ref[:, start - queries : start - queries + 128] = tile.astype(BF)
    pair_ref[:, keys:] = y_ref[:, queries + keys :].astype(BF)
    for copy in outs:
        copy.wait()


def pieces_forward(x, own, pieces, cosine, sine):
    me, plane = ids()
    rows_in, columns = own.shape
    rows, width = x.shape
    share = columns // lax.axis_size(CTX)
    places = tuple((away, offset, start, part.shape[0]) for away, offset, start, part in pieces)
    arrays = [part for _, _, _, part in pieces]
    hbm, vmem = pl.BlockSpec(memory_space=pltpu.HBM), pl.BlockSpec(memory_space=pltpu.VMEM)
    return pl.pallas_call(
        lambda *refs: pieces_kernel(places, rows_in, share, *refs),
        out_shape=(
            jax.ShapeDtypeStruct((rows, H * HD), BF),
            jax.ShapeDtypeStruct((rows, 2 * KV * HD), BF),
            pltpu.HBM((width, columns), BF),
        ),
        in_specs=[pl.BlockSpec(memory_space=pltpu.SMEM), vmem, hbm]
        + [hbm] * len(arrays)
        + [vmem, vmem],
        out_specs=(vmem, vmem, hbm),
        scratch_shapes=[
            pltpu.VMEM((rows, columns), F32),
            pltpu.VMEM((width, columns), BF),
            pltpu.SemaphoreType.DMA((len(arrays) + 1,)),
            pltpu.SemaphoreType.DMA((width // rows_in,)),
        ],
        compiler_params=pltpu.CompilerParams(vmem_limit_bytes=32 << 20),
        cost_estimate=pl.CostEstimate(
            flops=2 * rows * width * columns, bytes_accessed=4 * width * columns, transcendentals=0
        ),
        name="pieces",
    )(jnp.stack([me, plane]), x, in_hbm(own), *[in_hbm(part) for part in arrays], cosine, sine)


def gather_blocks(weight, before_fsdp, before_ctx):
    rows, columns = weight.shape
    me, plane = ids()
    share = columns // lax.axis_size(CTX)
    mine = lax.dynamic_slice(weight, (0, me * share), (rows, share))
    planes = lax.all_gather(after(mine, before_fsdp), FSDP)
    others = jnp.stack(
        [
            lax.dynamic_index_in_dim(planes, plane ^ away, 0, keepdims=False)
            for away in range(1, planes.shape[0])
        ]
    )
    return lax.all_gather(after(others, before_ctx), CTX)


def whole_of(own, blocks):
    ctx_count, others, rows, share = blocks.shape
    plane = lax.axis_index(FSDP)
    columns = ctx_count * share
    full = jnp.zeros(((others + 1) * rows, columns), own.dtype)
    full = lax.dynamic_update_slice(full, own, (plane * rows, 0))
    for away in range(1, others + 1):
        part = blocks[:, away - 1].transpose(1, 0, 2).reshape(rows, columns)
        full = lax.dynamic_update_slice(full, part, ((plane ^ away) * rows, 0))
    return full


def in_hbm(value):
    return pltpu.with_memory_space_constraint(value, pltpu.HBM)


def out_kernel(back, ids_ref, x_ref, own_ref, blocks_ref, *refs):
    hidden_ref, gain_ref = (None, None) if back else refs[:2]
    outs = refs if back else refs[2:]
    own_buf, buf, sems = outs[-3:]
    ctx_count, others, rows, share = buf.shape
    plane = ids_ref[1]

    def block_copy(c):
        return pltpu.make_async_copy(blocks_ref.at[c], buf.at[c], sems.at[c])

    own_copy = pltpu.make_async_copy(own_ref, own_buf, sems.at[ctx_count])
    own_copy.start()
    for c in range(ctx_count):
        block_copy(c).start()

    def features(away):
        return pl.ds(pl.multiple_of((plane ^ away) * rows, 128), rows)

    def columns(c):
        return pl.ds(pl.multiple_of(c * share, 128), share)

    own_copy.wait()
    if back:
        y_ref = outs[0]

        @pl.loop(0, ctx_count)
        def _(c):
            block_copy(c).wait()
            total = nn(x_ref[:, features(0)], own_buf[:, columns(c)])
            for away in range(1, others + 1):
                total += nn(x_ref[:, features(away)], buf[c, away - 1])
            y_ref[:, columns(c)] = total.astype(BF)

        return
    residual_ref, normed_ref = outs[:2]
    residual_ref[...] = hidden_ref[...].astype(F32)

    @pl.loop(0, ctx_count)
    def _(c):
        block_copy(c).wait()
        x = x_ref[:, columns(c)]
        residual_ref[:, features(0)] += nt(x, own_buf[:, columns(c)])
        for away in range(1, others + 1):
            residual_ref[:, features(away)] += nt(x, buf[c, away - 1])

    residual = residual_ref[...]
    normed_ref[...] = (residual * norm_scale(residual) * gain_ref[...]).astype(BF)


def out_call(back, x, own, blocks, extra, out_shape):
    vmem, hbm = pl.BlockSpec(memory_space=pltpu.VMEM), pl.BlockSpec(memory_space=pltpu.HBM)
    return pl.pallas_call(
        lambda *refs: out_kernel(back, *refs),
        out_shape=out_shape,
        in_specs=[pl.BlockSpec(memory_space=pltpu.SMEM), vmem, hbm, hbm] + [vmem] * len(extra),
        out_specs=jax.tree.map(lambda _: vmem, out_shape),
        scratch_shapes=[
            pltpu.VMEM(own.shape, own.dtype),
            pltpu.VMEM(blocks.shape, blocks.dtype),
            pltpu.SemaphoreType.DMA((blocks.shape[0] + 1,)),
        ],
        compiler_params=pltpu.CompilerParams(vmem_limit_bytes=24 << 20),
        cost_estimate=pl.CostEstimate(
            flops=2 * x.shape[0] * own.size * (blocks.shape[1] + 1),
            bytes_accessed=2 * own.size * (blocks.shape[1] + 1),
            transcendentals=0,
        ),
        name="out_b" if back else "out_f",
    )(jnp.stack(ids()), x, in_hbm(own), in_hbm(blocks), *extra)


def out_forward(attn_rows, own, blocks, hidden, gain):
    if blocks.shape[3] % 128:
        residual = hidden.astype(F32) + nt(attn_rows, whole_of(own, blocks))
        return residual, (residual * norm_scale(residual) * gain).astype(BF)
    out_shape = (
        jax.ShapeDtypeStruct(hidden.shape, F32),
        jax.ShapeDtypeStruct(hidden.shape, BF),
    )
    return out_call(False, attn_rows, own, blocks, [hidden, gain[None]], out_shape)


def out_back(x, own, blocks):
    if blocks.shape[3] % 128:
        return nn(x, whole_of(own, blocks)).astype(BF)
    out_shape = jax.ShapeDtypeStruct((x.shape[0], own.shape[1]), BF)
    return out_call(True, x, own, blocks, [], out_shape)


def one_back_kernel(
    query_ref, pair_ref, w_ref, hidden_ref, gain_ref, residual_ref, y_ref
):
    step = pl.program_id(0)
    rows = w_ref.shape[0]
    split = query_ref.shape[1]
    y_ref[:, pl.ds(pl.multiple_of(step * rows, 128), rows)] = nt(
        query_ref[...], w_ref[:, :split]
    ) + nt(pair_ref[...], w_ref[:, split:])

    @pl.when(step == pl.num_programs(0) - 1)
    def _():
        grad = y_ref[...]
        inputs = hidden_ref[...].astype(F32)
        scale = norm_scale(inputs)
        unit = inputs * scale
        scaled = gain_ref[...] * grad
        y_ref[...] = residual_ref[...] + scale * (
            scaled - unit * jnp.mean(scaled * unit, axis=-1, keepdims=True)
        )


def one_back(query_part, pair_part, weight, hidden, gain, residual_grad):
    rows, width = hidden.shape
    columns = weight.shape[1]
    tile = FFN_TILE

    def whole(array):
        return pl.BlockSpec(array.shape, lambda j: (0, 0))

    gain = gain[None]
    return pl.pallas_call(
        one_back_kernel,
        grid=(width // tile,),
        out_shape=jax.ShapeDtypeStruct((rows, width), F32),
        in_specs=[
            whole(query_part),
            pl.BlockSpec((rows, pair_part.shape[1]), lambda j: (0, 0)),
            pl.BlockSpec((tile, columns), lambda j: (j, 0)),
            whole(hidden),
            whole(gain),
            whole(residual_grad),
        ],
        out_specs=pl.BlockSpec((rows, width), lambda j: (0, 0)),
        compiler_params=pltpu.CompilerParams(vmem_limit_bytes=24 << 20),
        cost_estimate=pl.CostEstimate(
            flops=2 * rows * width * columns,
            bytes_accessed=2 * width * columns,
            transcendentals=0,
        ),
        name="one_b",
    )(query_part, pair_part, in_hbm(weight), hidden, gain, residual_grad)


def send_rows(values):
    if lax.axis_size(FSDP) != 4:
        return fetch_rows(values)
    third = swap(values, FSDP, 3)
    return [values, swap(values, FSDP, 1), third]


def relay_rows(planes):
    if lax.axis_size(FSDP) != 4:
        return planes
    values, first, third = planes
    return [values, first, swap(third, FSDP, 1), third]


def pass_rows(values):
    return relay_rows(send_rows(values))


def fetch_rows(values):
    count = lax.axis_size(FSDP)
    return [values] + [swap(values, FSDP, away) for away in range(1, count)]


def sum_rows(parts, forward):
    count = len(parts)
    if count == 4 and forward:
        passed = swap(parts[2], FSDP, 1).astype(F32)
        one = swap(parts[1], FSDP, 1)
        third = swap((parts[3].astype(F32) + passed).astype(BF), FSDP, 3)
        return [parts[0], one, third]
    return parts[:1] + [swap(parts[i], FSDP, i) for i in range(1, count)]


def by_feature(values):
    rows, width = values.shape
    ctx_count, fsdp_count = lax.axis_size(CTX), lax.axis_size(FSDP)
    blocks = values.reshape(rows, ctx_count, fsdp_count, width // (ctx_count * fsdp_count))
    return blocks.transpose(0, 2, 1, 3).reshape(rows, width)


def sum_over_ctx(part_for):
    pairs = lax.axis_size(CTX) // 2
    sent = jnp.stack([part_for(2 * pair + 1).astype(BF) for pair in range(pairs)])
    got = swap(sent, CTX, 1)
    sums = [part_for(2 * pair).astype(F32) + got[pair].astype(F32) for pair in range(pairs)]
    total = sums[0]
    for pair in range(1, pairs):
        total = total + swap(sums[pair].astype(BF), CTX, 2 * pair).astype(F32)
    return total


def ctx_rows_sum(values):
    height = values.shape[0] // lax.axis_size(CTX)
    me = lax.axis_index(CTX)

    def part(offset):
        return lax.dynamic_slice(
            values, ((me ^ offset) * height, 0), (height, values.shape[1])
        )

    return sum_over_ctx(part)


def key_offsets():
    count = lax.axis_size(CTX)
    return list(range(0, count, 2)) + list(range(1, count, 2))


def gather_keys(piece):
    same = [piece] + [swap(piece, CTX, far) for far in range(2, lax.axis_size(CTX), 2)]
    mine = jnp.concatenate(same, axis=0)
    return mine, swap(mine, CTX, 1)


def sum_pairs(kept, sent, cosine, sine):
    _, count, width = kept.shape
    pairs = lax.axis_size(CTX) // 2
    got = swap(sent, CTX, 1)
    sums = (kept.astype(F32) + got.astype(F32)).reshape(2, pairs, count // pairs, width)
    far = [swap(sums[:, pair].astype(BF), CTX, 2 * pair) for pair in range(1, pairs)]
    return pair_turn(sums[:, 0], far, cosine, sine), got


def half_mask(shape):
    return lax.broadcasted_iota(jnp.int32, shape, len(shape) - 1) % 128 < HD


def turn(values, cosine, sine):
    lanes = lax.broadcasted_iota(jnp.int32, values.shape, 1) % HD
    turned = jnp.where(
        lanes < HD // 2, pltpu.roll(values, 128 - HD // 2, 1), pltpu.roll(values, HD // 2, 1)
    )
    return values * cosine + turned * sine


def doubled(tile, odd):
    wide = tile.astype(F32)
    other = pltpu.roll(wide, HD, 1)
    return jnp.where(half_mask(tile.shape) == (odd == 0), wide, other).astype(BF)


def split_heads(tile_pair):
    zero = jnp.zeros((), tile_pair.dtype)
    parts = []
    for j in range(2):
        tile = tile_pair[:, j * 128 : (j + 1) * 128]
        mask = half_mask(tile.shape)
        parts += [jnp.where(mask, tile, zero), jnp.where(mask, zero, tile)]
    return jnp.concatenate(parts, axis=0)


def merge_heads(stacked):
    rows = stacked.shape[0] // 4
    tiles = []
    for j in range(2):
        even = stacked[2 * j * rows : (2 * j + 1) * rows]
        odd = stacked[(2 * j + 1) * rows : (2 * j + 2) * rows]
        tiles.append(jnp.where(half_mask(even.shape), even, odd))
    return jnp.concatenate(tiles, axis=1)


def key_chunks(refs, chunk):
    first = 0
    for k_ref, v_ref in refs:
        for start in range(0, k_ref.shape[0], chunk):
            at = slice(start, start + chunk)
            yield first + start, k_ref.at[at, :], v_ref.at[at, :]
        first += k_ref.shape[0]


def masked_scores(keys, queries, key_ref, own_ref, start):
    allowed = key_ref[start : start + keys.shape[0], :1] <= own_ref[...]
    bias = jnp.where(allowed, 0.0, -1e30).astype(F32)
    return nt(keys, queries) + jnp.concatenate([bias] * 4, axis=1)


def attend_kernel(
    chunk, q_ref, ka_ref, va_ref, kb_ref, vb_ref, key_ref, own_ref, rows_ref, attended_ref, log_ref
):
    odd = pl.program_id(0) % 2
    rows = q_ref.shape[0]
    queries = split_heads(q_ref[...])
    parts = list(key_chunks(((ka_ref, va_ref), (kb_ref, vb_ref)), chunk))
    scores = [
        masked_scores(doubled(k_ref[...], odd), queries, key_ref, own_ref, start)
        for start, k_ref, _ in parts
    ]
    top = jnp.max(scores[0], axis=0, keepdims=True)
    for score in scores[1:]:
        top = jnp.maximum(top, jnp.max(score, axis=0, keepdims=True))
    total = jnp.zeros_like(top)
    summed = jnp.zeros((4 * rows, 128), F32)
    for score, (_, _, v_ref) in zip(scores, parts):
        weights = jnp.exp(score - top)
        total += jnp.sum(weights, axis=0, keepdims=True)
        summed += tn(weights.astype(BF), doubled(v_ref[...], odd))
    log_ref[0] = top + jnp.log(total)
    attended = merge_heads(summed / jnp.transpose(jnp.broadcast_to(total, (128, 4 * rows))))
    attended_ref[...] = attended
    rows_ref[...] = attended.astype(BF)


def key_specs(parts):
    tiles = parts[0].shape[1] // 256
    specs, arrays = [], []
    for part in parts:
        specs.append(pl.BlockSpec((part.shape[0], 128), lambda g: (0, g // 2)))
        specs.append(pl.BlockSpec((part.shape[0], 128), lambda g: (0, tiles + g // 2)))
        arrays += [part, part]
    return specs, arrays


def attend(queries, keys_values, key_anchor, own_anchor):
    rows, width = queries.shape
    count = key_anchor.shape[0]
    specs, arrays = key_specs(keys_values)
    wide = pl.BlockSpec((rows, 256), lambda g: (0, g))
    return pl.pallas_call(
        lambda *refs: attend_kernel(KEY_CHUNK, *refs),
        grid=(KV,),
        out_shape=(
            jax.ShapeDtypeStruct((rows, width), BF),
            jax.ShapeDtypeStruct((rows, width), F32),
            jax.ShapeDtypeStruct((KV, 1, 4 * rows), F32),
        ),
        in_specs=[wide]
        + specs
        + [
            pl.BlockSpec((count, 128), lambda g: (0, 0)),
            pl.BlockSpec((1, rows), lambda g: (0, 0)),
        ],
        out_specs=(wide, wide, pl.BlockSpec((1, 1, 4 * rows), lambda g: (g, 0, 0))),
        compiler_params=pltpu.CompilerParams(vmem_limit_bytes=48 << 20),
        cost_estimate=pl.CostEstimate(
            flops=4 * rows * width * count,
            bytes_accessed=4 * count * KV * HD,
            transcendentals=rows * H * count,
        ),
        name="attend",
    )(queries, *arrays, key_anchor, own_anchor)


def attend_back_kernel(
    chunk, q_ref, grad_ref, attended_ref, ka_ref, va_ref, kb_ref, vb_ref, key_ref, own_ref, log_ref,
    cos_ref, sin_ref, dq_ref, kept_ref, sent_ref,
):
    odd = pl.program_id(0) % 2
    rows = q_ref.shape[0]
    half = ka_ref.shape[0]
    queries, grads = split_heads(q_ref[...]), split_heads(grad_ref[...])
    product = grads.astype(F32) * split_heads(attended_ref[...])
    delta = jnp.sum(jnp.transpose(product), axis=0, keepdims=True)
    log_total = log_ref[0]
    total = jnp.zeros((4 * rows, 128), F32)
    keep = half_mask((chunk, 128)) == (odd == 0)
    for start, k_ref, v_ref in key_chunks(((ka_ref, va_ref), (kb_ref, vb_ref)), chunk):
        keys, values = doubled(k_ref[...], odd), doubled(v_ref[...], odd)
        scores = masked_scores(keys, queries, key_ref, own_ref, start)
        probs = jnp.exp(scores - log_total)
        value_grad = nn(probs.astype(BF), grads)
        score_grad = (probs * (nt(values, grads) - delta)).astype(BF)
        key_grad = nn(score_grad, queries)
        total += tn(score_grad, keys)
        out_ref = kept_ref if start < half else sent_ref
        at = slice(start % half, start % half + chunk)
        for part, value in enumerate((key_grad, value_grad)):
            value = (value + pltpu.roll(value, HD, 1)).astype(BF)
            out_ref[part, at, :] = jnp.where(keep, value, out_ref[part, at, :])
    merged = merge_heads(total) * (1.0 / math.sqrt(HD))
    cosine, sine = cos_ref[...], sin_ref[...]
    for j in range(2):
        tile = slice(j * 128, (j + 1) * 128)
        dq_ref[:, tile] = turn(merged[:, tile], cosine, -sine).astype(BF)


def attend_back(queries, grads, attended, keys_values, key_anchor, own_anchor, logs, cosine, sine):
    rows, width = queries.shape
    count = key_anchor.shape[0]
    specs, arrays = key_specs(keys_values)
    wide = pl.BlockSpec((rows, 256), lambda g: (0, g))
    small = pl.BlockSpec((rows, 128), lambda g: (0, 0))
    pair = pl.BlockSpec((2, count // 2, 128), lambda g: (0, 0, g // 2))
    return pl.pallas_call(
        lambda *refs: attend_back_kernel(KEY_CHUNK, *refs),
        grid=(KV,),
        out_shape=(
            jax.ShapeDtypeStruct((rows, width), BF),
            jax.ShapeDtypeStruct((2, count // 2, KV * HD), BF),
            jax.ShapeDtypeStruct((2, count // 2, KV * HD), BF),
        ),
        in_specs=[wide, wide, wide]
        + specs
        + [
            pl.BlockSpec((count, 128), lambda g: (0, 0)),
            pl.BlockSpec((1, rows), lambda g: (0, 0)),
            pl.BlockSpec((1, 1, 4 * rows), lambda g: (g, 0, 0)),
            small,
            small,
        ],
        out_specs=(wide, pair, pair),
        compiler_params=pltpu.CompilerParams(vmem_limit_bytes=48 << 20),
        cost_estimate=pl.CostEstimate(
            flops=10 * rows * width * count,
            bytes_accessed=8 * count * KV * HD,
            transcendentals=rows * H * count,
        ),
        name="att_b",
    )(queries, grads, attended, *arrays, key_anchor, own_anchor, logs, cosine, sine)


def pair_turn_kernel(copies, own_ref, *refs):
    got, (cos_ref, sin_ref, y_ref) = refs[:-3], refs[-3:]
    total = own_ref[...]
    for ref in got:
        total = total + ref[...].astype(F32)
    cosine, sine = cos_ref[...], sin_ref[...]
    _, rows, width = total.shape
    tiles = [
        turn(total[0, :, start : start + 128], cosine, -sine).astype(BF)
        for start in range(0, width, 128)
    ]
    values = total[1].astype(BF)
    for copy in range(copies):
        at = slice(copy * rows, (copy + 1) * rows)
        for i, tile in enumerate(tiles):
            y_ref[at, i * 128 : (i + 1) * 128] = tile
        y_ref[at, width:] = values


def pair_turn(own, got, cosine, sine):
    _, rows, width = own.shape
    copies = lax.axis_size(FSDP)
    return pl.pallas_call(
        lambda *refs: pair_turn_kernel(copies, *refs),
        out_shape=jax.ShapeDtypeStruct((copies * rows, 2 * width), BF),
        name="turned",
    )(own, *got, cosine, sine)


def join_rows(x_buf, refs):
    @pl.when((pl.program_id(0) == 0))
    def _():
        rows = refs[0].shape[0]
        for i, ref in enumerate(refs):
            x_buf[i * rows : (i + 1) * rows] = ref[...]


def ffn_kernel(count, earlier, *refs):
    rows_refs, (act_ref, w_ref), refs = refs[:count], refs[count : count + 2], refs[count + 2 :]
    out_ref, refs = refs[earlier], refs[earlier + 1 :]
    sum_refs, (x_buf, sum_buf) = refs[:count], refs[count:]
    join_rows(x_buf, rows_refs)
    step = pl.program_id(0)
    gate_w, up_w = w_ref[0], w_ref[1]
    x = x_buf[...]
    gate, up = nn(x, gate_w), nn(x, up_w)
    act_grad = act_ref[...]
    sig = jax.nn.sigmoid(gate)
    silu = gate * sig
    gate_grad = (act_grad * up * sig * (1.0 + gate * (1.0 - sig))).astype(BF)
    up_grad = (act_grad * silu).astype(BF)
    out_ref[0], out_ref[1], out_ref[2] = gate_grad, up_grad, (silu * up).astype(BF)
    part = nt(gate_grad, gate_w) + nt(up_grad, up_w)

    @pl.when(step == 0)
    def _():
        sum_buf[...] = part

    @pl.when(step > 0)
    def _():
        sum_buf[...] += part

    @pl.when(step == pl.num_programs(0) - 1)
    def _():
        rows = sum_refs[0].shape[0]
        for i, ref in enumerate(sum_refs):
            ref[...] = sum_buf[i * rows : (i + 1) * rows].astype(ref.dtype)


def ffn_middle(blocks, act_grad, half, weights, kinds, earlier):
    width = blocks[0].shape[1]
    rows = blocks[0].shape[0] * len(blocks)
    hidden = weights.shape[2]
    tile = FFN_TILE
    whole = [pl.BlockSpec(block.shape, lambda j: (0, 0)) for block in blocks]
    out = pl.pallas_call(
        lambda *refs: ffn_kernel(len(blocks), len(earlier), *refs),
        grid=(hidden // tile,),
        out_shape=(
            pltpu.HBM((3, 2 * rows, hidden), BF),
            *[jax.ShapeDtypeStruct(block.shape, kind) for block, kind in zip(blocks, kinds)],
        ),
        in_specs=whole
        + [
            pl.BlockSpec((rows, tile), lambda j: (half, j)),
            pl.BlockSpec((2, width, tile), lambda j: (0, 0, j)),
        ]
        + [pl.BlockSpec(memory_space=pltpu.HBM)] * len(earlier),
        out_specs=(pl.BlockSpec((3, rows, tile), lambda j: (0, half, j)), *whole),
        input_output_aliases={len(blocks) + 2: 0} if earlier else {},
        scratch_shapes=[pltpu.VMEM((rows, width), BF), pltpu.VMEM((rows, width), F32)],
        compiler_params=pltpu.CompilerParams(vmem_limit_bytes=40 << 20),
        cost_estimate=pl.CostEstimate(
            flops=8 * rows * width * hidden,
            bytes_accessed=4 * width * hidden,
            transcendentals=rows * hidden,
        ),
        name="ffn",
    )(*blocks, act_grad, weights, *earlier)
    return out[0], list(out[1:])


def products_kernel(count, added, ids_ref, *refs):
    blocks, right, rest = refs[: 2 * count], refs[2 * count], refs[2 * count + 1 :]
    out_ref, left = rest[-2:]
    rows, height = blocks[0].shape
    for j in range(2):
        for i in range(count):
            at = (slice(i * rows, (i + 1) * rows), slice(j * height, (j + 1) * height))
            left[at] = blocks[j * count + i][...]
    part = tn(left[...], right[0])
    if added:
        part = part + rest[0][0].astype(F32)
    out_ref[0] = part.astype(BF)


def half_products(rows_of, parts, first, size, got, earlier):
    count = len(rows_of)
    rows, width = rows_of[0].shape
    matrices, _, hidden = parts.shape
    ctx_count = lax.axis_size(CTX)
    height = width // ctx_count
    kept = got is not None

    def left(j):
        def place(k, i, ids_ref):
            own = ids_ref[0] % 2
            return (0, 2 * (2 * i + j) + (own if kept else 1 - own))

        return pl.BlockSpec((rows, height), place)

    def out(start):
        return pl.BlockSpec((1, 2 * height, hidden), lambda k, i, ids_ref: (start + k, i, 0))

    right = pl.BlockSpec((1, rows * count, hidden), lambda k, i, ids_ref: (first + k, 0, 0))
    extra = ([got] if kept else []) + earlier
    operands = 2 * count + 1 + len(extra)
    return pl.pallas_call(
        lambda *refs: products_kernel(count, kept, *refs),
        grid_spec=pltpu.PrefetchScalarGridSpec(
            num_scalar_prefetch=1,
            grid=(size, ctx_count // 4),
            in_specs=[left(0)] * count
            + [left(1)] * count
            + [right]
            + [out(0)] * kept
            + [pl.BlockSpec(memory_space=pltpu.HBM)] * len(earlier),
            out_specs=out(first if kept else 0),
            scratch_shapes=[pltpu.VMEM((count * rows, 2 * height), BF)],
        ),
        out_shape=pltpu.HBM((matrices if kept else size, width // 2, hidden), BF),
        input_output_aliases={operands: 0} if earlier else {},
        compiler_params=pltpu.CompilerParams(vmem_limit_bytes=24 << 20),
        cost_estimate=pl.CostEstimate(
            flops=size * count * rows * width * hidden,
            bytes_accessed=size * width * hidden,
            transcendentals=0,
        ),
    )(jnp.stack(ids()), *rows_of, *rows_of, in_hbm(parts), *extra)


def ffn_gradient(rows_in, rows_out, parts):
    count = lax.axis_size(CTX)
    if count % 4 or (rows_in[0].shape[1] // count) % 128:
        left, grad = (jnp.concatenate(rows, axis=0) for rows in (rows_in, rows_out))
        products = [tn(left, parts[0]), tn(left, parts[1]), tn(grad, parts[2])]
        products = jnp.stack(products, axis=1).astype(BF)
        return lax.psum_scatter(products, CTX, scatter_dimension=0, tiled=True), parts
    calls = ((rows_out, 2, 1), (rows_in, 0, 2))
    got = []
    for rows_of, first, size in calls:
        sent = half_products(rows_of, parts, first, size, None, [])
        got.append(swap(sent, CTX, 1))
    kept = []
    for (rows_of, first, size), part in zip(calls, got):
        kept = [half_products(rows_of, parts, first, size, part, kept)]
    groups = [list(range(core, count, 2)) for core in range(2)]
    kept = kept[0].transpose(1, 0, 2)
    rows = lax.psum_scatter(kept, CTX, scatter_dimension=0, tiled=True, axis_index_groups=groups)
    return rows, after(parts, kept)


def widen_kernel(x_ref, y_ref):
    y_ref[...] = x_ref[...].astype(F32)


def widened(values, fast):
    if not fast:
        return values.astype(F32)
    values = values.transpose(1, 0, 2)
    matrices, rows, hidden = values.shape
    block = pl.BlockSpec((1, rows // 2, hidden), lambda k, i: (k, i, 0))
    return pl.pallas_call(
        widen_kernel,
        grid=(matrices, 2),
        out_shape=jax.ShapeDtypeStruct(values.shape, F32),
        in_specs=[block],
        out_specs=block,
        compiler_params=pltpu.CompilerParams(vmem_limit_bytes=16 << 20),
        name="wide",
    )(in_hbm(values)).transpose(1, 0, 2)


def down_back_kernel(count, *refs):
    rows_refs, (w_ref, y_ref, x_buf) = refs[:count], refs[count:]
    join_rows(x_buf, rows_refs)
    y_ref[...] = nn(x_buf[...], w_ref[0])


def down_back(blocks, weights):
    width = blocks[0].shape[1]
    rows = blocks[0].shape[0] * len(blocks)
    hidden = weights.shape[2]
    tile = FFN_TILE
    return pl.pallas_call(
        lambda *refs: down_back_kernel(len(blocks), *refs),
        grid=(hidden // tile,),
        out_shape=pltpu.HBM((rows, hidden), F32),
        in_specs=[pl.BlockSpec(block.shape, lambda j: (0, 0)) for block in blocks]
        + [pl.BlockSpec((1, width, tile), lambda j: (2, 0, j))],
        out_specs=pl.BlockSpec((rows, tile), lambda j: (0, j)),
        scratch_shapes=[pltpu.VMEM((rows, width), BF)],
        compiler_params=pltpu.CompilerParams(vmem_limit_bytes=24 << 20),
        cost_estimate=pl.CostEstimate(
            flops=2 * rows * width * hidden,
            bytes_accessed=2 * width * hidden,
            transcendentals=0,
        ),
        name="act",
    )(*blocks, weights)


def down_kernel(x_ref, w_ref, *y_refs):
    rows = x_ref.shape[1] // len(y_refs)
    total = nt(x_ref[0], w_ref[0])
    for i, y_ref in enumerate(y_refs):
        y_ref[...] = total[i * rows : (i + 1) * rows].astype(y_ref.dtype)


def down_forward(parts, weights, count):
    _, rows, hidden = parts.shape
    width = weights.shape[1]
    tile = FFN_TILE
    height = rows // count
    return pl.pallas_call(
        down_kernel,
        grid=(width // tile,),
        out_shape=tuple(
            jax.ShapeDtypeStruct((height, width), BF if i else F32) for i in range(count)
        ),
        in_specs=[
            pl.BlockSpec((1, rows, hidden), lambda j: (2, 0, 0)),
            pl.BlockSpec((1, tile, hidden), lambda j: (2, j, 0)),
        ],
        out_specs=tuple(pl.BlockSpec((height, tile), lambda j: (0, j)) for _ in range(count)),
        compiler_params=pltpu.CompilerParams(vmem_limit_bytes=24 << 20),
        cost_estimate=pl.CostEstimate(
            flops=2 * rows * width * hidden,
            bytes_accessed=2 * width * hidden,
            transcendentals=0,
        ),
        name="down",
    )(in_hbm(parts), weights)


def share_kernel(count, sizes, ids_ref, *refs):
    products = len(sizes)
    lefts = [refs[i * count : (i + 1) * count] for i in range(products)]
    rest = refs[products * count :]
    rights = []
    for size in sizes:
        rights.append(rest[:size])
        rest = rest[size:]
    bufs = rest[len(rest) - products :]
    terms, (kept_ref, sent_ref) = rest[: -products - 2], rest[-products - 2 : -products]
    half = kept_ref.shape[1]
    own = ids_ref[0] % 2 == 0

    @pl.when(pl.program_id(0) == 0)
    def _():
        for parts, buf in zip(rights, bufs):
            rows = buf.shape[0] // count
            for away in range(count):
                if len(parts) > 1:
                    block = parts[away][...]
                else:
                    start = (ids_ref[1] ^ away) * rows
                    block = parts[0][pl.ds(pl.multiple_of(start, 16), rows), :]
                buf[away * rows : (away + 1) * rows] = block

    def emit(part, column):
        at = slice(column, column + part.shape[1])
        kept_ref[0, :, at] = jnp.where(own, part[:half], part[half:])
        sent_ref[0, :, at] = jnp.where(own, part[half:], part[:half])

    column = 0
    for left, buf in zip(lefts, bufs):
        joined = jnp.concatenate([ref[...] for ref in left], axis=0)
        emit(tn(joined, buf[...]).astype(BF), column)
        column += buf.shape[1]
    for term in terms:
        tall = jnp.broadcast_to(term[...], (128, term.shape[1]))
        emit(jnp.transpose(tall).astype(BF), column)
        column += 128


def share_products(lefts, rights, terms):
    ctx_count = lax.axis_size(CTX)
    pairs = ctx_count // 2
    count = len(lefts[0])
    rows, width = lefts[0][0].shape
    height = width // ctx_count
    groups = [right if isinstance(right, list) else [right] for right in rights]
    widths = [group[0].shape[1] for group in groups]
    columns = sum(widths) + 128 * len(terms)

    def place(j, ids_ref):
        return (0, (ids_ref[0] // 2) ^ j)

    def whole(array):
        return pl.BlockSpec(array.shape, lambda j, ids_ref: (0, 0))

    shape = jax.ShapeDtypeStruct((pairs, height, columns), BF)
    out = pl.BlockSpec((1, height, columns), lambda j, ids_ref: (j, 0, 0))
    flat_lefts = [block for left in lefts for block in left]
    flat_rights = [block for group in groups for block in group]
    return pl.pallas_call(
        lambda *refs: share_kernel(count, [len(group) for group in groups], *refs),
        grid_spec=pltpu.PrefetchScalarGridSpec(
            num_scalar_prefetch=1,
            grid=(pairs,),
            in_specs=[pl.BlockSpec((rows, 2 * height), place) for _ in flat_lefts]
            + [whole(block) for block in flat_rights]
            + [pl.BlockSpec((1, 2 * height), place) for _ in terms],
            out_specs=(out, out),
            scratch_shapes=[pltpu.VMEM((count * rows, size), BF) for size in widths],
        ),
        out_shape=(shape, shape),
        compiler_params=pltpu.CompilerParams(vmem_limit_bytes=32 << 20),
        cost_estimate=pl.CostEstimate(
            flops=2 * count * rows * width * columns,
            bytes_accessed=2 * (count * rows + columns) * width,
            transcendentals=0,
        ),
        name="share_t" if terms else "share",
    )(jnp.stack(ids()), *flat_lefts, *flat_rights, *[term[None] for term in terms])


def in_fsdp_order(value):
    if not isinstance(value, list):
        return value
    plane = lax.axis_index(FSDP)
    stacked = jnp.stack(value)
    parts = [
        lax.dynamic_index_in_dim(stacked, plane ^ away, 0, keepdims=False)
        for away in range(len(value))
    ]
    return jnp.concatenate(parts, axis=0)


def share_start(lefts, rights, terms):
    pairs = lax.axis_size(CTX) // 2
    if (lefts[0][0].shape[1] // pairs) % 128:
        values = [tn(in_fsdp_order(a), in_fsdp_order(b)) for a, b in zip(lefts, rights)]
        values += [jnp.broadcast_to(term[:, None], (term.shape[0], 128)) for term in terms]
        return [ctx_rows_sum(jnp.concatenate(values, axis=1))]
    kept, sent = share_products(lefts, rights, terms)
    got = swap(sent, CTX, 1)
    parts = [kept[0], got[0]]
    for pair in range(1, pairs):
        part = (kept[pair].astype(F32) + got[pair].astype(F32)).astype(BF)
        parts.append(swap(part, CTX, 2 * pair))
    return parts


def finish_kernel(w_ref, gain_ref, *refs):
    parts, (grad_ref, gain_grad_ref, term_ref) = refs[:-3], refs[-3:]
    columns = grad_ref.shape[1]
    total = parts[0][...].astype(F32)
    for part in parts[1:]:
        total = total + part[...].astype(F32)
    grad = total[:, :columns]
    grad_ref[...] = grad
    row_sum = jnp.sum(w_ref[...].astype(F32) * grad, axis=1, keepdims=True)
    gain_grad_ref[...] = row_sum / gain_ref[...]
    term_ref[...] = total[:, columns:]


def finish_last(parts, weight_rows, gain_rows):
    rows, columns = weight_rows.shape
    wide = jax.ShapeDtypeStruct((rows, 128), F32)
    gains = jnp.broadcast_to(gain_rows[:, None], (rows, 128))
    return pl.pallas_call(
        finish_kernel,
        out_shape=(jax.ShapeDtypeStruct((rows, columns), F32), wide, wide),
        compiler_params=pltpu.CompilerParams(vmem_limit_bytes=16 << 20),
        name="finish",
    )(weight_rows, gains, *parts)


def share_finish(parts):
    total = parts[0].astype(F32)
    for part in parts[1:]:
        total = total + part.astype(F32)
    return total


def own_rows_of(values, height):
    index = lax.axis_index(CTX) * lax.axis_size(FSDP) + lax.axis_index(FSDP)
    return lax.dynamic_slice_in_dim(values, index * height, height, 0)


def feature_parts(values):
    count, plane = lax.axis_size(FSDP), lax.axis_index(FSDP)
    values = by_feature(values)
    rows, width = values.shape
    width //= count
    return [
        lax.dynamic_slice(values, (0, (plane ^ away) * width), (rows, width))
        for away in range(count)
    ]


def feature_rows(parts):
    return [swap(part, FSDP, away) if away else part for away, part in enumerate(parts)]


def own_features(terms):
    ctx_count, fsdp_count = lax.axis_size(CTX), lax.axis_size(FSDP)
    total = jnp.stack(terms)
    away = 1
    while away < fsdp_count:
        total = total + swap(total, FSDP, away)
        away *= 2
    blocks = total.reshape(len(terms), ctx_count, fsdp_count, -1)
    own = lax.dynamic_index_in_dim(blocks, lax.axis_index(FSDP), 2, keepdims=False)
    own = own.reshape(len(terms), -1)
    return [own[i] for i in range(len(terms))]


def layer(
    hidden_in,
    out_grad,
    positions,
    block_order,
    attn_gain,
    ffn_gain,
    qkv_weight,
    out_weight,
    ffn_weight,
):
    ctx_count, fsdp_count = lax.axis_size(CTX), lax.axis_size(FSDP)
    me, _ = ids()
    rows = hidden_in.shape[1]
    queries_width, kv_width = H * HD, KV * HD
    ffn_parts = in_hbm(ffn_weight.transpose(1, 0, 2))

    frequency = jnp.power(ROPE_BASE, -(jnp.arange(HD // 2, dtype=F32) * 2.0 / HD))
    angles = positions[0].astype(F32)[:, None] * frequency[None, :]
    cosine = jnp.tile(jnp.cos(angles), (1, 4))
    sine = jnp.tile(jnp.concatenate([-jnp.sin(angles), jnp.sin(angles)], axis=1), (1, 2))
    own_anchor = anchors_of(block_order, me, rows)[None]
    key_anchor = jnp.concatenate(
        [anchors_of(block_order, me ^ offset, rows) for offset in key_offsets()]
    )
    key_anchor = jnp.broadcast_to(key_anchor[:, None], (rows * ctx_count, 128))

    inputs = hidden_in[0].astype(F32)
    grad_in = out_grad[0]
    scale_one = norm_scale(inputs)
    normed_one = (inputs * scale_one * attn_gain).astype(BF)

    one_parts = feature_parts(normed_one)
    fast = ctx_count == 8 and (qkv_weight.shape[1] // ctx_count) % 128 == 0
    if fast:
        early = (cosine, sine, own_anchor, key_anchor, one_parts)
        qkv_pieces, marks = gather_pieces(qkv_weight, early)
        out_blocks = gather_blocks(out_weight, *marks)
        queries, pair, qkv_full = pieces_forward(
            normed_one, qkv_weight, qkv_pieces, cosine, sine
        )
    else:
        marks = (normed_one, normed_one)
        out_blocks = gather_blocks(out_weight, *marks)
        qkv_full = whole_of(qkv_weight, gather_blocks(qkv_weight, normed_one, normed_one))
        projected = nn(normed_one, qkv_full)
        turned = rotate(
            projected[:, : queries_width + kv_width].reshape(rows, H + KV, HD), positions[0]
        ).reshape(rows, queries_width + kv_width)
        queries = (turned[:, :queries_width] * (1.0 / math.sqrt(HD))).astype(BF)
        pair = jnp.concatenate(
            [turned[:, queries_width:], projected[:, queries_width + kv_width :]], axis=1
        ).astype(BF)
    own_one = feature_rows(after(one_parts, pair))
    keys_values = gather_keys(pair)
    rows_out = send_rows(after(grad_in, pair))
    attn_rows, attended, logs = attend(queries, keys_values, key_anchor, own_anchor)
    rows_out = relay_rows(after(rows_out, attn_rows))
    residual, normed_two = out_forward(
        attn_rows, out_weight, out_blocks, hidden_in[0], ffn_gain
    )
    scale_two = norm_scale(residual)
    rows_in = pass_rows(normed_two)
    rows_out = after(rows_out, normed_two)
    act_grad = down_back(rows_out, ffn_parts)

    all_attn = pass_rows(after(attn_rows, rows_in[2]))
    parts, partial = [], []
    half = fsdp_count // 2
    passing = 3 if fsdp_count == 4 else 0
    for index in range(2):
        blocks = rows_in[index * half : (index + 1) * half]
        kinds = [F32 if index * half + i in (0, passing) else BF for i in range(half)]
        out, terms = ffn_middle(blocks, in_hbm(act_grad), index, ffn_parts, kinds, parts)
        parts, partial = [out], partial + terms
    parts = parts[0]
    sum_grad = share_finish(sum_rows(partial, True))
    ffn_weight_grad, parts = ffn_gradient(rows_in, rows_out, parts)
    ffn_weight_grad = widened(ffn_weight_grad, fast)
    out_partial = list(down_forward(parts, ffn_parts, fsdp_count))

    unit_two = residual * scale_two
    ffn_gain_term = jnp.sum(sum_grad * unit_two, axis=0)
    scaled_two = ffn_gain * sum_grad
    residual_grad = grad_in.astype(F32) + scale_two * (
        scaled_two - unit_two * jnp.mean(scaled_two * unit_two, axis=-1, keepdims=True)
    )
    residual_bf = residual_grad.astype(BF)
    (ffn_term,) = own_features([ffn_gain_term])
    attn_grad = out_back(residual_bf, out_weight, out_blocks)
    query_part, kept, sent = attend_back(
        queries, attn_grad, attended, keys_values, key_anchor, own_anchor, logs, cosine, sine
    )
    query_planes = pass_rows(query_part)
    pair_copies, near = sum_pairs(kept, sent, cosine, sine)
    own_residual = feature_rows(feature_parts(after(residual_bf, near)))
    all_pair = lax.all_to_all(pair_copies, FSDP, split_axis=0, concat_axis=0, tiled=True)
    input_grad = one_back(
        query_part, pair_copies, qkv_full, hidden_in[0], attn_gain, residual_grad
    )
    out_sums = share_start([own_residual], [after(all_attn, input_grad)], [])
    out_sum = sum_rows([after(part, input_grad) for part in out_partial], False)
    qkv_sums = share_start(
        [own_one, own_one], [after(query_planes, (input_grad, ffn_term)), all_pair], [ffn_term]
    )
    own_rows = qkv_weight.shape[0] // ctx_count
    qkv_grad, gain_grad, term_grad = finish_last(
        qkv_sums, own_rows_of(qkv_full, own_rows), own_rows_of(attn_gain, own_rows)
    )
    output = (residual + share_finish(after(out_sum, qkv_sums[2:3]))).astype(BF)
    out_weight_grad = share_finish(out_sums)
    return (
        output[None],
        input_grad[None],
        qkv_grad,
        out_weight_grad,
        ffn_weight_grad,
        gain_grad[:, 0],
        term_grad[:, 0],
    )


def solution(mesh):
    step = sharded(mesh)
    return step


def sharded(mesh):
    return jax.shard_map(
        layer,
        mesh=mesh,
        in_specs=(
            P(FSDP, CTX, None),
            P(FSDP, CTX, None),
            P(FSDP, CTX),
            P(),
            P(),
            P(),
            P(FSDP, None),
            P(FSDP, None),
            P(None, None, FSDP),
        ),
        out_specs=(
            P(FSDP, CTX, None),
            P(FSDP, CTX, None),
            P((CTX, FSDP), None),
            P((CTX, FSDP), None),
            P(CTX, None, FSDP),
            P((CTX, FSDP)),
            P((CTX, FSDP)),
        ),
        check_vma=False,
    )
```

```python
import math

import jax
import jax.numpy as jnp
from jax import lax
from jax.experimental import pallas as pl
from jax.experimental.pallas import tpu as pltpu
from jax.sharding import PartitionSpec as P


H = 32
KV = 8
HD = 64

NORM_EPS = 1e-05
ROPE_BASE = 500000.0
FFN_TILE = 512
KEY_CHUNK = 256


BF = jnp.bfloat16
CTX, FSDP = "ctx", "fsdp"
F32 = jnp.float32


def mm(a, b, dims):
    return lax.dot_general(a, b, (dims, ((), ())), preferred_element_type=F32)


def nn(a, b):
    return mm(a, b, ((1,), (0,)))


def nt(a, b):
    return mm(a, b, ((1,), (1,)))


def tn(a, b):
    return mm(a, b, ((0,), (0,)))


def swap(value, axis, offset):
    count = lax.axis_size(axis)
    return lax.ppermute(value, axis, [(i, i ^ offset) for i in range(count)])


def rotate(values, token_places):
    head_dim = values.shape[-1]
    half_dim = head_dim // 2
    frequency = jnp.power(ROPE_BASE, -(jnp.arange(half_dim, dtype=F32) * 2.0 / head_dim))
    angles = token_places.astype(F32)[:, None] * frequency[None, :]
    cosine = jnp.concatenate([jnp.cos(angles), jnp.cos(angles)], axis=-1)[:, None, :]
    sine_part = jnp.concatenate([jnp.sin(angles), jnp.sin(angles)], axis=-1)[:, None, :]
    turned = jnp.concatenate([-values[..., half_dim:], values[..., :half_dim]], axis=-1)
    return values * cosine + turned * sine_part


def norm_scale(values):
    return lax.rsqrt(jnp.mean(values * values, axis=-1, keepdims=True) + NORM_EPS)


def lookup(entries, row_ids):
    matches = row_ids[:, None] == jnp.arange(entries.shape[0], dtype=jnp.int32)[None, :]
    return jnp.sum(jnp.where(matches, entries[None, :], 0), axis=1)


def anchors_of(block_order, owner, row_count):
    block_len = row_count // 2
    row_ids = owner * row_count + jnp.arange(row_count, dtype=jnp.int32)
    return lookup(block_order, row_ids // block_len) * block_len + row_ids % block_len


def after(value, *earlier):
    return lax.optimization_barrier((value, earlier))[0]


def ids():
    return lax.axis_index(CTX), lax.axis_index(FSDP)


def gather_pieces(weight, early):
    rows, columns = weight.shape
    share = columns // lax.axis_size(CTX)
    half = rows // 2
    mine = lax.dynamic_slice(weight, (0, lax.axis_index(CTX) * share), (rows, share))
    planes = {}
    planes[3] = swap(mine, FSDP, 3)
    planes[1] = swap(mine, FSDP, 1)
    planes[2] = swap(after(planes[3], early), FSDP, 1)
    pieces = []
    for away in (1, 3, 2):
        first = planes[away]
        along_x, along_y = swap(first, CTX, 2), swap(first, CTX, 4)
        if away == 1:
            corners = [(6, 0, swap(along_y, CTX, 2))]
        elif away == 3:
            corners = [(6, 0, swap(along_x, CTX, 4))]
        else:
            top, low = swap(along_y[:half], CTX, 2), swap(along_x[half:], CTX, 4)
            corners = [(6, 0, jnp.concatenate([top, low], axis=0))]
        parts = [(0, 0, first), (2, 0, along_x), (4, 0, along_y)] + corners
        for offset, start, part in parts:
            pieces.append((away, offset, start, part))
            pieces.append((away, offset + 1, start, swap(part, CTX, 1)))
    return pieces, (planes[2], pieces[-2][3])


def pieces_kernel(places, rows_in, share, ids_ref, x_ref, own_ref, *refs):
    count = len(places)
    piece_refs, refs = refs[:count], refs[count:]
    cos_ref, sin_ref, q_ref, pair_ref, full_ref, y_ref, buf, in_sems, out_sems = refs
    me, plane = ids_ref[0], ids_ref[1]

    def block(away):
        return pl.ds(pl.multiple_of((plane ^ away) * rows_in, 128), rows_in)

    own_copy = pltpu.make_async_copy(own_ref, buf.at[block(0)], in_sems.at[count])
    own_copy.start()
    copies = []
    for i, (away, offset, start, height) in enumerate(places):
        at = pl.ds(pl.multiple_of((plane ^ away) * rows_in + start, 128), height)
        columns = pl.ds(pl.multiple_of((me ^ offset) * share, 128), share)
        copies.append(pltpu.make_async_copy(piece_refs[i], buf.at[at, columns], in_sems.at[i]))
        copies[-1].start()
    outs = []
    order = [0] + list(dict.fromkeys(away for away, _, _, _ in places))
    for away in order:
        if away:
            for copy, place in zip(copies, places):
                if place[0] == away:
                    copy.wait()
        else:
            own_copy.wait()
        outs.append(
            pltpu.make_async_copy(buf.at[block(away)], full_ref.at[block(away)], out_sems.at[away])
        )
        outs[-1].start()
        part = nn(x_ref[:, block(away)], buf[block(away)])
        y_ref[...] = part if away == 0 else y_ref[...] + part
    cosine, sine = cos_ref[...], sin_ref[...]
    queries, keys = H * HD, KV * HD
    for start in range(0, queries + keys, 128):
        tile = turn(y_ref[:, start : start + 128], cosine, sine)
        if start < queries:
            q_ref[:, start : start + 128] = (tile * (1.0 / math.sqrt(HD))).astype(BF)
        else:
            pair_ref[:, start - queries : start - queries + 128] = tile.astype(BF)
    pair_ref[:, keys:] = y_ref[:, queries + keys :].astype(BF)
    for copy in outs:
        copy.wait()


def pieces_forward(x, own, pieces, cosine, sine):
    me, plane = ids()
    rows_in, columns = own.shape
    rows, width = x.shape
    share = columns // lax.axis_size(CTX)
    places = tuple((away, offset, start, part.shape[0]) for away, offset, start, part in pieces)
    arrays = [part for _, _, _, part in pieces]
    hbm, vmem = pl.BlockSpec(memory_space=pltpu.HBM), pl.BlockSpec(memory_space=pltpu.VMEM)
    return pl.pallas_call(
        lambda *refs: pieces_kernel(places, rows_in, share, *refs),
        out_shape=(
            jax.ShapeDtypeStruct((rows, H * HD), BF),
            jax.ShapeDtypeStruct((rows, 2 * KV * HD), BF),
            pltpu.HBM((width, columns), BF),
        ),
        in_specs=[pl.BlockSpec(memory_space=pltpu.SMEM), vmem, hbm]
        + [hbm] * len(arrays)
        + [vmem, vmem],
        out_specs=(vmem, vmem, hbm),
        scratch_shapes=[
            pltpu.VMEM((rows, columns), F32),
            pltpu.VMEM((width, columns), BF),
            pltpu.SemaphoreType.DMA((len(arrays) + 1,)),
            pltpu.SemaphoreType.DMA((width // rows_in,)),
        ],
        compiler_params=pltpu.CompilerParams(vmem_limit_bytes=32 << 20),
        cost_estimate=pl.CostEstimate(
            flops=2 * rows * width * columns, bytes_accessed=4 * width * columns, transcendentals=0
        ),
        name="pieces",
    )(jnp.stack([me, plane]), x, in_hbm(own), *[in_hbm(part) for part in arrays], cosine, sine)


def gather_blocks(weight, before_fsdp, before_ctx):
    rows, columns = weight.shape
    me, plane = ids()
    share = columns // lax.axis_size(CTX)
    mine = lax.dynamic_slice(weight, (0, me * share), (rows, share))
    planes = lax.all_gather(after(mine, before_fsdp), FSDP)
    others = jnp.stack(
        [
            lax.dynamic_index_in_dim(planes, plane ^ away, 0, keepdims=False)
            for away in range(1, planes.shape[0])
        ]
    )
    return lax.all_gather(after(others, before_ctx), CTX)


def whole_of(own, blocks):
    ctx_count, others, rows, share = blocks.shape
    plane = lax.axis_index(FSDP)
    columns = ctx_count * share
    full = jnp.zeros(((others + 1) * rows, columns), own.dtype)
    full = lax.dynamic_update_slice(full, own, (plane * rows, 0))
    for away in range(1, others + 1):
        part = blocks[:, away - 1].transpose(1, 0, 2).reshape(rows, columns)
        full = lax.dynamic_update_slice(full, part, ((plane ^ away) * rows, 0))
    return full


def in_hbm(value):
    return pltpu.with_memory_space_constraint(value, pltpu.HBM)


def out_kernel(back, ids_ref, x_ref, own_ref, blocks_ref, *refs):
    hidden_ref, gain_ref = (None, None) if back else refs[:2]
    outs = refs if back else refs[2:]
    own_buf, buf, sems = outs[-3:]
    ctx_count, others, rows, share = buf.shape
    plane = ids_ref[1]

    def block_copy(c):
        return pltpu.make_async_copy(blocks_ref.at[c], buf.at[c], sems.at[c])

    own_copy = pltpu.make_async_copy(own_ref, own_buf, sems.at[ctx_count])
    own_copy.start()
    for c in range(ctx_count):
        block_copy(c).start()

    def features(away):
        return pl.ds(pl.multiple_of((plane ^ away) * rows, 128), rows)

    def columns(c):
        return pl.ds(pl.multiple_of(c * share, 128), share)

    own_copy.wait()
    if back:
        y_ref = outs[0]

        @pl.loop(0, ctx_count)
        def _(c):
            block_copy(c).wait()
            total = nn(x_ref[:, features(0)], own_buf[:, columns(c)])
            for away in range(1, others + 1):
                total += nn(x_ref[:, features(away)], buf[c, away - 1])
            y_ref[:, columns(c)] = total.astype(BF)

        return
    residual_ref, normed_ref = outs[:2]
    residual_ref[...] = hidden_ref[...].astype(F32)

    @pl.loop(0, ctx_count)
    def _(c):
        block_copy(c).wait()
        x = x_ref[:, columns(c)]
        residual_ref[:, features(0)] += nt(x, own_buf[:, columns(c)])
        for away in range(1, others + 1):
            residual_ref[:, features(away)] += nt(x, buf[c, away - 1])

    residual = residual_ref[...]
    normed_ref[...] = (residual * norm_scale(residual) * gain_ref[...]).astype(BF)


def out_call(back, x, own, blocks, extra, out_shape):
    vmem, hbm = pl.BlockSpec(memory_space=pltpu.VMEM), pl.BlockSpec(memory_space=pltpu.HBM)
    return pl.pallas_call(
        lambda *refs: out_kernel(back, *refs),
        out_shape=out_shape,
        in_specs=[pl.BlockSpec(memory_space=pltpu.SMEM), vmem, hbm, hbm] + [vmem] * len(extra),
        out_specs=jax.tree.map(lambda _: vmem, out_shape),
        scratch_shapes=[
            pltpu.VMEM(own.shape, own.dtype),
            pltpu.VMEM(blocks.shape, blocks.dtype),
            pltpu.SemaphoreType.DMA((blocks.shape[0] + 1,)),
        ],
        compiler_params=pltpu.CompilerParams(vmem_limit_bytes=24 << 20),
        cost_estimate=pl.CostEstimate(
            flops=2 * x.shape[0] * own.size * (blocks.shape[1] + 1),
            bytes_accessed=2 * own.size * (blocks.shape[1] + 1),
            transcendentals=0,
        ),
        name="out_b" if back else "out_f",
    )(jnp.stack(ids()), x, in_hbm(own), in_hbm(blocks), *extra)


def out_forward(attn_rows, own, blocks, hidden, gain):
    if blocks.shape[3] % 128:
        residual = hidden.astype(F32) + nt(attn_rows, whole_of(own, blocks))
        return residual, (residual * norm_scale(residual) * gain).astype(BF)
    out_shape = (
        jax.ShapeDtypeStruct(hidden.shape, F32),
        jax.ShapeDtypeStruct(hidden.shape, BF),
    )
    return out_call(False, attn_rows, own, blocks, [hidden, gain[None]], out_shape)


def out_back(x, own, blocks):
    if blocks.shape[3] % 128:
        return nn(x, whole_of(own, blocks)).astype(BF)
    out_shape = jax.ShapeDtypeStruct((x.shape[0], own.shape[1]), BF)
    return out_call(True, x, own, blocks, [], out_shape)


def one_back_kernel(
    query_ref, pair_ref, w_ref, hidden_ref, gain_ref, residual_ref, y_ref
):
    step = pl.program_id(0)
    rows = w_ref.shape[0]
    split = query_ref.shape[1]
    y_ref[:, pl.ds(pl.multiple_of(step * rows, 128), rows)] = nt(
        query_ref[...], w_ref[:, :split]
    ) + nt(pair_ref[...], w_ref[:, split:])

    @pl.when(step == pl.num_programs(0) - 1)
    def _():
        grad = y_ref[...]
        inputs = hidden_ref[...].astype(F32)
        scale = norm_scale(inputs)
        unit = inputs * scale
        scaled = gain_ref[...] * grad
        y_ref[...] = residual_ref[...] + scale * (
            scaled - unit * jnp.mean(scaled * unit, axis=-1, keepdims=True)
        )


def one_back(query_part, pair_part, weight, hidden, gain, residual_grad):
    rows, width = hidden.shape
    columns = weight.shape[1]
    tile = FFN_TILE

    def whole(array):
        return pl.BlockSpec(array.shape, lambda j: (0, 0))

    gain = gain[None]
    return pl.pallas_call(
        one_back_kernel,
        grid=(width // tile,),
        out_shape=jax.ShapeDtypeStruct((rows, width), F32),
        in_specs=[
            whole(query_part),
            pl.BlockSpec((rows, pair_part.shape[1]), lambda j: (0, 0)),
            pl.BlockSpec((tile, columns), lambda j: (j, 0)),
            whole(hidden),
            whole(gain),
            whole(residual_grad),
        ],
        out_specs=pl.BlockSpec((rows, width), lambda j: (0, 0)),
        compiler_params=pltpu.CompilerParams(vmem_limit_bytes=24 << 20),
        cost_estimate=pl.CostEstimate(
            flops=2 * rows * width * columns,
            bytes_accessed=2 * width * columns,
            transcendentals=0,
        ),
        name="one_b",
    )(query_part, pair_part, in_hbm(weight), hidden, gain, residual_grad)


def send_rows(values):
    if lax.axis_size(FSDP) != 4:
        return fetch_rows(values)
    third = swap(values, FSDP, 3)
    return [values, swap(values, FSDP, 1), third]


def relay_rows(planes):
    if lax.axis_size(FSDP) != 4:
        return planes
    values, first, third = planes
    return [values, first, swap(third, FSDP, 1), third]


def pass_rows(values):
    return relay_rows(send_rows(values))


def fetch_rows(values):
    count = lax.axis_size(FSDP)
    return [values] + [swap(values, FSDP, away) for away in range(1, count)]


def sum_rows(parts, forward):
    count = len(parts)
    if count == 4 and forward:
        passed = swap(parts[2], FSDP, 1).astype(F32)
        one = swap(parts[1], FSDP, 1)
        third = swap((parts[3].astype(F32) + passed).astype(BF), FSDP, 3)
        return [parts[0], one, third]
    return parts[:1] + [swap(parts[i], FSDP, i) for i in range(1, count)]


def by_feature(values):
    rows, width = values.shape
    ctx_count, fsdp_count = lax.axis_size(CTX), lax.axis_size(FSDP)
    blocks = values.reshape(rows, ctx_count, fsdp_count, width // (ctx_count * fsdp_count))
    return blocks.transpose(0, 2, 1, 3).reshape(rows, width)


def sum_over_ctx(part_for):
    pairs = lax.axis_size(CTX) // 2
    sent = jnp.stack([part_for(2 * pair + 1).astype(BF) for pair in range(pairs)])
    got = swap(sent, CTX, 1)
    sums = [part_for(2 * pair).astype(F32) + got[pair].astype(F32) for pair in range(pairs)]
    total = sums[0]
    for pair in range(1, pairs):
        total = total + swap(sums[pair].astype(BF), CTX, 2 * pair).astype(F32)
    return total


def ctx_rows_sum(values):
    height = values.shape[0] // lax.axis_size(CTX)
    me = lax.axis_index(CTX)

    def part(offset):
        return lax.dynamic_slice(
            values, ((me ^ offset) * height, 0), (height, values.shape[1])
        )

    return sum_over_ctx(part)


def key_offsets():
    count = lax.axis_size(CTX)
    return list(range(0, count, 2)) + list(range(1, count, 2))


def gather_keys(piece):
    same = [piece] + [swap(piece, CTX, far) for far in range(2, lax.axis_size(CTX), 2)]
    mine = jnp.concatenate(same, axis=0)
    return mine, swap(mine, CTX, 1)


def sum_pairs(kept, sent, cosine, sine):
    _, count, width = kept.shape
    pairs = lax.axis_size(CTX) // 2
    got = swap(sent, CTX, 1)
    sums = (kept.astype(F32) + got.astype(F32)).reshape(2, pairs, count // pairs, width)
    far = [swap(sums[:, pair].astype(BF), CTX, 2 * pair) for pair in range(1, pairs)]
    return pair_turn(sums[:, 0], far, cosine, sine), got


def half_mask(shape):
    return lax.broadcasted_iota(jnp.int32, shape, len(shape) - 1) % 128 < HD


def turn(values, cosine, sine):
    lanes = lax.broadcasted_iota(jnp.int32, values.shape, 1) % HD
    turned = jnp.where(
        lanes < HD // 2, pltpu.roll(values, 128 - HD // 2, 1), pltpu.roll(values, HD // 2, 1)
    )
    return values * cosine + turned * sine


def doubled(tile, odd):
    wide = tile.astype(F32)
    other = pltpu.roll(wide, HD, 1)
    return jnp.where(half_mask(tile.shape) == (odd == 0), wide, other).astype(BF)


def split_heads(tile_pair):
    zero = jnp.zeros((), tile_pair.dtype)
    parts = []
    for j in range(2):
        tile = tile_pair[:, j * 128 : (j + 1) * 128]
        mask = half_mask(tile.shape)
        parts += [jnp.where(mask, tile, zero), jnp.where(mask, zero, tile)]
    return jnp.concatenate(parts, axis=0)


def merge_heads(stacked):
    rows = stacked.shape[0] // 4
    tiles = []
    for j in range(2):
        even = stacked[2 * j * rows : (2 * j + 1) * rows]
        odd = stacked[(2 * j + 1) * rows : (2 * j + 2) * rows]
        tiles.append(jnp.where(half_mask(even.shape), even, odd))
    return jnp.concatenate(tiles, axis=1)


def key_chunks(refs, chunk):
    first = 0
    for k_ref, v_ref in refs:
        for start in range(0, k_ref.shape[0], chunk):
            at = slice(start, start + chunk)
            yield first + start, k_ref.at[at, :], v_ref.at[at, :]
        first += k_ref.shape[0]


def masked_scores(keys, queries, key_ref, own_ref, start):
    allowed = key_ref[start : start + keys.shape[0], :1] <= own_ref[...]
    bias = jnp.where(allowed, 0.0, -1e30).astype(F32)
    return nt(keys, queries) + jnp.concatenate([bias] * 4, axis=1)


def attend_kernel(
    chunk, q_ref, ka_ref, va_ref, kb_ref, vb_ref, key_ref, own_ref, rows_ref, attended_ref, log_ref
):
    odd = pl.program_id(0) % 2
    rows = q_ref.shape[0]
    queries = split_heads(q_ref[...])
    parts = list(key_chunks(((ka_ref, va_ref), (kb_ref, vb_ref)), chunk))
    scores = [
        masked_scores(doubled(k_ref[...], odd), queries, key_ref, own_ref, start)
        for start, k_ref, _ in parts
    ]
    top = jnp.max(scores[0], axis=0, keepdims=True)
    for score in scores[1:]:
        top = jnp.maximum(top, jnp.max(score, axis=0, keepdims=True))
    total = jnp.zeros_like(top)
    summed = jnp.zeros((4 * rows, 128), F32)
    for score, (_, _, v_ref) in zip(scores, parts):
        weights = jnp.exp(score - top)
        total += jnp.sum(weights, axis=0, keepdims=True)
        summed += tn(weights.astype(BF), doubled(v_ref[...], odd))
    log_ref[0] = top + jnp.log(total)
    attended = merge_heads(summed / jnp.transpose(jnp.broadcast_to(total, (128, 4 * rows))))
    attended_ref[...] = attended
    rows_ref[...] = attended.astype(BF)


def key_specs(parts):
    tiles = parts[0].shape[1] // 256
    specs, arrays = [], []
    for part in parts:
        specs.append(pl.BlockSpec((part.shape[0], 128), lambda g: (0, g // 2)))
        specs.append(pl.BlockSpec((part.shape[0], 128), lambda g: (0, tiles + g // 2)))
        arrays += [part, part]
    return specs, arrays


def attend(queries, keys_values, key_anchor, own_anchor):
    rows, width = queries.shape
    count = key_anchor.shape[0]
    specs, arrays = key_specs(keys_values)
    wide = pl.BlockSpec((rows, 256), lambda g: (0, g))
    return pl.pallas_call(
        lambda *refs: attend_kernel(KEY_CHUNK, *refs),
        grid=(KV,),
        out_shape=(
            jax.ShapeDtypeStruct((rows, width), BF),
            jax.ShapeDtypeStruct((rows, width), F32),
            jax.ShapeDtypeStruct((KV, 1, 4 * rows), F32),
        ),
        in_specs=[wide]
        + specs
        + [
            pl.BlockSpec((count, 128), lambda g: (0, 0)),
            pl.BlockSpec((1, rows), lambda g: (0, 0)),
        ],
        out_specs=(wide, wide, pl.BlockSpec((1, 1, 4 * rows), lambda g: (g, 0, 0))),
        compiler_params=pltpu.CompilerParams(vmem_limit_bytes=48 << 20),
        cost_estimate=pl.CostEstimate(
            flops=4 * rows * width * count,
            bytes_accessed=4 * count * KV * HD,
            transcendentals=rows * H * count,
        ),
        name="attend",
    )(queries, *arrays, key_anchor, own_anchor)


def attend_back_kernel(
    chunk, q_ref, grad_ref, attended_ref, ka_ref, va_ref, kb_ref, vb_ref, key_ref, own_ref, log_ref,
    cos_ref, sin_ref, dq_ref, kept_ref, sent_ref,
):
    odd = pl.program_id(0) % 2
    rows = q_ref.shape[0]
    half = ka_ref.shape[0]
    queries, grads = split_heads(q_ref[...]), split_heads(grad_ref[...])
    product = grads.astype(F32) * split_heads(attended_ref[...])
    delta = jnp.sum(jnp.transpose(product), axis=0, keepdims=True)
    log_total = log_ref[0]
    total = jnp.zeros((4 * rows, 128), F32)
    keep = half_mask((chunk, 128)) == (odd == 0)
    for start, k_ref, v_ref in key_chunks(((ka_ref, va_ref), (kb_ref, vb_ref)), chunk):
        keys, values = doubled(k_ref[...], odd), doubled(v_ref[...], odd)
        scores = masked_scores(keys, queries, key_ref, own_ref, start)
        probs = jnp.exp(scores - log_total)
        value_grad = nn(probs.astype(BF), grads)
        score_grad = (probs * (nt(values, grads) - delta)).astype(BF)
        key_grad = nn(score_grad, queries)
        total += tn(score_grad, keys)
        out_ref = kept_ref if start < half else sent_ref
        at = slice(start % half, start % half + chunk)
        for part, value in enumerate((key_grad, value_grad)):
            value = (value + pltpu.roll(value, HD, 1)).astype(BF)
            out_ref[part, at, :] = jnp.where(keep, value, out_ref[part, at, :])
    merged = merge_heads(total) * (1.0 / math.sqrt(HD))
    cosine, sine = cos_ref[...], sin_ref[...]
    for j in range(2):
        tile = slice(j * 128, (j + 1) * 128)
        dq_ref[:, tile] = turn(merged[:, tile], cosine, -sine).astype(BF)


def attend_back(queries, grads, attended, keys_values, key_anchor, own_anchor, logs, cosine, sine):
    rows, width = queries.shape
    count = key_anchor.shape[0]
    specs, arrays = key_specs(keys_values)
    wide = pl.BlockSpec((rows, 256), lambda g: (0, g))
    small = pl.BlockSpec((rows, 128), lambda g: (0, 0))
    pair = pl.BlockSpec((2, count // 2, 128), lambda g: (0, 0, g // 2))
    return pl.pallas_call(
        lambda *refs: attend_back_kernel(KEY_CHUNK, *refs),
        grid=(KV,),
        out_shape=(
            jax.ShapeDtypeStruct((rows, width), BF),
            jax.ShapeDtypeStruct((2, count // 2, KV * HD), BF),
            jax.ShapeDtypeStruct((2, count // 2, KV * HD), BF),
        ),
        in_specs=[wide, wide, wide]
        + specs
        + [
            pl.BlockSpec((count, 128), lambda g: (0, 0)),
            pl.BlockSpec((1, rows), lambda g: (0, 0)),
            pl.BlockSpec((1, 1, 4 * rows), lambda g: (g, 0, 0)),
            small,
            small,
        ],
        out_specs=(wide, pair, pair),
        compiler_params=pltpu.CompilerParams(vmem_limit_bytes=48 << 20),
        cost_estimate=pl.CostEstimate(
            flops=10 * rows * width * count,
            bytes_accessed=8 * count * KV * HD,
            transcendentals=rows * H * count,
        ),
        name="att_b",
    )(queries, grads, attended, *arrays, key_anchor, own_anchor, logs, cosine, sine)


def pair_turn_kernel(copies, own_ref, *refs):
    got, (cos_ref, sin_ref, y_ref) = refs[:-3], refs[-3:]
    total = own_ref[...]
    for ref in got:
        total = total + ref[...].astype(F32)
    cosine, sine = cos_ref[...], sin_ref[...]
    _, rows, width = total.shape
    tiles = [
        turn(total[0, :, start : start + 128], cosine, -sine).astype(BF)
        for start in range(0, width, 128)
    ]
    values = total[1].astype(BF)
    for copy in range(copies):
        at = slice(copy * rows, (copy + 1) * rows)
        for i, tile in enumerate(tiles):
            y_ref[at, i * 128 : (i + 1) * 128] = tile
        y_ref[at, width:] = values


def pair_turn(own, got, cosine, sine):
    _, rows, width = own.shape
    copies = lax.axis_size(FSDP)
    return pl.pallas_call(
        lambda *refs: pair_turn_kernel(copies, *refs),
        out_shape=jax.ShapeDtypeStruct((copies * rows, 2 * width), BF),
        name="turned",
    )(own, *got, cosine, sine)


def join_rows(x_buf, refs):
    @pl.when((pl.program_id(0) == 0))
    def _():
        rows = refs[0].shape[0]
        for i, ref in enumerate(refs):
            x_buf[i * rows : (i + 1) * rows] = ref[...]


def ffn_kernel(count, earlier, *refs):
    rows_refs, (act_ref, w_ref), refs = refs[:count], refs[count : count + 2], refs[count + 2 :]
    out_ref, refs = refs[earlier], refs[earlier + 1 :]
    sum_refs, (x_buf, sum_buf) = refs[:count], refs[count:]
    join_rows(x_buf, rows_refs)
    step = pl.program_id(0)
    gate_w, up_w = w_ref[0], w_ref[1]
    x = x_buf[...]
    gate, up = nn(x, gate_w), nn(x, up_w)
    act_grad = act_ref[...]
    sig = jax.nn.sigmoid(gate)
    silu = gate * sig
    gate_grad = (act_grad * up * sig * (1.0 + gate * (1.0 - sig))).astype(BF)
    up_grad = (act_grad * silu).astype(BF)
    out_ref[0], out_ref[1], out_ref[2] = gate_grad, up_grad, (silu * up).astype(BF)
    part = nt(gate_grad, gate_w) + nt(up_grad, up_w)

    @pl.when(step == 0)
    def _():
        sum_buf[...] = part

    @pl.when(step > 0)
    def _():
        sum_buf[...] += part

    @pl.when(step == pl.num_programs(0) - 1)
    def _():
        rows = sum_refs[0].shape[0]
        for i, ref in enumerate(sum_refs):
            ref[...] = sum_buf[i * rows : (i + 1) * rows].astype(ref.dtype)


def ffn_middle(blocks, act_grad, half, weights, kinds, earlier):
    width = blocks[0].shape[1]
    rows = blocks[0].shape[0] * len(blocks)
    hidden = weights.shape[2]
    tile = FFN_TILE
    whole = [pl.BlockSpec(block.shape, lambda j: (0, 0)) for block in blocks]
    out = pl.pallas_call(
        lambda *refs: ffn_kernel(len(blocks), len(earlier), *refs),
        grid=(hidden // tile,),
        out_shape=(
            pltpu.HBM((3, 2 * rows, hidden), BF),
            *[jax.ShapeDtypeStruct(block.shape, kind) for block, kind in zip(blocks, kinds)],
        ),
        in_specs=whole
        + [
            pl.BlockSpec((rows, tile), lambda j: (half, j)),
            pl.BlockSpec((2, width, tile), lambda j: (0, 0, j)),
        ]
        + [pl.BlockSpec(memory_space=pltpu.HBM)] * len(earlier),
        out_specs=(pl.BlockSpec((3, rows, tile), lambda j: (0, half, j)), *whole),
        input_output_aliases={len(blocks) + 2: 0} if earlier else {},
        scratch_shapes=[pltpu.VMEM((rows, width), BF), pltpu.VMEM((rows, width), F32)],
        compiler_params=pltpu.CompilerParams(vmem_limit_bytes=40 << 20),
        cost_estimate=pl.CostEstimate(
            flops=8 * rows * width * hidden,
            bytes_accessed=4 * width * hidden,
            transcendentals=rows * hidden,
        ),
        name="ffn",
    )(*blocks, act_grad, weights, *earlier)
    return out[0], list(out[1:])


def products_kernel(count, added, ids_ref, *refs):
    blocks, right, rest = refs[: 2 * count], refs[2 * count], refs[2 * count + 1 :]
    out_ref, left = rest[-2:]
    rows, height = blocks[0].shape
    for j in range(2):
        for i in range(count):
            at = (slice(i * rows, (i + 1) * rows), slice(j * height, (j + 1) * height))
            left[at] = blocks[j * count + i][...]
    part = tn(left[...], right[0])
    if added:
        part = part + rest[0][0].astype(F32)
    out_ref[0] = part.astype(BF)


def half_products(rows_of, parts, first, size, got, earlier):
    count = len(rows_of)
    rows, width = rows_of[0].shape
    matrices, _, hidden = parts.shape
    ctx_count = lax.axis_size(CTX)
    height = width // ctx_count
    kept = got is not None

    def left(j):
        def place(k, i, ids_ref):
            own = ids_ref[0] % 2
            return (0, 2 * (2 * i + j) + (own if kept else 1 - own))

        return pl.BlockSpec((rows, height), place)

    def out(start):
        return pl.BlockSpec((1, 2 * height, hidden), lambda k, i, ids_ref: (start + k, i, 0))

    right = pl.BlockSpec((1, rows * count, hidden), lambda k, i, ids_ref: (first + k, 0, 0))
    extra = ([got] if kept else []) + earlier
    operands = 2 * count + 1 + len(extra)
    return pl.pallas_call(
        lambda *refs: products_kernel(count, kept, *refs),
        grid_spec=pltpu.PrefetchScalarGridSpec(
            num_scalar_prefetch=1,
            grid=(size, ctx_count // 4),
            in_specs=[left(0)] * count
            + [left(1)] * count
            + [right]
            + [out(0)] * kept
            + [pl.BlockSpec(memory_space=pltpu.HBM)] * len(earlier),
            out_specs=out(first if kept else 0),
            scratch_shapes=[pltpu.VMEM((count * rows, 2 * height), BF)],
        ),
        out_shape=pltpu.HBM((matrices if kept else size, width // 2, hidden), BF),
        input_output_aliases={operands: 0} if earlier else {},
        compiler_params=pltpu.CompilerParams(vmem_limit_bytes=24 << 20),
        cost_estimate=pl.CostEstimate(
            flops=size * count * rows * width * hidden,
            bytes_accessed=size * width * hidden,
            transcendentals=0,
        ),
    )(jnp.stack(ids()), *rows_of, *rows_of, in_hbm(parts), *extra)


def ffn_gradient(rows_in, rows_out, parts):
    count = lax.axis_size(CTX)
    if count % 4 or (rows_in[0].shape[1] // count) % 128:
        left, grad = (jnp.concatenate(rows, axis=0) for rows in (rows_in, rows_out))
        products = [tn(left, parts[0]), tn(left, parts[1]), tn(grad, parts[2])]
        products = jnp.stack(products, axis=1).astype(BF)
        return lax.psum_scatter(products, CTX, scatter_dimension=0, tiled=True), parts
    calls = ((rows_out, 2, 1), (rows_in, 0, 2))
    got = []
    for rows_of, first, size in calls:
        sent = half_products(rows_of, parts, first, size, None, [])
        got.append(swap(sent, CTX, 1))
    kept = []
    for (rows_of, first, size), part in zip(calls, got):
        kept = [half_products(rows_of, parts, first, size, part, kept)]
    groups = [list(range(core, count, 2)) for core in range(2)]
    kept = kept[0].transpose(1, 0, 2)
    rows = lax.psum_scatter(kept, CTX, scatter_dimension=0, tiled=True, axis_index_groups=groups)
    return rows, after(parts, kept)


def widen_kernel(x_ref, y_ref):
    y_ref[...] = x_ref[...].astype(F32)


def widened(values, fast):
    if not fast:
        return values.astype(F32)
    values = values.transpose(1, 0, 2)
    matrices, rows, hidden = values.shape
    block = pl.BlockSpec((1, rows // 4, hidden), lambda k, i: (k, i, 0))
    return pl.pallas_call(
        widen_kernel,
        grid=(matrices, 4),
        out_shape=jax.ShapeDtypeStruct(values.shape, F32),
        in_specs=[block],
        out_specs=block,
        compiler_params=pltpu.CompilerParams(vmem_limit_bytes=16 << 20),
        name="wide",
    )(in_hbm(values)).transpose(1, 0, 2)


def down_back_kernel(count, *refs):
    rows_refs, (w_ref, y_ref, x_buf) = refs[:count], refs[count:]
    join_rows(x_buf, rows_refs)
    y_ref[...] = nn(x_buf[...], w_ref[0])


def down_back(blocks, weights):
    width = blocks[0].shape[1]
    rows = blocks[0].shape[0] * len(blocks)
    hidden = weights.shape[2]
    tile = FFN_TILE
    return pl.pallas_call(
        lambda *refs: down_back_kernel(len(blocks), *refs),
        grid=(hidden // tile,),
        out_shape=pltpu.HBM((rows, hidden), F32),
        in_specs=[pl.BlockSpec(block.shape, lambda j: (0, 0)) for block in blocks]
        + [pl.BlockSpec((1, width, tile), lambda j: (2, 0, j))],
        out_specs=pl.BlockSpec((rows, tile), lambda j: (0, j)),
        scratch_shapes=[pltpu.VMEM((rows, width), BF)],
        compiler_params=pltpu.CompilerParams(vmem_limit_bytes=24 << 20),
        cost_estimate=pl.CostEstimate(
            flops=2 * rows * width * hidden,
            bytes_accessed=2 * width * hidden,
            transcendentals=0,
        ),
        name="act",
    )(*blocks, weights)


def down_kernel(x_ref, w_ref, *y_refs):
    rows = x_ref.shape[1] // len(y_refs)
    total = nt(x_ref[0], w_ref[0])
    for i, y_ref in enumerate(y_refs):
        y_ref[...] = total[i * rows : (i + 1) * rows].astype(y_ref.dtype)


def down_forward(parts, weights, count):
    _, rows, hidden = parts.shape
    width = weights.shape[1]
    tile = FFN_TILE
    height = rows // count
    return pl.pallas_call(
        down_kernel,
        grid=(width // tile,),
        out_shape=tuple(
            jax.ShapeDtypeStruct((height, width), BF if i else F32) for i in range(count)
        ),
        in_specs=[
            pl.BlockSpec((1, rows, hidden), lambda j: (2, 0, 0)),
            pl.BlockSpec((1, tile, hidden), lambda j: (2, j, 0)),
        ],
        out_specs=tuple(pl.BlockSpec((height, tile), lambda j: (0, j)) for _ in range(count)),
        compiler_params=pltpu.CompilerParams(vmem_limit_bytes=24 << 20),
        cost_estimate=pl.CostEstimate(
            flops=2 * rows * width * hidden,
            bytes_accessed=2 * width * hidden,
            transcendentals=0,
        ),
        name="down",
    )(in_hbm(parts), weights)


def share_kernel(count, sizes, ids_ref, *refs):
    products = len(sizes)
    lefts = [refs[i * count : (i + 1) * count] for i in range(products)]
    rest = refs[products * count :]
    rights = []
    for size in sizes:
        rights.append(rest[:size])
        rest = rest[size:]
    bufs = rest[len(rest) - products :]
    terms, (kept_ref, sent_ref) = rest[: -products - 2], rest[-products - 2 : -products]
    half = kept_ref.shape[1]
    own = ids_ref[0] % 2 == 0

    @pl.when(pl.program_id(0) == 0)
    def _():
        for parts, buf in zip(rights, bufs):
            rows = buf.shape[0] // count
            for away in range(count):
                if len(parts) > 1:
                    block = parts[away][...]
                else:
                    start = (ids_ref[1] ^ away) * rows
                    block = parts[0][pl.ds(pl.multiple_of(start, 16), rows), :]
                buf[away * rows : (away + 1) * rows] = block

    def emit(part, column):
        at = slice(column, column + part.shape[1])
        kept_ref[0, :, at] = jnp.where(own, part[:half], part[half:])
        sent_ref[0, :, at] = jnp.where(own, part[half:], part[:half])

    column = 0
    for left, buf in zip(lefts, bufs):
        joined = jnp.concatenate([ref[...] for ref in left], axis=0)
        emit(tn(joined, buf[...]).astype(BF), column)
        column += buf.shape[1]
    for term in terms:
        tall = jnp.broadcast_to(term[...], (128, term.shape[1]))
        emit(jnp.transpose(tall).astype(BF), column)
        column += 128


def share_products(lefts, rights, terms):
    ctx_count = lax.axis_size(CTX)
    pairs = ctx_count // 2
    count = len(lefts[0])
    rows, width = lefts[0][0].shape
    height = width // ctx_count
    groups = [right if isinstance(right, list) else [right] for right in rights]
    widths = [group[0].shape[1] for group in groups]
    columns = sum(widths) + 128 * len(terms)

    def place(j, ids_ref):
        return (0, (ids_ref[0] // 2) ^ j)

    def whole(array):
        return pl.BlockSpec(array.shape, lambda j, ids_ref: (0, 0))

    shape = jax.ShapeDtypeStruct((pairs, height, columns), BF)
    out = pl.BlockSpec((1, height, columns), lambda j, ids_ref: (j, 0, 0))
    flat_lefts = [block for left in lefts for block in left]
    flat_rights = [block for group in groups for block in group]
    return pl.pallas_call(
        lambda *refs: share_kernel(count, [len(group) for group in groups], *refs),
        grid_spec=pltpu.PrefetchScalarGridSpec(
            num_scalar_prefetch=1,
            grid=(pairs,),
            in_specs=[pl.BlockSpec((rows, 2 * height), place) for _ in flat_lefts]
            + [whole(block) for block in flat_rights]
            + [pl.BlockSpec((1, 2 * height), place) for _ in terms],
            out_specs=(out, out),
            scratch_shapes=[pltpu.VMEM((count * rows, size), BF) for size in widths],
        ),
        out_shape=(shape, shape),
        compiler_params=pltpu.CompilerParams(vmem_limit_bytes=32 << 20),
        cost_estimate=pl.CostEstimate(
            flops=2 * count * rows * width * columns,
            bytes_accessed=2 * (count * rows + columns) * width,
            transcendentals=0,
        ),
        name="share_t" if terms else "share",
    )(jnp.stack(ids()), *flat_lefts, *flat_rights, *[term[None] for term in terms])


def in_fsdp_order(value):
    if not isinstance(value, list):
        return value
    plane = lax.axis_index(FSDP)
    stacked = jnp.stack(value)
    parts = [
        lax.dynamic_index_in_dim(stacked, plane ^ away, 0, keepdims=False)
        for away in range(len(value))
    ]
    return jnp.concatenate(parts, axis=0)


def share_start(lefts, rights, terms):
    pairs = lax.axis_size(CTX) // 2
    if (lefts[0][0].shape[1] // pairs) % 128:
        values = [tn(in_fsdp_order(a), in_fsdp_order(b)) for a, b in zip(lefts, rights)]
        values += [jnp.broadcast_to(term[:, None], (term.shape[0], 128)) for term in terms]
        return [ctx_rows_sum(jnp.concatenate(values, axis=1))]
    kept, sent = share_products(lefts, rights, terms)
    got = swap(sent, CTX, 1)
    parts = [kept[0], got[0]]
    for pair in range(1, pairs):
        part = (kept[pair].astype(F32) + got[pair].astype(F32)).astype(BF)
        parts.append(swap(part, CTX, 2 * pair))
    return parts


def finish_kernel(w_ref, gain_ref, *refs):
    parts, (grad_ref, gain_grad_ref, term_ref) = refs[:-3], refs[-3:]
    columns = grad_ref.shape[1]
    total = parts[0][...].astype(F32)
    for part in parts[1:]:
        total = total + part[...].astype(F32)
    grad = total[:, :columns]
    grad_ref[...] = grad
    row_sum = jnp.sum(w_ref[...].astype(F32) * grad, axis=1, keepdims=True)
    gain_grad_ref[...] = row_sum / gain_ref[...]
    term_ref[...] = total[:, columns:]


def finish_last(parts, weight_rows, gain_rows):
    rows, columns = weight_rows.shape
    wide = jax.ShapeDtypeStruct((rows, 128), F32)
    gains = jnp.broadcast_to(gain_rows[:, None], (rows, 128))
    return pl.pallas_call(
        finish_kernel,
        out_shape=(jax.ShapeDtypeStruct((rows, columns), F32), wide, wide),
        compiler_params=pltpu.CompilerParams(vmem_limit_bytes=16 << 20),
        name="finish",
    )(weight_rows, gains, *parts)


def share_finish(parts):
    total = parts[0].astype(F32)
    for part in parts[1:]:
        total = total + part.astype(F32)
    return total


def own_rows_of(values, height):
    index = lax.axis_index(CTX) * lax.axis_size(FSDP) + lax.axis_index(FSDP)
    return lax.dynamic_slice_in_dim(values, index * height, height, 0)


def feature_parts(values):
    count, plane = lax.axis_size(FSDP), lax.axis_index(FSDP)
    values = by_feature(values)
    rows, width = values.shape
    width //= count
    return [
        lax.dynamic_slice(values, (0, (plane ^ away) * width), (rows, width))
        for away in range(count)
    ]


def feature_rows(parts):
    return [swap(part, FSDP, away) if away else part for away, part in enumerate(parts)]


def own_features(terms):
    ctx_count, fsdp_count = lax.axis_size(CTX), lax.axis_size(FSDP)
    total = jnp.stack(terms)
    away = 1
    while away < fsdp_count:
        total = total + swap(total, FSDP, away)
        away *= 2
    blocks = total.reshape(len(terms), ctx_count, fsdp_count, -1)
    own = lax.dynamic_index_in_dim(blocks, lax.axis_index(FSDP), 2, keepdims=False)
    own = own.reshape(len(terms), -1)
    return [own[i] for i in range(len(terms))]


def layer(
    hidden_in,
    out_grad,
    positions,
    block_order,
    attn_gain,
    ffn_gain,
    qkv_weight,
    out_weight,
    ffn_weight,
):
    ctx_count, fsdp_count = lax.axis_size(CTX), lax.axis_size(FSDP)
    me, _ = ids()
    rows = hidden_in.shape[1]
    queries_width, kv_width = H * HD, KV * HD
    ffn_parts = in_hbm(ffn_weight.transpose(1, 0, 2))

    frequency = jnp.power(ROPE_BASE, -(jnp.arange(HD // 2, dtype=F32) * 2.0 / HD))
    angles = positions[0].astype(F32)[:, None] * frequency[None, :]
    cosine = jnp.tile(jnp.cos(angles), (1, 4))
    sine = jnp.tile(jnp.concatenate([-jnp.sin(angles), jnp.sin(angles)], axis=1), (1, 2))
    own_anchor = anchors_of(block_order, me, rows)[None]
    key_anchor = jnp.concatenate(
        [anchors_of(block_order, me ^ offset, rows) for offset in key_offsets()]
    )
    key_anchor = jnp.broadcast_to(key_anchor[:, None], (rows * ctx_count, 128))

    inputs = hidden_in[0].astype(F32)
    grad_in = out_grad[0]
    scale_one = norm_scale(inputs)
    normed_one = (inputs * scale_one * attn_gain).astype(BF)

    one_parts = feature_parts(normed_one)
    fast = ctx_count == 8 and (qkv_weight.shape[1] // ctx_count) % 128 == 0
    if fast:
        early = (cosine, sine, own_anchor, key_anchor, one_parts)
        qkv_pieces, marks = gather_pieces(qkv_weight, early)
        out_blocks = gather_blocks(out_weight, *marks)
        queries, pair, qkv_full = pieces_forward(
            normed_one, qkv_weight, qkv_pieces, cosine, sine
        )
    else:
        marks = (normed_one, normed_one)
        out_blocks = gather_blocks(out_weight, *marks)
        qkv_full = whole_of(qkv_weight, gather_blocks(qkv_weight, normed_one, normed_one))
        projected = nn(normed_one, qkv_full)
        turned = rotate(
            projected[:, : queries_width + kv_width].reshape(rows, H + KV, HD), positions[0]
        ).reshape(rows, queries_width + kv_width)
        queries = (turned[:, :queries_width] * (1.0 / math.sqrt(HD))).astype(BF)
        pair = jnp.concatenate(
            [turned[:, queries_width:], projected[:, queries_width + kv_width :]], axis=1
        ).astype(BF)
    own_one = feature_rows(after(one_parts, pair))
    keys_values = gather_keys(pair)
    rows_out = send_rows(after(grad_in, pair))
    attn_rows, attended, logs = attend(queries, keys_values, key_anchor, own_anchor)
    rows_out = relay_rows(after(rows_out, attn_rows))
    residual, normed_two = out_forward(
        attn_rows, out_weight, out_blocks, hidden_in[0], ffn_gain
    )
    scale_two = norm_scale(residual)
    rows_in = pass_rows(normed_two)
    rows_out = after(rows_out, normed_two)
    act_grad = down_back(rows_out, ffn_parts)

    all_attn = pass_rows(after(attn_rows, rows_in[2]))
    parts, partial = [], []
    half = fsdp_count // 2
    passing = 3 if fsdp_count == 4 else 0
    for index in range(2):
        blocks = rows_in[index * half : (index + 1) * half]
        kinds = [F32 if index * half + i in (0, passing) else BF for i in range(half)]
        out, terms = ffn_middle(blocks, in_hbm(act_grad), index, ffn_parts, kinds, parts)
        parts, partial = [out], partial + terms
    parts = parts[0]
    sum_grad = share_finish(sum_rows(partial, True))
    ffn_weight_grad, parts = ffn_gradient(rows_in, rows_out, parts)
    ffn_weight_grad = widened(ffn_weight_grad, fast)
    out_partial = list(down_forward(parts, ffn_parts, fsdp_count))

    unit_two = residual * scale_two
    ffn_gain_term = jnp.sum(sum_grad * unit_two, axis=0)
    scaled_two = ffn_gain * sum_grad
    residual_grad = grad_in.astype(F32) + scale_two * (
        scaled_two - unit_two * jnp.mean(scaled_two * unit_two, axis=-1, keepdims=True)
    )
    residual_bf = residual_grad.astype(BF)
    (ffn_term,) = own_features([ffn_gain_term])
    attn_grad = out_back(residual_bf, out_weight, out_blocks)
    query_part, kept, sent = attend_back(
        queries, attn_grad, attended, keys_values, key_anchor, own_anchor, logs, cosine, sine
    )
    query_planes = pass_rows(query_part)
    pair_copies, near = sum_pairs(kept, sent, cosine, sine)
    own_residual = feature_rows(feature_parts(after(residual_bf, near)))
    all_pair = lax.all_to_all(pair_copies, FSDP, split_axis=0, concat_axis=0, tiled=True)
    input_grad = one_back(
        query_part, pair_copies, qkv_full, hidden_in[0], attn_gain, residual_grad
    )
    out_sums = share_start([own_residual], [after(all_attn, input_grad)], [])
    out_sum = sum_rows([after(part, input_grad) for part in out_partial], False)
    qkv_sums = share_start(
        [own_one, own_one], [after(query_planes, (input_grad, ffn_term)), all_pair], [ffn_term]
    )
    own_rows = qkv_weight.shape[0] // ctx_count
    qkv_grad, gain_grad, term_grad = finish_last(
        qkv_sums, own_rows_of(qkv_full, own_rows), own_rows_of(attn_gain, own_rows)
    )
    out_weight_grad = share_finish(out_sums)
    output = (residual + share_finish(after(out_sum, out_weight_grad))).astype(BF)
    return (
        output[None],
        input_grad[None],
        qkv_grad,
        out_weight_grad,
        ffn_weight_grad,
        gain_grad[:, 0],
        term_grad[:, 0],
    )


def solution(mesh):
    step = sharded(mesh)
    return step


def sharded(mesh):
    return jax.shard_map(
        layer,
        mesh=mesh,
        in_specs=(
            P(FSDP, CTX, None),
            P(FSDP, CTX, None),
            P(FSDP, CTX),
            P(),
            P(),
            P(),
            P(FSDP, None),
            P(FSDP, None),
            P(None, None, FSDP),
        ),
        out_specs=(
            P(FSDP, CTX, None),
            P(FSDP, CTX, None),
            P((CTX, FSDP), None),
            P((CTX, FSDP), None),
            P(CTX, None, FSDP),
            P((CTX, FSDP)),
            P((CTX, FSDP)),
        ),
        check_vma=False,
    )
```
